32 devices in a mesh: dp: 4 (over x, core), fsdp: 8 (over z, y).
Axes of the slice: x: 2, y: 2, z: 4, core: 2. Of those that a mesh axis runs over, the one named last changes fastest.
Arguments:
- tokens: bfloat16 [16384, 768], P(('dp', 'fsdp')), may hold values from -6 to 6
- seg_ids: int32 [16384], P(('dp', 'fsdp')), may hold values from 0 to 63, never falling along the last dimension, each value on 1 to 1024 neighbouring positions
- out_grad: bfloat16 [16384, 768], P(('dp', 'fsdp')), may hold values from -6 to 6
- first_gain: bfloat16 [768], P('fsdp'), may hold values from 0.5 to 1.5
- first_bias: bfloat16 [768], P('fsdp'), may hold values from -1.75 to 1.75
- second_gain: bfloat16 [768], P('fsdp'), may hold values from 0.5 to 1.5
- second_bias: bfloat16 [768], P('fsdp'), may hold values from -1.75 to 1.75
- qkv_weight: bfloat16 [768, 2304], P('fsdp'), may hold values from -0.21875 to 0.21875
- qkv_bias: bfloat16 [2304], P('fsdp'), may hold values from -1.75 to 1.75
- dense_weight: bfloat16 [768, 768], P('fsdp'), may hold values from -1.25 to 1.25
- up_weight: bfloat16 [768, 3072], P('fsdp'), may hold values from -0.21875 to 0.21875
- up_bias: bfloat16 [3072], P('fsdp'), may hold values from -1.75 to 1.75
- down_weight: bfloat16 [3072, 768], P('fsdp'), may hold values from -0.109375 to 0.109375
- out_bias: bfloat16 [768], P('fsdp'), may hold values from -1.75 to 1.75
Outputs:
- output: bfloat16 [16384, 768], P(('dp', 'fsdp'))
- input_grad: bfloat16 [16384, 768], P(('dp', 'fsdp'))
- first_gain_grad: float32 [768], P('fsdp')
- first_bias_grad: float32 [768], P('fsdp')
- second_gain_grad: float32 [768], P('fsdp')
- second_bias_grad: float32 [768], P('fsdp')
- qkv_weight_grad: float32 [768, 2304], P('fsdp')
- qkv_bias_grad: float32 [2304], P('fsdp')
- dense_weight_grad: float32 [768, 768], P('fsdp')
- up_weight_grad: float32 [768, 3072], P('fsdp')
- up_bias_grad: float32 [3072], P('fsdp')
- down_weight_grad: float32 [3072, 768], P('fsdp')
- out_bias_grad: float32 [768], P('fsdp')
- doc_norms: float32 [64], replicated
The draws below stay inside these ranges and needn't reach their ends.
Inputs may be any that keep to these rules, and one draw needn't show every extreme that they name: seg_ids never falls along the stream; each document has 1 to 1024 tokens, one exactly 1024; every number below 64 occurs.
All inputs are finite; a program needn't handle non-finite values.
Results may differ from the reference program's by a relative error of at most 0.0093.
Values may be sent and summed in bfloat16 or wider, within the bound.
A program may use at most 128 MiB of HBM per device.

```python
import math
import jax
import jax.numpy as jnp
import numpy as np
from jax import lax

D = 768
H = 12
HD = 64
FF = 3072
ROT = 16
ROW = 2048
TOK_DEV = 512
DOC_MOST = 1024
TOKENS = 16384
DOCS = 64


def block_scale(stream_key, extent, cuts, least, largest):
    def one(axis_at, blocks):
        heights = jax.random.uniform(jax.random.fold_in(jax.random.fold_in(stream_key, 6), axis_at), (blocks,), jnp.float32, least / len(cuts), largest / len(cuts))
        return jnp.repeat(jnp.exp(heights), extent[axis_at] // blocks).reshape((-1,) + (1,) * (len(extent) - axis_at - 1))

    level = one(*cuts[0])
    for cut in cuts[1:]:
        level = level * one(*cut)
    return level


def profile(number_of, total, limit, lean):
    loads = [(1 << 20) // math.isqrt(standing ** lean) + 1 for standing in range(2, number_of + 1)]
    surplus, given = total - limit - (number_of - 1), [1] * (number_of - 1)
    while surplus > 0:
        candidates = [i for i in range(number_of - 1) if given[i] < limit]
        pool, remaining = sum([loads[i] for i in candidates]), surplus
        for i in candidates:
            more = min(limit - given[i], max(1, remaining * loads[i] // pool), surplus)
            given[i] = given[i] + more
            surplus = surplus - more
    return np.array([limit] + given)


def uneven_parts(key, amount, total, most, lean):
    if amount == 2:
        one = jax.random.randint(key, (), max(1, total - most), min(most, total - 1) + 1)
        return jnp.stack([one, total - one])
    sizes = jnp.asarray(profile(amount, total, most, lean), jnp.int32)
    couples = (amount - 1) // 2
    giver, sink = sizes[1:1 + 2 * couples:2], sizes[2:2 + 2 * couples:2]
    room = jnp.minimum(giver - 1, most - sink)
    shifted = jax.random.randint(jax.random.fold_in(key, 1), (couples,), 0, 1 << 20) % (room + 1)
    sizes = sizes.at[1:1 + 2 * couples:2].set(giver - shifted).at[2:2 + 2 * couples:2].set(sink + shifted)
    return sizes[jax.random.permutation(jax.random.fold_in(key, 2), amount)]


def normal_values(key, extent, scale, limit, shards=(), kind=jnp.bfloat16):
    loudness = block_scale(key, extent, shards, -0.22, 0.18) if shards else 1.0
    array = jax.random.normal(key, extent, jnp.float32) * scale * loudness
    return jnp.minimum(jnp.maximum(array, -limit), limit).astype(kind)


def setup_inputs(seed: int = 0) -> dict:
    keys = jax.random.split(jax.random.key(seed), 15)
    tokens = normal_values(keys[0], (TOKENS, D), 1.0, 6.0, ((0, 32),))
    seg_ids = jnp.searchsorted(jnp.cumsum(uneven_parts(keys[1], DOCS, TOKENS, DOC_MOST, 2)), jnp.arange(TOKENS), side="right").astype(jnp.int32)
    out_grad = normal_values(keys[2], (TOKENS, D), 1.0, 6.0, ((0, 32),))
    first_gain = jnp.clip(1.0 + 0.1 * jax.random.normal(keys[3], (D,), jnp.float32), 0.5, 1.5).astype(jnp.bfloat16)
    first_bias = normal_values(keys[4], (D,), 0.3, 1.75, ((0, 8),))
    second_gain = jnp.clip(1.0 + 0.1 * jax.random.normal(keys[5], (D,), jnp.float32), 0.5, 1.5).astype(jnp.bfloat16)
    second_bias = normal_values(keys[6], (D,), 0.3, 1.75, ((0, 8),))
    qkv_weight = normal_values(keys[7], (D, 3 * D), D ** -0.5, 0.21875, ((0, 8),))
    qkv_bias = normal_values(keys[8], (3 * D,), 0.3, 1.75, ((0, 8),))
    dense_weight = normal_values(keys[9], (D, D), (D // 32) ** -0.5, 1.25, ((0, 8),))
    up_weight = normal_values(keys[10], (D, FF), D ** -0.5, 0.21875, ((0, 8),))
    up_bias = normal_values(keys[11], (FF,), 0.3, 1.75, ((0, 8),))
    down_weight = normal_values(keys[12], (FF, D), FF ** -0.5, 0.109375, ((0, 8),))
    out_bias = normal_values(keys[13], (D,), 0.3, 1.75, ((0, 8),))
    return {"tokens": tokens, "seg_ids": seg_ids, "out_grad": out_grad, "first_gain": first_gain, "first_bias": first_bias, "second_gain": second_gain, "second_bias": second_bias, "qkv_weight": qkv_weight, "qkv_bias": qkv_bias, "dense_weight": dense_weight, "up_weight": up_weight, "up_bias": up_bias, "down_weight": down_weight, "out_bias": out_bias}


@jax.custom_vjp
def low(v):
    return lax.optimization_barrier(v.astype(jnp.bfloat16)).astype(jnp.float32)

@jax.custom_vjp
def low_back(v):
    return v

def low_keep(v):
    return (low(v), None)

def low_pass(kept, grad):
    return (grad,)

def back_keep(v):
    return (v, None)

def back_low(kept, grad):
    return (low(grad),)
low.defvjp(low_keep, low_pass)
low_back.defvjp(back_keep, back_low)

def product(left, right):
    return jnp.dot(left, right, precision=lax.Precision.HIGHEST)

def layer_norm(values, gain, bias):
    middle = lax.optimization_barrier(jnp.mean(values, -1, keepdims=True))
    centred = values - middle
    factor = lax.rsqrt(lax.optimization_barrier(jnp.mean(centred * centred, -1, keepdims=True)) + 1e-05)
    return centred * factor * gain + bias

def rotary_tables(positions):
    half = ROT // 2
    inverse = 10000.0 ** (-(2.0 * jnp.arange(half, dtype=jnp.float32)) / ROT)
    angles = positions.astype(jnp.float32)[:, None] * inverse[None, :]
    cosine = jnp.cos(angles)
    sine = jnp.sin(angles)
    return (jnp.concatenate([cosine, cosine], -1), jnp.concatenate([sine, sine], -1))

def rotate(values, cosine, sine):
    half = ROT // 2
    part = values[..., :ROT]
    turned = jnp.concatenate([-part[..., half:], part[..., :half]], -1)
    moved = part * cosine[:, None, :] + turned * sine[:, None, :]
    return jnp.concatenate([moved, values[..., ROT:]], -1)

def forward(stream, gain_first, shift_first, gain_second, shift_second, qkv_mat, qkv_add, dense_mat, up_mat, up_add, down_mat, out_add, segment):
    count_rows = stream.shape[0]
    first_in = low(layer_norm(stream, gain_first, shift_first))
    second_in = low(layer_norm(stream, gain_second, shift_second))
    projected = low_back(product(first_in, qkv_mat) + qkv_add).reshape(count_rows, H, 3, HD)
    positions = jnp.arange(count_rows, dtype=jnp.int32)
    cosine, sine = rotary_tables(positions % ROW)
    scale = 1.0 / math.sqrt(HD)
    query = low(rotate(projected[:, :, 0], cosine, sine) * scale)
    key = low(rotate(projected[:, :, 1], cosine, sine))
    value = low(projected[:, :, 2])
    width = min(512, TOK_DEV)
    padding = jnp.zeros((DOC_MOST, H, HD), jnp.float32)
    key_padded = jnp.concatenate([padding, key], 0)
    value_padded = jnp.concatenate([padding, value], 0)
    segment_padded = jnp.concatenate([jnp.full((DOC_MOST,), -1, jnp.int32), segment.astype(jnp.int32)], 0)

    def block(start):
        query_block = lax.dynamic_slice_in_dim(query, start, width, 0)
        key_block = lax.dynamic_slice_in_dim(key_padded, start, width + DOC_MOST, 0)
        value_block = lax.dynamic_slice_in_dim(value_padded, start, width + DOC_MOST, 0)
        query_doc = lax.dynamic_slice_in_dim(segment.astype(jnp.int32), start, width, 0)
        key_doc = lax.dynamic_slice_in_dim(segment_padded, start, width + DOC_MOST, 0)
        query_pos = start + jnp.arange(width, dtype=jnp.int32)
        key_pos = start - DOC_MOST + jnp.arange(width + DOC_MOST, dtype=jnp.int32)
        allowed = (query_doc[:, None] == key_doc[None, :]) & (key_pos[None, :] <= query_pos[:, None]) & (key_pos[None, :] >= 0)
        scores = low_back(jnp.einsum('qhd,khd->hqk', query_block, key_block, precision=lax.Precision.HIGHEST))
        scores = jnp.where(allowed[None], scores, -1e+30)
        top = lax.optimization_barrier(jnp.max(scores, -1, keepdims=True))
        weights = jnp.where(allowed[None], jnp.exp(scores - top), 0.0)
        weights = weights / lax.optimization_barrier(jnp.sum(weights, -1, keepdims=True))
        return jnp.einsum('hqk,khd->qhd', low(weights), value_block, precision=lax.Precision.HIGHEST)
    starts = jnp.arange(count_rows // width, dtype=jnp.int32) * width
    context = lax.map(jax.checkpoint(block), starts).reshape(count_rows, H * HD)
    context = low(low_back(context))
    pre = low_back(product(second_in, up_mat) + up_add)
    activation = low(jax.nn.gelu(pre, approximate=False))
    result = stream + product(context, dense_mat) + product(activation, down_mat) + out_add
    return (result, activation)

def reference(tokens, seg_ids, out_grad, first_gain, first_bias, second_gain, second_bias, qkv_weight, qkv_bias, dense_weight, up_weight, up_bias, down_weight, out_bias):
    stream = tokens.astype(jnp.float32)
    gain_first = first_gain.astype(jnp.float32)
    shift_first = first_bias.astype(jnp.float32)
    gain_second = second_gain.astype(jnp.float32)
    shift_second = second_bias.astype(jnp.float32)
    qkv_mat = qkv_weight.astype(jnp.float32)
    qkv_add = qkv_bias.astype(jnp.float32)
    dense_mat = dense_weight.astype(jnp.float32)
    up_mat = up_weight.astype(jnp.float32)
    up_add = up_bias.astype(jnp.float32)
    down_mat = down_weight.astype(jnp.float32)
    out_add = out_bias.astype(jnp.float32)

    def run(stream, gain_first, shift_first, gain_second, shift_second, qkv_mat, qkv_add, dense_mat, up_mat, up_add, down_mat, out_add):
        return forward(stream, gain_first, shift_first, gain_second, shift_second, qkv_mat, qkv_add, dense_mat, up_mat, up_add, down_mat, out_add, seg_ids)
    result, pullback, activation = jax.vjp(run, stream, gain_first, shift_first, gain_second, shift_second, qkv_mat, qkv_add, dense_mat, up_mat, up_add, down_mat, out_add, has_aux=True)
    cotangent = out_grad.astype(jnp.float32)
    grads = pullback(cotangent)
    token_norm = lax.optimization_barrier(jnp.sum(activation * activation, -1)) * lax.optimization_barrier(jnp.sum(cotangent * cotangent, -1)) / (FF * D)
    doc_sums = jax.ops.segment_sum(token_norm, seg_ids, DOCS)
    doc_counts = jax.ops.segment_sum(jnp.ones_like(token_norm), seg_ids, DOCS)
    doc_norms = doc_sums / doc_counts
    return (result.astype(jnp.bfloat16), grads[0].astype(jnp.bfloat16), grads[1], grads[2], grads[3], grads[4], grads[5], grads[6], grads[7], grads[8], grads[9], grads[10], grads[11], doc_norms)
```

```python
import functools
import math

import jax
import jax.numpy as jnp
from jax import lax
from jax.experimental import pallas as pl
from jax.experimental.pallas import tpu as pltpu
from jax.sharding import PartitionSpec as P

D = 768
H = 12
HD = 64
FF = 3072
ROT = 16
ROW = 2048
DOC_DEV = 2
LANES = 128
PAIRS = D // LANES
MESH = pl.DeviceIdType.MESH
VMEM_LIMIT = 60 * 1024 * 1024


class Layout:
    def __init__(self, dp, fsdp):
        self.dp, self.fsdp = dp, fsdp
        self.nc = 2
        self.nx = dp // 2
        ny = 1
        while (2 * ny) * (2 * ny) <= fsdp:
            ny *= 2
        self.ny, self.nz = ny, fsdp // ny
        self.sub = max(1, self.nx // 2)
        self.unit = 4 // self.nx
        self.down_unit = 2 // self.sub

    def coords(self):
        d, f = lax.axis_index("dp"), lax.axis_index("fsdp")
        return d // 2, d % 2, f // self.ny, f % self.ny

    def device(self, x, c, z, y):
        return {"dp": x * 2 + c, "fsdp": z * self.ny + y}


def wrap(value, size):
    return lax.rem(value + size, size)


GROUPS = ("att", "up", "down")
CHUNKS = tuple((g, i) for g in range(3) for i in range(3))


def block_shape(lay, group, shard_rows):
    if group < 2:
        return (2, lay.nx, 3, lay.unit, lay.nz, lay.ny, shard_rows, LANES)
    return (3, lay.sub, lay.down_unit, lay.nz, lay.ny, 2, lay.nx // lay.sub, shard_rows, LANES)


def view(lay, ref, group, i, c, x, z, y):
    if group < 2:
        return ref.at[c, x, i, :, z, y]
    if isinstance(x, slice):
        return ref.at[i, :, :, z, y, c, :]
    return ref.at[i, lax.rem(x, lay.sub), :, z, y, c, x // lay.sub]


ALL = slice(None)


def part_shape(lay, group, x_all, z_all, y_all, shard_rows):
    tail = ()
    if z_all:
        tail += (lay.nz,)
    if y_all:
        tail += (lay.ny,)
    if group < 2:
        head = ((lay.nx,) if x_all else ()) + (lay.unit,)
        return head + tail + (shard_rows, LANES)
    if x_all:
        return (lay.sub, lay.down_unit) + tail + (lay.nx // lay.sub, shard_rows, LANES)
    return (lay.down_unit,) + tail + (shard_rows, LANES)


def barrier_with(peers):
    sem = pltpu.get_barrier_semaphore()
    for peer in peers:
        pl.semaphore_signal(sem, inc=1, device_id=peer, device_id_type=MESH)
    pl.semaphore_wait(sem, len(peers))


def line_peers(lay):
    x, c, z, y = lay.coords()
    xs = [lay.device(wrap(x + k, lay.nx), c, z, y) for k in range(1, lay.nx)]
    ys = [lay.device(x, c, z, wrap(y + k, lay.ny)) for k in range(1, lay.ny)]
    zs = [lay.device(x, c, wrap(z + k, lay.nz), y) for k in range(1, lay.nz)]
    cs = [lay.device(x, 1 - c, z, y)]
    return xs, cs, zs, ys


def remote(src, dst, ssem, rsem, device):
    copy = pltpu.make_async_remote_copy(
        src_ref=src, dst_ref=dst, send_sem=ssem, recv_sem=rsem, device_id=device, device_id_type=MESH
    )
    copy.start()
    return copy


def gather_kernel(
    lay, u_att, u_up, u_down, small, tok, seg,
    g_att, g_up, g_down, g_small, tok_halo, seg_halo,
    local_sem, z_s, z_r, y_s, y_r, x_s, x_r, c_s, c_r, sm_s, sm_r, h_s, h_r,
):
    x, c, z, y = lay.coords()
    xs, cs, zs, ys = line_peers(lay)
    total = lay.dp * lay.fsdp
    b = lax.axis_index("dp") * lay.fsdp + lax.axis_index("fsdp")

    def stream(k):
        t = wrap(b + k, total)
        return {"dp": t // lay.fsdp, "fsdp": lax.rem(t, lay.fsdp)}

    around = [stream(2), stream(-2), stream(1), stream(-1)]
    barrier_with(xs + cs + zs + ys + around)
    gs = (g_att, g_up, g_down)
    us = (u_att, u_up, u_down)

    locals_ = [
        pltpu.make_async_copy(u_att.at[c, x], g_att.at[c, x, :, :, z, y], local_sem.at[0]),
        pltpu.make_async_copy(u_up.at[c, x], g_up.at[c, x, :, :, z, y], local_sem.at[1]),
        pltpu.make_async_copy(
            u_down.at[:, lax.rem(x, lay.sub), :, c, x // lay.sub],
            g_down.at[:, lax.rem(x, lay.sub), :, z, y, c, x // lay.sub],
            local_sem.at[2],
        ),
        pltpu.make_async_copy(small, g_small.at[z, y], local_sem.at[3]),
    ]
    for copy in locals_:
        copy.start()
    sends = []
    halo_z = [
        remote(tok, tok_halo.at[0], h_s.at[0], h_r.at[0], around[0]),
        remote(seg, seg_halo.at[0], h_s.at[1], h_r.at[1], around[0]),
        remote(seg, seg_halo.at[1], h_s.at[2], h_r.at[2], around[2]),
    ]
    for copy in locals_:
        copy.wait()
    sends += halo_z
    stage_z, stage_1, stage_2, stage_c = {}, {}, {}, {}
    n = len(CHUNKS)

    def issue_z(t):
        g, i = CHUNKS[t]
        piece = view(lay, gs[g], g, i, c, x, z, y)
        stage_z[t] = [
            remote(piece, piece, z_s.at[t, k], z_r.at[t, k], zs[k]) for k in range(lay.nz - 1)
        ]

    def issue_1(t):
        g, i = CHUNKS[t]
        piece = view(lay, gs[g], g, i, c, x, ALL, y)
        peers, ss, rs = (ys, y_s, y_r) if i < 2 else (xs, x_s, x_r)
        stage_1[t] = [remote(piece, piece, ss.at[t, k], rs.at[t, k], p) for k, p in enumerate(peers)]

    def issue_2(t):
        g, i = CHUNKS[t]
        if i < 2:
            piece = view(lay, gs[g], g, i, c, x, ALL, ALL)
            peers, ss, rs = xs, x_s, x_r
        else:
            piece = view(lay, gs[g], g, i, c, ALL, ALL, y)
            peers, ss, rs = ys, y_s, y_r
        stage_2[t] = [remote(piece, piece, ss.at[t, k], rs.at[t, k], p) for k, p in enumerate(peers)]

    def issue_c(t):
        g, i = CHUNKS[t]
        piece = view(lay, gs[g], g, i, c, ALL, ALL, ALL)
        stage_c[t] = [remote(piece, piece, c_s.at[t], c_r.at[t], cs[0])]

    def arrived(copies):
        for copy in copies:
            copy.wait_recv()
        sends.extend(copies)

    for t in range(n + 4):
        if t < n:
            issue_z(t)
        if t == 0:
            small_z = [
                remote(g_small.at[z, y], g_small.at[z, y], sm_s.at[k], sm_r.at[k], zs[k])
                for k in range(lay.nz - 1)
            ]
        if t == 1:
            arrived(small_z)
            small_y = [
                remote(
                    g_small.at[:, y], g_small.at[:, y],
                    sm_s.at[lay.nz - 1 + k], sm_r.at[lay.nz - 1 + k], ys[k],
                )
                for k in range(lay.ny - 1)
            ]
            halo_z[0].wait_recv()
            halo_z[1].wait_recv()
            halo_z[2].wait_recv()
            even = lax.rem(b, 2) == 0
            own = pltpu.make_async_remote_copy(
                src_ref=tok, dst_ref=tok_halo.at[1], send_sem=h_s.at[3], recv_sem=h_r.at[3],
                device_id=around[2], device_id_type=MESH,
            )
            passed = pltpu.make_async_remote_copy(
                src_ref=tok_halo.at[0], dst_ref=tok_halo.at[1], send_sem=h_s.at[3],
                recv_sem=h_r.at[3], device_id=around[3], device_id_type=MESH,
            )

            @pl.when(even)
            def _():
                own.start()

            @pl.when(jnp.logical_not(even))
            def _():
                passed.start()

        if 0 <= t - 1 < n:
            arrived(stage_z[t - 1])
            issue_1(t - 1)
        if 0 <= t - 2 < n:
            arrived(stage_1[t - 2])
            issue_2(t - 2)
        if 0 <= t - 3 < n:
            arrived(stage_2[t - 3])
            issue_c(t - 3)
        if 0 <= t - 4 < n:
            arrived(stage_c[t - 4])
    arrived(small_y)
    own.wait()
    for copy in sends:
        copy.wait_send()


def hbm(count):
    return [pl.BlockSpec(memory_space=pltpu.HBM)] * count


def dma(*shape):
    return pltpu.SemaphoreType.DMA(shape)


def gather(lay, u_att, u_up, u_down, small, tok, seg):
    r = u_att.shape[-2]
    n = len(CHUNKS)
    bf = jnp.bfloat16
    outs = (
        jax.ShapeDtypeStruct(block_shape(lay, 0, r), bf),
        jax.ShapeDtypeStruct(block_shape(lay, 1, r), bf),
        jax.ShapeDtypeStruct(block_shape(lay, 2, r), bf),
        jax.ShapeDtypeStruct((lay.nz, lay.ny) + small.shape, bf),
        jax.ShapeDtypeStruct((2,) + tok.shape, bf),
        jax.ShapeDtypeStruct((2,) + seg.shape, jnp.int32),
    )
    lx, ly, lz = max(1, lay.nx - 1), max(1, lay.ny - 1), max(1, lay.nz - 1)
    return pl.pallas_call(
        functools.partial(gather_kernel, lay),
        name="gather_weights",
        out_shape=outs,
        in_specs=hbm(6),
        out_specs=tuple(hbm(6)),
        scratch_shapes=[
            dma(4), dma(n, lz), dma(n, lz), dma(n, ly), dma(n, ly), dma(n, lx), dma(n, lx),
            dma(n), dma(n), dma(lz + ly), dma(lz + ly), dma(4), dma(4),
        ],
        compiler_params=pltpu.CompilerParams(collective_id=0, has_side_effects=True),
    )(u_att, u_up, u_down, small, tok, seg)


def reduce_kernel(
    lay, p_att, p_up, p_down, vec,
    f_att, f_up, f_down, vec_out,
    ca, ra1, rb1, ra2, rb2, ra3, v_c, v_x, v_y, v_z, *sems,
):
    (c_s, c_r, x_s, x_r, y_s, y_r, z_s, z_r, fx_s, fx_r, fc_s, fc_r, v_s, v_r) = sems
    x, c, z, y = lay.coords()
    xs, cs, zs, ys = line_peers(lay)
    barrier_with(xs + cs + zs + ys)
    ps = (p_att, p_up, p_down)
    fs = (f_att, f_up, f_down)
    n = len(CHUNKS)
    sends = []
    bf = jnp.bfloat16
    f32 = jnp.float32

    def arrived(copies):
        for copy in copies:
            copy.wait_recv()
        sends.extend(copies)

    v_c[c] = vec[...]
    vec_stage = [remote(v_c.at[c], v_c.at[c], v_s.at[0], v_r.at[0], cs[0])]
    arrived(vec_stage)
    v_x[x] = v_c[0] + v_c[1]
    vec_stage = [
        remote(v_x.at[x], v_x.at[x], v_s.at[1 + k], v_r.at[1 + k], p) for k, p in enumerate(xs)
    ]
    state = {"stage": vec_stage}

    def vec_step(step):
        if step == 0:
            arrived(state["stage"])
            v_y[y] = sum([v_x[k] for k in range(1, lay.nx)], v_x[0])
            at = lay.nx
            state["stage"] = [
                remote(v_y.at[y], v_y.at[y], v_s.at[at + k], v_r.at[at + k], p)
                for k, p in enumerate(ys)
            ]
        elif step == 1:
            arrived(state["stage"])
            v_z[z] = sum([v_y[k] for k in range(1, lay.ny)], v_y[0])
            at = lay.nx + lay.ny - 1
            state["stage"] = [
                remote(v_z.at[z], v_z.at[z], v_s.at[at + k], v_r.at[at + k], p)
                for k, p in enumerate(zs)
            ]
        elif step == 2:
            arrived(state["stage"])
            vec_out[...] = sum([v_z[k] for k in range(1, lay.nz)], v_z[0])

    def add_into(dst, srcs):
        lead = dst.shape[:-2]
        count = math.prod(lead)

        def body(j, carry):
            index = []
            rest = j
            for size in reversed(lead):
                index.append(lax.rem(rest, size))
                rest = rest // size
            index = tuple(reversed(index))
            total = dst[index].astype(f32)
            for src in srcs:
                total = total + src[index].astype(f32)
            dst[index] = total.astype(bf)
            return carry

        lax.fori_loop(0, count, body, 0)

    st_c, st_1, st_2, st_3, st_x, st_f = {}, {}, {}, {}, {}, {}

    def recv(bufs, t):
        g, i = CHUNKS[t]
        return bufs, g, i

    def buf(ref, g, i):
        return ref[g].at[i]

    def issue_core(t):
        g, i = CHUNKS[t]
        st_c[t] = [
            remote(
                view(lay, ps[g], g, i, 1 - c, ALL, ALL, ALL), buf(ca, g, i),
                c_s.at[t], c_r.at[t], cs[0],
            )
        ]

    def issue_1(t):
        g, i = CHUNKS[t]
        add_into(view(lay, ps[g], g, i, c, ALL, ALL, ALL), [buf(ca, g, i)])
        if i < 2:
            st_1[t] = [
                remote(
                    view(lay, ps[g], g, i, c, wrap(x + 1 + k, lay.nx), ALL, ALL),
                    buf(ra1, g, i).at[k], x_s.at[t, k], x_r.at[t, k], p,
                )
                for k, p in enumerate(xs)
            ]
        else:
            st_1[t] = [
                remote(
                    view(lay, ps[g], g, i, c, ALL, ALL, wrap(y + 1 + k, lay.ny)),
                    buf(rb1, g, 0).at[k], y_s.at[t, k], y_r.at[t, k], p,
                )
                for k, p in enumerate(ys)
            ]

    def issue_2(t):
        g, i = CHUNKS[t]
        if i < 2:
            add_into(
                view(lay, ps[g], g, i, c, x, ALL, ALL),
                [buf(ra1, g, i).at[k] for k in range(lay.nx - 1)],
            )
            st_2[t] = [
                remote(
                    view(lay, ps[g], g, i, c, x, ALL, wrap(y + 1 + k, lay.ny)),
                    buf(ra2, g, i).at[k], y_s.at[t, k], y_r.at[t, k], p,
                )
                for k, p in enumerate(ys)
            ]
        else:
            add_into(
                view(lay, ps[g], g, i, c, ALL, ALL, y),
                [buf(rb1, g, 0).at[k] for k in range(lay.ny - 1)],
            )
            st_2[t] = [
                remote(
                    view(lay, ps[g], g, i, c, wrap(x + 1 + k, lay.nx), ALL, y),
                    buf(rb2, g, 0).at[k], x_s.at[t, k], x_r.at[t, k], p,
                )
                for k, p in enumerate(xs)
            ]

    def issue_3(t):
        g, i = CHUNKS[t]
        second = (
            [buf(ra2, g, i).at[k] for k in range(lay.ny - 1)]
            if i < 2
            else [buf(rb2, g, 0).at[k] for k in range(lay.nx - 1)]
        )
        add_into(view(lay, ps[g], g, i, c, x, ALL, y), second)
        st_3[t] = [
            remote(
                view(lay, ps[g], g, i, c, x, wrap(z + 1 + k, lay.nz), y),
                buf(ra3, g, i).at[k], z_s.at[t, k], z_r.at[t, k], p,
            )
            for k, p in enumerate(zs)
        ]

    def final(ref, g, i, cc, xx):
        if g < 2:
            return ref.at[cc, xx, i]
        if isinstance(xx, slice):
            return ref.at[i, :, :, cc, :]
        return ref.at[i, lax.rem(xx, lay.sub), :, cc, xx // lay.sub]

    def issue_x(t):
        g, i = CHUNKS[t]
        own = view(lay, ps[g], g, i, c, x, z, y)
        srcs = [buf(ra3, g, i).at[k] for k in range(lay.nz - 1)]
        out = final(fs[g], g, i, c, x)
        for u in range(own.shape[0]):
            total = own[u].astype(f32)
            for src in srcs:
                total = total + src[u].astype(f32)
            out[u] = total.astype(bf)
        st_x[t] = [remote(out, out, fx_s.at[t, k], fx_r.at[t, k], p) for k, p in enumerate(xs)]

    def issue_f(t):
        g, i = CHUNKS[t]
        out = final(fs[g], g, i, c, ALL)
        st_f[t] = [remote(out, out, fc_s.at[t], fc_r.at[t], cs[0])]

    for t in range(n + 6):
        if t < n:
            issue_core(t)
        if 0 <= t - 1 < n:
            arrived(st_c[t - 1])
            issue_1(t - 1)
        if 0 <= t - 2 < n:
            arrived(st_1[t - 2])
            issue_2(t - 2)
        if 0 <= t - 3 < n:
            arrived(st_2[t - 3])
            issue_3(t - 3)
        if 0 <= t - 4 < n:
            arrived(st_3[t - 4])
            issue_x(t - 4)
        if 0 <= t - 5 < n:
            arrived(st_x[t - 5])
            issue_f(t - 5)
        if 0 <= t - 6 < n:
            arrived(st_f[t - 6])
        if 1 <= t <= 3:
            vec_step(t - 1)
    for copy in sends:
        copy.wait_send()


def final_shape(lay, group, r):
    if group < 2:
        return (2, lay.nx, 3, lay.unit, r, LANES)
    return (3, lay.sub, lay.down_unit, 2, lay.nx // lay.sub, r, LANES)


def reduce(lay, p_att, p_up, p_down, vec):
    r = p_att.shape[-2]
    n = len(CHUNKS)
    bf = jnp.bfloat16
    outs = tuple(jax.ShapeDtypeStruct(final_shape(lay, g, r), bf) for g in range(3)) + (
        jax.ShapeDtypeStruct(vec.shape, vec.dtype),
    )
    lx, ly, lz = max(1, lay.nx - 1), max(1, lay.ny - 1), max(1, lay.nz - 1)

    def bufs(chunks, peers, x_all, z_all, y_all):
        return [
            pltpu.VMEM((chunks,) + peers + part_shape(lay, g, x_all, z_all, y_all, r), bf)
            for g in range(3)
        ]

    scratch = [
        bufs(3, (), True, True, True),
        bufs(2, (lx,), False, True, True),
        bufs(1, (ly,), True, True, False),
        bufs(2, (ly,), False, True, False),
        bufs(1, (lx,), False, True, False),
        bufs(3, (lz,), False, False, False),
    ]
    vecs = [pltpu.VMEM((k,) + vec.shape, jnp.float32) for k in (2, lay.nx, lay.ny, lay.nz)]
    nv = 1 + lay.nx + lay.ny + lay.nz
    sems = [
        dma(n), dma(n), dma(n, lx), dma(n, lx), dma(n, ly), dma(n, ly), dma(n, lz), dma(n, lz),
        dma(n, lx), dma(n, lx), dma(n), dma(n), dma(nv), dma(nv),
    ]
    vmem = [pl.BlockSpec(memory_space=pltpu.VMEM)]
    return pl.pallas_call(
        functools.partial(reduce_kernel, lay),
        name="reduce_grads",
        out_shape=outs,
        in_specs=vmem * 4,
        out_specs=tuple(vmem * 4),
        scratch_shapes=scratch + vecs + sems,
        compiler_params=pltpu.CompilerParams(
            collective_id=1, has_side_effects=True, vmem_limit_bytes=VMEM_LIMIT
        ),
    )(p_att, p_up, p_down, vec)


NT = (((1,), (1,)), ((), ()))
NN = (((1,), (0,)), ((), ()))


def attention_kernel(rows, least_ref, qseg_ref, kseg_ref, q_ref, k_ref, v_ref, do_ref,
                     ctx_ref, dq_ref, dk_ref, dv_ref, bias, dk_acc, dv_acc):
    f32, bf = jnp.float32, jnp.bfloat16
    span = 3 * rows

    @pl.when(pl.program_id(0) == 0)
    def _():
        key_at = lax.broadcasted_iota(jnp.int32, (span, rows), 0)
        query_at = lax.broadcasted_iota(jnp.int32, (span, rows), 1) + 2 * rows
        allowed = (kseg_ref[...] == qseg_ref[...]) & (key_at <= query_at) & (key_at >= least_ref[0])
        bias[...] = jnp.where(allowed, 0.0, -1e30)

    tile = 256
    lane = lax.broadcasted_iota(jnp.int32, (tile, LANES), 1)
    v_t = v_ref[...].T
    k_t = k_ref[...].T
    do_t = do_ref[...].astype(f32).T
    dk_acc[...] = jnp.zeros_like(dk_acc)
    dv_acc[...] = jnp.zeros_like(dv_acc)
    for t in range(rows // tile):
        cols = slice(t * tile, (t + 1) * tile)
        kl = 2 * rows + (t + 1) * tile
        ctx_t, dq_t = [], []
        for hh in range(2):
            mine = (lane // HD) == hh
            zero = jnp.zeros((), bf)
            qm = jnp.where(mine, q_ref[cols, :], zero)
            dom = jnp.where(mine, do_ref[cols, :], zero)
            st = lax.dot_general(k_ref[:kl, :], qm, NT, preferred_element_type=f32)
            st = st + bias[:kl, cols]
            top = jnp.max(st, 0, keepdims=True)
            p = jnp.exp(st - top)
            w = p * (1.0 / jnp.sum(p, 0, keepdims=True))
            wb = w.astype(bf)
            half = slice(hh * HD, (hh + 1) * HD)
            o_t = lax.dot_general(v_t[half, :kl], wb, NN, preferred_element_type=f32)
            dp = lax.dot_general(v_ref[:kl, :], dom, NT, preferred_element_type=f32)
            delta = jnp.sum(o_t * do_t[half, cols], 0, keepdims=True)
            ds = (w * (dp - delta)).astype(bf)
            ctx_t.append(o_t)
            dq_t.append(lax.dot_general(k_t[half, :kl], ds, NN, preferred_element_type=f32))
            dk_acc[:kl, :] += lax.dot_general(ds, qm, NN, preferred_element_type=f32)
            dv_acc[:kl, :] += lax.dot_general(wb, dom, NN, preferred_element_type=f32)
        ctx_ref[cols, :] = jnp.concatenate(ctx_t, 0).T.astype(bf)
        dq_ref[cols, :] = jnp.concatenate(dq_t, 0).T
    dk_ref[...] = dk_acc[...]
    dv_ref[...] = dv_acc[...]


def attention(least, qseg, kseg, q, k, v, do):
    rows = q.shape[0]
    span = 3 * rows
    f32 = jnp.float32
    own = pl.BlockSpec((rows, LANES), lambda p: (0, p))
    wide = pl.BlockSpec((span, LANES), lambda p: (0, p))
    return pl.pallas_call(
        functools.partial(attention_kernel, rows),
        name="attention",
        grid=(PAIRS,),
        out_shape=(
            jax.ShapeDtypeStruct((rows, D), jnp.bfloat16),
            jax.ShapeDtypeStruct((rows, D), f32),
            jax.ShapeDtypeStruct((span, D), f32),
            jax.ShapeDtypeStruct((span, D), f32),
        ),
        in_specs=[
            pl.BlockSpec(memory_space=pltpu.SMEM),
            pl.BlockSpec((1, rows), lambda p: (0, 0)),
            pl.BlockSpec((span, 1), lambda p: (0, 0)),
            own, wide, wide, own,
        ],
        out_specs=(own, own, wide, wide),
        scratch_shapes=[
            pltpu.VMEM((span, rows), f32), pltpu.VMEM((span, LANES), f32), pltpu.VMEM((span, LANES), f32),
        ],
        compiler_params=pltpu.CompilerParams(vmem_limit_bytes=VMEM_LIMIT),
    )(least, qseg, kseg, q, k, v, do)


def norm_parts(values):
    middle = jnp.mean(values, -1, keepdims=True)
    centred = values - middle
    factor = lax.rsqrt(jnp.mean(centred * centred, -1, keepdims=True) + 1e-05)
    return centred * factor, factor


def norm_back(grad, gain, normed, factor):
    inner = grad * gain
    return factor * (
        inner
        - jnp.mean(inner, -1, keepdims=True)
        - normed * jnp.mean(inner * normed, -1, keepdims=True)
    )


def rotary_tables(positions):
    half = ROT // 2
    inverse = 10000.0 ** (-(2.0 * jnp.arange(half, dtype=jnp.float32)) / ROT)
    angles = positions.astype(jnp.float32)[:, None] * inverse[None, :]
    cosine = jnp.cos(angles)
    sine = jnp.sin(angles)
    return (jnp.concatenate([cosine, cosine], -1), jnp.concatenate([sine, sine], -1))


def rotate(values, cosine, sine):
    half = ROT // 2
    part = values[..., :ROT]
    turned = jnp.concatenate([-part[..., half:], part[..., :half]], -1)
    moved = part * cosine[:, None, :] + turned * sine[:, None, :]
    return jnp.concatenate([moved, values[..., ROT:]], -1)


def rotate_back(grad, cosine, sine):
    half = ROT // 2
    part = grad[..., :ROT]
    upper = part * sine[:, None, :]
    turned = jnp.concatenate([upper[..., half:], -upper[..., :half]], -1)
    moved = part * cosine[:, None, :] + turned
    return jnp.concatenate([moved, grad[..., ROT:]], -1)


def gelu_slope(pre):
    return 0.5 * (1.0 + lax.erf(pre / math.sqrt(2.0))) + pre * jnp.exp(
        -0.5 * pre * pre
    ) / math.sqrt(2.0 * math.pi)


def to_blocks(matrix, rows):
    return matrix.reshape(rows, -1, LANES).transpose(1, 0, 2)


def per_device(
    lay, tokens, seg_ids, out_grad, first_gain, first_bias, second_gain, second_bias,
    qkv_weight, qkv_bias, dense_weight, up_weight, up_bias, down_weight, out_bias,
):
    f32, bf = jnp.float32, jnp.bfloat16
    rows = tokens.shape[0]
    r = qkv_weight.shape[0]
    fsdp = lay.fsdp
    qkv_kinds = qkv_weight.reshape(r, H, 3, HD).transpose(0, 2, 1, 3).reshape(r, 3 * D)
    att_shape = block_shape(lay, 0, r)
    u_att = to_blocks(jnp.concatenate([qkv_kinds, dense_weight], 1), r)
    u_att = u_att.reshape(att_shape[:4] + att_shape[6:])
    u_up = to_blocks(up_weight, r).reshape(att_shape[:4] + att_shape[6:])
    down_shape = block_shape(lay, 2, r)
    u_down = (
        down_weight.reshape(4, r, PAIRS, LANES).transpose(2, 0, 1, 3)
        .reshape(down_shape[:3] + down_shape[5:])
    )
    vectors = (first_gain, first_bias, second_gain, second_bias, out_bias, qkv_bias, up_bias)
    sizes = [v.shape[0] for v in vectors]
    small = jnp.concatenate(vectors)
    small = jnp.pad(small, (0, 16 * LANES - small.shape[0])).reshape(16, LANES)
    seg_block = seg_ids.reshape(rows // LANES, LANES)
    g_att, g_up, g_down, g_small, tok_halo, seg_halo = gather(
        lay, u_att, u_up, u_down, small, tokens, seg_block
    )
    g_small = g_small.reshape(fsdp, 16 * LANES)
    full, at = [], 0
    for size in sizes:
        full.append(g_small[:, at : at + size].reshape(-1).astype(f32))
        at += size
    gain_first, shift_first, gain_second, shift_second, out_add, qkv_add, up_add = full
    att_mat = g_att.reshape(24, D, LANES).transpose(1, 0, 2).reshape(D, 4 * D)
    up_mat = g_up.reshape(24, D, LANES).transpose(1, 0, 2).reshape(D, FF)
    down_mat = g_down.reshape(PAIRS, FF, LANES).transpose(1, 0, 2).reshape(FF, D)
    q_mat, k_mat, v_mat, dense_mat = (att_mat[:, k * D : (k + 1) * D] for k in range(4))
    q_add, k_add, v_add = (qkv_add.reshape(H, 3, HD)[:, k].reshape(D) for k in range(3))

    block = lax.axis_index(("dp", "fsdp"))
    stream = tokens.astype(f32)
    tok_all = jnp.concatenate([tok_halo[0], tok_halo[1], tokens], 0).astype(f32)
    normed_all, factor_all = norm_parts(tok_all)
    first_all = (normed_all * gain_first + shift_first).astype(bf)
    normed, factor = normed_all[2 * rows :], factor_all[2 * rows :]
    first_in = first_all[2 * rows :]
    second_in = (normed * gain_second + shift_second).astype(bf)

    def mm(a, b):
        return jnp.dot(a, b, preferred_element_type=f32)

    key_pos = (block - 2) * rows + jnp.arange(3 * rows, dtype=jnp.int32)
    cosine, sine = rotary_tables((key_pos + ROW) % ROW)
    own_cos, own_sin = cosine[2 * rows :], sine[2 * rows :]
    scale = 1.0 / math.sqrt(HD)
    q_proj = (mm(first_in, q_mat) + q_add).reshape(rows, H, HD)
    query = (rotate(q_proj, own_cos, own_sin) * scale).astype(bf).reshape(rows, D)
    k_proj = (mm(first_all, k_mat) + k_add).reshape(3 * rows, H, HD)
    key = rotate(k_proj, cosine, sine).astype(bf).reshape(3 * rows, D)
    value = (mm(first_all, v_mat) + v_add).astype(bf)
    context_grad = lax.dot_general(out_grad, dense_mat, NT, preferred_element_type=f32).astype(bf)
    seg_all = jnp.concatenate([seg_halo[0], seg_halo[1], seg_block], 0).reshape(3 * rows, 1)
    least = jnp.maximum(0, 2 * rows - block * rows).astype(jnp.int32).reshape(1)
    context, dq, dk, dv = attention(
        least, seg_ids.reshape(1, rows), seg_all, query, key, value, context_grad
    )
    pre = mm(second_in, up_mat) + up_add
    activation = jax.nn.gelu(pre, approximate=False).astype(bf)
    result = stream + mm(context, dense_mat) + mm(activation, down_mat) + out_add
    output = result.astype(bf)

    cotangent = out_grad.astype(f32)
    down_grad = mm(activation.T, out_grad)
    dense_grad = mm(context.T, out_grad)
    hidden_grad = lax.dot_general(out_grad, down_mat, NT, preferred_element_type=f32)
    pre_grad = (hidden_grad * gelu_slope(pre)).astype(bf)
    up_grad = mm(second_in.T, pre_grad)
    second_grad = lax.dot_general(pre_grad, up_mat, NT, preferred_element_type=f32)
    dq = rotate_back((dq * scale).reshape(rows, H, HD), own_cos, own_sin).reshape(rows, D).astype(bf)
    dk = rotate_back(dk.reshape(3 * rows, H, HD), cosine, sine).reshape(3 * rows, D).astype(bf)
    dv = dv.astype(bf)
    q_grad = mm(first_in.T, dq)
    k_grad = mm(first_all.T, dk)
    v_grad = mm(first_all.T, dv)
    first_grad_all = lax.dot_general(dk, k_mat, NT, preferred_element_type=f32) + lax.dot_general(
        dv, v_mat, NT, preferred_element_type=f32
    )
    first_grad = first_grad_all[2 * rows :] + lax.dot_general(
        dq, q_mat, NT, preferred_element_type=f32
    )
    devices = lay.dp * fsdp
    for distance in (2, 1):
        low = (2 - distance) * rows
        route = [(i, (i - distance) % devices) for i in range(devices)]
        first_grad = first_grad + lax.ppermute(
            first_grad_all[low : low + rows].astype(bf), ("dp", "fsdp"), route
        ).astype(f32)
    input_grad = (
        cotangent
        + norm_back(first_grad, gain_first, normed, factor)
        + norm_back(second_grad, gain_second, normed, factor)
    ).astype(bf)

    docs = DOC_DEV * devices
    token_norm = (
        jnp.sum(jnp.square(activation.astype(f32)), -1) * jnp.sum(cotangent * cotangent, -1) / (FF * D)
    )
    member = (seg_ids[:, None] == jnp.arange(docs, dtype=jnp.int32)[None, :]).astype(f32)
    doc_sums = jnp.sum(token_norm[:, None] * member, 0)
    doc_counts = jnp.sum(member, 0)
    qkv_bias_grad = jnp.stack(
        [jnp.sum(v.astype(f32), 0).reshape(H, HD) for v in (dq, dk, dv)], 1
    ).reshape(3 * D)
    grads = (
        jnp.sum(first_grad * normed, 0),
        jnp.sum(first_grad, 0),
        jnp.sum(second_grad * normed, 0),
        jnp.sum(second_grad, 0),
        jnp.sum(cotangent, 0),
        qkv_bias_grad,
        jnp.sum(pre_grad.astype(f32), 0),
    )
    vec = jnp.concatenate(grads + (doc_sums, doc_counts))
    count = vec.shape[0]
    vec_rows = -(-count // (8 * LANES)) * 8
    vec = jnp.pad(vec, (0, vec_rows * LANES - count)).reshape(vec_rows, LANES)

    def blocks(matrix, shape):
        return matrix.astype(bf).reshape(matrix.shape[0], -1, LANES).transpose(1, 0, 2).reshape(shape)

    p_att = blocks(jnp.concatenate([q_grad, k_grad, v_grad, dense_grad], 1), att_shape)
    p_up = blocks(up_grad, att_shape)
    p_down = blocks(down_grad, down_shape)
    f_att, f_up, f_down, vec = reduce(lay, p_att, p_up, p_down, vec)
    vec = vec.reshape(-1)
    shard = lax.axis_index("fsdp")
    pieces, at = [], 0
    for size in sizes:
        pieces.append(lax.dynamic_slice_in_dim(vec, at + shard * size, size))
        at += size * fsdp
    totals, counts = vec[at : at + docs], vec[at + docs : at + 2 * docs]
    f_att = f_att.reshape(24, r, LANES).transpose(1, 0, 2).reshape(r, 4 * D).astype(f32)
    qkv_out = f_att[:, : 3 * D].reshape(r, 3, H, HD).transpose(0, 2, 1, 3).reshape(r, 3 * D)
    up_out = f_up.reshape(24, r, LANES).transpose(1, 0, 2).reshape(r, FF).astype(f32)
    down_out = (
        f_down.reshape(PAIRS, 4, r, LANES).transpose(1, 2, 0, 3).reshape(4 * r, D).astype(f32)
    )
    return (
        output,
        input_grad,
        pieces[0],
        pieces[1],
        pieces[2],
        pieces[3],
        qkv_out,
        pieces[5],
        f_att[:, 3 * D :],
        up_out,
        pieces[6],
        down_out,
        pieces[4],
        totals / counts,
    )


def solution(mesh):
    lay = Layout(mesh.shape["dp"], mesh.shape["fsdp"])
    both = P(("dp", "fsdp"))
    split = P("fsdp")
    in_specs = (both, both, both) + (split,) * 11
    out_specs = (both, both) + (split,) * 11 + (P(),)
    return jax.shard_map(
        functools.partial(per_device, lay), mesh=mesh, in_specs=in_specs, out_specs=out_specs,
        check_vma=False,
    )
```

```python
import functools
import math

import jax
import jax.numpy as jnp
from jax import lax
from jax.experimental import pallas as pl
from jax.experimental.pallas import tpu as pltpu
from jax.sharding import PartitionSpec as P

D = 768
H = 12
HD = 64
FF = 3072
ROT = 16
ROW = 2048
DOC_DEV = 2
LANES = 128
PAIRS = D // LANES
MESH = pl.DeviceIdType.MESH
VMEM_LIMIT = 60 * 1024 * 1024


class Layout:
    def __init__(self, dp, fsdp):
        self.dp, self.fsdp = dp, fsdp
        self.nc = 2
        self.nx = dp // 2
        ny = 1
        while (2 * ny) * (2 * ny) <= fsdp:
            ny *= 2
        self.ny, self.nz = ny, fsdp // ny
        self.sub = max(1, self.nx // 2)
        self.unit = 4 // self.nx
        self.down_unit = 2 // self.sub

    def coords(self):
        d, f = lax.axis_index("dp"), lax.axis_index("fsdp")
        return d // 2, d % 2, f // self.ny, f % self.ny

    def device(self, x, c, z, y):
        return {"dp": x * 2 + c, "fsdp": z * self.ny + y}


def wrap(value, size):
    return lax.rem(value + size, size)


CHUNKS = tuple((g, i) for g in range(3) for i in range(3))
ALL = slice(None)


def grad_shape(lay, group, r):
    return (lay.nz, lay.ny, r, 4 * D) if group < 2 else (lay.nz, lay.ny, 4, r, D)


def span_of(lay, group, i, c, x):
    if group < 2:
        width = 512 // lay.nx
        if x is ALL:
            return pl.ds(pl.multiple_of(1024 * i + 512 * c, LANES), 512), None
        return pl.ds(pl.multiple_of(1024 * i + 512 * c + width * x, LANES), width), None
    width = 256 // lay.sub
    if x is ALL:
        return pl.ds(256 * i, 256), pl.ds(2 * c, 2)
    start = 256 * i + width * lax.rem(x, lay.sub)
    return pl.ds(pl.multiple_of(start, LANES), width), 2 * c + x // lay.sub


def view(lay, ref, group, i, c, x, z, y):
    cols, quarter = span_of(lay, group, i, c, x)
    if group < 2:
        return ref.at[z, y, :, cols]
    return ref.at[z, y, quarter, :, cols]


def shard_view(lay, ref, group, i, c, x):
    cols, quarter = span_of(lay, group, i, c, x)
    if group < 2:
        return ref.at[:, cols]
    return ref.at[quarter, :, cols]


def part_shape(lay, group, x_all, z_all, y_all, r):
    lead = ((lay.nz,) if z_all else ()) + ((lay.ny,) if y_all else ())
    if group < 2:
        return lead + (r, 512 if x_all else 512 // lay.nx)
    return lead + ((2, r, 256) if x_all else (r, 256 // lay.sub))


def barrier_with(peers):
    sem = pltpu.get_barrier_semaphore()
    for peer in peers:
        pl.semaphore_signal(sem, inc=1, device_id=peer, device_id_type=MESH)
    pl.semaphore_wait(sem, len(peers))


def line_peers(lay):
    x, c, z, y = lay.coords()
    xs = [lay.device(wrap(x + k, lay.nx), c, z, y) for k in range(1, lay.nx)]
    ys = [lay.device(x, c, z, wrap(y + k, lay.ny)) for k in range(1, lay.ny)]
    zs = [lay.device(x, c, wrap(z + k, lay.nz), y) for k in range(1, lay.nz)]
    cs = [lay.device(x, 1 - c, z, y)]
    return xs, cs, zs, ys


def remote(src, dst, ssem, rsem, device):
    return pltpu.make_async_remote_copy(
        src_ref=src, dst_ref=dst, send_sem=ssem, recv_sem=rsem, device_id=device, device_id_type=MESH
    )


def start(copies):
    for copy in copies:
        copy.start()


def arrive(copies):
    for copy in copies:
        copy.wait_recv()


def sent(copies):
    for copy in copies:
        copy.wait_send()


def hbm(count):
    return [pl.BlockSpec(memory_space=pltpu.HBM)] * count


def dma(*shape):
    return pltpu.SemaphoreType.DMA(shape)


NT = (((1,), (1,)), ((), ()))
NN = (((1,), (0,)), ((), ()))
F32 = jnp.float32
BF = jnp.bfloat16


def mm(a, b, dims=NN):
    return lax.dot_general(a, b, dims, preferred_element_type=F32)


def norm_parts(values):
    middle = jnp.mean(values, -1, keepdims=True)
    centred = values - middle
    factor = lax.rsqrt(jnp.mean(centred * centred, -1, keepdims=True) + 1e-05)
    return centred * factor, factor


class Gather:
    def __init__(self, lay, gs, sems):
        (z_s, z_r, y_s, y_r, x_s, x_r, c_s, c_r) = sems
        x, c, z, y = lay.coords()
        xs, cs, zs, ys = line_peers(lay)
        self.stages = []
        for t, (g, i) in enumerate(CHUNKS):
            by_y, by_x = (ys, y_s, y_r), (xs, x_s, x_r)
            first, second = (by_y, by_x) if i < 2 else (by_x, by_y)
            middle = (x, ALL, ALL) if i < 2 else (ALL, ALL, y)
            steps = [
                ((zs, z_s, z_r), (x, z, y)),
                (first, (x, ALL, y)),
                (second, middle),
            ]
            stages = []
            for (peers, ss, rs), (px, pz, py) in steps:
                piece = view(lay, gs[g], g, i, c, px, pz, py)
                stages.append(
                    [remote(piece, piece, ss.at[t, k], rs.at[t, k], p) for k, p in enumerate(peers)]
                )
            piece = view(lay, gs[g], g, i, c, ALL, ALL, ALL)
            stages.append([remote(piece, piece, c_s.at[t], c_r.at[t], cs[0])])
            self.stages.append(stages)

    def issue(self, t, stage):
        start(self.stages[t][stage])

    def pass_on(self, t, stage):
        arrive(self.stages[t][stage - 1])
        start(self.stages[t][stage])

    def done(self, t):
        arrive(self.stages[t][3])

    def drain(self):
        for stages in self.stages:
            for copies in stages:
                sent(copies)


def rope(u, cos, low, high):
    return u * cos + pltpu.roll(u, LANES - 8, 1) * low + pltpu.roll(u, 8, 1) * high


def front_kernel(
    lay, rows,
    u_att, u_up, u_down, small, tok, grad, seg,
    g_up, g_down, p_att, fg_prev, fg_own, attn_out, vectors, up_add, att_sums,
    g_att, g_small, tok_halo, seg_halo, first_all, first_t, q_s, k_s, v_s, do_s, ctx_s, ctx_t,
    dq_s, dk_s, dv_s, cos_s, low_s, high_s, bias, dk_acc, dv_acc, qkv_add,
    local_sem, z_s, z_r, y_s, y_r, x_s, x_r, c_s, c_r, sm_s, sm_r, h_s, h_r,
):
    span = 3 * rows
    r = u_att.shape[0]
    x, c, z, y = lay.coords()
    xs, cs, zs, ys = line_peers(lay)
    total = lay.dp * lay.fsdp
    b = lax.axis_index("dp") * lay.fsdp + lax.axis_index("fsdp")

    def stream(k):
        t = wrap(b + k, total)
        return {"dp": t // lay.fsdp, "fsdp": lax.rem(t, lay.fsdp)}

    around = [stream(2), stream(-2), stream(1), stream(-1)]
    barrier_with(xs + cs + zs + ys + around)
    gs = (g_att, g_up, g_down)
    us = (u_att, u_up, u_down)
    locals_ = [pltpu.make_async_copy(small, g_small.at[z, y], local_sem.at[9])]
    for t, (g, i) in enumerate(CHUNKS):
        locals_.append(
            pltpu.make_async_copy(
                shard_view(lay, us[g], g, i, c, x), view(lay, gs[g], g, i, c, x, z, y), local_sem.at[t]
            )
        )
    start(locals_)
    even = lax.rem(b, 2) == 0
    half = rows // 2
    halo, own, passed = [], [], []
    for k in range(2):
        part = pl.ds(k * half, half)
        halo.append(remote(tok.at[part], tok_halo.at[0, part], h_s.at[k], h_r.at[k], around[0]))
        own.append(remote(tok.at[part], tok_halo.at[1, part], h_s.at[2 + k], h_r.at[2 + k], around[2]))
        passed.append(
            remote(tok_halo.at[0, part], tok_halo.at[1, part], h_s.at[2 + k], h_r.at[2 + k], around[3])
        )
    segs = [
        remote(seg, seg_halo.at[0], h_s.at[4], h_r.at[4], around[0]),
        remote(seg, seg_halo.at[1], h_s.at[5], h_r.at[5], around[2]),
    ]
    small_z = [
        remote(g_small.at[z, y], g_small.at[z, y], sm_s.at[k], sm_r.at[k], p) for k, p in enumerate(zs)
    ]
    small_y = [
        remote(g_small.at[:, y], g_small.at[:, y], sm_s.at[lay.nz + k], sm_r.at[lay.nz + k], p)
        for k, p in enumerate(ys)
    ]
    net = Gather(lay, gs, (z_s, z_r, y_s, y_r, x_s, x_r, c_s, c_r))

    for copy in locals_:
        copy.wait()
    start(small_z)
    start(segs)
    for t in range(3):
        net.issue(t, 0)
    start(halo)

    @pl.when(even)
    def _():
        start(own)

    def norm_rows(values):
        return norm_parts(values.astype(F32))[0]

    normed = norm_rows(tok[...])
    net.pass_on(0, 1)
    arrive(small_z)
    start(small_y)

    def tables(k, carry):
        at = pl.ds(pl.multiple_of(k * 256, 256), 256)
        lane = lax.broadcasted_iota(jnp.int32, (256, LANES), 1) % HD
        row = lax.broadcasted_iota(jnp.int32, (256, LANES), 0) + k * 256
        place = lax.rem((b - 2) * rows + row + 4 * ROW, ROW).astype(F32)
        rate = jnp.exp((lane % 8).astype(F32) * (-math.log(10000.0) / 8.0))
        angle = place * rate
        sine = jnp.sin(angle)
        cos_s[at, :] = jnp.where(lane < ROT, jnp.cos(angle), 1.0)
        low_s[at, :] = jnp.where(lane < 8, -sine, 0.0)
        high_s[at, :] = jnp.where((lane >= 8) & (lane < ROT), sine, 0.0)
        return carry

    net.pass_on(1, 1)
    lax.fori_loop(0, span // 256, tables, 0)
    net.pass_on(2, 1)
    arrive(small_y)

    pieces = jnp.concatenate(
        [g_small[a, e] for a in range(lay.nz) for e in range(lay.ny)], 1
    )
    depth = lay.fsdp * LANES
    slot = lax.broadcasted_iota(jnp.int32, (depth, 256), 0)
    owner, lane_in = slot // LANES, slot % LANES
    inside = lane_in < r

    def place(row, count, per, offset, target, at):
        col = lax.broadcasted_iota(jnp.int32, (depth, 256), 1) + at
        hot = inside & (target(per * r * owner + offset * r + lane_in) == col)
        return mm(pieces[row : row + count], hot.astype(BF))

    def kinds(n):
        return ((n // HD) % 3) * D + (n // (3 * HD)) * HD + n % HD

    for j in range(3):
        vectors[:, 256 * j : 256 * (j + 1)] = place(0, 8, 1, 0, lambda n: n, 256 * j)
    net.pass_on(0, 2)

    def place_qkv(j, carry):
        at = pl.multiple_of(j * 256, 256)
        value = place(5, 1, 3, 0, kinds, at)
        for q in range(1, 3):
            value = value + place(5 + q, 1, 3, q, kinds, at)
        qkv_add[:, pl.ds(at, 256)] = value
        return carry

    lax.fori_loop(0, 9, place_qkv, 0)
    arrive([halo[0]])

    @pl.when(jnp.logical_not(even))
    def _():
        passed[0].start()

    net.pass_on(1, 2)
    net.pass_on(2, 2)

    def place_up(j, carry):
        at = pl.multiple_of(j * 256, 256)
        value = place(8, 1, 4, 0, lambda n: n, at)
        for q in range(1, 4):
            value = value + place(8 + q, 1, 4, q, lambda n: n, at)
        up_add[:, pl.ds(at, 256)] = value
        return carry

    lax.fori_loop(0, 12, place_up, 0)
    arrive([halo[1]])

    @pl.when(jnp.logical_not(even))
    def _():
        passed[1].start()

    net.issue(3, 0)
    net.issue(4, 0)
    gain, shift = vectors[0:1, :], vectors[1:2, :]
    own_rows = pl.ds(2 * rows, rows)
    first = (normed * gain + shift).astype(BF)
    first_all[own_rows, :] = first
    first_t[:, own_rows] = first.T

    arrive(segs)
    least = jnp.maximum(0, 2 * rows - b * rows)
    keys_doc = jnp.concatenate([seg_halo[0], seg_halo[1], seg[...]], 1).astype(F32)
    keys_doc = jnp.concatenate([keys_doc] * (LANES // 8), 0).T
    query_doc = seg[0:1, :].astype(F32)

    for k in range(6):
        at = slice(k * 256, (k + 1) * 256)
        key_at = lax.broadcasted_iota(jnp.int32, (256, rows), 0) + k * 256
        query_at = lax.broadcasted_iota(jnp.int32, (256, rows), 1) + 2 * rows
        allowed = (keys_doc[at, 0:1] == query_doc) & (key_at <= query_at) & (key_at >= least)
        bias[at, :] = jnp.where(allowed, 0.0, -1e30)
    net.pass_on(0, 3)
    net.pass_on(1, 3)
    net.pass_on(2, 3)
    net.issue(5, 0)
    for t in range(3):
        net.done(t)
    net.pass_on(3, 1)

    def weight(first_col, width):
        value = g_att[:, :, :, pl.ds(first_col, width)]
        return value.reshape(D, width)

    scale = 1.0 / math.sqrt(HD)
    do_s[...] = mm(grad[...], weight(3 * D, D), NT).astype(BF)

    def project(kind, j, at, out, factor):
        col = pl.multiple_of(kind * D + 256 * j, 256)
        value = mm(first_all[at, :], weight(col, 256)) + qkv_add[:, pl.ds(col, 256)]
        for k in range(2):
            u = value[:, k * LANES : (k + 1) * LANES]
            if kind < 2:
                u = rope(u, cos_s[at, :], low_s[at, :], high_s[at, :])
            if factor is not None:
                u = u * factor
            out[:, pl.ds(pl.multiple_of(256 * j + LANES * k, LANES), LANES)] = u.astype(BF)

    def own_projections(j, carry):
        project(0, j, own_rows, q_s, scale)
        project(1, j, own_rows, k_s.at[own_rows], None)
        project(2, j, own_rows, v_s.at[own_rows], None)
        return carry

    lax.fori_loop(0, 3, own_projections, 0)
    net.pass_on(4, 1)
    own[0].wait_recv()
    own[1].wait_recv()
    net.pass_on(5, 1)
    for k in range(2):
        at = slice(k * rows, (k + 1) * rows)
        before = (norm_rows(tok_halo[k]) * gain + shift).astype(BF)
        first_all[at, :] = before
        first_t[:, at] = before.T
    net.pass_on(3, 2)

    def earlier_projections(j, carry):
        for k in range(2):
            at = pl.ds(k * rows, rows)
            project(1, j, at, k_s.at[at], None)
            project(2, j, at, v_s.at[at], None)
        return carry

    lax.fori_loop(0, 3, earlier_projections, 0)
    net.issue(6, 0)
    net.pass_on(4, 2)

    later = [
        [lambda: net.pass_on(5, 2), lambda: net.issue(7, 0), lambda: net.pass_on(6, 1)],
        [lambda: net.pass_on(3, 3), lambda: net.issue(8, 0)],
        [lambda: net.pass_on(4, 3), lambda: net.pass_on(7, 1), lambda: net.pass_on(6, 2)],
        [lambda: net.pass_on(5, 3), lambda: net.pass_on(8, 1), lambda: net.pass_on(7, 2)],
        [lambda: net.pass_on(6, 3), lambda: net.pass_on(8, 2)],
        [lambda: net.pass_on(7, 3)],
    ]
    tile = 256

    def pair(p, carry):
        lanes = pl.ds(pl.multiple_of(p * LANES, LANES), LANES)
        v_pair, k_pair = v_s[:, lanes], k_s[:, lanes]
        v_t, k_t = v_pair.T, k_pair.T
        do_t = do_s[:, lanes].astype(F32).T
        lane = lax.broadcasted_iota(jnp.int32, (tile, LANES), 1)
        zero = jnp.zeros((), BF)
        for t in range(rows // tile):
            cols = slice(t * tile, (t + 1) * tile)
            kl = 2 * rows + (t + 1) * tile
            outs, dqs = [], []
            for hh in range(2):
                mine = (lane // HD) == hh
                qm = jnp.where(mine, q_s[cols, lanes], zero)
                dom = jnp.where(mine, do_s[cols, lanes], zero)
                st = mm(k_pair[:kl], qm, NT) + bias[:kl, cols]
                top = jnp.max(st, 0, keepdims=True)
                e = jnp.exp(st - top)
                w = e * (1.0 / jnp.sum(e, 0, keepdims=True))
                wb = w.astype(BF)
                part = slice(hh * HD, (hh + 1) * HD)
                o_t = mm(v_t[part, :kl], wb)
                delta = jnp.sum(o_t * do_t[part, cols], 0, keepdims=True)
                ds = (w * (mm(v_pair[:kl], dom, NT) - delta)).astype(BF)
                outs.append(o_t)
                dqs.append(mm(k_t[part, :kl], ds))
                dk_part, dv_part = mm(ds, qm), mm(wb, dom)
                if hh == 0 and t == 0:
                    dk_acc[:kl, :] = dk_part
                    dv_acc[:kl, :] = dv_part
                    dk_acc[kl:, :] = jnp.zeros((span - kl, LANES), F32)
                    dv_acc[kl:, :] = jnp.zeros((span - kl, LANES), F32)
                else:
                    dk_acc[:kl, :] += dk_part
                    dv_acc[:kl, :] += dv_part
            o_pair = jnp.concatenate(outs, 0)
            ctx_t[lanes, cols] = o_pair.astype(BF)
            ctx_s[cols, lanes] = o_pair.T.astype(BF)
            dq = jnp.concatenate(dqs, 0).T * scale
            at = slice(2 * rows + t * tile, 2 * rows + (t + 1) * tile)
            dq_s[cols, lanes] = rope(dq, cos_s[at, :], -low_s[at, :], -high_s[at, :]).astype(BF)
        dk_s[:, lanes] = rope(dk_acc[...], cos_s[...], -low_s[...], -high_s[...]).astype(BF)
        dv_s[:, lanes] = dv_acc[...].astype(BF)
        for k, events in enumerate(later):

            @pl.when(p == k)
            def _(events=events):
                for event in events:
                    event()

        return carry

    lax.fori_loop(0, PAIRS, pair, 0)
    net.pass_on(8, 3)

    def earlier_grad(k, carry):
        at = pl.ds(pl.multiple_of(k * 256, 256), 256)
        value = mm(dk_s[at, :], weight(D, D), NT) + mm(dv_s[at, :], weight(2 * D, D), NT)
        fg_prev[at, :] = value.astype(BF)
        return carry

    lax.fori_loop(0, 2 * rows // 256, earlier_grad, 0)
    for k in range(rows // 256):
        at = slice(2 * rows + 256 * k, 2 * rows + 256 * (k + 1))
        near = slice(256 * k, 256 * (k + 1))
        fg_own[near, :] = (
            mm(dk_s[at, :], weight(D, D), NT)
            + mm(dv_s[at, :], weight(2 * D, D), NT)
            + mm(dq_s[near, :], weight(0, D), NT)
        )

    def weight_grads(j, carry):
        col = pl.multiple_of(256 * j, 256)
        cols = pl.ds(col, 256)

        def put(kind, value):
            p_att[:, :, :, pl.ds(pl.multiple_of(kind * D + col, 256), 256)] = value.astype(BF).reshape(
                lay.nz, lay.ny, r, 256
            )

        put(0, mm(first_t[:, own_rows], dq_s[:, cols]))
        put(1, mm(first_t[...], dk_s[:, cols]))
        put(2, mm(first_t[...], dv_s[:, cols]))
        put(3, mm(ctx_t[...], grad[:, cols]))
        attn_out[:, cols] = mm(ctx_s[...], weight(pl.multiple_of(3 * D + col, 256), 256))
        return carry

    lax.fori_loop(0, 3, weight_grads, 0)
    for k, ref in enumerate((dq_s, dk_s, dv_s)):
        att_sums[k : k + 1, :] = jnp.sum(ref[...].astype(F32), 0, keepdims=True)
    att_sums[3:8, :] = jnp.zeros((5, D), F32)
    for t in range(3, 9):
        net.done(t)
    net.drain()
    sent(small_z + small_y + segs + halo + own)


def front(lay, u_att, u_up, u_down, small, tok, grad, seg):
    rows = tok.shape[0]
    span = 3 * rows
    r = u_att.shape[0]
    n = len(CHUNKS)
    outs = (
        jax.ShapeDtypeStruct(grad_shape(lay, 1, r), BF),
        jax.ShapeDtypeStruct(grad_shape(lay, 2, r), BF),
        jax.ShapeDtypeStruct(grad_shape(lay, 0, r), BF),
        jax.ShapeDtypeStruct((2 * rows, D), BF),
        jax.ShapeDtypeStruct((rows, D), F32),
        jax.ShapeDtypeStruct((rows, D), F32),
        jax.ShapeDtypeStruct((8, D), F32),
        jax.ShapeDtypeStruct((1, FF), F32),
        jax.ShapeDtypeStruct((8, D), F32),
    )
    vmem = pl.BlockSpec(memory_space=pltpu.VMEM)
    lx, ly, lz = max(1, lay.nx - 1), max(1, lay.ny - 1), max(1, lay.nz - 1)

    def v(shape, dtype=BF):
        return pltpu.VMEM(shape, dtype)

    return pl.pallas_call(
        functools.partial(front_kernel, lay, rows),
        name="front",
        out_shape=outs,
        in_specs=hbm(3) + [vmem] * 4,
        out_specs=tuple(hbm(2)) + (vmem,) * 7,
        scratch_shapes=[
            v(grad_shape(lay, 0, r)), v((lay.nz, lay.ny, 16, LANES)), v((2, rows, D)),
            v((2, 8, rows), jnp.int32), v((span, D)), v((D, span)), v((rows, D)), v((span, D)),
            v((span, D)), v((rows, D)), v((rows, D)), v((D, rows)), v((rows, D)), v((span, D)),
            v((span, D)), v((span, LANES), F32), v((span, LANES), F32), v((span, LANES), F32),
            v((span, rows), F32), v((span, LANES), F32), v((span, LANES), F32), v((1, 3 * D), F32),
            dma(n + 1), dma(n, lz), dma(n, lz), dma(n, ly), dma(n, ly), dma(n, lx), dma(n, lx),
            dma(n), dma(n), dma(lay.nz + ly), dma(lay.nz + ly), dma(6), dma(6),
        ],
        compiler_params=pltpu.CompilerParams(
            collective_id=0, has_side_effects=True, vmem_limit_bytes=VMEM_LIMIT
        ),
    )(u_att, u_up, u_down, small, tok, grad, seg)


def go(*args):
    copy = remote(*args)
    copy.start()
    return copy


def reduce_kernel(
    lay, p_att, p_up, p_down, vec,
    f_att, f_up, f_down, vec_out,
    ca, ra1, rb1, ra2, rb2, ra3, v_c, v_x, v_y, v_z, *sems,
):
    (c_s, c_r, x_s, x_r, y_s, y_r, z_s, z_r, fx_s, fx_r, fc_s, fc_r, v_s, v_r) = sems
    x, c, z, y = lay.coords()
    xs, cs, zs, ys = line_peers(lay)
    barrier_with(xs + cs + zs + ys)
    ps = (p_att, p_up, p_down)
    fs = (f_att, f_up, f_down)
    n = len(CHUNKS)
    sends = []
    bf = jnp.bfloat16
    f32 = jnp.float32

    def arrived(copies):
        for copy in copies:
            copy.wait_recv()
        sends.extend(copies)

    v_c[c] = vec[...]
    vec_stage = [go(v_c.at[c], v_c.at[c], v_s.at[0], v_r.at[0], cs[0])]
    arrived(vec_stage)
    v_x[x] = v_c[0] + v_c[1]
    vec_stage = [
        go(v_x.at[x], v_x.at[x], v_s.at[1 + k], v_r.at[1 + k], p) for k, p in enumerate(xs)
    ]
    state = {"stage": vec_stage}

    def vec_step(step):
        if step == 0:
            arrived(state["stage"])
            v_y[y] = sum([v_x[k] for k in range(1, lay.nx)], v_x[0])
            at = lay.nx
            state["stage"] = [
                go(v_y.at[y], v_y.at[y], v_s.at[at + k], v_r.at[at + k], p)
                for k, p in enumerate(ys)
            ]
        elif step == 1:
            arrived(state["stage"])
            v_z[z] = sum([v_y[k] for k in range(1, lay.ny)], v_y[0])
            at = lay.nx + lay.ny - 1
            state["stage"] = [
                go(v_z.at[z], v_z.at[z], v_s.at[at + k], v_r.at[at + k], p)
                for k, p in enumerate(zs)
            ]
        elif step == 2:
            arrived(state["stage"])
            vec_out[...] = sum([v_z[k] for k in range(1, lay.nz)], v_z[0])

    def add_into(dst, srcs):
        lead = dst.shape[:-2]
        count = math.prod(lead)

        def body(j, carry):
            index = []
            rest = j
            for size in reversed(lead):
                index.append(lax.rem(rest, size))
                rest = rest // size
            index = tuple(reversed(index))
            total = dst[index].astype(f32)
            for src in srcs:
                total = total + src[index].astype(f32)
            dst[index] = total.astype(bf)
            return carry

        lax.fori_loop(0, count, body, 0)

    st_c, st_1, st_2, st_3, st_x, st_f = {}, {}, {}, {}, {}, {}

    def recv(bufs, t):
        g, i = CHUNKS[t]
        return bufs, g, i

    def buf(ref, g, i):
        return ref[g].at[i]

    def issue_core(t):
        g, i = CHUNKS[t]
        st_c[t] = [
            go(
                view(lay, ps[g], g, i, 1 - c, ALL, ALL, ALL), buf(ca, g, i),
                c_s.at[t], c_r.at[t], cs[0],
            )
        ]

    def issue_1(t):
        g, i = CHUNKS[t]
        add_into(view(lay, ps[g], g, i, c, ALL, ALL, ALL), [buf(ca, g, i)])
        if i < 2:
            st_1[t] = [
                go(
                    view(lay, ps[g], g, i, c, wrap(x + 1 + k, lay.nx), ALL, ALL),
                    buf(ra1, g, i).at[k], x_s.at[t, k], x_r.at[t, k], p,
                )
                for k, p in enumerate(xs)
            ]
        else:
            st_1[t] = [
                go(
                    view(lay, ps[g], g, i, c, ALL, ALL, wrap(y + 1 + k, lay.ny)),
                    buf(rb1, g, 0).at[k], y_s.at[t, k], y_r.at[t, k], p,
                )
                for k, p in enumerate(ys)
            ]

    def issue_2(t):
        g, i = CHUNKS[t]
        if i < 2:
            add_into(
                view(lay, ps[g], g, i, c, x, ALL, ALL),
                [buf(ra1, g, i).at[k] for k in range(lay.nx - 1)],
            )
            st_2[t] = [
                go(
                    view(lay, ps[g], g, i, c, x, ALL, wrap(y + 1 + k, lay.ny)),
                    buf(ra2, g, i).at[k], y_s.at[t, k], y_r.at[t, k], p,
                )
                for k, p in enumerate(ys)
            ]
        else:
            add_into(
                view(lay, ps[g], g, i, c, ALL, ALL, y),
                [buf(rb1, g, 0).at[k] for k in range(lay.ny - 1)],
            )
            st_2[t] = [
                go(
                    view(lay, ps[g], g, i, c, wrap(x + 1 + k, lay.nx), ALL, y),
                    buf(rb2, g, 0).at[k], x_s.at[t, k], x_r.at[t, k], p,
                )
                for k, p in enumerate(xs)
            ]

    def issue_3(t):
        g, i = CHUNKS[t]
        second = (
            [buf(ra2, g, i).at[k] for k in range(lay.ny - 1)]
            if i < 2
            else [buf(rb2, g, 0).at[k] for k in range(lay.nx - 1)]
        )
        add_into(view(lay, ps[g], g, i, c, x, ALL, y), second)
        st_3[t] = [
            go(
                view(lay, ps[g], g, i, c, x, wrap(z + 1 + k, lay.nz), y),
                buf(ra3, g, i).at[k], z_s.at[t, k], z_r.at[t, k], p,
            )
            for k, p in enumerate(zs)
        ]

    def issue_x(t):
        g, i = CHUNKS[t]
        own = view(lay, ps[g], g, i, c, x, z, y)
        srcs = [buf(ra3, g, i).at[k] for k in range(lay.nz - 1)]
        out = shard_view(lay, fs[g], g, i, c, x)
        total = own[...].astype(f32)
        for src in srcs:
            total = total + src[...].astype(f32)
        out[...] = total.astype(bf)
        st_x[t] = [go(out, out, fx_s.at[t, k], fx_r.at[t, k], p) for k, p in enumerate(xs)]

    def issue_f(t):
        g, i = CHUNKS[t]
        out = shard_view(lay, fs[g], g, i, c, ALL)
        st_f[t] = [go(out, out, fc_s.at[t], fc_r.at[t], cs[0])]

    for t in range(n + 6):
        if t < n:
            issue_core(t)
        if 0 <= t - 1 < n:
            arrived(st_c[t - 1])
            issue_1(t - 1)
        if 0 <= t - 2 < n:
            arrived(st_1[t - 2])
            issue_2(t - 2)
        if 0 <= t - 3 < n:
            arrived(st_2[t - 3])
            issue_3(t - 3)
        if 0 <= t - 4 < n:
            arrived(st_3[t - 4])
            issue_x(t - 4)
        if 0 <= t - 5 < n:
            arrived(st_x[t - 5])
            issue_f(t - 5)
        if 0 <= t - 6 < n:
            arrived(st_f[t - 6])
        if 1 <= t <= 3:
            vec_step(t - 1)
    for copy in sends:
        copy.wait_send()


def reduce(lay, p_att, p_up, p_down, vec):
    r = p_att.shape[2]
    n = len(CHUNKS)
    bf = jnp.bfloat16
    outs = tuple(jax.ShapeDtypeStruct((r, 4 * D) if g < 2 else (4, r, D), bf) for g in range(3)) + (
        jax.ShapeDtypeStruct(vec.shape, vec.dtype),
    )
    lx, ly, lz = max(1, lay.nx - 1), max(1, lay.ny - 1), max(1, lay.nz - 1)

    def bufs(chunks, peers, x_all, z_all, y_all):
        return [
            pltpu.VMEM((chunks,) + peers + part_shape(lay, g, x_all, z_all, y_all, r), bf)
            for g in range(3)
        ]

    scratch = [
        bufs(3, (), True, True, True),
        bufs(2, (lx,), False, True, True),
        bufs(1, (ly,), True, True, False),
        bufs(2, (ly,), False, True, False),
        bufs(1, (lx,), False, True, False),
        bufs(3, (lz,), False, False, False),
    ]
    vecs = [pltpu.VMEM((k,) + vec.shape, jnp.float32) for k in (2, lay.nx, lay.ny, lay.nz)]
    nv = 1 + lay.nx + lay.ny + lay.nz
    sems = [
        dma(n), dma(n), dma(n, lx), dma(n, lx), dma(n, ly), dma(n, ly), dma(n, lz), dma(n, lz),
        dma(n, lx), dma(n, lx), dma(n), dma(n), dma(nv), dma(nv),
    ]
    vmem = [pl.BlockSpec(memory_space=pltpu.VMEM)]
    return pl.pallas_call(
        functools.partial(reduce_kernel, lay),
        name="reduce_grads",
        out_shape=outs,
        in_specs=vmem * 4,
        out_specs=tuple(vmem * 4),
        scratch_shapes=scratch + vecs + sems,
        compiler_params=pltpu.CompilerParams(
            collective_id=1, has_side_effects=True, vmem_limit_bytes=VMEM_LIMIT
        ),
    )(p_att, p_up, p_down, vec)


def norm_back(grad, gain, normed, factor):
    inner = grad * gain
    return factor * (
        inner
        - jnp.mean(inner, -1, keepdims=True)
        - normed * jnp.mean(inner * normed, -1, keepdims=True)
    )


def gelu_slope(pre):
    return 0.5 * (1.0 + lax.erf(pre / math.sqrt(2.0))) + pre * jnp.exp(
        -0.5 * pre * pre
    ) / math.sqrt(2.0 * math.pi)


def per_device(
    lay, tokens, seg_ids, out_grad, first_gain, first_bias, second_gain, second_bias,
    qkv_weight, qkv_bias, dense_weight, up_weight, up_bias, down_weight, out_bias,
):
    f32, bf = jnp.float32, jnp.bfloat16
    rows = tokens.shape[0]
    r = qkv_weight.shape[0]
    fsdp = lay.fsdp
    qkv_kinds = qkv_weight.reshape(r, H, 3, HD).transpose(0, 2, 1, 3).reshape(r, 3 * D)
    u_att = jnp.concatenate([qkv_kinds, dense_weight], 1)
    u_down = down_weight.reshape(4, r, D)
    vectors = (first_gain, first_bias, second_gain, second_bias, out_bias, qkv_bias, up_bias)
    sizes = [v.shape[0] for v in vectors]
    small = jnp.pad(jnp.concatenate(vectors).reshape(12, r), ((0, 4), (0, LANES - r)))
    seg_rows = jnp.broadcast_to(seg_ids[None, :], (8, rows))
    g_up, g_down, p_att, fg_prev, first_grad, attn_out, full, up_add, att_sums = front(
        lay, u_att, up_weight, u_down, small, tokens, out_grad, seg_rows
    )
    gain_first, gain_second, shift_second, out_add = full[0], full[2], full[3], full[4]
    up_mat = g_up.reshape(D, FF)
    down_mat = g_down.reshape(FF, D)
    stream = tokens.astype(f32)
    normed, factor = norm_parts(stream)
    second_in = (normed * gain_second + shift_second).astype(bf)
    pre = mm(second_in, up_mat) + up_add
    activation = jax.nn.gelu(pre, approximate=False).astype(bf)
    result = stream + attn_out + mm(activation, down_mat) + out_add
    output = result.astype(bf)

    cotangent = out_grad.astype(f32)
    down_grad = mm(activation.T, out_grad)
    hidden_grad = lax.dot_general(out_grad, down_mat, NT, preferred_element_type=f32)
    pre_grad = (hidden_grad * gelu_slope(pre)).astype(bf)
    up_grad = mm(second_in.T, pre_grad)
    second_grad = lax.dot_general(pre_grad, up_mat, NT, preferred_element_type=f32)
    devices = lay.dp * fsdp
    for distance in (2, 1):
        low = (2 - distance) * rows
        route = [(i, (i - distance) % devices) for i in range(devices)]
        first_grad = first_grad + lax.ppermute(
            fg_prev[low : low + rows], ("dp", "fsdp"), route
        ).astype(f32)
    input_grad = (
        cotangent
        + norm_back(first_grad, gain_first, normed, factor)
        + norm_back(second_grad, gain_second, normed, factor)
    ).astype(bf)

    docs = DOC_DEV * devices
    token_norm = (
        jnp.sum(jnp.square(activation.astype(f32)), -1) * jnp.sum(cotangent * cotangent, -1) / (FF * D)
    )
    member = (seg_ids[:, None] == jnp.arange(docs, dtype=jnp.int32)[None, :]).astype(f32)
    doc_sums = jnp.sum(token_norm[:, None] * member, 0)
    doc_counts = jnp.sum(member, 0)
    qkv_bias_grad = att_sums[:3].reshape(3, H, HD).transpose(1, 0, 2).reshape(3 * D)
    grads = (
        jnp.sum(first_grad * normed, 0),
        jnp.sum(first_grad, 0),
        jnp.sum(second_grad * normed, 0),
        jnp.sum(second_grad, 0),
        jnp.sum(cotangent, 0),
        qkv_bias_grad,
        jnp.sum(pre_grad.astype(f32), 0),
    )
    vec = jnp.concatenate(grads + (doc_sums, doc_counts))
    count = vec.shape[0]
    vec_rows = -(-count // (8 * LANES)) * 8
    vec = jnp.pad(vec, (0, vec_rows * LANES - count)).reshape(vec_rows, LANES)
    p_up = up_grad.astype(bf).reshape(grad_shape(lay, 1, r))
    p_down = down_grad.astype(bf).reshape(grad_shape(lay, 2, r))
    f_att, f_up, f_down, vec = reduce(lay, p_att, p_up, p_down, vec)
    vec = vec.reshape(-1)
    shard = lax.axis_index("fsdp")
    pieces, at = [], 0
    for size in sizes:
        pieces.append(lax.dynamic_slice_in_dim(vec, at + shard * size, size))
        at += size * fsdp
    totals, counts = vec[at : at + docs], vec[at + docs : at + 2 * docs]
    f_att = f_att.astype(f32)
    qkv_out = f_att[:, : 3 * D].reshape(r, 3, H, HD).transpose(0, 2, 1, 3).reshape(r, 3 * D)
    return (
        output,
        input_grad,
        pieces[0],
        pieces[1],
        pieces[2],
        pieces[3],
        qkv_out,
        pieces[5],
        f_att[:, 3 * D :],
        f_up.astype(f32),
        pieces[6],
        f_down.reshape(4 * r, D).astype(f32),
        pieces[4],
        totals / counts,
    )


def solution(mesh):
    lay = Layout(mesh.shape["dp"], mesh.shape["fsdp"])
    both = P(("dp", "fsdp"))
    split = P("fsdp")
    in_specs = (both, both, both) + (split,) * 11
    out_specs = (both, both) + (split,) * 11 + (P(),)
    return jax.shard_map(
        functools.partial(per_device, lay), mesh=mesh, in_specs=in_specs, out_specs=out_specs,
        check_vma=False,
    )
```

```python
import functools
import math

import jax
import jax.numpy as jnp
from jax import lax
from jax.experimental import pallas as pl
from jax.experimental.pallas import tpu as pltpu
from jax.sharding import PartitionSpec as P

D = 768
H = 12
HD = 64
FF = 3072
ROT = 16
ROW = 2048
DOC_DEV = 2
LANES = 128
PAIRS = D // LANES
MESH = pl.DeviceIdType.MESH
VMEM_LIMIT = 60 * 1024 * 1024


class Layout:
    def __init__(self, dp, fsdp):
        self.dp, self.fsdp = dp, fsdp
        self.nc = 2
        self.nx = dp // 2
        ny = 1
        while (2 * ny) * (2 * ny) <= fsdp:
            ny *= 2
        self.ny, self.nz = ny, fsdp // ny
        self.sub = max(1, self.nx // 2)
        self.unit = 4 // self.nx
        self.down_unit = 2 // self.sub

    def coords(self):
        d, f = lax.axis_index("dp"), lax.axis_index("fsdp")
        return d // 2, d % 2, f // self.ny, f % self.ny

    def device(self, x, c, z, y):
        return {"dp": x * 2 + c, "fsdp": z * self.ny + y}


def wrap(value, size):
    return lax.rem(value + size, size)


CHUNKS = tuple((g, i) for g in range(3) for i in range(3))
ALL = slice(None)


def grad_shape(lay, group, r):
    return (lay.nz, lay.ny, r, 4 * D) if group < 2 else (lay.nz, lay.ny, 4, r, D)


def span_of(lay, group, i, c, x):
    if group < 2:
        width = 512 // lay.nx
        if x is ALL:
            return pl.ds(pl.multiple_of(1024 * i + 512 * c, LANES), 512), None
        return pl.ds(pl.multiple_of(1024 * i + 512 * c + width * x, LANES), width), None
    width = 256 // lay.sub
    if x is ALL:
        return pl.ds(256 * i, 256), pl.ds(2 * c, 2)
    start = 256 * i + width * lax.rem(x, lay.sub)
    return pl.ds(pl.multiple_of(start, LANES), width), 2 * c + x // lay.sub


def view(lay, ref, group, i, c, x, z, y):
    cols, quarter = span_of(lay, group, i, c, x)
    if group < 2:
        return ref.at[z, y, :, cols]
    return ref.at[z, y, quarter, :, cols]


def shard_view(lay, ref, group, i, c, x):
    cols, quarter = span_of(lay, group, i, c, x)
    if group < 2:
        return ref.at[:, cols]
    return ref.at[quarter, :, cols]


def part_shape(lay, group, x_all, z_all, y_all, r):
    lead = ((lay.nz,) if z_all else ()) + ((lay.ny,) if y_all else ())
    if group < 2:
        return lead + (r, 512 if x_all else 512 // lay.nx)
    return lead + ((2, r, 256) if x_all else (r, 256 // lay.sub))


def barrier_with(peers):
    sem = pltpu.get_barrier_semaphore()
    for peer in peers:
        pl.semaphore_signal(sem, inc=1, device_id=peer, device_id_type=MESH)
    pl.semaphore_wait(sem, len(peers))


def line_peers(lay):
    x, c, z, y = lay.coords()
    xs = [lay.device(wrap(x + k, lay.nx), c, z, y) for k in range(1, lay.nx)]
    ys = [lay.device(x, c, z, wrap(y + k, lay.ny)) for k in range(1, lay.ny)]
    zs = [lay.device(x, c, wrap(z + k, lay.nz), y) for k in range(1, lay.nz)]
    cs = [lay.device(x, 1 - c, z, y)]
    return xs, cs, zs, ys


def remote(src, dst, ssem, rsem, device):
    return pltpu.make_async_remote_copy(
        src_ref=src, dst_ref=dst, send_sem=ssem, recv_sem=rsem, device_id=device, device_id_type=MESH
    )


def start(copies):
    for copy in copies:
        copy.start()


def arrive(copies):
    for copy in copies:
        copy.wait_recv()


def sent(copies):
    for copy in copies:
        copy.wait_send()


def hbm(count):
    return [pl.BlockSpec(memory_space=pltpu.HBM)] * count


def dma(*shape):
    return pltpu.SemaphoreType.DMA(shape)


NT = (((1,), (1,)), ((), ()))
NN = (((1,), (0,)), ((), ()))
F32 = jnp.float32
BF = jnp.bfloat16


def mm(a, b, dims=NN):
    return lax.dot_general(a, b, dims, preferred_element_type=F32)


def norm_parts(values):
    middle = jnp.mean(values, -1, keepdims=True)
    centred = values - middle
    factor = lax.rsqrt(jnp.mean(centred * centred, -1, keepdims=True) + 1e-05)
    return centred * factor, factor


class Gather:
    def __init__(self, lay, gs, sems):
        (z_s, z_r, y_s, y_r, x_s, x_r, c_s, c_r) = sems
        x, c, z, y = lay.coords()
        xs, cs, zs, ys = line_peers(lay)
        self.stages = []
        for t, (g, i) in enumerate(CHUNKS):
            by_y, by_x = (ys, y_s, y_r), (xs, x_s, x_r)
            first, second = (by_y, by_x) if i < 2 else (by_x, by_y)
            middle = (x, ALL, ALL) if i < 2 else (ALL, ALL, y)
            steps = [
                ((zs, z_s, z_r), (x, z, y)),
                (first, (x, ALL, y)),
                (second, middle),
            ]
            stages = []
            for (peers, ss, rs), (px, pz, py) in steps:
                piece = view(lay, gs[g], g, i, c, px, pz, py)
                stages.append(
                    [remote(piece, piece, ss.at[t, k], rs.at[t, k], p) for k, p in enumerate(peers)]
                )
            piece = view(lay, gs[g], g, i, c, ALL, ALL, ALL)
            stages.append([remote(piece, piece, c_s.at[t], c_r.at[t], cs[0])])
            self.stages.append(stages)

    def issue(self, t, stage):
        start(self.stages[t][stage])

    def pass_on(self, t, stage):
        arrive(self.stages[t][stage - 1])
        start(self.stages[t][stage])

    def done(self, t):
        arrive(self.stages[t][3])

    def drain(self):
        for stages in self.stages:
            for copies in stages:
                sent(copies)


def rope(u, cos, low, high):
    return u * cos + pltpu.roll(u, LANES - 8, 1) * low + pltpu.roll(u, 8, 1) * high


def front_kernel(
    lay, rows,
    u_att, u_up, u_down, small, tok, grad, seg,
    g_up, g_down, p_att, fg_prev, fg_own, attn_out, vectors, up_add, att_sums,
    g_att, g_small, tok_halo, seg_halo, first_all, first_t, q_s, k_s, v_s, do_s, ctx_s, ctx_t,
    dq_s, dk_s, dv_s, cos_s, low_s, high_s, bias, dk_acc, dv_acc, qkv_add,
    local_sem, z_s, z_r, y_s, y_r, x_s, x_r, c_s, c_r, sm_s, sm_r, h_s, h_r,
):
    span = 3 * rows
    r = u_att.shape[0]
    x, c, z, y = lay.coords()
    xs, cs, zs, ys = line_peers(lay)
    total = lay.dp * lay.fsdp
    b = lax.axis_index("dp") * lay.fsdp + lax.axis_index("fsdp")

    def stream(k):
        t = wrap(b + k, total)
        return {"dp": t // lay.fsdp, "fsdp": lax.rem(t, lay.fsdp)}

    around = [stream(2), stream(-2), stream(1), stream(-1)]
    barrier_with(xs + cs + zs + ys + around)
    gs = (g_att, g_up, g_down)
    us = (u_att, u_up, u_down)
    locals_ = [pltpu.make_async_copy(small, g_small.at[z, y], local_sem.at[9])]
    for t, (g, i) in enumerate(CHUNKS):
        locals_.append(
            pltpu.make_async_copy(
                shard_view(lay, us[g], g, i, c, x), view(lay, gs[g], g, i, c, x, z, y), local_sem.at[t]
            )
        )
    start(locals_)
    even = lax.rem(b, 2) == 0
    half = rows // 2
    halo, own, passed = [], [], []
    for k in range(2):
        part = pl.ds(k * half, half)
        halo.append(remote(tok.at[part], tok_halo.at[0, part], h_s.at[k], h_r.at[k], around[0]))
        own.append(remote(tok.at[part], tok_halo.at[1, part], h_s.at[2 + k], h_r.at[2 + k], around[2]))
        passed.append(
            remote(tok_halo.at[0, part], tok_halo.at[1, part], h_s.at[2 + k], h_r.at[2 + k], around[3])
        )
    segs = [
        remote(seg, seg_halo.at[0], h_s.at[4], h_r.at[4], around[0]),
        remote(seg, seg_halo.at[1], h_s.at[5], h_r.at[5], around[2]),
    ]
    small_z = [
        remote(g_small.at[z, y], g_small.at[z, y], sm_s.at[k], sm_r.at[k], p) for k, p in enumerate(zs)
    ]
    small_y = [
        remote(g_small.at[:, y], g_small.at[:, y], sm_s.at[lay.nz + k], sm_r.at[lay.nz + k], p)
        for k, p in enumerate(ys)
    ]
    net = Gather(lay, gs, (z_s, z_r, y_s, y_r, x_s, x_r, c_s, c_r))

    for copy in locals_:
        copy.wait()
    start(small_z)
    start(segs)
    for t in range(3):
        net.issue(t, 0)
    start(halo)

    @pl.when(even)
    def _():
        start(own)

    def norm_rows(values):
        return norm_parts(values.astype(F32))[0]

    normed = norm_rows(tok[...])
    net.pass_on(0, 1)
    arrive(small_z)
    start(small_y)

    def tables(k, carry):
        at = pl.ds(pl.multiple_of(k * 256, 256), 256)
        lane = lax.broadcasted_iota(jnp.int32, (256, LANES), 1) % HD
        row = lax.broadcasted_iota(jnp.int32, (256, LANES), 0) + k * 256
        place = lax.rem((b - 2) * rows + row + 4 * ROW, ROW).astype(F32)
        rate = jnp.exp((lane % 8).astype(F32) * (-math.log(10000.0) / 8.0))
        angle = place * rate
        sine = jnp.sin(angle)
        cos_s[at, :] = jnp.where(lane < ROT, jnp.cos(angle), 1.0)
        low_s[at, :] = jnp.where(lane < 8, -sine, 0.0)
        high_s[at, :] = jnp.where((lane >= 8) & (lane < ROT), sine, 0.0)
        return carry

    net.pass_on(1, 1)
    lax.fori_loop(0, span // 256, tables, 0)
    net.pass_on(2, 1)
    arrive(small_y)

    pieces = jnp.concatenate(
        [g_small[a, e] for a in range(lay.nz) for e in range(lay.ny)], 1
    )
    depth = lay.fsdp * LANES
    slot = lax.broadcasted_iota(jnp.int32, (depth, 256), 0)
    owner, lane_in = slot // LANES, slot % LANES
    inside = lane_in < r

    def place(row, count, per, offset, target, at):
        col = lax.broadcasted_iota(jnp.int32, (depth, 256), 1) + at
        hot = inside & (target(per * r * owner + offset * r + lane_in) == col)
        return mm(pieces[row : row + count], hot.astype(BF))

    def kinds(n):
        return ((n // HD) % 3) * D + (n // (3 * HD)) * HD + n % HD

    for j in range(3):
        vectors[:, 256 * j : 256 * (j + 1)] = place(0, 8, 1, 0, lambda n: n, 256 * j)
    net.pass_on(0, 2)

    def place_qkv(j, carry):
        at = pl.multiple_of(j * 256, 256)
        value = place(5, 1, 3, 0, kinds, at)
        for q in range(1, 3):
            value = value + place(5 + q, 1, 3, q, kinds, at)
        qkv_add[:, pl.ds(at, 256)] = value
        return carry

    lax.fori_loop(0, 9, place_qkv, 0)
    arrive([halo[0]])

    @pl.when(jnp.logical_not(even))
    def _():
        passed[0].start()

    net.pass_on(1, 2)
    net.pass_on(2, 2)

    def place_up(j, carry):
        at = pl.multiple_of(j * 256, 256)
        value = place(8, 1, 4, 0, lambda n: n, at)
        for q in range(1, 4):
            value = value + place(8 + q, 1, 4, q, lambda n: n, at)
        up_add[:, pl.ds(at, 256)] = value
        return carry

    lax.fori_loop(0, 12, place_up, 0)
    arrive([halo[1]])

    @pl.when(jnp.logical_not(even))
    def _():
        passed[1].start()

    net.issue(3, 0)
    net.issue(4, 0)
    gain, shift = vectors[0:1, :], vectors[1:2, :]
    own_rows = pl.ds(2 * rows, rows)
    first = (normed * gain + shift).astype(BF)
    first_all[own_rows, :] = first
    first_t[:, own_rows] = first.T

    arrive(segs)
    least = jnp.maximum(0, 2 * rows - b * rows)
    keys_doc = jnp.concatenate([seg_halo[0], seg_halo[1], seg[...]], 1).astype(F32)
    keys_doc = jnp.concatenate([keys_doc] * (LANES // 8), 0).T
    query_doc = seg[0:1, :].astype(F32)

    for k in range(6):
        at = slice(k * 256, (k + 1) * 256)
        key_at = lax.broadcasted_iota(jnp.int32, (256, rows), 0) + k * 256
        query_at = lax.broadcasted_iota(jnp.int32, (256, rows), 1) + 2 * rows
        allowed = (keys_doc[at, 0:1] == query_doc) & (key_at <= query_at) & (key_at >= least)
        bias[at, :] = jnp.where(allowed, 0.0, -1e30)
    net.pass_on(0, 3)
    net.pass_on(1, 3)
    net.pass_on(2, 3)
    net.issue(5, 0)
    for t in range(3):
        net.done(t)
    net.pass_on(3, 1)

    def weight(first_col, width):
        value = g_att[:, :, :, pl.ds(first_col, width)]
        return value.reshape(D, width)

    scale = 1.0 / math.sqrt(HD)
    do_s[...] = mm(grad[...], weight(3 * D, D), NT).astype(BF)

    def project(kind, j, at, out, factor):
        col = pl.multiple_of(kind * D + 256 * j, 256)
        value = mm(first_all[at, :], weight(col, 256)) + qkv_add[:, pl.ds(col, 256)]
        for k in range(2):
            u = value[:, k * LANES : (k + 1) * LANES]
            if kind < 2:
                u = rope(u, cos_s[at, :], low_s[at, :], high_s[at, :])
            if factor is not None:
                u = u * factor
            out[:, pl.ds(pl.multiple_of(256 * j + LANES * k, LANES), LANES)] = u.astype(BF)

    def own_projections(j, carry):
        project(0, j, own_rows, q_s, scale)
        project(1, j, own_rows, k_s.at[own_rows], None)
        project(2, j, own_rows, v_s.at[own_rows], None)
        return carry

    lax.fori_loop(0, 3, own_projections, 0)
    net.pass_on(4, 1)
    own[0].wait_recv()
    own[1].wait_recv()
    net.pass_on(5, 1)
    for k in range(2):
        at = slice(k * rows, (k + 1) * rows)
        before = (norm_rows(tok_halo[k]) * gain + shift).astype(BF)
        first_all[at, :] = before
        first_t[:, at] = before.T
    net.pass_on(3, 2)

    def earlier_projections(j, carry):
        for k in range(2):
            at = pl.ds(k * rows, rows)
            project(1, j, at, k_s.at[at], None)
            project(2, j, at, v_s.at[at], None)
        return carry

    lax.fori_loop(0, 3, earlier_projections, 0)
    net.issue(6, 0)
    net.pass_on(4, 2)

    later = [
        [lambda: net.pass_on(5, 2), lambda: net.issue(7, 0), lambda: net.pass_on(6, 1)],
        [lambda: net.pass_on(3, 3), lambda: net.issue(8, 0)],
        [lambda: net.pass_on(4, 3), lambda: net.pass_on(7, 1), lambda: net.pass_on(6, 2)],
        [lambda: net.pass_on(5, 3), lambda: net.pass_on(8, 1), lambda: net.pass_on(7, 2)],
        [lambda: net.pass_on(6, 3), lambda: net.pass_on(8, 2)],
        [lambda: net.pass_on(7, 3)],
    ]
    tile = 256

    def pair(p, carry):
        lanes = pl.ds(pl.multiple_of(p * LANES, LANES), LANES)
        v_pair, k_pair = v_s[:, lanes], k_s[:, lanes]
        v_t, k_t = v_pair.T, k_pair.T
        do_t = do_s[:, lanes].astype(F32).T
        lane = lax.broadcasted_iota(jnp.int32, (tile, LANES), 1)
        zero = jnp.zeros((), BF)
        for t in range(rows // tile):
            cols = slice(t * tile, (t + 1) * tile)
            kl = 2 * rows + (t + 1) * tile
            outs, dqs = [], []
            for hh in range(2):
                mine = (lane // HD) == hh
                qm = jnp.where(mine, q_s[cols, lanes], zero)
                dom = jnp.where(mine, do_s[cols, lanes], zero)
                st = mm(k_pair[:kl], qm, NT) + bias[:kl, cols]
                top = jnp.max(st, 0, keepdims=True)
                e = jnp.exp(st - top)
                w = e * (1.0 / jnp.sum(e, 0, keepdims=True))
                wb = w.astype(BF)
                part = slice(hh * HD, (hh + 1) * HD)
                o_t = mm(v_t[part, :kl], wb)
                delta = jnp.sum(o_t * do_t[part, cols], 0, keepdims=True)
                ds = (w * (mm(v_pair[:kl], dom, NT) - delta)).astype(BF)
                outs.append(o_t)
                dqs.append(mm(k_t[part, :kl], ds))
                dk_part, dv_part = mm(ds, qm), mm(wb, dom)
                if hh == 0 and t == 0:
                    dk_acc[:kl, :] = dk_part
                    dv_acc[:kl, :] = dv_part
                    dk_acc[kl:, :] = jnp.zeros((span - kl, LANES), F32)
                    dv_acc[kl:, :] = jnp.zeros((span - kl, LANES), F32)
                else:
                    dk_acc[:kl, :] += dk_part
                    dv_acc[:kl, :] += dv_part
            o_pair = jnp.concatenate(outs, 0)
            ctx_t[lanes, cols] = o_pair.astype(BF)
            ctx_s[cols, lanes] = o_pair.T.astype(BF)
            dq = jnp.concatenate(dqs, 0).T * scale
            at = slice(2 * rows + t * tile, 2 * rows + (t + 1) * tile)
            dq_s[cols, lanes] = rope(dq, cos_s[at, :], -low_s[at, :], -high_s[at, :]).astype(BF)
        dk_s[:, lanes] = rope(dk_acc[...], cos_s[...], -low_s[...], -high_s[...]).astype(BF)
        dv_s[:, lanes] = dv_acc[...].astype(BF)
        for k, events in enumerate(later):

            @pl.when(p == k)
            def _(events=events):
                for event in events:
                    event()

        return carry

    lax.fori_loop(0, PAIRS, pair, 0)
    net.pass_on(8, 3)

    def earlier_grad(k, carry):
        at = pl.ds(pl.multiple_of(k * 256, 256), 256)
        value = mm(dk_s[at, :], weight(D, D), NT) + mm(dv_s[at, :], weight(2 * D, D), NT)
        fg_prev[at, :] = value.astype(BF)
        return carry

    lax.fori_loop(0, 2 * rows // 256, earlier_grad, 0)
    for k in range(rows // 256):
        at = slice(2 * rows + 256 * k, 2 * rows + 256 * (k + 1))
        near = slice(256 * k, 256 * (k + 1))
        fg_own[near, :] = (
            mm(dk_s[at, :], weight(D, D), NT)
            + mm(dv_s[at, :], weight(2 * D, D), NT)
            + mm(dq_s[near, :], weight(0, D), NT)
        )

    def weight_grads(j, carry):
        col = pl.multiple_of(256 * j, 256)
        cols = pl.ds(col, 256)

        def put(kind, value):
            p_att[:, :, :, pl.ds(pl.multiple_of(kind * D + col, 256), 256)] = value.astype(BF).reshape(
                lay.nz, lay.ny, r, 256
            )

        put(0, mm(first_t[:, own_rows], dq_s[:, cols]))
        put(1, mm(first_t[...], dk_s[:, cols]))
        put(2, mm(first_t[...], dv_s[:, cols]))
        put(3, mm(ctx_t[...], grad[:, cols]))
        attn_out[:, cols] = mm(ctx_s[...], weight(pl.multiple_of(3 * D + col, 256), 256))
        return carry

    lax.fori_loop(0, 3, weight_grads, 0)
    for k, ref in enumerate((dq_s, dk_s, dv_s)):
        att_sums[k : k + 1, :] = jnp.sum(ref[...].astype(F32), 0, keepdims=True)
    att_sums[3:8, :] = jnp.zeros((5, D), F32)
    for t in range(3, 9):
        net.done(t)
    net.drain()
    sent(small_z + small_y + segs + halo + own)


def front(lay, u_att, u_up, u_down, small, tok, grad, seg):
    rows = tok.shape[0]
    span = 3 * rows
    r = u_att.shape[0]
    n = len(CHUNKS)
    outs = (
        jax.ShapeDtypeStruct(grad_shape(lay, 1, r), BF),
        jax.ShapeDtypeStruct(grad_shape(lay, 2, r), BF),
        jax.ShapeDtypeStruct(grad_shape(lay, 0, r), BF),
        jax.ShapeDtypeStruct((2 * rows, D), BF),
        jax.ShapeDtypeStruct((rows, D), F32),
        jax.ShapeDtypeStruct((rows, D), F32),
        jax.ShapeDtypeStruct((8, D), F32),
        jax.ShapeDtypeStruct((1, FF), F32),
        jax.ShapeDtypeStruct((8, D), F32),
    )
    vmem = pl.BlockSpec(memory_space=pltpu.VMEM)
    lx, ly, lz = max(1, lay.nx - 1), max(1, lay.ny - 1), max(1, lay.nz - 1)

    def v(shape, dtype=BF):
        return pltpu.VMEM(shape, dtype)

    return pl.pallas_call(
        functools.partial(front_kernel, lay, rows),
        name="front",
        out_shape=outs,
        in_specs=hbm(3) + [vmem] * 4,
        out_specs=tuple(hbm(2)) + (vmem,) * 7,
        scratch_shapes=[
            v(grad_shape(lay, 0, r)), v((lay.nz, lay.ny, 16, LANES)), v((2, rows, D)),
            v((2, 8, rows), jnp.int32), v((span, D)), v((D, span)), v((rows, D)), v((span, D)),
            v((span, D)), v((rows, D)), v((rows, D)), v((D, rows)), v((rows, D)), v((span, D)),
            v((span, D)), v((span, LANES), F32), v((span, LANES), F32), v((span, LANES), F32),
            v((span, rows), F32), v((span, LANES), F32), v((span, LANES), F32), v((1, 3 * D), F32),
            dma(n + 1), dma(n, lz), dma(n, lz), dma(n, ly), dma(n, ly), dma(n, lx), dma(n, lx),
            dma(n), dma(n), dma(lay.nz + ly), dma(lay.nz + ly), dma(6), dma(6),
        ],
        compiler_params=pltpu.CompilerParams(
            collective_id=0, has_side_effects=True, vmem_limit_bytes=VMEM_LIMIT
        ),
    )(u_att, u_up, u_down, small, tok, grad, seg)


class Reduce:
    def __init__(self, lay, ps, fs, bufs, sems):
        (ca, ra1, rb1, ra2, rb2, ra3) = bufs
        (c_s, c_r, x_s, x_r, y_s, y_r, z_s, z_r, fx_s, fx_r, fc_s, fc_r) = sems
        x, c, z, y = lay.coords()
        xs, cs, zs, ys = line_peers(lay)
        self.steps = []
        for t, (g, i) in enumerate(CHUNKS):
            p, f = ps[g], fs[g]
            other_x = [wrap(x + 1 + k, lay.nx) for k in range(lay.nx - 1)]
            other_y = [wrap(y + 1 + k, lay.ny) for k in range(lay.ny - 1)]
            other_z = [wrap(z + 1 + k, lay.nz) for k in range(lay.nz - 1)]

            def over_x(pieces, slot):
                return [
                    remote(piece, slot.at[k], x_s.at[t, k], x_r.at[t, k], xs[k])
                    for k, piece in enumerate(pieces)
                ]

            def over_y(pieces, slot):
                return [
                    remote(piece, slot.at[k], y_s.at[t, k], y_r.at[t, k], ys[k])
                    for k, piece in enumerate(pieces)
                ]

            def into(dst, slot, count):
                return functools.partial(add_into, dst, [slot.at[k] for k in range(count)])

            core_slot = ca[g].at[i]
            core = [
                remote(view(lay, p, g, i, 1 - c, ALL, ALL, ALL), core_slot, c_s.at[t], c_r.at[t], cs[0])
            ]
            add_core = functools.partial(add_into, view(lay, p, g, i, c, ALL, ALL, ALL), [core_slot])
            if i < 2:
                slot1, slot2 = ra1[g].at[i], ra2[g].at[i]
                first = over_x([view(lay, p, g, i, c, k, ALL, ALL) for k in other_x], slot1)
                add_1 = into(view(lay, p, g, i, c, x, ALL, ALL), slot1, lay.nx - 1)
                second = over_y([view(lay, p, g, i, c, x, ALL, k) for k in other_y], slot2)
                add_2 = into(view(lay, p, g, i, c, x, ALL, y), slot2, lay.ny - 1)
            else:
                slot1, slot2 = rb1[g].at[0], rb2[g].at[0]
                first = over_y([view(lay, p, g, i, c, ALL, ALL, k) for k in other_y], slot1)
                add_1 = into(view(lay, p, g, i, c, ALL, ALL, y), slot1, lay.ny - 1)
                second = over_x([view(lay, p, g, i, c, k, ALL, y) for k in other_x], slot2)
                add_2 = into(view(lay, p, g, i, c, x, ALL, y), slot2, lay.nx - 1)
            slot3 = ra3[g].at[i]
            third = [
                remote(view(lay, p, g, i, c, x, k, y), slot3.at[n], z_s.at[t, n], z_r.at[t, n], zs[n])
                for n, k in enumerate(other_z)
            ]
            out = shard_view(lay, f, g, i, c, x)
            own = view(lay, p, g, i, c, x, z, y)
            finish = functools.partial(
                set_sum, out, [own] + [slot3.at[k] for k in range(lay.nz - 1)]
            )
            share_x = [
                remote(out, out, fx_s.at[t, k], fx_r.at[t, k], peer) for k, peer in enumerate(xs)
            ]
            both = shard_view(lay, f, g, i, c, ALL)
            share_c = [remote(both, both, fc_s.at[t], fc_r.at[t], cs[0])]
            self.steps.append(
                (
                    (core, first, second, third, share_x, share_c),
                    (None, add_core, add_1, add_2, finish, None),
                )
            )

    def step(self, t, k):
        copies, adds = self.steps[t]
        if k > 0:
            arrive(copies[k - 1])
        if k < len(copies):
            if adds[k] is not None:
                adds[k]()
            start(copies[k])

    def drain(self):
        for copies, _ in self.steps:
            for group in copies:
                sent(group)


def set_sum(out, srcs):
    total = srcs[0][...].astype(F32)
    for src in srcs[1:]:
        total = total + src[...].astype(F32)
    out[...] = total.astype(BF)


def add_into(dst, srcs):
    lead = dst.shape[:-2]

    def body(j, carry):
        index = []
        rest = j
        for size in reversed(lead):
            index.append(lax.rem(rest, size))
            rest = rest // size
        index = tuple(reversed(index))
        total = dst[index].astype(F32)
        for src in srcs:
            total = total + src[index].astype(F32)
        dst[index] = total.astype(BF)
        return carry

    lax.fori_loop(0, math.prod(lead), body, 0)


def norm_back(grad, gain, normed, factor):
    inner = grad * gain
    return factor * (
        inner
        - jnp.mean(inner, -1, keepdims=True)
        - normed * jnp.mean(inner * normed, -1, keepdims=True)
    )


FF_CHUNKS = FF // D


def back_kernel(
    lay, rows, docs,
    g_up, g_down, p_att, fg_prev, fg_own, attn_out, vectors, up_add, att_sums, tok, grad, seg,
    output, input_grad, f_att, f_up, f_down, vec_out,
    p_up, p_down, w_up, w_down, second_in, second_t, act_s, pg_s, sg_acc, hop, home,
    ca, ra1, rb1, ra2, rb2, ra3, v_c, v_x, v_y, v_z, *sems,
):
    (c_s, c_r, x_s, x_r, y_s, y_r, z_s, z_r, fx_s, fx_r, fc_s, fc_r, v_s, v_r, w_sem, h_s, h_r) = sems
    r = p_att.shape[2]
    x, c, z, y = lay.coords()
    xs, cs, zs, ys = line_peers(lay)
    total = lay.dp * lay.fsdp
    b = lax.axis_index("dp") * lay.fsdp + lax.axis_index("fsdp")

    def stream(k):
        t = wrap(b + k, total)
        return {"dp": t // lay.fsdp, "fsdp": lax.rem(t, lay.fsdp)}

    around = [stream(2), stream(-2), stream(1), stream(-1)]
    near_z = lay.nz // FF_CHUNKS
    loads = []
    for k in range(FF_CHUNKS):
        slot = k % 2
        loads.append(
            (
                pltpu.make_async_copy(
                    g_up.at[:, :, :, pl.ds(D * k, D)], w_up.at[slot], w_sem.at[0, k]
                ),
                pltpu.make_async_copy(
                    g_down.at[pl.ds(near_z * k, near_z)], w_down.at[slot], w_sem.at[1, k]
                ),
            )
        )
    start(loads[0])
    start(loads[1])
    barrier_with(xs + cs + zs + ys + around)
    net = Reduce(
        lay, (p_att, p_up, p_down), (f_att, f_up, f_down), (ca, ra1, rb1, ra2, rb2, ra3), sems[:12]
    )
    for t in range(3):
        net.step(t, 0)
    even = lax.rem(b, 2) == 0
    one, two = fg_prev.at[pl.ds(rows, rows)], fg_prev.at[pl.ds(0, rows)]
    to_next = remote(one, hop, h_s.at[0], h_r.at[0], around[2])
    to_last = remote(one, hop, h_s.at[0], h_r.at[0], around[3])
    to_owner = remote(two, home, h_s.at[1], h_r.at[1], around[1])

    @pl.when(even)
    def _():
        to_next.start()
        to_owner.start()

    @pl.when(jnp.logical_not(even))
    def _():
        to_last.start()

    gain_first, gain_second = vectors[0:1, :], vectors[2:3, :]
    normed, factor = norm_parts(tok[...].astype(F32))
    value = (normed * gain_second + vectors[3:4, :]).astype(BF)
    second_in[...] = value
    second_t[...] = value.T
    cot = grad[...].astype(F32)
    output_base = attn_out
    output_base[...] = attn_out[...] + tok[...].astype(F32) + vectors[4:5, :]
    sg_acc[...] = jnp.zeros_like(sg_acc)
    mine = v_c.at[c]
    mine[...] = jnp.zeros((16, D), F32)
    for t in range(3):
        net.step(t, 1)

    events = [
        [(0, 2)],
        [(3, 0), (2, 2), (1, 2), (0, 3)],
        [(4, 0), (3, 1), (2, 3), (1, 3), (0, 4)],
        [(1, 4), (2, 4), (0, 5)],
    ]
    root = math.sqrt(0.5)
    level = 1.0 / math.sqrt(2.0 * math.pi)

    def forward_halo():
        to_last.wait_recv()

        @pl.when(jnp.logical_not(even))
        def _():
            add_into(two.reshape((2, rows // 2, D)), [hop.reshape((2, rows // 2, D))])
            to_owner.start()

    def chunk(k, squares):
        slot = lax.rem(k, 2)
        for n in range(FF_CHUNKS):

            @pl.when(k == n)
            def _(n=n):
                loads[n][0].wait()
                loads[n][1].wait()

        down = w_down[slot].reshape(D, D)
        for j in range(3):
            tile = slice(256 * j, 256 * (j + 1))
            col = pl.ds(pl.multiple_of(D * k + 256 * j, 256), 256)
            pre = mm(second_in[...], w_up[slot, :, :, :, tile].reshape(D, 256)) + up_add[:, col]
            hidden = mm(grad[...], down[tile, :], NT)
            half = 0.5 + 0.5 * lax.erf(pre * root)
            act = (pre * half).astype(BF)
            slope = half + pre * jnp.exp(-0.5 * pre * pre) * level
            pg = (hidden * slope).astype(BF)
            act_s[:, tile] = act
            pg_s[:, tile] = pg
            wide = act.astype(F32)
            squares = squares + jnp.sum(wide * wide, -1, keepdims=True)
            v_c[c, pl.ds(8 + k, 1), tile] = jnp.sum(pg.astype(F32), 0, keepdims=True)
        p_up[:, :, :, pl.ds(pl.multiple_of(D * k, 256), D)] = (
            mm(second_t[...], pg_s[...]).astype(BF).reshape(lay.nz, lay.ny, r, D)
        )
        p_down[pl.ds(near_z * k, near_z)] = (
            mm(act_s[...].T, grad[...]).astype(BF).reshape(near_z, lay.ny, 4, r, D)
        )
        output_base[...] += mm(act_s[...], down)
        sg_acc[...] += mm(pg_s[...], w_up[slot].reshape(D, D), NT)
        for n in range(FF_CHUNKS):

            @pl.when(k == n)
            def _(n=n):
                if n + 2 < FF_CHUNKS:
                    start(loads[n + 2])
                for event in events[n]:
                    net.step(*event)
                if n == 2:
                    forward_halo()

        return squares

    squares = lax.fori_loop(0, FF_CHUNKS, chunk, jnp.zeros((rows, 1), F32))
    net.step(5, 0)
    net.step(4, 1)
    net.step(3, 2)
    output[...] = output_base[...].astype(BF)
    net.step(6, 0)
    net.step(5, 1)
    net.step(7, 0)
    net.step(8, 0)

    to_owner.wait_recv()
    total_first = fg_own[...] + home[...].astype(F32)
    keep = jnp.where(even, 1.0, 0.0).astype(F32)
    fg_own[...] = total_first + hop[...].astype(F32) * keep
    first_grad = fg_own[...]
    second_grad = sg_acc[...]
    normed, factor = norm_parts(tok[...].astype(F32))
    input_grad[...] = (
        grad[...].astype(F32)
        + norm_back(first_grad, gain_first, normed, factor)
        + norm_back(second_grad, gain_second, normed, factor)
    ).astype(BF)
    net.step(4, 2)
    net.step(6, 1)

    def put(k, value):
        v_c[c, k : k + 1, :] = value

    put(0, jnp.sum(first_grad * normed, 0, keepdims=True))
    put(1, jnp.sum(first_grad, 0, keepdims=True))
    put(2, jnp.sum(second_grad * normed, 0, keepdims=True))
    put(3, jnp.sum(second_grad, 0, keepdims=True))
    cot = grad[...].astype(F32)
    put(4, jnp.sum(cot, 0, keepdims=True))
    for k in range(3):
        put(5 + k, att_sums[k : k + 1, :])
    token_norm = squares * jnp.sum(cot * cot, -1, keepdims=True) * (1.0 / (FF * D))
    docs_of = jnp.concatenate([seg[...].astype(F32)] * (LANES // 8), 0).T[:, 0:1]
    doc = lax.broadcasted_iota(jnp.int32, (rows, D), 1).astype(F32)
    member = jnp.where((docs_of == doc) & (doc < docs), 1.0, 0.0)
    put(12, jnp.sum(token_norm * member, 0, keepdims=True))
    put(13, jnp.sum(member, 0, keepdims=True))

    at = [0, 1, lay.nx, lay.nx + lay.ny - 1]

    def spread(ref, own, peers, base):
        return [
            remote(ref.at[own], ref.at[own], v_s.at[base + k], v_r.at[base + k], p)
            for k, p in enumerate(peers)
        ]

    vec_c = spread(v_c, c, cs, at[0])
    vec_x = spread(v_x, x, xs, at[1])
    vec_y = spread(v_y, y, ys, at[2])
    vec_z = spread(v_z, z, zs, at[3])

    def add_all(ref, size):
        value = ref[0]
        for k in range(1, size):
            value = value + ref[k]
        return value

    start(vec_c)
    net.step(3, 3)
    net.step(5, 2)
    arrive(vec_c)
    v_x[x] = add_all(v_c, 2)
    start(vec_x)
    net.step(7, 1)
    net.step(8, 1)
    net.step(4, 3)
    arrive(vec_x)
    v_y[y] = add_all(v_x, lay.nx)
    start(vec_y)
    net.step(5, 3)
    net.step(3, 4)
    net.step(6, 2)
    arrive(vec_y)
    v_z[z] = add_all(v_y, lay.ny)
    start(vec_z)
    net.step(4, 4)
    net.step(1, 5)
    net.step(2, 5)
    net.step(8, 2)
    net.step(6, 3)
    net.step(7, 2)
    arrive(vec_z)
    vec_out[...] = add_all(v_z, lay.nz)
    net.step(5, 4)
    net.step(3, 5)
    net.step(8, 3)
    net.step(7, 3)
    net.step(4, 5)
    net.step(5, 5)
    for t in (6, 8, 7):
        net.step(t, 4)
    for t in (6, 8, 7):
        net.step(t, 5)
    for t in range(9):
        net.step(t, 6)
    net.drain()
    sent(vec_c + vec_x + vec_y + vec_z)
    to_next.wait_send()
    to_owner.wait_send()


def back(lay, g_up, g_down, p_att, fg_prev, fg_own, attn_out, vectors, up_add, att_sums, tok, grad, seg):
    rows = tok.shape[0]
    r = p_att.shape[2]
    n = len(CHUNKS)
    docs = DOC_DEV * lay.dp * lay.fsdp
    outs = (
        jax.ShapeDtypeStruct((rows, D), BF),
        jax.ShapeDtypeStruct((rows, D), BF),
        jax.ShapeDtypeStruct((r, 4 * D), BF),
        jax.ShapeDtypeStruct((r, 4 * D), BF),
        jax.ShapeDtypeStruct((4, r, D), BF),
        jax.ShapeDtypeStruct((16, D), F32),
    )
    lx, ly, lz = max(1, lay.nx - 1), max(1, lay.ny - 1), max(1, lay.nz - 1)

    def v(shape, dtype=BF):
        return pltpu.VMEM(shape, dtype)

    def bufs(chunks, peers, x_all, z_all, y_all):
        return [v((chunks,) + peers + part_shape(lay, g, x_all, z_all, y_all, r)) for g in range(3)]

    scratch = [
        v(grad_shape(lay, 1, r)), v(grad_shape(lay, 2, r)),
        v((2, lay.nz, lay.ny, r, D)), v((2, lay.nz // FF_CHUNKS, lay.ny, 4, r, D)),
        v((rows, D)), v((D, rows)), v((rows, D)), v((rows, D)), v((rows, D), F32),
        v((rows, D)), v((rows, D)),
        bufs(3, (), True, True, True),
        bufs(2, (lx,), False, True, True),
        bufs(1, (ly,), True, True, False),
        bufs(2, (ly,), False, True, False),
        bufs(1, (lx,), False, True, False),
        bufs(3, (lz,), False, False, False),
    ]
    vecs = [v((k, 16, D), F32) for k in (2, lay.nx, lay.ny, lay.nz)]
    nv = 1 + lay.nx + lay.ny + lay.nz
    sems = [
        dma(n), dma(n), dma(n, lx), dma(n, lx), dma(n, ly), dma(n, ly), dma(n, lz), dma(n, lz),
        dma(n, lx), dma(n, lx), dma(n), dma(n), dma(nv), dma(nv), dma(2, FF_CHUNKS), dma(2), dma(2),
    ]
    vmem = pl.BlockSpec(memory_space=pltpu.VMEM)
    return pl.pallas_call(
        functools.partial(back_kernel, lay, rows, docs),
        name="back",
        out_shape=outs,
        in_specs=hbm(2) + [vmem] * 10,
        out_specs=(vmem,) * 6,
        scratch_shapes=scratch + vecs + sems,
        compiler_params=pltpu.CompilerParams(
            collective_id=1, has_side_effects=True, vmem_limit_bytes=VMEM_LIMIT
        ),
    )(g_up, g_down, p_att, fg_prev, fg_own, attn_out, vectors, up_add, att_sums, tok, grad, seg)


def per_device(
    lay, tokens, seg_ids, out_grad, first_gain, first_bias, second_gain, second_bias,
    qkv_weight, qkv_bias, dense_weight, up_weight, up_bias, down_weight, out_bias,
):
    rows = tokens.shape[0]
    r = qkv_weight.shape[0]
    fsdp = lay.fsdp
    qkv_kinds = qkv_weight.reshape(r, H, 3, HD).transpose(0, 2, 1, 3).reshape(r, 3 * D)
    u_att = jnp.concatenate([qkv_kinds, dense_weight], 1)
    u_down = down_weight.reshape(4, r, D)
    vectors = (first_gain, first_bias, second_gain, second_bias, out_bias, qkv_bias, up_bias)
    small = jnp.pad(jnp.concatenate(vectors).reshape(12, r), ((0, 4), (0, LANES - r)))
    seg_rows = jnp.broadcast_to(seg_ids[None, :], (8, rows))
    passed = front(lay, u_att, up_weight, u_down, small, tokens, out_grad, seg_rows)
    output, input_grad, f_att, f_up, f_down, vec = back(lay, *passed, tokens, out_grad, seg_rows)
    docs = DOC_DEV * lay.dp * fsdp
    shard = lax.axis_index("fsdp")
    plain = lax.dynamic_slice_in_dim(vec[:5], shard * r, r, 1)
    kinds = vec[5:8].reshape(3, H, HD).transpose(1, 0, 2).reshape(3 * D)
    qkv_add = lax.dynamic_slice_in_dim(kinds, shard * 3 * r, 3 * r)
    up_add = lax.dynamic_slice_in_dim(vec[8:12].reshape(FF), shard * 4 * r, 4 * r)
    qkv_out = (
        f_att[:, : 3 * D].astype(F32).reshape(r, 3, H, HD).transpose(0, 2, 1, 3).reshape(r, 3 * D)
    )
    return (
        output,
        input_grad,
        plain[0],
        plain[1],
        plain[2],
        plain[3],
        qkv_out,
        qkv_add,
        f_att[:, 3 * D :].astype(F32),
        f_up.astype(F32),
        up_add,
        f_down.reshape(4 * r, D).astype(F32),
        plain[4],
        vec[12, :docs] / vec[13, :docs],
    )


def solution(mesh):
    lay = Layout(mesh.shape["dp"], mesh.shape["fsdp"])
    both = P(("dp", "fsdp"))
    split = P("fsdp")
    in_specs = (both, both, both) + (split,) * 11
    out_specs = (both, both) + (split,) * 11 + (P(),)
    return jax.shard_map(
        functools.partial(per_device, lay), mesh=mesh, in_specs=in_specs, out_specs=out_specs,
        check_vma=False,
    )
```

```python
import functools
import math

import jax
import jax.numpy as jnp
from jax import lax
from jax.experimental import pallas as pl
from jax.experimental.pallas import tpu as pltpu
from jax.sharding import PartitionSpec as P

D = 768
H = 12
HD = 64
FF = 3072
ROT = 16
ROW = 2048
DOC_DEV = 2
LANES = 128
PAIRS = D // LANES
MESH = pl.DeviceIdType.MESH
VMEM_LIMIT = 60 * 1024 * 1024


class Layout:
    def __init__(self, dp, fsdp):
        self.dp, self.fsdp = dp, fsdp
        self.nc = 2
        self.nx = dp // 2
        ny = 1
        while (2 * ny) * (2 * ny) <= fsdp:
            ny *= 2
        self.ny, self.nz = ny, fsdp // ny
        self.sub = max(1, self.nx // 2)
        self.unit = 4 // self.nx
        self.down_unit = 2 // self.sub

    def coords(self):
        d, f = lax.axis_index("dp"), lax.axis_index("fsdp")
        return d // 2, d % 2, f // self.ny, f % self.ny

    def device(self, x, c, z, y):
        return {"dp": x * 2 + c, "fsdp": z * self.ny + y}


def wrap(value, size):
    return lax.rem(value + size, size)


CHUNKS = tuple((g, i) for g in range(3) for i in range(3))
ALL = slice(None)


def grad_shape(lay, group, r):
    return (lay.nz, lay.ny, r, 4 * D) if group < 2 else (lay.nz, lay.ny, 4, r, D)


def span_of(lay, group, i, c, x):
    if group < 2:
        width = 512 // lay.nx
        if x is ALL:
            return pl.ds(pl.multiple_of(1024 * i + 512 * c, LANES), 512), None
        return pl.ds(pl.multiple_of(1024 * i + 512 * c + width * x, LANES), width), None
    width = 256 // lay.sub
    if x is ALL:
        return pl.ds(256 * i, 256), pl.ds(2 * c, 2)
    start = 256 * i + width * lax.rem(x, lay.sub)
    return pl.ds(pl.multiple_of(start, LANES), width), 2 * c + x // lay.sub


def view(lay, ref, group, i, c, x, z, y):
    cols, quarter = span_of(lay, group, i, c, x)
    if group < 2:
        return ref.at[z, y, :, cols]
    return ref.at[z, y, quarter, :, cols]


def shard_view(lay, ref, group, i, c, x):
    cols, quarter = span_of(lay, group, i, c, x)
    if group < 2:
        return ref.at[:, cols]
    return ref.at[quarter, :, cols]


def part_shape(lay, group, x_all, z_all, y_all, r):
    lead = ((lay.nz,) if z_all else ()) + ((lay.ny,) if y_all else ())
    if group < 2:
        return lead + (r, 512 if x_all else 512 // lay.nx)
    return lead + ((2, r, 256) if x_all else (r, 256 // lay.sub))


def barrier_with(peers):
    sem = pltpu.get_barrier_semaphore()
    for peer in peers:
        pl.semaphore_signal(sem, inc=1, device_id=peer, device_id_type=MESH)
    pl.semaphore_wait(sem, len(peers))


def line_peers(lay):
    x, c, z, y = lay.coords()
    xs = [lay.device(wrap(x + k, lay.nx), c, z, y) for k in range(1, lay.nx)]
    ys = [lay.device(x, c, z, wrap(y + k, lay.ny)) for k in range(1, lay.ny)]
    zs = [lay.device(x, c, wrap(z + k, lay.nz), y) for k in range(1, lay.nz)]
    cs = [lay.device(x, 1 - c, z, y)]
    return xs, cs, zs, ys


def remote(src, dst, ssem, rsem, device):
    return pltpu.make_async_remote_copy(
        src_ref=src, dst_ref=dst, send_sem=ssem, recv_sem=rsem, device_id=device, device_id_type=MESH
    )


def start(copies):
    for copy in copies:
        copy.start()


def arrive(copies):
    for copy in copies:
        copy.wait_recv()


def sent(copies):
    for copy in copies:
        copy.wait_send()


def hbm(count):
    return [pl.BlockSpec(memory_space=pltpu.HBM)] * count


def dma(*shape):
    return pltpu.SemaphoreType.DMA(shape)


NT = (((1,), (1,)), ((), ()))
NN = (((1,), (0,)), ((), ()))
F32 = jnp.float32
BF = jnp.bfloat16


def mm(a, b, dims=NN):
    return lax.dot_general(a, b, dims, preferred_element_type=F32)


def norm_parts(values):
    middle = jnp.mean(values, -1, keepdims=True)
    centred = values - middle
    factor = lax.rsqrt(jnp.mean(centred * centred, -1, keepdims=True) + 1e-05)
    return centred * factor, factor


def small_plan(r):
    plan, at = [], 0
    for size, within in [(r, LANES)] * 5 + [(3 * r, HD), (4 * r, LANES)]:
        unit = math.gcd(size, within)
        plan.append((at, size // unit, unit))
        at += size // unit
    return plan


def pack_small(vectors, r):
    rows = [
        jnp.tile(v.reshape(-1, unit), (1, LANES // unit))
        for v, (_, _, unit) in zip(vectors, small_plan(r))
    ]
    packed = jnp.concatenate(rows, 0).astype(F32)
    return jnp.pad(packed, ((0, -packed.shape[0] % 8), (0, 0)))


class Gather:
    def __init__(self, lay, gs, sems):
        (z_s, z_r, y_s, y_r, x_s, x_r, c_s, c_r) = sems
        x, c, z, y = lay.coords()
        xs, cs, zs, ys = line_peers(lay)
        self.stages = []
        for t, (g, i) in enumerate(CHUNKS):
            by_y, by_x = (ys, y_s, y_r), (xs, x_s, x_r)
            first, second = (by_y, by_x) if i < 2 else (by_x, by_y)
            middle = (x, ALL, ALL) if i < 2 else (ALL, ALL, y)
            steps = [
                ((zs, z_s, z_r), (x, z, y)),
                (first, (x, ALL, y)),
                (second, middle),
            ]
            stages = []
            for (peers, ss, rs), (px, pz, py) in steps:
                piece = view(lay, gs[g], g, i, c, px, pz, py)
                stages.append(
                    [remote(piece, piece, ss.at[t, k], rs.at[t, k], p) for k, p in enumerate(peers)]
                )
            piece = view(lay, gs[g], g, i, c, ALL, ALL, ALL)
            stages.append([remote(piece, piece, c_s.at[t], c_r.at[t], cs[0])])
            self.stages.append(stages)

    def issue(self, t, stage):
        start(self.stages[t][stage])

    def pass_on(self, t, stage):
        arrive(self.stages[t][stage - 1])
        start(self.stages[t][stage])

    def done(self, t):
        arrive(self.stages[t][3])

    def drain(self):
        for stages in self.stages:
            for copies in stages:
                sent(copies)


def rope(u, cos, low, high):
    return u * cos + pltpu.roll(u, LANES - 8, 1) * low + pltpu.roll(u, 8, 1) * high


def front_kernel(
    lay, rows,
    u_att, u_up, u_down, small, tok, grad, seg,
    g_up, g_down, p_att, fg_prev, fg_own, attn_out, vectors, up_add, att_sums,
    g_att, g_small, tok_halo, seg_halo, first_all, first_t, q_s, k_s, v_s, do_s, ctx_s, ctx_t,
    dq_s, dk_s, dv_s, cos_s, low_s, high_s, bias, dk_acc, dv_acc, qkv_add, s_s, w_s, d_s,
    local_sem, z_s, z_r, y_s, y_r, x_s, x_r, c_s, c_r, sm_s, sm_r, h_s, h_r,
):
    span = 3 * rows
    r = u_att.shape[0]
    x, c, z, y = lay.coords()
    xs, cs, zs, ys = line_peers(lay)
    total = lay.dp * lay.fsdp
    b = lax.axis_index("dp") * lay.fsdp + lax.axis_index("fsdp")

    def stream(k):
        t = wrap(b + k, total)
        return {"dp": t // lay.fsdp, "fsdp": lax.rem(t, lay.fsdp)}

    around = [stream(2), stream(-2), stream(1), stream(-1)]
    barrier_with(xs + cs + zs + ys + around)
    gs = (g_att, g_up, g_down)
    us = (u_att, u_up, u_down)
    locals_ = [pltpu.make_async_copy(small, g_small.at[z, y], local_sem.at[9])]
    for t, (g, i) in enumerate(CHUNKS):
        locals_.append(
            pltpu.make_async_copy(
                shard_view(lay, us[g], g, i, c, x), view(lay, gs[g], g, i, c, x, z, y), local_sem.at[t]
            )
        )
    start(locals_)
    even = lax.rem(b, 2) == 0
    half = rows // 2
    halo, own, passed = [], [], []
    for k in range(2):
        part = pl.ds(k * half, half)
        halo.append(remote(tok.at[part], tok_halo.at[0, part], h_s.at[k], h_r.at[k], around[0]))
        own.append(remote(tok.at[part], tok_halo.at[1, part], h_s.at[2 + k], h_r.at[2 + k], around[2]))
        passed.append(
            remote(tok_halo.at[0, part], tok_halo.at[1, part], h_s.at[2 + k], h_r.at[2 + k], around[3])
        )
    segs = [
        remote(seg, seg_halo.at[0], h_s.at[4], h_r.at[4], around[0]),
        remote(seg, seg_halo.at[1], h_s.at[5], h_r.at[5], around[2]),
    ]
    small_z = [
        remote(g_small.at[z, y], g_small.at[z, y], sm_s.at[k], sm_r.at[k], p) for k, p in enumerate(zs)
    ]
    small_y = [
        remote(g_small.at[:, y], g_small.at[:, y], sm_s.at[lay.nz + k], sm_r.at[lay.nz + k], p)
        for k, p in enumerate(ys)
    ]
    net = Gather(lay, gs, (z_s, z_r, y_s, y_r, x_s, x_r, c_s, c_r))

    for copy in locals_:
        copy.wait()
    start(small_z)
    start(segs)
    for t in range(3):
        net.issue(t, 0)
    start(halo)

    @pl.when(even)
    def _():
        start(own)

    def norm_rows(values):
        return norm_parts(values.astype(F32))[0]

    normed = norm_rows(tok[...])
    net.pass_on(0, 1)
    arrive(small_z)
    start(small_y)

    def tables(k, carry):
        at = pl.ds(pl.multiple_of(k * 256, 256), 256)
        lane = lax.broadcasted_iota(jnp.int32, (256, LANES), 1) % HD
        row = lax.broadcasted_iota(jnp.int32, (256, LANES), 0) + k * 256
        place = lax.rem((b - 2) * rows + row + 4 * ROW, ROW).astype(F32)
        rate = jnp.exp((lane % 8).astype(F32) * (-math.log(10000.0) / 8.0))
        angle = place * rate
        sine = jnp.sin(angle)
        cos_s[at, :] = jnp.where(lane < ROT, jnp.cos(angle), 1.0)
        low_s[at, :] = jnp.where(lane < 8, -sine, 0.0)
        high_s[at, :] = jnp.where((lane >= 8) & (lane < ROT), sine, 0.0)
        return carry

    net.pass_on(1, 1)
    lax.fori_loop(0, span // 256, tables, 0)
    net.pass_on(2, 1)
    arrive(small_y)

    lane_row = lax.broadcasted_iota(jnp.int32, (1, LANES), 1)

    def line(first_row, per, unit, length, source):
        out = []
        for block in range(length // LANES):
            value = None
            for k in range(LANES // unit):
                at = source(block * (LANES // unit) + k)
                owner = at // per
                row = first_row + at % per
                piece = g_small[owner // lay.ny, owner % lay.ny, row : row + 1, :]
                value = piece if value is None else jnp.where(lane_row // unit == k, piece, value)
            out.append(value)
        return jnp.concatenate(out, 1)

    plan = small_plan(r)
    for j in range(5):
        vectors[j : j + 1, :] = line(*plan[j], D, lambda n: n)
    vectors[5:8, :] = jnp.zeros((3, D), F32)
    unit = plan[5][2]
    a_head = HD // unit

    def natural(n):
        kind, rest = divmod(n, D // unit)
        head, part = divmod(rest, a_head)
        return head * 3 * a_head + kind * a_head + part

    qkv_add[...] = line(*plan[5], 3 * D, natural)
    up_add[...] = line(*plan[6], FF, lambda n: n)
    net.pass_on(0, 2)

    arrive([halo[0]])

    @pl.when(jnp.logical_not(even))
    def _():
        passed[0].start()

    net.pass_on(1, 2)
    net.pass_on(2, 2)

    arrive([halo[1]])

    @pl.when(jnp.logical_not(even))
    def _():
        passed[1].start()

    net.issue(3, 0)
    net.issue(4, 0)
    gain, shift = vectors[0:1, :], vectors[1:2, :]
    own_rows = pl.ds(2 * rows, rows)
    first = (normed * gain + shift).astype(BF)
    first_all[own_rows, :] = first
    first_t[:, own_rows] = first.T

    arrive(segs)
    least = jnp.maximum(0, 2 * rows - b * rows)
    keys_doc = jnp.concatenate([seg_halo[0], seg_halo[1], seg[...]], 1).astype(F32)
    keys_doc = jnp.concatenate([keys_doc] * (LANES // 8), 0).T
    query_doc = seg[0:1, :].astype(F32)

    for k in range(6):
        at = slice(k * 256, (k + 1) * 256)
        key_at = lax.broadcasted_iota(jnp.int32, (256, rows), 0) + k * 256
        query_at = lax.broadcasted_iota(jnp.int32, (256, rows), 1) + 2 * rows
        allowed = (keys_doc[at, 0:1] == query_doc) & (key_at <= query_at) & (key_at >= least)
        bias[at, :] = jnp.where(allowed, 0.0, -1e30)
    net.pass_on(0, 3)
    net.pass_on(1, 3)
    net.pass_on(2, 3)
    net.issue(5, 0)
    for t in range(3):
        net.done(t)
    net.pass_on(3, 1)

    def weight(first_col, width):
        value = g_att[:, :, :, pl.ds(first_col, width)]
        return value.reshape(D, width)

    scale = 1.0 / math.sqrt(HD)
    do_s[...] = mm(grad[...], weight(3 * D, D), NT).astype(BF)

    def project(kind, j, at, out, factor):
        col = pl.multiple_of(kind * D + 256 * j, 256)
        value = mm(first_all[at, :], weight(col, 256)) + qkv_add[:, pl.ds(col, 256)]
        for k in range(2):
            u = value[:, k * LANES : (k + 1) * LANES]
            if kind < 2:
                u = rope(u, cos_s[at, :], low_s[at, :], high_s[at, :])
            if factor is not None:
                u = u * factor
            out[:, pl.ds(pl.multiple_of(256 * j + LANES * k, LANES), LANES)] = u.astype(BF)

    def own_projections(j, carry):
        project(0, j, own_rows, q_s, scale)
        project(1, j, own_rows, k_s.at[own_rows], None)
        project(2, j, own_rows, v_s.at[own_rows], None)
        return carry

    lax.fori_loop(0, 3, own_projections, 0)
    net.pass_on(4, 1)
    own[0].wait_recv()
    own[1].wait_recv()
    net.pass_on(5, 1)
    for k in range(2):
        at = slice(k * rows, (k + 1) * rows)
        before = (norm_rows(tok_halo[k]) * gain + shift).astype(BF)
        first_all[at, :] = before
        first_t[:, at] = before.T
    net.pass_on(3, 2)

    def earlier_projections(j, carry):
        for k in range(2):
            at = pl.ds(k * rows, rows)
            project(1, j, at, k_s.at[at], None)
            project(2, j, at, v_s.at[at], None)
        return carry

    lax.fori_loop(0, 3, earlier_projections, 0)
    net.issue(6, 0)
    net.pass_on(4, 2)

    later = [
        [lambda: net.pass_on(5, 2), lambda: net.issue(7, 0), lambda: net.pass_on(6, 1)],
        [lambda: net.pass_on(3, 3), lambda: net.issue(8, 0)],
        [lambda: net.pass_on(4, 3), lambda: net.pass_on(7, 1), lambda: net.pass_on(6, 2)],
        [lambda: net.pass_on(5, 3), lambda: net.pass_on(8, 1), lambda: net.pass_on(7, 2)],
        [lambda: net.pass_on(6, 3), lambda: net.pass_on(8, 2)],
        [lambda: net.pass_on(7, 3)],
    ]
    tile = 256

    def pair(p, carry):
        lanes = pl.ds(pl.multiple_of(p * LANES, LANES), LANES)
        v_t, k_t = v_s[:, lanes].T, k_s[:, lanes].T
        do_t = do_s[:, lanes].astype(F32).T
        lane = lax.broadcasted_iota(jnp.int32, (tile, LANES), 1)
        zero = jnp.zeros((), BF)
        for t in range(rows // tile):
            cols = slice(t * tile, (t + 1) * tile)
            kl = 2 * rows + (t + 1) * tile
            pieces = [slice(k * tile, (k + 1) * tile) for k in range(kl // tile)]
            qms = [jnp.where((lane // HD) == hh, q_s[cols, lanes], zero) for hh in range(2)]
            doms = [jnp.where((lane // HD) == hh, do_s[cols, lanes], zero) for hh in range(2)]
            tops, norms = [], []
            for hh in range(2):
                top = None
                for at in pieces:
                    st = mm(k_s[at, lanes], qms[hh], NT) + bias[at, cols]
                    s_s[hh, at, :] = st
                    most = jnp.max(st, 0, keepdims=True)
                    top = most if top is None else jnp.maximum(top, most)
                tops.append(top)
            for hh in range(2):
                total_e = None
                for at in pieces:
                    e = jnp.exp(s_s[hh, at, :] - tops[hh])
                    s_s[hh, at, :] = e
                    part = jnp.sum(e, 0, keepdims=True)
                    total_e = part if total_e is None else total_e + part
                norms.append(1.0 / total_e)
            outs, dqs = [], []
            for hh in range(2):
                for at in pieces:
                    w_s[hh, at, :] = (s_s[hh, at, :] * norms[hh]).astype(BF)
            for hh in range(2):
                part = slice(hh * HD, (hh + 1) * HD)
                o_t = mm(v_t[part, :kl], w_s[hh, :kl, :])
                delta = jnp.sum(o_t * do_t[part, cols], 0, keepdims=True)
                outs.append(o_t)
                for at in pieces:
                    dp = mm(v_s[at, lanes], doms[hh], NT)
                    d_s[hh, at, :] = ((s_s[hh, at, :] * norms[hh]) * (dp - delta)).astype(BF)
                dqs.append(mm(k_t[part, :kl], d_s[hh, :kl, :]))
            for k, at in enumerate(pieces):
                dk = mm(d_s[0, at, :], qms[0]) + mm(d_s[1, at, :], qms[1])
                dv = mm(w_s[0, at, :], doms[0]) + mm(w_s[1, at, :], doms[1])
                if t == 0 or k == len(pieces) - 1:
                    dk_acc[at, :] = dk
                    dv_acc[at, :] = dv
                else:
                    dk_acc[at, :] += dk
                    dv_acc[at, :] += dv
            o_pair = jnp.concatenate(outs, 0)
            ctx_t[lanes, cols] = o_pair.astype(BF)
            ctx_s[cols, lanes] = o_pair.T.astype(BF)
            dq = jnp.concatenate(dqs, 0).T * scale
            at = slice(2 * rows + t * tile, 2 * rows + (t + 1) * tile)
            dq_s[cols, lanes] = rope(dq, cos_s[at, :], -low_s[at, :], -high_s[at, :]).astype(BF)
        dk_s[:, lanes] = rope(dk_acc[...], cos_s[...], -low_s[...], -high_s[...]).astype(BF)
        dv_s[:, lanes] = dv_acc[...].astype(BF)
        for k, events in enumerate(later):

            @pl.when(p == k)
            def _(events=events):
                for event in events:
                    event()

        return carry

    lax.fori_loop(0, PAIRS, pair, 0)
    net.pass_on(8, 3)

    def earlier_grad(k, carry):
        at = pl.ds(pl.multiple_of(k * 256, 256), 256)
        value = mm(dk_s[at, :], weight(D, D), NT) + mm(dv_s[at, :], weight(2 * D, D), NT)
        fg_prev[at, :] = value.astype(BF)
        return carry

    lax.fori_loop(0, 2 * rows // 256, earlier_grad, 0)
    for k in range(rows // 256):
        at = slice(2 * rows + 256 * k, 2 * rows + 256 * (k + 1))
        near = slice(256 * k, 256 * (k + 1))
        fg_own[near, :] = (
            mm(dk_s[at, :], weight(D, D), NT)
            + mm(dv_s[at, :], weight(2 * D, D), NT)
            + mm(dq_s[near, :], weight(0, D), NT)
        )

    def weight_grads(j, carry):
        col = pl.multiple_of(256 * j, 256)
        cols = pl.ds(col, 256)

        def put(kind, value):
            p_att[:, :, :, pl.ds(pl.multiple_of(kind * D + col, 256), 256)] = value.astype(BF).reshape(
                lay.nz, lay.ny, r, 256
            )

        put(0, mm(first_t[:, own_rows], dq_s[:, cols]))
        put(1, mm(first_t[...], dk_s[:, cols]))
        put(2, mm(first_t[...], dv_s[:, cols]))
        put(3, mm(ctx_t[...], grad[:, cols]))
        attn_out[:, cols] = mm(ctx_s[...], weight(pl.multiple_of(3 * D + col, 256), 256))
        return carry

    lax.fori_loop(0, 3, weight_grads, 0)
    for k, ref in enumerate((dq_s, dk_s, dv_s)):
        att_sums[k : k + 1, :] = jnp.sum(ref[...].astype(F32), 0, keepdims=True)
    att_sums[3:8, :] = jnp.zeros((5, D), F32)
    for t in range(3, 9):
        net.done(t)
    net.drain()
    sent(small_z + small_y + segs + halo + own)


def front(lay, u_att, u_up, u_down, small, tok, grad, seg):
    rows = tok.shape[0]
    span = 3 * rows
    r = u_att.shape[0]
    n = len(CHUNKS)
    outs = (
        jax.ShapeDtypeStruct(grad_shape(lay, 1, r), BF),
        jax.ShapeDtypeStruct(grad_shape(lay, 2, r), BF),
        jax.ShapeDtypeStruct(grad_shape(lay, 0, r), BF),
        jax.ShapeDtypeStruct((2 * rows, D), BF),
        jax.ShapeDtypeStruct((rows, D), F32),
        jax.ShapeDtypeStruct((rows, D), F32),
        jax.ShapeDtypeStruct((8, D), F32),
        jax.ShapeDtypeStruct((1, FF), F32),
        jax.ShapeDtypeStruct((8, D), F32),
    )
    vmem = pl.BlockSpec(memory_space=pltpu.VMEM)
    lx, ly, lz = max(1, lay.nx - 1), max(1, lay.ny - 1), max(1, lay.nz - 1)

    def v(shape, dtype=BF):
        return pltpu.VMEM(shape, dtype)

    return pl.pallas_call(
        functools.partial(front_kernel, lay, rows),
        name="front",
        out_shape=outs,
        in_specs=hbm(3) + [vmem] * 4,
        out_specs=tuple(hbm(2)) + (vmem,) * 7,
        scratch_shapes=[
            v(grad_shape(lay, 0, r)), v((lay.nz, lay.ny) + small.shape, F32), v((2, rows, D)),
            v((2, 8, rows), jnp.int32), v((span, D)), v((D, span)), v((rows, D)), v((span, D)),
            v((span, D)), v((rows, D)), v((rows, D)), v((D, rows)), v((rows, D)), v((span, D)),
            v((span, D)), v((span, LANES), F32), v((span, LANES), F32), v((span, LANES), F32),
            v((span, rows), F32), v((span, LANES), F32), v((span, LANES), F32), v((1, 3 * D), F32),
            v((2, span, 256), F32), v((2, span, 256)), v((2, span, 256)),
            dma(n + 1), dma(n, lz), dma(n, lz), dma(n, ly), dma(n, ly), dma(n, lx), dma(n, lx),
            dma(n), dma(n), dma(lay.nz + ly), dma(lay.nz + ly), dma(6), dma(6),
        ],
        compiler_params=pltpu.CompilerParams(
            collective_id=0, has_side_effects=True, vmem_limit_bytes=VMEM_LIMIT
        ),
    )(u_att, u_up, u_down, small, tok, grad, seg)


class Reduce:
    def __init__(self, lay, ps, fs, bufs, sems):
        (ca, ra1, rb1, ra2, rb2, ra3) = bufs
        (c_s, c_r, x_s, x_r, y_s, y_r, z_s, z_r, fx_s, fx_r, fc_s, fc_r) = sems
        x, c, z, y = lay.coords()
        xs, cs, zs, ys = line_peers(lay)
        self.steps = []
        for t, (g, i) in enumerate(CHUNKS):
            p, f = ps[g], fs[g]
            other_x = [wrap(x + 1 + k, lay.nx) for k in range(lay.nx - 1)]
            other_y = [wrap(y + 1 + k, lay.ny) for k in range(lay.ny - 1)]
            other_z = [wrap(z + 1 + k, lay.nz) for k in range(lay.nz - 1)]

            def over_x(pieces, slot):
                return [
                    remote(piece, slot.at[k], x_s.at[t, k], x_r.at[t, k], xs[k])
                    for k, piece in enumerate(pieces)
                ]

            def over_y(pieces, slot):
                return [
                    remote(piece, slot.at[k], y_s.at[t, k], y_r.at[t, k], ys[k])
                    for k, piece in enumerate(pieces)
                ]

            def into(dst, slot, count):
                return functools.partial(add_into, dst, [slot.at[k] for k in range(count)])

            core_slot = ca[g].at[i]
            core = [
                remote(view(lay, p, g, i, 1 - c, ALL, ALL, ALL), core_slot, c_s.at[t], c_r.at[t], cs[0])
            ]
            add_core = functools.partial(add_into, view(lay, p, g, i, c, ALL, ALL, ALL), [core_slot])
            if i < 2:
                slot1, slot2 = ra1[g].at[i], ra2[g].at[i]
                first = over_x([view(lay, p, g, i, c, k, ALL, ALL) for k in other_x], slot1)
                add_1 = into(view(lay, p, g, i, c, x, ALL, ALL), slot1, lay.nx - 1)
                second = over_y([view(lay, p, g, i, c, x, ALL, k) for k in other_y], slot2)
                add_2 = into(view(lay, p, g, i, c, x, ALL, y), slot2, lay.ny - 1)
            else:
                slot1, slot2 = rb1[g].at[0], rb2[g].at[0]
                first = over_y([view(lay, p, g, i, c, ALL, ALL, k) for k in other_y], slot1)
                add_1 = into(view(lay, p, g, i, c, ALL, ALL, y), slot1, lay.ny - 1)
                second = over_x([view(lay, p, g, i, c, k, ALL, y) for k in other_x], slot2)
                add_2 = into(view(lay, p, g, i, c, x, ALL, y), slot2, lay.nx - 1)
            slot3 = ra3[g].at[i]
            third = [
                remote(view(lay, p, g, i, c, x, k, y), slot3.at[n], z_s.at[t, n], z_r.at[t, n], zs[n])
                for n, k in enumerate(other_z)
            ]
            out = shard_view(lay, f, g, i, c, x)
            own = view(lay, p, g, i, c, x, z, y)
            finish = functools.partial(
                set_sum, out, [own] + [slot3.at[k] for k in range(lay.nz - 1)]
            )
            share_x = [
                remote(out, out, fx_s.at[t, k], fx_r.at[t, k], peer) for k, peer in enumerate(xs)
            ]
            both = shard_view(lay, f, g, i, c, ALL)
            share_c = [remote(both, both, fc_s.at[t], fc_r.at[t], cs[0])]
            self.steps.append(
                (
                    (core, first, second, third, share_x, share_c),
                    (None, add_core, add_1, add_2, finish, None),
                )
            )

    def step(self, t, k):
        copies, adds = self.steps[t]
        if k > 0:
            arrive(copies[k - 1])
        if k < len(copies):
            if adds[k] is not None:
                adds[k]()
            start(copies[k])

    def drain(self):
        for copies, _ in self.steps:
            for group in copies:
                sent(group)


def set_sum(out, srcs):
    total = srcs[0][...].astype(F32)
    for src in srcs[1:]:
        total = total + src[...].astype(F32)
    out[...] = total.astype(BF)


def add_into(dst, srcs):
    lead = dst.shape[:-2]

    def body(j, carry):
        index = []
        rest = j
        for size in reversed(lead):
            index.append(lax.rem(rest, size))
            rest = rest // size
        index = tuple(reversed(index))
        total = dst[index].astype(F32)
        for src in srcs:
            total = total + src[index].astype(F32)
        dst[index] = total.astype(BF)
        return carry

    lax.fori_loop(0, math.prod(lead), body, 0)


def norm_back(grad, gain, normed, factor):
    inner = grad * gain
    return factor * (
        inner
        - jnp.mean(inner, -1, keepdims=True)
        - normed * jnp.mean(inner * normed, -1, keepdims=True)
    )


FF_CHUNKS = FF // D


def back_kernel(
    lay, rows, docs,
    g_up, g_down, p_att, fg_prev, fg_own, attn_out, vectors, up_add, att_sums, tok, grad, seg,
    output, input_grad, f_att, f_up, f_down, vec_out,
    p_up, p_down, w_up, w_down, second_in, second_t, act_s, pg_s, sg_acc, hop, home,
    ca, ra1, rb1, ra2, rb2, ra3, v_c, v_x, v_y, v_z, *sems,
):
    (c_s, c_r, x_s, x_r, y_s, y_r, z_s, z_r, fx_s, fx_r, fc_s, fc_r, v_s, v_r, w_sem, h_s, h_r) = sems
    r = p_att.shape[2]
    x, c, z, y = lay.coords()
    xs, cs, zs, ys = line_peers(lay)
    total = lay.dp * lay.fsdp
    b = lax.axis_index("dp") * lay.fsdp + lax.axis_index("fsdp")

    def stream(k):
        t = wrap(b + k, total)
        return {"dp": t // lay.fsdp, "fsdp": lax.rem(t, lay.fsdp)}

    around = [stream(2), stream(-2), stream(1), stream(-1)]
    near_z = lay.nz // FF_CHUNKS
    loads = []
    for k in range(FF_CHUNKS):
        slot = k % 2
        loads.append(
            (
                pltpu.make_async_copy(
                    g_up.at[:, :, :, pl.ds(D * k, D)], w_up.at[slot], w_sem.at[0, k]
                ),
                pltpu.make_async_copy(
                    g_down.at[pl.ds(near_z * k, near_z)], w_down.at[slot], w_sem.at[1, k]
                ),
            )
        )
    start(loads[0])
    start(loads[1])
    barrier_with(xs + cs + zs + ys + around)
    net = Reduce(
        lay, (p_att, p_up, p_down), (f_att, f_up, f_down), (ca, ra1, rb1, ra2, rb2, ra3), sems[:12]
    )
    for t in range(3):
        net.step(t, 0)
    even = lax.rem(b, 2) == 0
    one, two = fg_prev.at[pl.ds(rows, rows)], fg_prev.at[pl.ds(0, rows)]
    to_next = remote(one, hop, h_s.at[0], h_r.at[0], around[2])
    to_last = remote(one, hop, h_s.at[0], h_r.at[0], around[3])
    to_owner = remote(two, home, h_s.at[1], h_r.at[1], around[1])

    @pl.when(even)
    def _():
        to_next.start()
        to_owner.start()

    @pl.when(jnp.logical_not(even))
    def _():
        to_last.start()

    gain_first, gain_second = vectors[0:1, :], vectors[2:3, :]
    normed, factor = norm_parts(tok[...].astype(F32))
    value = (normed * gain_second + vectors[3:4, :]).astype(BF)
    second_in[...] = value
    second_t[...] = value.T
    cot = grad[...].astype(F32)
    output_base = attn_out
    output_base[...] = attn_out[...] + tok[...].astype(F32) + vectors[4:5, :]
    sg_acc[...] = jnp.zeros_like(sg_acc)
    mine = v_c.at[c]
    mine[...] = jnp.zeros((16, D), F32)
    net.step(0, 1)
    net.step(1, 1)

    events = [
        [(2, 1)],
        [(3, 0), (0, 2)],
        [(4, 0), (3, 1), (2, 2), (0, 3)],
        [(4, 1), (1, 2), (5, 0)],
    ]
    root = math.sqrt(0.5)
    level = 1.0 / math.sqrt(2.0 * math.pi)

    def forward_halo():
        to_last.wait_recv()

        @pl.when(jnp.logical_not(even))
        def _():
            add_into(two.reshape((2, rows // 2, D)), [hop.reshape((2, rows // 2, D))])
            to_owner.start()

    def chunk(k, squares):
        slot = lax.rem(k, 2)
        for n in range(FF_CHUNKS):

            @pl.when(k == n)
            def _(n=n):
                loads[n][0].wait()
                loads[n][1].wait()

        down = w_down[slot].reshape(D, D)
        for j in range(3):
            tile = slice(256 * j, 256 * (j + 1))
            col = pl.ds(pl.multiple_of(D * k + 256 * j, 256), 256)
            pre = mm(second_in[...], w_up[slot, :, :, :, tile].reshape(D, 256)) + up_add[:, col]
            hidden = mm(grad[...], down[tile, :], NT)
            half = 0.5 + 0.5 * lax.erf(pre * root)
            act = (pre * half).astype(BF)
            slope = half + pre * jnp.exp(-0.5 * pre * pre) * level
            pg = (hidden * slope).astype(BF)
            act_s[:, tile] = act
            pg_s[:, tile] = pg
            wide = act.astype(F32)
            squares = squares + jnp.sum(wide * wide, -1, keepdims=True)
            v_c[c, pl.ds(8 + k, 1), tile] = jnp.sum(pg.astype(F32), 0, keepdims=True)
        p_up[:, :, :, pl.ds(pl.multiple_of(D * k, 256), D)] = (
            mm(second_t[...], pg_s[...]).astype(BF).reshape(lay.nz, lay.ny, r, D)
        )
        p_down[pl.ds(near_z * k, near_z)] = (
            mm(act_s[...].T, grad[...]).astype(BF).reshape(near_z, lay.ny, 4, r, D)
        )
        output_base[...] += mm(act_s[...], down)
        sg_acc[...] += mm(pg_s[...], w_up[slot].reshape(D, D), NT)
        for n in range(FF_CHUNKS):

            @pl.when(k == n)
            def _(n=n):
                if n + 2 < FF_CHUNKS:
                    start(loads[n + 2])
                for event in events[n]:
                    net.step(*event)
                if n == 2:
                    forward_halo()

        return squares

    squares = lax.fori_loop(0, FF_CHUNKS, chunk, jnp.zeros((rows, 1), F32))
    for t in (7, 8, 6):
        net.step(t, 0)
    output[...] = output_base[...].astype(BF)
    for t, k in ((3, 2), (0, 4), (1, 3), (5, 1), (7, 1), (8, 1), (6, 1), (2, 3)):
        net.step(t, k)

    to_owner.wait_recv()
    total_first = fg_own[...] + home[...].astype(F32)
    keep = jnp.where(even, 1.0, 0.0).astype(F32)
    fg_own[...] = total_first + hop[...].astype(F32) * keep
    first_grad = fg_own[...]
    second_grad = sg_acc[...]
    normed, factor = norm_parts(tok[...].astype(F32))
    input_grad[...] = (
        grad[...].astype(F32)
        + norm_back(first_grad, gain_first, normed, factor)
        + norm_back(second_grad, gain_second, normed, factor)
    ).astype(BF)
    for t, k in ((3, 3), (1, 4), (4, 2), (2, 4), (0, 5)):
        net.step(t, k)

    def put(k, value):
        v_c[c, k : k + 1, :] = value

    put(0, jnp.sum(first_grad * normed, 0, keepdims=True))
    put(1, jnp.sum(first_grad, 0, keepdims=True))
    put(2, jnp.sum(second_grad * normed, 0, keepdims=True))
    put(3, jnp.sum(second_grad, 0, keepdims=True))
    cot = grad[...].astype(F32)
    put(4, jnp.sum(cot, 0, keepdims=True))
    for k in range(3):
        put(5 + k, att_sums[k : k + 1, :])
    token_norm = squares * jnp.sum(cot * cot, -1, keepdims=True) * (1.0 / (FF * D))
    docs_of = jnp.concatenate([seg[...].astype(F32)] * (LANES // 8), 0).T[:, 0:1]
    doc = lax.broadcasted_iota(jnp.int32, (rows, D), 1).astype(F32)
    member = jnp.where((docs_of == doc) & (doc < docs), 1.0, 0.0)
    put(12, jnp.sum(token_norm * member, 0, keepdims=True))
    put(13, jnp.sum(member, 0, keepdims=True))

    at = [0, 1, lay.nx, lay.nx + lay.ny - 1]

    def spread(ref, own, peers, base):
        return [
            remote(ref.at[own], ref.at[own], v_s.at[base + k], v_r.at[base + k], p)
            for k, p in enumerate(peers)
        ]

    vec_c = spread(v_c, c, cs, at[0])
    vec_x = spread(v_x, x, xs, at[1])
    vec_y = spread(v_y, y, ys, at[2])
    vec_z = spread(v_z, z, zs, at[3])

    def add_all(ref, size):
        value = ref[0]
        for k in range(1, size):
            value = value + ref[k]
        return value

    start(vec_c)
    net.step(5, 2)
    net.step(3, 4)
    arrive(vec_c)
    v_x[x] = add_all(v_c, 2)
    start(vec_x)
    for t, k in ((7, 2), (8, 2), (4, 3), (6, 2), (1, 5), (2, 5)):
        net.step(t, k)
    arrive(vec_x)
    v_y[y] = add_all(v_x, lay.nx)
    start(vec_y)
    for t, k in ((7, 3), (4, 4), (5, 3)):
        net.step(t, k)
    arrive(vec_y)
    v_z[z] = add_all(v_y, lay.ny)
    start(vec_z)
    for t, k in ((6, 3), (3, 5), (7, 4), (8, 3), (4, 5), (5, 4)):
        net.step(t, k)
    arrive(vec_z)
    vec_out[...] = add_all(v_z, lay.nz)
    for t, k in ((7, 5), (5, 5), (6, 4), (8, 4), (6, 5), (8, 5)):
        net.step(t, k)
    for t in range(9):
        net.step(t, 6)
    net.drain()
    sent(vec_c + vec_x + vec_y + vec_z)
    to_next.wait_send()
    to_owner.wait_send()


def back(lay, g_up, g_down, p_att, fg_prev, fg_own, attn_out, vectors, up_add, att_sums, tok, grad, seg):
    rows = tok.shape[0]
    r = p_att.shape[2]
    n = len(CHUNKS)
    docs = DOC_DEV * lay.dp * lay.fsdp
    outs = (
        jax.ShapeDtypeStruct((rows, D), BF),
        jax.ShapeDtypeStruct((rows, D), BF),
        jax.ShapeDtypeStruct((r, 4 * D), BF),
        jax.ShapeDtypeStruct((r, 4 * D), BF),
        jax.ShapeDtypeStruct((4, r, D), BF),
        jax.ShapeDtypeStruct((16, D), F32),
    )
    lx, ly, lz = max(1, lay.nx - 1), max(1, lay.ny - 1), max(1, lay.nz - 1)

    def v(shape, dtype=BF):
        return pltpu.VMEM(shape, dtype)

    def bufs(chunks, peers, x_all, z_all, y_all):
        return [v((chunks,) + peers + part_shape(lay, g, x_all, z_all, y_all, r)) for g in range(3)]

    scratch = [
        v(grad_shape(lay, 1, r)), v(grad_shape(lay, 2, r)),
        v((2, lay.nz, lay.ny, r, D)), v((2, lay.nz // FF_CHUNKS, lay.ny, 4, r, D)),
        v((rows, D)), v((D, rows)), v((rows, D)), v((rows, D)), v((rows, D), F32),
        v((rows, D)), v((rows, D)),
        bufs(3, (), True, True, True),
        bufs(2, (lx,), False, True, True),
        bufs(1, (ly,), True, True, False),
        bufs(2, (ly,), False, True, False),
        bufs(1, (lx,), False, True, False),
        bufs(3, (lz,), False, False, False),
    ]
    vecs = [v((k, 16, D), F32) for k in (2, lay.nx, lay.ny, lay.nz)]
    nv = 1 + lay.nx + lay.ny + lay.nz
    sems = [
        dma(n), dma(n), dma(n, lx), dma(n, lx), dma(n, ly), dma(n, ly), dma(n, lz), dma(n, lz),
        dma(n, lx), dma(n, lx), dma(n), dma(n), dma(nv), dma(nv), dma(2, FF_CHUNKS), dma(2), dma(2),
    ]
    vmem = pl.BlockSpec(memory_space=pltpu.VMEM)
    return pl.pallas_call(
        functools.partial(back_kernel, lay, rows, docs),
        name="back",
        out_shape=outs,
        in_specs=hbm(2) + [vmem] * 10,
        out_specs=(vmem,) * 6,
        scratch_shapes=scratch + vecs + sems,
        compiler_params=pltpu.CompilerParams(
            collective_id=1, has_side_effects=True, vmem_limit_bytes=VMEM_LIMIT
        ),
    )(g_up, g_down, p_att, fg_prev, fg_own, attn_out, vectors, up_add, att_sums, tok, grad, seg)


def per_device(
    lay, tokens, seg_ids, out_grad, first_gain, first_bias, second_gain, second_bias,
    qkv_weight, qkv_bias, dense_weight, up_weight, up_bias, down_weight, out_bias,
):
    rows = tokens.shape[0]
    r = qkv_weight.shape[0]
    fsdp = lay.fsdp
    qkv_kinds = qkv_weight.reshape(r, H, 3, HD).transpose(0, 2, 1, 3).reshape(r, 3 * D)
    u_att = jnp.concatenate([qkv_kinds, dense_weight], 1)
    u_down = down_weight.reshape(4, r, D)
    vectors = (first_gain, first_bias, second_gain, second_bias, out_bias, qkv_bias, up_bias)
    small = pack_small(vectors, r)
    seg_rows = jnp.broadcast_to(seg_ids[None, :], (8, rows))
    passed = front(lay, u_att, up_weight, u_down, small, tokens, out_grad, seg_rows)
    output, input_grad, f_att, f_up, f_down, vec = back(lay, *passed, tokens, out_grad, seg_rows)
    docs = DOC_DEV * lay.dp * fsdp
    shard = lax.axis_index("fsdp")
    plain = lax.dynamic_slice_in_dim(vec[:5], shard * r, r, 1)
    kinds = vec[5:8].reshape(3, H, HD).transpose(1, 0, 2).reshape(3 * D)
    qkv_add = lax.dynamic_slice_in_dim(kinds, shard * 3 * r, 3 * r)
    up_add = lax.dynamic_slice_in_dim(vec[8:12].reshape(FF), shard * 4 * r, 4 * r)
    qkv_out = (
        f_att[:, : 3 * D].astype(F32).reshape(r, 3, H, HD).transpose(0, 2, 1, 3).reshape(r, 3 * D)
    )
    return (
        output,
        input_grad,
        plain[0],
        plain[1],
        plain[2],
        plain[3],
        qkv_out,
        qkv_add,
        f_att[:, 3 * D :].astype(F32),
        f_up.astype(F32),
        up_add,
        f_down.reshape(4 * r, D).astype(F32),
        plain[4],
        vec[12, :docs] / vec[13, :docs],
    )


def solution(mesh):
    lay = Layout(mesh.shape["dp"], mesh.shape["fsdp"])
    both = P(("dp", "fsdp"))
    split = P("fsdp")
    in_specs = (both, both, both) + (split,) * 11
    out_specs = (both, both) + (split,) * 11 + (P(),)
    return jax.shard_map(
        functools.partial(per_device, lay), mesh=mesh, in_specs=in_specs, out_specs=out_specs,
        check_vma=False,
    )
```

```python
import functools
import math

import jax
import jax.numpy as jnp
from jax import lax
from jax.experimental import pallas as pl
from jax.experimental.pallas import tpu as pltpu
from jax.sharding import PartitionSpec as P

D = 768
H = 12
HD = 64
FF = 3072
ROT = 16
ROW = 2048
DOC_DEV = 2
LANES = 128
PAIRS = D // LANES
MESH = pl.DeviceIdType.MESH
VMEM_LIMIT = 60 * 1024 * 1024


class Layout:
    def __init__(self, dp, fsdp):
        self.dp, self.fsdp = dp, fsdp
        self.nc = 2
        self.nx = dp // 2
        ny = 1
        while (2 * ny) * (2 * ny) <= fsdp:
            ny *= 2
        self.ny, self.nz = ny, fsdp // ny
        self.sub = max(1, self.nx // 2)
        self.unit = 4 // self.nx
        self.down_unit = 2 // self.sub

    def coords(self):
        d, f = lax.axis_index("dp"), lax.axis_index("fsdp")
        return d // 2, d % 2, f // self.ny, f % self.ny

    def device(self, x, c, z, y):
        return {"dp": x * 2 + c, "fsdp": z * self.ny + y}


def wrap(value, size):
    return lax.rem(value + size, size)


CHUNKS = tuple((g, i) for g in range(3) for i in range(3))
ALL = slice(None)


def grad_shape(lay, group, r):
    return (lay.nz, lay.ny, r, 4 * D) if group < 2 else (lay.nz, lay.ny, 4, r, D)


def span_of(lay, group, i, c, x):
    if group < 2:
        width = 512 // lay.nx
        if x is ALL:
            return pl.ds(pl.multiple_of(1024 * i + 512 * c, LANES), 512), None
        return pl.ds(pl.multiple_of(1024 * i + 512 * c + width * x, LANES), width), None
    width = 256 // lay.sub
    if x is ALL:
        return pl.ds(256 * i, 256), pl.ds(2 * c, 2)
    start = 256 * i + width * lax.rem(x, lay.sub)
    return pl.ds(pl.multiple_of(start, LANES), width), 2 * c + x // lay.sub


def view(lay, ref, group, i, c, x, z, y):
    cols, quarter = span_of(lay, group, i, c, x)
    if group < 2:
        return ref.at[z, y, :, cols]
    return ref.at[z, y, quarter, :, cols]


def shard_view(lay, ref, group, i, c, x):
    cols, quarter = span_of(lay, group, i, c, x)
    if group < 2:
        return ref.at[:, cols]
    return ref.at[quarter, :, cols]


def part_shape(lay, group, x_all, z_all, y_all, r):
    lead = ((lay.nz,) if z_all else ()) + ((lay.ny,) if y_all else ())
    if group < 2:
        return lead + (r, 512 if x_all else 512 // lay.nx)
    return lead + ((2, r, 256) if x_all else (r, 256 // lay.sub))


def barrier_with(peers):
    sem = pltpu.get_barrier_semaphore()
    for peer in peers:
        pl.semaphore_signal(sem, inc=1, device_id=peer, device_id_type=MESH)
    pl.semaphore_wait(sem, len(peers))


def line_peers(lay):
    x, c, z, y = lay.coords()
    xs = [lay.device(wrap(x + k, lay.nx), c, z, y) for k in range(1, lay.nx)]
    ys = [lay.device(x, c, z, wrap(y + k, lay.ny)) for k in range(1, lay.ny)]
    zs = [lay.device(x, c, wrap(z + k, lay.nz), y) for k in range(1, lay.nz)]
    cs = [lay.device(x, 1 - c, z, y)]
    return xs, cs, zs, ys


def remote(src, dst, ssem, rsem, device):
    return pltpu.make_async_remote_copy(
        src_ref=src, dst_ref=dst, send_sem=ssem, recv_sem=rsem, device_id=device, device_id_type=MESH
    )


def start(copies):
    for copy in copies:
        copy.start()


def arrive(copies):
    for copy in copies:
        copy.wait_recv()


def sent(copies):
    for copy in copies:
        copy.wait_send()


def hbm(count):
    return [pl.BlockSpec(memory_space=pltpu.HBM)] * count


def dma(*shape):
    return pltpu.SemaphoreType.DMA(shape)


NT = (((1,), (1,)), ((), ()))
NN = (((1,), (0,)), ((), ()))
F32 = jnp.float32
BF = jnp.bfloat16


def mm(a, b, dims=NN):
    return lax.dot_general(a, b, dims, preferred_element_type=F32)


def norm_parts(values):
    middle = jnp.mean(values, -1, keepdims=True)
    centred = values - middle
    factor = lax.rsqrt(jnp.mean(centred * centred, -1, keepdims=True) + 1e-05)
    return centred * factor, factor


def small_plan(r):
    plan, at = [], 0
    for size, within in [(r, LANES)] * 5 + [(3 * r, HD), (4 * r, LANES)]:
        unit = math.gcd(size, within)
        plan.append((at, size // unit, unit))
        at += size // unit
    return plan


def pack_small(vectors, r):
    rows = [
        jnp.tile(v.reshape(-1, unit), (1, LANES // unit))
        for v, (_, _, unit) in zip(vectors, small_plan(r))
    ]
    packed = jnp.concatenate(rows, 0).astype(F32)
    return jnp.pad(packed, ((0, -packed.shape[0] % 8), (0, 0)))


class Gather:
    def __init__(self, lay, us, gs, sems):
        (z_s, z_r, y_s, y_r, x_s, x_r, c_s, c_r) = sems
        x, c, z, y = lay.coords()
        xs, cs, zs, ys = line_peers(lay)
        self.stages = []
        for t, (g, i) in enumerate(CHUNKS):
            by_y, by_x = (ys, y_s, y_r), (xs, x_s, x_r)
            first, second = (by_y, by_x) if i < 2 else (by_x, by_y)
            middle = (x, ALL, ALL) if i < 2 else (ALL, ALL, y)
            steps = [
                ((zs, z_s, z_r), (x, z, y)),
                (first, (x, ALL, y)),
                (second, middle),
            ]
            stages = []
            for (peers, ss, rs), (px, pz, py) in steps:
                piece = view(lay, gs[g], g, i, c, px, pz, py)
                source = shard_view(lay, us[g], g, i, c, x) if len(stages) == 0 else piece
                stages.append(
                    [remote(source, piece, ss.at[t, k], rs.at[t, k], p) for k, p in enumerate(peers)]
                )
            piece = view(lay, gs[g], g, i, c, ALL, ALL, ALL)
            stages.append([remote(piece, piece, c_s.at[t], c_r.at[t], cs[0])])
            self.stages.append(stages)

    def issue(self, t, stage):
        start(self.stages[t][stage])

    def pass_on(self, t, stage):
        arrive(self.stages[t][stage - 1])
        start(self.stages[t][stage])

    def done(self, t):
        arrive(self.stages[t][3])

    def drain(self):
        for stages in self.stages:
            for copies in stages:
                sent(copies)


def rope(u, cos, low, high):
    return u * cos + pltpu.roll(u, LANES - 8, 1) * low + pltpu.roll(u, 8, 1) * high


def front_kernel(
    lay, rows,
    u_att, u_up, u_down, small, tok, grad, seg,
    g_up, g_down, p_att, fg_prev, fg_own, attn_out, vectors, up_add, att_sums,
    g_att, g_small, tok_halo, seg_halo, first_all, first_t, q_s, k_s, v_s, do_s, ctx_s, ctx_t,
    dq_s, dk_s, dv_s, cos_s, low_s, high_s, bias, dk_acc, dv_acc, qkv_add, s_s, w_s, d_s,
    local_sem, z_s, z_r, y_s, y_r, x_s, x_r, c_s, c_r, sm_s, sm_r, h_s, h_r,
):
    span = 3 * rows
    r = u_att.shape[0]
    n_chunks = len(CHUNKS)
    x, c, z, y = lay.coords()
    xs, cs, zs, ys = line_peers(lay)
    total = lay.dp * lay.fsdp
    b = lax.axis_index("dp") * lay.fsdp + lax.axis_index("fsdp")

    def stream(k):
        t = wrap(b + k, total)
        return {"dp": t // lay.fsdp, "fsdp": lax.rem(t, lay.fsdp)}

    around = [stream(2), stream(-2), stream(1), stream(-1)]
    gs = (g_att, g_up, g_down)
    us = (u_att, u_up, u_down)
    locals_ = []
    for t, (g, i) in enumerate(CHUNKS):
        locals_.append(
            pltpu.make_async_copy(
                shard_view(lay, us[g], g, i, c, x), view(lay, gs[g], g, i, c, x, z, y), local_sem.at[t]
            )
        )
    locals_.append(pltpu.make_async_copy(small, g_small.at[z, y], local_sem.at[n_chunks]))
    start(locals_)
    barrier_with(xs + cs + zs + ys + around)
    even = lax.rem(b, 2) == 0
    half = rows // 2
    halo, own, passed = [], [], []
    for k in range(2):
        part = pl.ds(k * half, half)
        halo.append(remote(tok.at[part], tok_halo.at[0, part], h_s.at[k], h_r.at[k], around[0]))
        own.append(remote(tok.at[part], tok_halo.at[1, part], h_s.at[2 + k], h_r.at[2 + k], around[2]))
        passed.append(
            remote(tok_halo.at[0, part], tok_halo.at[1, part], h_s.at[2 + k], h_r.at[2 + k], around[3])
        )
    segs = [
        remote(seg, seg_halo.at[0], h_s.at[4], h_r.at[4], around[0]),
        remote(seg, seg_halo.at[1], h_s.at[5], h_r.at[5], around[2]),
    ]
    small_z = [
        remote(small, g_small.at[z, y], sm_s.at[k], sm_r.at[k], p) for k, p in enumerate(zs)
    ]
    small_y = [
        remote(g_small.at[:, y], g_small.at[:, y], sm_s.at[lay.nz + k], sm_r.at[lay.nz + k], p)
        for k, p in enumerate(ys)
    ]
    net = Gather(lay, us, gs, (z_s, z_r, y_s, y_r, x_s, x_r, c_s, c_r))
    net.issue(0, 0)
    net.issue(2, 0)
    start(small_z)
    start(segs)
    net.issue(1, 0)

    def tables(k, carry):
        at = pl.ds(pl.multiple_of(k * 256, 256), 256)
        lane = lax.broadcasted_iota(jnp.int32, (256, LANES), 1) % HD
        row = lax.broadcasted_iota(jnp.int32, (256, LANES), 0) + k * 256
        place = lax.rem((b - 2) * rows + row + 4 * ROW, ROW).astype(F32)
        rate = jnp.exp((lane % 8).astype(F32) * (-math.log(10000.0) / 8.0))
        angle = place * rate
        sine = jnp.sin(angle)
        cos_s[at, :] = jnp.where(lane < ROT, jnp.cos(angle), 1.0)
        low_s[at, :] = jnp.where(lane < 8, -sine, 0.0)
        high_s[at, :] = jnp.where((lane >= 8) & (lane < ROT), sine, 0.0)
        return carry

    lax.fori_loop(0, 2, tables, 0)
    for t in (0, 2, 1, n_chunks):
        locals_[t].wait()
    net.pass_on(0, 1)
    lax.fori_loop(2, 3, tables, 0)
    net.pass_on(2, 1)
    lax.fori_loop(3, 5, tables, 0)
    arrive(small_z)
    start(small_y)
    net.pass_on(0, 2)
    net.pass_on(1, 1)
    halo[0].start()
    lax.fori_loop(5, span // 256, tables, 0)
    arrive(small_y)
    net.pass_on(2, 2)

    lane_row = lax.broadcasted_iota(jnp.int32, (1, LANES), 1)

    def line(first_row, per, unit, length, source):
        out = []
        for block in range(length // LANES):
            value = None
            for k in range(LANES // unit):
                at = source(block * (LANES // unit) + k)
                owner = at // per
                row = first_row + at % per
                piece = g_small[owner // lay.ny, owner % lay.ny, row : row + 1, :]
                value = piece if value is None else jnp.where(lane_row // unit == k, piece, value)
            out.append(value)
        return jnp.concatenate(out, 1)

    def norm_rows(values):
        return norm_parts(values.astype(F32))[0]

    plan = small_plan(r)
    for j in range(5):
        vectors[j : j + 1, :] = line(*plan[j], D, lambda n: n)
    vectors[5:8, :] = jnp.zeros((3, D), F32)
    unit = plan[5][2]
    a_head = HD // unit

    def natural(n):
        kind, rest = divmod(n, D // unit)
        head, part = divmod(rest, a_head)
        return head * 3 * a_head + kind * a_head + part

    qkv_add[...] = line(*plan[5], 3 * D, natural)
    net.pass_on(1, 2)
    up_add[...] = line(*plan[6], FF, lambda n: n)

    def pass_halo(k):
        arrive([halo[k]])

        @pl.when(even)
        def _():
            own[k].start()

        @pl.when(jnp.logical_not(even))
        def _():
            passed[k].start()

    halo[1].start()
    gain, shift = vectors[0:1, :], vectors[1:2, :]
    own_rows = pl.ds(2 * rows, rows)
    first = (norm_rows(tok[...]) * gain + shift).astype(BF)
    first_all[own_rows, :] = first
    first_t[:, own_rows] = first.T
    pass_halo(0)
    arrive(segs)
    least = jnp.maximum(0, 2 * rows - b * rows)
    keys_doc = jnp.concatenate([seg_halo[0], seg_halo[1], seg[...]], 1).astype(F32)
    keys_doc = jnp.concatenate([keys_doc] * (LANES // 8), 0).T
    query_doc = seg[0:1, :].astype(F32)

    for k in range(6):
        at = slice(k * 256, (k + 1) * 256)
        key_at = lax.broadcasted_iota(jnp.int32, (256, rows), 0) + k * 256
        query_at = lax.broadcasted_iota(jnp.int32, (256, rows), 1) + 2 * rows
        allowed = (keys_doc[at, 0:1] == query_doc) & (key_at <= query_at) & (key_at >= least)
        bias[at, :] = jnp.where(allowed, 0.0, -1e30)
    for t in range(3, n_chunks):
        locals_[t].wait()
    net.issue(5, 0)
    net.pass_on(0, 3)
    net.pass_on(2, 3)
    net.issue(3, 0)

    def weight(first_col, width):
        value = g_att[:, :, :, pl.ds(first_col, width)]
        return value.reshape(D, width)

    scale = 1.0 / math.sqrt(HD)

    def project(kind, j, at, out, factor):
        col = pl.multiple_of(kind * D + 256 * j, 256)
        value = mm(first_all[at, :], weight(col, 256)) + qkv_add[:, pl.ds(col, 256)]
        for k in range(2):
            u = value[:, k * LANES : (k + 1) * LANES]
            if kind < 2:
                u = rope(u, cos_s[at, :], low_s[at, :], high_s[at, :])
            if factor is not None:
                u = u * factor
            out[:, pl.ds(pl.multiple_of(256 * j + LANES * k, LANES), LANES)] = u.astype(BF)

    def own_queries(j, carry):
        project(0, j, own_rows, q_s, scale)
        return carry

    def own_keys(j, carry):
        project(1, j, own_rows, k_s.at[own_rows], None)
        return carry

    def own_values(j, carry):
        project(2, j, own_rows, v_s.at[own_rows], None)
        return carry

    net.done(0)
    lax.fori_loop(0, 3, own_queries, 0)
    lax.fori_loop(0, 1, own_keys, 0)
    pass_halo(1)
    net.pass_on(1, 3)
    net.issue(4, 0)
    net.done(2)
    do_s[...] = mm(grad[...], weight(3 * D, D), NT).astype(BF)
    lax.fori_loop(2, 3, own_values, 0)
    net.pass_on(5, 1)
    net.done(1)
    lax.fori_loop(1, 3, own_keys, 0)
    lax.fori_loop(0, 2, own_values, 0)
    own[0].wait_recv()
    net.pass_on(3, 1)
    net.issue(8, 0)
    own[1].wait_recv()
    for k in range(2):
        at = slice(k * rows, (k + 1) * rows)
        before = (norm_rows(tok_halo[k]) * gain + shift).astype(BF)
        first_all[at, :] = before
        first_t[:, at] = before.T
    net.pass_on(4, 1)
    net.pass_on(5, 2)

    def earlier_projections(j, carry):
        for k in range(2):
            at = pl.ds(k * rows, rows)
            project(1, j, at, k_s.at[at], None)
            project(2, j, at, v_s.at[at], None)
        return carry

    lax.fori_loop(0, 3, earlier_projections, 0)
    net.pass_on(3, 2)
    net.issue(6, 0)

    go, send, end = net.pass_on, net.issue, net.done
    later = [
        [(go, 8, 1), (send, 7, 0), (go, 4, 2)],
        [(go, 5, 3)],
        [(go, 6, 1)],
        [(go, 3, 3), (go, 7, 1)],
        [(go, 8, 2), (go, 6, 2)],
        [(go, 4, 3), (go, 7, 2)],
        [],
        [(go, 8, 3)],
        [],
        [(go, 6, 3)],
        [(go, 7, 3)],
        [],
    ]
    tile = 256

    def pair(p, carry):
        lanes = pl.ds(pl.multiple_of(p * LANES, LANES), LANES)
        v_t, k_t = v_s[:, lanes].T, k_s[:, lanes].T
        do_t = do_s[:, lanes].astype(F32).T
        lane = lax.broadcasted_iota(jnp.int32, (tile, LANES), 1)
        zero = jnp.zeros((), BF)
        for t in range(rows // tile):
            cols = slice(t * tile, (t + 1) * tile)
            kl = 2 * rows + (t + 1) * tile
            pieces = [slice(k * tile, (k + 1) * tile) for k in range(kl // tile)]
            qms = [jnp.where((lane // HD) == hh, q_s[cols, lanes], zero) for hh in range(2)]
            doms = [jnp.where((lane // HD) == hh, do_s[cols, lanes], zero) for hh in range(2)]
            tops, norms = [], []
            for hh in range(2):
                top = None
                for at in pieces:
                    st = mm(k_s[at, lanes], qms[hh], NT) + bias[at, cols]
                    s_s[hh, at, :] = st
                    most = jnp.max(st, 0, keepdims=True)
                    top = most if top is None else jnp.maximum(top, most)
                tops.append(top)
            for hh in range(2):
                total_e = None
                for at in pieces:
                    e = jnp.exp(s_s[hh, at, :] - tops[hh])
                    s_s[hh, at, :] = e
                    part = jnp.sum(e, 0, keepdims=True)
                    total_e = part if total_e is None else total_e + part
                norms.append(1.0 / total_e)
            outs, dqs = [], []
            for hh in range(2):
                for at in pieces:
                    w_s[hh, at, :] = (s_s[hh, at, :] * norms[hh]).astype(BF)
            for hh in range(2):
                part = slice(hh * HD, (hh + 1) * HD)
                o_t = mm(v_t[part, :kl], w_s[hh, :kl, :])
                delta = jnp.sum(o_t * do_t[part, cols], 0, keepdims=True)
                outs.append(o_t)
                for at in pieces:
                    dp = mm(v_s[at, lanes], doms[hh], NT)
                    d_s[hh, at, :] = ((s_s[hh, at, :] * norms[hh]) * (dp - delta)).astype(BF)
                dqs.append(mm(k_t[part, :kl], d_s[hh, :kl, :]))
            for k, at in enumerate(pieces):
                dk = mm(d_s[0, at, :], qms[0]) + mm(d_s[1, at, :], qms[1])
                dv = mm(w_s[0, at, :], doms[0]) + mm(w_s[1, at, :], doms[1])
                if t == 0 or k == len(pieces) - 1:
                    dk_acc[at, :] = dk
                    dv_acc[at, :] = dv
                else:
                    dk_acc[at, :] += dk
                    dv_acc[at, :] += dv
            o_pair = jnp.concatenate(outs, 0)
            ctx_t[lanes, cols] = o_pair.astype(BF)
            ctx_s[cols, lanes] = o_pair.T.astype(BF)
            dq = jnp.concatenate(dqs, 0).T * scale
            at = slice(2 * rows + t * tile, 2 * rows + (t + 1) * tile)
            dq_s[cols, lanes] = rope(dq, cos_s[at, :], -low_s[at, :], -high_s[at, :]).astype(BF)
            for k in range(PAIRS):

                @pl.when(p == k)
                def _(k=k, t=t):
                    for event, *where in later[2 * k + t]:
                        event(*where)

        dk_s[:, lanes] = rope(dk_acc[...], cos_s[...], -low_s[...], -high_s[...]).astype(BF)
        dv_s[:, lanes] = dv_acc[...].astype(BF)
        return carry

    lax.fori_loop(0, PAIRS, pair, 0)

    def earlier_grad(k, carry):
        at = pl.ds(pl.multiple_of(k * 256, 256), 256)
        value = mm(dk_s[at, :], weight(D, D), NT) + mm(dv_s[at, :], weight(2 * D, D), NT)
        fg_prev[at, :] = value.astype(BF)
        return carry

    lax.fori_loop(0, 2 * rows // 256, earlier_grad, 0)
    for k in range(rows // 256):
        at = slice(2 * rows + 256 * k, 2 * rows + 256 * (k + 1))
        near = slice(256 * k, 256 * (k + 1))
        fg_own[near, :] = (
            mm(dk_s[at, :], weight(D, D), NT)
            + mm(dv_s[at, :], weight(2 * D, D), NT)
            + mm(dq_s[near, :], weight(0, D), NT)
        )

    def weight_grads(j, carry):
        col = pl.multiple_of(256 * j, 256)
        cols = pl.ds(col, 256)

        def put(kind, value):
            p_att[:, :, :, pl.ds(pl.multiple_of(kind * D + col, 256), 256)] = value.astype(BF).reshape(
                lay.nz, lay.ny, r, 256
            )

        put(0, mm(first_t[:, own_rows], dq_s[:, cols]))
        put(1, mm(first_t[...], dk_s[:, cols]))
        put(2, mm(first_t[...], dv_s[:, cols]))
        put(3, mm(ctx_t[...], grad[:, cols]))
        attn_out[:, cols] = mm(ctx_s[...], weight(pl.multiple_of(3 * D + col, 256), 256))
        return carry

    lax.fori_loop(0, 3, weight_grads, 0)
    for k, ref in enumerate((dq_s, dk_s, dv_s)):
        att_sums[k : k + 1, :] = jnp.sum(ref[...].astype(F32), 0, keepdims=True)
    att_sums[3:8, :] = jnp.zeros((5, D), F32)
    for t in range(3, 9):
        net.done(t)
    net.drain()
    sent(small_z + small_y + segs + halo + own)


def front(lay, u_att, u_up, u_down, small, tok, grad, seg):
    rows = tok.shape[0]
    span = 3 * rows
    r = u_att.shape[0]
    n = len(CHUNKS)
    outs = (
        jax.ShapeDtypeStruct(grad_shape(lay, 1, r), BF),
        jax.ShapeDtypeStruct(grad_shape(lay, 2, r), BF),
        jax.ShapeDtypeStruct(grad_shape(lay, 0, r), BF),
        jax.ShapeDtypeStruct((2 * rows, D), BF),
        jax.ShapeDtypeStruct((rows, D), F32),
        jax.ShapeDtypeStruct((rows, D), F32),
        jax.ShapeDtypeStruct((8, D), F32),
        jax.ShapeDtypeStruct((1, FF), F32),
        jax.ShapeDtypeStruct((8, D), F32),
    )
    vmem = pl.BlockSpec(memory_space=pltpu.VMEM)
    lx, ly, lz = max(1, lay.nx - 1), max(1, lay.ny - 1), max(1, lay.nz - 1)

    def v(shape, dtype=BF):
        return pltpu.VMEM(shape, dtype)

    return pl.pallas_call(
        functools.partial(front_kernel, lay, rows),
        name="front",
        out_shape=outs,
        in_specs=hbm(3) + [vmem] * 4,
        out_specs=tuple(hbm(2)) + (vmem,) * 7,
        scratch_shapes=[
            v(grad_shape(lay, 0, r)), v((lay.nz, lay.ny) + small.shape, F32), v((2, rows, D)),
            v((2, 8, rows), jnp.int32), v((span, D)), v((D, span)), v((rows, D)), v((span, D)),
            v((span, D)), v((rows, D)), v((rows, D)), v((D, rows)), v((rows, D)), v((span, D)),
            v((span, D)), v((span, LANES), F32), v((span, LANES), F32), v((span, LANES), F32),
            v((span, rows), F32), v((span, LANES), F32), v((span, LANES), F32), v((1, 3 * D), F32),
            v((2, span, 256), F32), v((2, span, 256)), v((2, span, 256)),
            dma(n + 1), dma(n, lz), dma(n, lz), dma(n, ly), dma(n, ly), dma(n, lx), dma(n, lx),
            dma(n), dma(n), dma(lay.nz + ly), dma(lay.nz + ly), dma(6), dma(6),
        ],
        compiler_params=pltpu.CompilerParams(
            collective_id=0, has_side_effects=True, vmem_limit_bytes=VMEM_LIMIT
        ),
    )(u_att, u_up, u_down, small, tok, grad, seg)


class Reduce:
    def __init__(self, lay, ps, fs, bufs, sems):
        (ca, ra1, rb1, ra2, rb2, ra3) = bufs
        (c_s, c_r, x_s, x_r, y_s, y_r, z_s, z_r, fx_s, fx_r, fc_s, fc_r) = sems
        x, c, z, y = lay.coords()
        xs, cs, zs, ys = line_peers(lay)
        self.steps = []
        for t, (g, i) in enumerate(CHUNKS):
            p, f = ps[g], fs[g]
            other_x = [wrap(x + 1 + k, lay.nx) for k in range(lay.nx - 1)]
            other_y = [wrap(y + 1 + k, lay.ny) for k in range(lay.ny - 1)]
            other_z = [wrap(z + 1 + k, lay.nz) for k in range(lay.nz - 1)]

            def over_x(pieces, slot):
                return [
                    remote(piece, slot.at[k], x_s.at[t, k], x_r.at[t, k], xs[k])
                    for k, piece in enumerate(pieces)
                ]

            def over_y(pieces, slot):
                return [
                    remote(piece, slot.at[k], y_s.at[t, k], y_r.at[t, k], ys[k])
                    for k, piece in enumerate(pieces)
                ]

            def into(dst, slot, count):
                return functools.partial(add_into, dst, [slot.at[k] for k in range(count)])

            core_slot = ca[g].at[i]
            core = [
                remote(view(lay, p, g, i, 1 - c, ALL, ALL, ALL), core_slot, c_s.at[t], c_r.at[t], cs[0])
            ]
            add_core = functools.partial(add_into, view(lay, p, g, i, c, ALL, ALL, ALL), [core_slot])
            if i < 2:
                slot1, slot2 = ra1[g].at[i], ra2[g].at[i]
                first = over_x([view(lay, p, g, i, c, k, ALL, ALL) for k in other_x], slot1)
                add_1 = into(view(lay, p, g, i, c, x, ALL, ALL), slot1, lay.nx - 1)
                second = over_y([view(lay, p, g, i, c, x, ALL, k) for k in other_y], slot2)
                add_2 = into(view(lay, p, g, i, c, x, ALL, y), slot2, lay.ny - 1)
            else:
                slot1, slot2 = rb1[g].at[0], rb2[g].at[0]
                first = over_y([view(lay, p, g, i, c, ALL, ALL, k) for k in other_y], slot1)
                add_1 = into(view(lay, p, g, i, c, ALL, ALL, y), slot1, lay.ny - 1)
                second = over_x([view(lay, p, g, i, c, k, ALL, y) for k in other_x], slot2)
                add_2 = into(view(lay, p, g, i, c, x, ALL, y), slot2, lay.nx - 1)
            slot3 = ra3[g].at[i]
            third = [
                remote(view(lay, p, g, i, c, x, k, y), slot3.at[n], z_s.at[t, n], z_r.at[t, n], zs[n])
                for n, k in enumerate(other_z)
            ]
            out = shard_view(lay, f, g, i, c, x)
            own = view(lay, p, g, i, c, x, z, y)
            finish = functools.partial(
                set_sum, out, [own] + [slot3.at[k] for k in range(lay.nz - 1)]
            )
            share_x = [
                remote(out, out, fx_s.at[t, k], fx_r.at[t, k], peer) for k, peer in enumerate(xs)
            ]
            both = shard_view(lay, f, g, i, c, ALL)
            share_c = [remote(both, both, fc_s.at[t], fc_r.at[t], cs[0])]
            self.steps.append(
                (
                    (core, first, second, third, share_x, share_c),
                    (None, add_core, add_1, add_2, finish, None),
                )
            )

    def step(self, t, k):
        copies, adds = self.steps[t]
        if k > 0:
            arrive(copies[k - 1])
        if k < len(copies):
            if adds[k] is not None:
                adds[k]()
            start(copies[k])

    def drain(self):
        for copies, _ in self.steps:
            for group in copies:
                sent(group)


def set_sum(out, srcs):
    total = srcs[0][...].astype(F32)
    for src in srcs[1:]:
        total = total + src[...].astype(F32)
    out[...] = total.astype(BF)


def add_into(dst, srcs):
    lead = dst.shape[:-2]

    def body(j, carry):
        index = []
        rest = j
        for size in reversed(lead):
            index.append(lax.rem(rest, size))
            rest = rest // size
        index = tuple(reversed(index))
        total = dst[index].astype(F32)
        for src in srcs:
            total = total + src[index].astype(F32)
        dst[index] = total.astype(BF)
        return carry

    lax.fori_loop(0, math.prod(lead), body, 0)


def norm_back(grad, gain, normed, factor):
    inner = grad * gain
    return factor * (
        inner
        - jnp.mean(inner, -1, keepdims=True)
        - normed * jnp.mean(inner * normed, -1, keepdims=True)
    )


FF_CHUNKS = FF // D


def back_kernel(
    lay, rows, docs,
    g_up, g_down, p_att, fg_prev, fg_own, attn_out, vectors, up_add, att_sums, tok, grad, seg,
    output, input_grad, f_att, f_up, f_down, vec_out,
    p_up, p_down, w_up, w_down, second_in, second_t, act_s, pg_s, sg_acc, hop, home,
    ca, ra1, rb1, ra2, rb2, ra3, v_c, v_x, v_y, v_z, *sems,
):
    (c_s, c_r, x_s, x_r, y_s, y_r, z_s, z_r, fx_s, fx_r, fc_s, fc_r, v_s, v_r, w_sem, h_s, h_r) = sems
    r = p_att.shape[2]
    x, c, z, y = lay.coords()
    xs, cs, zs, ys = line_peers(lay)
    total = lay.dp * lay.fsdp
    b = lax.axis_index("dp") * lay.fsdp + lax.axis_index("fsdp")

    def stream(k):
        t = wrap(b + k, total)
        return {"dp": t // lay.fsdp, "fsdp": lax.rem(t, lay.fsdp)}

    around = [stream(2), stream(-2), stream(1), stream(-1)]
    near_z = lay.nz // FF_CHUNKS
    loads = []
    for k in range(FF_CHUNKS):
        slot = k % 2
        loads.append(
            (
                pltpu.make_async_copy(
                    g_up.at[:, :, :, pl.ds(D * k, D)], w_up.at[slot], w_sem.at[0, k]
                ),
                pltpu.make_async_copy(
                    g_down.at[pl.ds(near_z * k, near_z)], w_down.at[slot], w_sem.at[1, k]
                ),
            )
        )
    start(loads[0])
    start(loads[1])
    barrier_with(xs + cs + zs + ys + around)
    net = Reduce(
        lay, (p_att, p_up, p_down), (f_att, f_up, f_down), (ca, ra1, rb1, ra2, rb2, ra3), sems[:12]
    )
    for t in range(3):
        net.step(t, 0)
    net.step(0, 1)
    net.step(1, 1)
    net.step(2, 1)
    even = lax.rem(b, 2) == 0
    quarter = rows // 4
    to_next, to_last, to_owner = [], [], []
    for k in range(4):
        near = fg_prev.at[pl.ds(rows + k * quarter, quarter)]
        far = fg_prev.at[pl.ds(k * quarter, quarter)]
        part = pl.ds(k * quarter, quarter)
        to_next.append(remote(near, hop.at[part], h_s.at[k], h_r.at[k], around[2]))
        to_last.append(remote(near, hop.at[part], h_s.at[k], h_r.at[k], around[3]))
        to_owner.append(remote(far, home.at[part], h_s.at[4 + k], h_r.at[4 + k], around[1]))

    def hop_halo(k):
        @pl.when(even)
        def _():
            to_next[k].start()

        @pl.when(jnp.logical_not(even))
        def _():
            to_last[k].start()

    def forward_halo(k):
        to_last[k].wait_recv()
        at = pl.ds(k * quarter, quarter)

        @pl.when(jnp.logical_not(even))
        def _():
            fg_prev[at, :] = (fg_prev[at, :].astype(F32) + hop[at, :].astype(F32)).astype(BF)

        to_owner[k].start()

    hop_halo(0)

    gain_first, gain_second = vectors[0:1, :], vectors[2:3, :]
    normed, factor = norm_parts(tok[...].astype(F32))
    value = (normed * gain_second + vectors[3:4, :]).astype(BF)
    second_in[...] = value
    second_t[...] = value.T
    cot = grad[...].astype(F32)
    output_base = attn_out
    output_base[...] = attn_out[...] + tok[...].astype(F32) + vectors[4:5, :]
    sg_acc[...] = jnp.zeros_like(sg_acc)
    mine = v_c.at[c]
    mine[...] = jnp.zeros((16, D), F32)

    step = net.step
    events = [
        [(hop_halo, 1)],
        [],
        [(step, 2, 2)],
        [(step, 3, 0), (step, 0, 2)],
        [(step, 3, 1), (forward_halo, 0), (hop_halo, 2)],
        [(step, 4, 0), (step, 1, 2)],
        [(step, 4, 1), (forward_halo, 1), (hop_halo, 3), (step, 2, 3)],
        [(step, 5, 0), (step, 6, 0), (step, 7, 0), (step, 8, 0), (step, 0, 3)],
    ]
    root = math.sqrt(0.5)
    level = 1.0 / math.sqrt(2.0 * math.pi)

    def chunk(k, squares):
        slot = lax.rem(k, 2)
        for n in range(FF_CHUNKS):

            @pl.when(k == n)
            def _(n=n):
                loads[n][0].wait()
                loads[n][1].wait()

        down = w_down[slot].reshape(D, D)
        for j in range(3):
            tile = slice(256 * j, 256 * (j + 1))
            col = pl.ds(pl.multiple_of(D * k + 256 * j, 256), 256)
            pre = mm(second_in[...], w_up[slot, :, :, :, tile].reshape(D, 256)) + up_add[:, col]
            hidden = mm(grad[...], down[tile, :], NT)
            half = 0.5 + 0.5 * lax.erf(pre * root)
            act = (pre * half).astype(BF)
            slope = half + pre * jnp.exp(-0.5 * pre * pre) * level
            pg = (hidden * slope).astype(BF)
            act_s[:, tile] = act
            pg_s[:, tile] = pg
            wide = act.astype(F32)
            squares = squares + jnp.sum(wide * wide, -1, keepdims=True)
            v_c[c, pl.ds(8 + k, 1), tile] = jnp.sum(pg.astype(F32), 0, keepdims=True)

        def hook(half):
            for n in range(FF_CHUNKS):

                @pl.when(k == n)
                def _(n=n):
                    if half == 1 and n + 2 < FF_CHUNKS:
                        start(loads[n + 2])
                    for event, *where in events[2 * n + half]:
                        event(*where)

        hook(0)
        p_up[:, :, :, pl.ds(pl.multiple_of(D * k, 256), D)] = (
            mm(second_t[...], pg_s[...]).astype(BF).reshape(lay.nz, lay.ny, r, D)
        )
        p_down[pl.ds(near_z * k, near_z)] = (
            mm(act_s[...].T, grad[...]).astype(BF).reshape(near_z, lay.ny, 4, r, D)
        )
        output_base[...] += mm(act_s[...], down)
        sg_acc[...] += mm(pg_s[...], w_up[slot].reshape(D, D), NT)
        hook(1)
        return squares

    squares = lax.fori_loop(0, FF_CHUNKS, chunk, jnp.zeros((rows, 1), F32))
    run = lambda *pairs: [step(t, k) for t, k in pairs]
    run((5, 1), (6, 1), (3, 2))
    output[...] = output_base[...].astype(BF)
    forward_halo(2)
    run((1, 3), (8, 1), (7, 1), (2, 4))
    cot_sum = jnp.sum(grad[...].astype(F32), 0, keepdims=True)
    run((0, 4))
    forward_halo(3)

    def put(k, value):
        v_c[c, k : k + 1, :] = value

    put(4, cot_sum)
    for k in range(3):
        put(5 + k, att_sums[k : k + 1, :])
    cot = grad[...].astype(F32)
    token_norm = squares * jnp.sum(cot * cot, -1, keepdims=True) * (1.0 / (FF * D))
    docs_of = jnp.concatenate([seg[...].astype(F32)] * (LANES // 8), 0).T[:, 0:1]
    doc = lax.broadcasted_iota(jnp.int32, (rows, D), 1).astype(F32)
    member = jnp.where((docs_of == doc) & (doc < docs), 1.0, 0.0)
    put(12, jnp.sum(token_norm * member, 0, keepdims=True))
    put(13, jnp.sum(member, 0, keepdims=True))
    run((4, 2))
    keep = jnp.where(even, 1.0, 0.0).astype(F32)

    def norms(k):
        to_owner[k].wait_recv()
        at = slice(k * quarter, (k + 1) * quarter)
        first_grad = fg_own[at, :] + home[at, :].astype(F32) + hop[at, :].astype(F32) * keep
        second_grad = sg_acc[at, :]
        normed, factor = norm_parts(tok[at, :].astype(F32))
        input_grad[at, :] = (
            grad[at, :].astype(F32)
            + norm_back(first_grad, gain_first, normed, factor)
            + norm_back(second_grad, gain_second, normed, factor)
        ).astype(BF)
        sums = [first_grad * normed, first_grad, second_grad * normed, second_grad]
        return [jnp.sum(value, 0, keepdims=True) for value in sums]

    def add_up(left, right):
        return [p + q for p, q in zip(left, right)]

    sums = norms(0)
    run((5, 2), (1, 4))
    sums = add_up(sums, norms(1))
    run((6, 2), (3, 3))
    sums = add_up(sums, norms(2))
    sums = add_up(sums, norms(3))
    for k in range(4):
        put(k, sums[k])
    run((8, 2))

    at = [0, 1, lay.nx, lay.nx + lay.ny - 1]

    def spread(ref, own, peers, base):
        return [
            remote(ref.at[own], ref.at[own], v_s.at[base + k], v_r.at[base + k], p)
            for k, p in enumerate(peers)
        ]

    vec_c = spread(v_c, c, cs, at[0])
    vec_x = spread(v_x, x, xs, at[1])
    vec_y = spread(v_y, y, ys, at[2])
    vec_z = spread(v_z, z, zs, at[3])

    def add_all(ref, size):
        value = ref[0]
        for k in range(1, size):
            value = value + ref[k]
        return value

    start(vec_c)
    run((7, 2), (4, 3))
    arrive(vec_c)
    v_x[x] = add_all(v_c, 2)
    start(vec_x)
    run((2, 5), (0, 5), (3, 4), (6, 3), (5, 3))
    arrive(vec_x)
    v_y[y] = add_all(v_x, lay.nx)
    start(vec_y)
    run((1, 5), (8, 3), (4, 4), (3, 5), (7, 3))
    arrive(vec_y)
    v_z[z] = add_all(v_y, lay.ny)
    start(vec_z)
    run((6, 4), (5, 4), (4, 5), (8, 4), (6, 5), (5, 5), (7, 4), (8, 5))
    arrive(vec_z)
    vec_out[...] = add_all(v_z, lay.nz)
    run((7, 5))
    for t in range(9):
        net.step(t, 6)
    net.drain()
    sent(vec_c + vec_x + vec_y + vec_z)
    sent(to_next + to_owner)


def back(lay, g_up, g_down, p_att, fg_prev, fg_own, attn_out, vectors, up_add, att_sums, tok, grad, seg):
    rows = tok.shape[0]
    r = p_att.shape[2]
    n = len(CHUNKS)
    docs = DOC_DEV * lay.dp * lay.fsdp
    outs = (
        jax.ShapeDtypeStruct((rows, D), BF),
        jax.ShapeDtypeStruct((rows, D), BF),
        jax.ShapeDtypeStruct((r, 4 * D), BF),
        jax.ShapeDtypeStruct((r, 4 * D), BF),
        jax.ShapeDtypeStruct((4, r, D), BF),
        jax.ShapeDtypeStruct((16, D), F32),
    )
    lx, ly, lz = max(1, lay.nx - 1), max(1, lay.ny - 1), max(1, lay.nz - 1)

    def v(shape, dtype=BF):
        return pltpu.VMEM(shape, dtype)

    def bufs(chunks, peers, x_all, z_all, y_all):
        return [v((chunks,) + peers + part_shape(lay, g, x_all, z_all, y_all, r)) for g in range(3)]

    scratch = [
        v(grad_shape(lay, 1, r)), v(grad_shape(lay, 2, r)),
        v((2, lay.nz, lay.ny, r, D)), v((2, lay.nz // FF_CHUNKS, lay.ny, 4, r, D)),
        v((rows, D)), v((D, rows)), v((rows, D)), v((rows, D)), v((rows, D), F32),
        v((rows, D)), v((rows, D)),
        bufs(3, (), True, True, True),
        bufs(2, (lx,), False, True, True),
        bufs(1, (ly,), True, True, False),
        bufs(2, (ly,), False, True, False),
        bufs(1, (lx,), False, True, False),
        bufs(3, (lz,), False, False, False),
    ]
    vecs = [v((k, 16, D), F32) for k in (2, lay.nx, lay.ny, lay.nz)]
    nv = 1 + lay.nx + lay.ny + lay.nz
    sems = [
        dma(n), dma(n), dma(n, lx), dma(n, lx), dma(n, ly), dma(n, ly), dma(n, lz), dma(n, lz),
        dma(n, lx), dma(n, lx), dma(n), dma(n), dma(nv), dma(nv), dma(2, FF_CHUNKS), dma(8), dma(8),
    ]
    vmem = pl.BlockSpec(memory_space=pltpu.VMEM)
    return pl.pallas_call(
        functools.partial(back_kernel, lay, rows, docs),
        name="back",
        out_shape=outs,
        in_specs=hbm(2) + [vmem] * 10,
        out_specs=(vmem,) * 6,
        scratch_shapes=scratch + vecs + sems,
        compiler_params=pltpu.CompilerParams(
            collective_id=1, has_side_effects=True, vmem_limit_bytes=VMEM_LIMIT
        ),
    )(g_up, g_down, p_att, fg_prev, fg_own, attn_out, vectors, up_add, att_sums, tok, grad, seg)


def per_device(
    lay, tokens, seg_ids, out_grad, first_gain, first_bias, second_gain, second_bias,
    qkv_weight, qkv_bias, dense_weight, up_weight, up_bias, down_weight, out_bias,
):
    rows = tokens.shape[0]
    r = qkv_weight.shape[0]
    fsdp = lay.fsdp
    qkv_kinds = qkv_weight.reshape(r, H, 3, HD).transpose(0, 2, 1, 3).reshape(r, 3 * D)
    u_att = jnp.concatenate([qkv_kinds, dense_weight], 1)
    u_down = down_weight.reshape(4, r, D)
    vectors = (first_gain, first_bias, second_gain, second_bias, out_bias, qkv_bias, up_bias)
    small = pack_small(vectors, r)
    seg_rows = jnp.broadcast_to(seg_ids[None, :], (8, rows))
    passed = front(lay, u_att, up_weight, u_down, small, tokens, out_grad, seg_rows)
    output, input_grad, f_att, f_up, f_down, vec = back(lay, *passed, tokens, out_grad, seg_rows)
    docs = DOC_DEV * lay.dp * fsdp
    shard = lax.axis_index("fsdp")
    plain = lax.dynamic_slice_in_dim(vec[:5], shard * r, r, 1)
    kinds = vec[5:8].reshape(3, H, HD).transpose(1, 0, 2).reshape(3 * D)
    qkv_add = lax.dynamic_slice_in_dim(kinds, shard * 3 * r, 3 * r)
    up_add = lax.dynamic_slice_in_dim(vec[8:12].reshape(FF), shard * 4 * r, 4 * r)
    qkv_out = (
        f_att[:, : 3 * D].astype(F32).reshape(r, 3, H, HD).transpose(0, 2, 1, 3).reshape(r, 3 * D)
    )
    return (
        output,
        input_grad,
        plain[0],
        plain[1],
        plain[2],
        plain[3],
        qkv_out,
        qkv_add,
        f_att[:, 3 * D :].astype(F32),
        f_up.astype(F32),
        up_add,
        f_down.reshape(4 * r, D).astype(F32),
        plain[4],
        vec[12, :docs] / vec[13, :docs],
    )


def solution(mesh):
    lay = Layout(mesh.shape["dp"], mesh.shape["fsdp"])
    both = P(("dp", "fsdp"))
    split = P("fsdp")
    in_specs = (both, both, both) + (split,) * 11
    out_specs = (both, both) + (split,) * 11 + (P(),)
    return jax.shard_map(
        functools.partial(per_device, lay), mesh=mesh, in_specs=in_specs, out_specs=out_specs,
        check_vma=False,
    )
```

```python
import functools
import math

import jax
import jax.numpy as jnp
from jax import lax
from jax.experimental import pallas as pl
from jax.experimental.pallas import tpu as pltpu
from jax.sharding import PartitionSpec as P

D = 768
H = 12
HD = 64
FF = 3072
ROT = 16
ROW = 2048
DOC_DEV = 2
LANES = 128
PAIRS = D // LANES
MESH = pl.DeviceIdType.MESH
VMEM_LIMIT = 60 * 1024 * 1024


class Layout:
    def __init__(self, dp, fsdp):
        self.dp, self.fsdp = dp, fsdp
        self.nc = 2
        self.nx = dp // 2
        ny = 1
        while (2 * ny) * (2 * ny) <= fsdp:
            ny *= 2
        self.ny, self.nz = ny, fsdp // ny
        self.sub = max(1, self.nx // 2)
        self.unit = 4 // self.nx
        self.down_unit = 2 // self.sub

    def coords(self):
        d, f = lax.axis_index("dp"), lax.axis_index("fsdp")
        return d // 2, d % 2, f // self.ny, f % self.ny

    def device(self, x, c, z, y):
        return {"dp": x * 2 + c, "fsdp": z * self.ny + y}


def wrap(value, size):
    return lax.rem(value + size, size)


CHUNKS = tuple((g, i) for g in range(3) for i in range(3))
ALL = slice(None)


def grad_shape(lay, group, r):
    return (lay.nz, lay.ny, r, 4 * D) if group < 2 else (lay.nz, lay.ny, 4, r, D)


def span_of(lay, group, i, c, x):
    if group < 2:
        width = 512 // lay.nx
        if x is ALL:
            return pl.ds(pl.multiple_of(1024 * i + 512 * c, LANES), 512), None
        return pl.ds(pl.multiple_of(1024 * i + 512 * c + width * x, LANES), width), None
    width = 256 // lay.sub
    if x is ALL:
        return pl.ds(256 * i, 256), pl.ds(2 * c, 2)
    start = 256 * i + width * lax.rem(x, lay.sub)
    return pl.ds(pl.multiple_of(start, LANES), width), 2 * c + x // lay.sub


def view(lay, ref, group, i, c, x, z, y):
    cols, quarter = span_of(lay, group, i, c, x)
    if group < 2:
        return ref.at[z, y, :, cols]
    return ref.at[z, y, quarter, :, cols]


def shard_view(lay, ref, group, i, c, x):
    cols, quarter = span_of(lay, group, i, c, x)
    if group < 2:
        return ref.at[:, cols]
    return ref.at[quarter, :, cols]


def part_shape(lay, group, x_all, z_all, y_all, r):
    lead = ((lay.nz,) if z_all else ()) + ((lay.ny,) if y_all else ())
    if group < 2:
        return lead + (r, 512 if x_all else 512 // lay.nx)
    return lead + ((2, r, 256) if x_all else (r, 256 // lay.sub))


def barrier_with(peers):
    sem = pltpu.get_barrier_semaphore()
    for peer in peers:
        pl.semaphore_signal(sem, inc=1, device_id=peer, device_id_type=MESH)
    pl.semaphore_wait(sem, len(peers))


def line_peers(lay):
    x, c, z, y = lay.coords()
    xs = [lay.device(wrap(x + k, lay.nx), c, z, y) for k in range(1, lay.nx)]
    ys = [lay.device(x, c, z, wrap(y + k, lay.ny)) for k in range(1, lay.ny)]
    zs = [lay.device(x, c, wrap(z + k, lay.nz), y) for k in range(1, lay.nz)]
    cs = [lay.device(x, 1 - c, z, y)]
    return xs, cs, zs, ys


def remote(src, dst, ssem, rsem, device):
    return pltpu.make_async_remote_copy(
        src_ref=src, dst_ref=dst, send_sem=ssem, recv_sem=rsem, device_id=device, device_id_type=MESH
    )


def start(copies):
    for copy in copies:
        copy.start()


def arrive(copies):
    for copy in copies:
        copy.wait_recv()


def sent(copies):
    for copy in copies:
        copy.wait_send()


def hbm(count):
    return [pl.BlockSpec(memory_space=pltpu.HBM)] * count


def dma(*shape):
    return pltpu.SemaphoreType.DMA(shape)


NT = (((1,), (1,)), ((), ()))
NN = (((1,), (0,)), ((), ()))
F32 = jnp.float32
BF = jnp.bfloat16


def mm(a, b, dims=NN):
    return lax.dot_general(a, b, dims, preferred_element_type=F32)


def norm_parts(values):
    middle = jnp.mean(values, -1, keepdims=True)
    centred = values - middle
    factor = lax.rsqrt(jnp.mean(centred * centred, -1, keepdims=True) + 1e-05)
    return centred * factor, factor


def small_plan(r):
    plan, at = [], 0
    for size, within in [(r, LANES)] * 5 + [(3 * r, HD), (4 * r, LANES)]:
        plan.append((at, size, math.gcd(size, within)))
        at += -(-size // LANES)
    return plan


SMALL_ROWS = 16


class Gather:
    def __init__(self, lay, us, gs, sems):
        (z_s, z_r, y_s, y_r, x_s, x_r, c_s, c_r) = sems
        x, c, z, y = lay.coords()
        xs, cs, zs, ys = line_peers(lay)
        self.stages = []
        for t, (g, i) in enumerate(CHUNKS):
            by_y, by_x = (ys, y_s, y_r), (xs, x_s, x_r)
            first, second = (by_y, by_x) if i < 2 else (by_x, by_y)
            middle = (x, ALL, ALL) if i < 2 else (ALL, ALL, y)
            steps = [
                ((zs, z_s, z_r), (x, z, y)),
                (first, (x, ALL, y)),
                (second, middle),
            ]
            stages = []
            for (peers, ss, rs), (px, pz, py) in steps:
                piece = view(lay, gs[g], g, i, c, px, pz, py)
                source = shard_view(lay, us[g], g, i, c, x) if len(stages) == 0 else piece
                stages.append(
                    [remote(source, piece, ss.at[t, k], rs.at[t, k], p) for k, p in enumerate(peers)]
                )
            piece = view(lay, gs[g], g, i, c, ALL, ALL, ALL)
            stages.append([remote(piece, piece, c_s.at[t], c_r.at[t], cs[0])])
            self.stages.append(stages)

    def issue(self, t, stage):
        start(self.stages[t][stage])

    def pass_on(self, t, stage):
        arrive(self.stages[t][stage - 1])
        start(self.stages[t][stage])

    def done(self, t):
        arrive(self.stages[t][3])

    def drain(self):
        for stages in self.stages:
            for copies in stages:
                sent(copies)


def rope(u, cos, low, high):
    return u * cos + pltpu.roll(u, LANES - 8, 1) * low + pltpu.roll(u, 8, 1) * high


def front_kernel(
    lay, rows,
    u_up, u_down, qkv, dense, tok, grad, seg, v0, v1, v2, v3, v4, v5, v6,
    g_up, g_down, p_out, prev_out, own_out, attn_hbm, vectors, up_add, att_sums,
    small, u_att, p_att, fg_prev, fg_own, attn_out, g_att, g_small, tok_halo, seg_halo, first_all, first_t, q_s, k_s, v_s, do_s, ctx_s, ctx_t,
    dq_s, dk_s, dv_s, cos_s, low_s, high_s, bias, dk_acc, dv_acc, qkv_add, s_s, w_s, d_s,
    local_sem, z_s, z_r, y_s, y_r, x_s, x_r, c_s, c_r, sm_s, sm_r, h_s, h_r, out_sem,
):
    span = 3 * rows
    r = qkv.shape[0]
    n_chunks = len(CHUNKS)
    x, c, z, y = lay.coords()
    xs, cs, zs, ys = line_peers(lay)
    total = lay.dp * lay.fsdp
    plan = small_plan(r)
    for (row, size, _), ref in zip(plan, (v0, v1, v2, v3, v4, v5, v6)):
        value = ref[...].astype(F32).reshape(1, size)
        for k in range(-(-size // LANES)):
            width = min(LANES, size - k * LANES)
            small[row + k : row + k + 1, :width] = value[:, k * LANES : k * LANES + width]
    left = lax.broadcasted_iota(jnp.int32, (r, LANES), 1) < HD
    for p in range(PAIRS):
        parts = [qkv[:, (3 * p + k) * LANES : (3 * p + k + 1) * LANES].astype(F32) for k in range(3)]
        kinds = (
            jnp.where(left, parts[0], parts[1]),
            pltpu.roll(jnp.where(left, parts[2], parts[0]), HD, 1),
            jnp.where(left, parts[1], parts[2]),
        )
        for k, part in enumerate(kinds):
            u_att[:, k * D + p * LANES : k * D + (p + 1) * LANES] = part.astype(BF)
    u_att[:, 3 * D :] = dense[...]
    b = lax.axis_index("dp") * lay.fsdp + lax.axis_index("fsdp")

    def stream(k):
        t = wrap(b + k, total)
        return {"dp": t // lay.fsdp, "fsdp": lax.rem(t, lay.fsdp)}

    around = [stream(2), stream(-2), stream(1), stream(-1)]
    gs = (g_att, g_up, g_down)
    us = (u_att, u_up, u_down)
    locals_ = []
    for t, (g, i) in enumerate(CHUNKS):
        locals_.append(
            pltpu.make_async_copy(
                shard_view(lay, us[g], g, i, c, x), view(lay, gs[g], g, i, c, x, z, y), local_sem.at[t]
            )
        )
    locals_.append(pltpu.make_async_copy(small, g_small.at[z, y], local_sem.at[n_chunks]))
    start(locals_)
    barrier_with(xs + cs + zs + ys + around)
    even = lax.rem(b, 2) == 0
    half = rows // 2
    halo, own, passed = [], [], []
    for k in range(2):
        part = pl.ds(k * half, half)
        halo.append(remote(tok.at[part], tok_halo.at[0, part], h_s.at[k], h_r.at[k], around[0]))
        own.append(remote(tok.at[part], tok_halo.at[1, part], h_s.at[2 + k], h_r.at[2 + k], around[2]))
        passed.append(
            remote(tok_halo.at[0, part], tok_halo.at[1, part], h_s.at[2 + k], h_r.at[2 + k], around[3])
        )
    segs = [
        remote(seg, seg_halo.at[0], h_s.at[4], h_r.at[4], around[0]),
        remote(seg, seg_halo.at[1], h_s.at[5], h_r.at[5], around[2]),
    ]
    small_z = [
        remote(small, g_small.at[z, y], sm_s.at[k], sm_r.at[k], p) for k, p in enumerate(zs)
    ]
    small_y = [
        remote(g_small.at[:, y], g_small.at[:, y], sm_s.at[lay.nz + k], sm_r.at[lay.nz + k], p)
        for k, p in enumerate(ys)
    ]
    net = Gather(lay, us, gs, (z_s, z_r, y_s, y_r, x_s, x_r, c_s, c_r))
    net.issue(0, 0)
    net.issue(2, 0)
    start(small_z)
    start(segs)
    net.issue(1, 0)

    def tables(k, carry):
        at = pl.ds(pl.multiple_of(k * 256, 256), 256)
        lane = lax.broadcasted_iota(jnp.int32, (256, LANES), 1) % HD
        row = lax.broadcasted_iota(jnp.int32, (256, LANES), 0) + k * 256
        place = lax.rem((b - 2) * rows + row + 4 * ROW, ROW).astype(F32)
        rate = jnp.exp((lane % 8).astype(F32) * (-math.log(10000.0) / 8.0))
        angle = place * rate
        sine = jnp.sin(angle)
        cos_s[at, :] = jnp.where(lane < ROT, jnp.cos(angle), 1.0)
        low_s[at, :] = jnp.where(lane < 8, -sine, 0.0)
        high_s[at, :] = jnp.where((lane >= 8) & (lane < ROT), sine, 0.0)
        return carry

    lax.fori_loop(0, 2, tables, 0)
    for t in (0, 2, 1, n_chunks):
        locals_[t].wait()
    net.pass_on(0, 1)
    lax.fori_loop(2, 3, tables, 0)
    net.pass_on(2, 1)
    lax.fori_loop(3, 5, tables, 0)
    arrive(small_z)
    start(small_y)
    net.pass_on(0, 2)
    net.pass_on(1, 1)
    halo[0].start()
    lax.fori_loop(5, span // 256, tables, 0)
    arrive(small_y)
    net.pass_on(2, 2)

    lane_row = lax.broadcasted_iota(jnp.int32, (1, LANES), 1)

    def line(first_row, size, unit, length, source):
        out = []
        for block in range(length // LANES):
            value = None
            for k in range(LANES // unit):
                owner, local = divmod(source(block * (LANES // unit) + k), size // unit)
                row, lane = divmod(local * unit, LANES)
                row += first_row
                piece = g_small[owner // lay.ny, owner % lay.ny, row : row + 1, :]
                if lane != k * unit:
                    piece = pltpu.roll(piece, (k * unit - lane) % LANES, 1)
                value = piece if value is None else jnp.where(lane_row // unit == k, piece, value)
            out.append(value)
        return jnp.concatenate(out, 1)

    def norm_rows(values):
        return norm_parts(values.astype(F32))[0]

    for j in range(5):
        vectors[j : j + 1, :] = line(*plan[j], D, lambda n: n)
    vectors[5:8, :] = jnp.zeros((3, D), F32)
    unit = plan[5][2]
    a_head = HD // unit

    def natural(n):
        kind, rest = divmod(n, D // unit)
        head, part = divmod(rest, a_head)
        return head * 3 * a_head + kind * a_head + part

    qkv_add[...] = line(*plan[5], 3 * D, natural)
    net.pass_on(1, 2)
    up_add[...] = line(*plan[6], FF, lambda n: n)

    def pass_halo(k):
        arrive([halo[k]])

        @pl.when(even)
        def _():
            own[k].start()

        @pl.when(jnp.logical_not(even))
        def _():
            passed[k].start()

    halo[1].start()
    gain, shift = vectors[0:1, :], vectors[1:2, :]
    own_rows = pl.ds(2 * rows, rows)
    first = (norm_rows(tok[...]) * gain + shift).astype(BF)
    first_all[own_rows, :] = first
    first_t[:, own_rows] = first.T
    pass_halo(0)
    arrive(segs)
    least = jnp.maximum(0, 2 * rows - b * rows)
    keys_doc = jnp.concatenate([seg_halo[0], seg_halo[1], seg[...]], 1).astype(F32)
    keys_doc = jnp.broadcast_to(keys_doc, (LANES, span)).T
    query_doc = seg[0:1, :].astype(F32)

    for k in range(6):
        at = slice(k * 256, (k + 1) * 256)
        key_at = lax.broadcasted_iota(jnp.int32, (256, rows), 0) + k * 256
        query_at = lax.broadcasted_iota(jnp.int32, (256, rows), 1) + 2 * rows
        allowed = (keys_doc[at, 0:1] == query_doc) & (key_at <= query_at) & (key_at >= least)
        bias[at, :] = jnp.where(allowed, 0.0, -1e30)
    for t in range(3, n_chunks):
        locals_[t].wait()
    net.issue(5, 0)
    net.pass_on(0, 3)
    net.pass_on(2, 3)
    net.issue(3, 0)

    def weight(first_col, width):
        value = g_att[:, :, :, pl.ds(first_col, width)]
        return value.reshape(D, width)

    scale = 1.0 / math.sqrt(HD)

    def project(kind, j, at, out, factor):
        col = pl.multiple_of(kind * D + 256 * j, 256)
        value = mm(first_all[at, :], weight(col, 256)) + qkv_add[:, pl.ds(col, 256)]
        for k in range(2):
            u = value[:, k * LANES : (k + 1) * LANES]
            if kind < 2:
                u = rope(u, cos_s[at, :], low_s[at, :], high_s[at, :])
            if factor is not None:
                u = u * factor
            out[:, pl.ds(pl.multiple_of(256 * j + LANES * k, LANES), LANES)] = u.astype(BF)

    def own_queries(j, carry):
        project(0, j, own_rows, q_s, scale)
        return carry

    def own_keys(j, carry):
        project(1, j, own_rows, k_s.at[own_rows], None)
        return carry

    def own_values(j, carry):
        project(2, j, own_rows, v_s.at[own_rows], None)
        return carry

    net.done(0)
    lax.fori_loop(0, 3, own_queries, 0)
    lax.fori_loop(0, 1, own_keys, 0)
    pass_halo(1)
    net.pass_on(1, 3)
    net.issue(4, 0)
    net.done(2)
    do_s[...] = mm(grad[...], weight(3 * D, D), NT).astype(BF)
    lax.fori_loop(2, 3, own_values, 0)
    net.pass_on(5, 1)
    net.done(1)
    lax.fori_loop(1, 3, own_keys, 0)
    lax.fori_loop(0, 2, own_values, 0)
    own[0].wait_recv()
    net.pass_on(3, 1)
    net.issue(8, 0)
    own[1].wait_recv()
    for k in range(2):
        at = slice(k * rows, (k + 1) * rows)
        before = (norm_rows(tok_halo[k]) * gain + shift).astype(BF)
        first_all[at, :] = before
        first_t[:, at] = before.T
    net.pass_on(4, 1)
    net.pass_on(5, 2)

    def earlier_projections(j, carry):
        for k in range(2):
            at = pl.ds(k * rows, rows)
            project(1, j, at, k_s.at[at], None)
            project(2, j, at, v_s.at[at], None)
        return carry

    lax.fori_loop(0, 3, earlier_projections, 0)
    net.pass_on(3, 2)
    net.issue(6, 0)

    go, send, end = net.pass_on, net.issue, net.done
    later = [
        [(go, 8, 1), (send, 7, 0), (go, 4, 2)],
        [(go, 5, 3)],
        [(go, 6, 1)],
        [(go, 3, 3), (go, 7, 1)],
        [(go, 8, 2), (go, 6, 2)],
        [(go, 4, 3), (go, 7, 2)],
        [],
        [(go, 8, 3)],
        [],
        [(go, 6, 3)],
        [(go, 7, 3)],
        [],
    ]
    tile = 256

    def pair(p, carry):
        lanes = pl.ds(pl.multiple_of(p * LANES, LANES), LANES)
        v_t, k_t = v_s[:, lanes].T, k_s[:, lanes].T
        do_t = do_s[:, lanes].astype(F32).T
        lane = lax.broadcasted_iota(jnp.int32, (tile, LANES), 1)
        zero = jnp.zeros((), BF)
        for t in range(rows // tile):
            cols = slice(t * tile, (t + 1) * tile)
            kl = 2 * rows + (t + 1) * tile
            pieces = [slice(k * tile, (k + 1) * tile) for k in range(kl // tile)]
            qms = [jnp.where((lane // HD) == hh, q_s[cols, lanes], zero) for hh in range(2)]
            doms = [jnp.where((lane // HD) == hh, do_s[cols, lanes], zero) for hh in range(2)]
            tops, norms = [], []
            for hh in range(2):
                top = None
                for at in pieces:
                    st = mm(k_s[at, lanes], qms[hh], NT) + bias[at, cols]
                    s_s[hh, at, :] = st
                    most = jnp.max(st, 0, keepdims=True)
                    top = most if top is None else jnp.maximum(top, most)
                tops.append(top)
            for hh in range(2):
                total_e = None
                for at in pieces:
                    e = jnp.exp(s_s[hh, at, :] - tops[hh])
                    s_s[hh, at, :] = e
                    part = jnp.sum(e, 0, keepdims=True)
                    total_e = part if total_e is None else total_e + part
                norms.append(1.0 / total_e)
            outs, dqs = [], []
            for hh in range(2):
                for at in pieces:
                    w_s[hh, at, :] = (s_s[hh, at, :] * norms[hh]).astype(BF)
            for hh in range(2):
                part = slice(hh * HD, (hh + 1) * HD)
                o_t = mm(v_t[part, :kl], w_s[hh, :kl, :])
                delta = jnp.sum(o_t * do_t[part, cols], 0, keepdims=True)
                outs.append(o_t)
                for at in pieces:
                    dp = mm(v_s[at, lanes], doms[hh], NT)
                    d_s[hh, at, :] = ((s_s[hh, at, :] * norms[hh]) * (dp - delta)).astype(BF)
                dqs.append(mm(k_t[part, :kl], d_s[hh, :kl, :]))
            for k, at in enumerate(pieces):
                dk = mm(d_s[0, at, :], qms[0]) + mm(d_s[1, at, :], qms[1])
                dv = mm(w_s[0, at, :], doms[0]) + mm(w_s[1, at, :], doms[1])
                if t == 0 or k == len(pieces) - 1:
                    dk_acc[at, :] = dk
                    dv_acc[at, :] = dv
                else:
                    dk_acc[at, :] += dk
                    dv_acc[at, :] += dv
            o_pair = jnp.concatenate(outs, 0)
            ctx_t[lanes, cols] = o_pair.astype(BF)
            ctx_s[cols, lanes] = o_pair.T.astype(BF)
            dq = jnp.concatenate(dqs, 0).T * scale
            at = slice(2 * rows + t * tile, 2 * rows + (t + 1) * tile)
            dq_s[cols, lanes] = rope(dq, cos_s[at, :], -low_s[at, :], -high_s[at, :]).astype(BF)
            for k in range(PAIRS):

                @pl.when(p == k)
                def _(k=k, t=t):
                    for event, *where in later[2 * k + t]:
                        event(*where)

        dk_s[:, lanes] = rope(dk_acc[...], cos_s[...], -low_s[...], -high_s[...]).astype(BF)
        dv_s[:, lanes] = dv_acc[...].astype(BF)
        return carry

    lax.fori_loop(0, PAIRS, pair, 0)

    def earlier_grad(k, carry):
        at = pl.ds(pl.multiple_of(k * 256, 256), 256)
        value = mm(dk_s[at, :], weight(D, D), NT) + mm(dv_s[at, :], weight(2 * D, D), NT)
        fg_prev[at, :] = value.astype(BF)
        return carry

    lax.fori_loop(0, 2 * rows // 256, earlier_grad, 0)
    outs = [pltpu.make_async_copy(fg_prev, prev_out, out_sem.at[0])]
    outs[0].start()
    for k in range(rows // 256):
        at = slice(2 * rows + 256 * k, 2 * rows + 256 * (k + 1))
        near = slice(256 * k, 256 * (k + 1))
        fg_own[near, :] = (
            mm(dk_s[at, :], weight(D, D), NT)
            + mm(dv_s[at, :], weight(2 * D, D), NT)
            + mm(dq_s[near, :], weight(0, D), NT)
        )

    outs.append(pltpu.make_async_copy(fg_own, own_out, out_sem.at[1]))
    outs[1].start()

    def weight_grads(j, carry):
        col = pl.multiple_of(256 * j, 256)
        cols = pl.ds(col, 256)

        def put(kind, value):
            p_att[:, :, :, pl.ds(pl.multiple_of(kind * D + col, 256), 256)] = value.astype(BF).reshape(
                lay.nz, lay.ny, r, 256
            )

        put(0, mm(first_t[:, own_rows], dq_s[:, cols]))
        put(1, mm(first_t[...], dk_s[:, cols]))
        put(2, mm(first_t[...], dv_s[:, cols]))
        put(3, mm(ctx_t[...], grad[:, cols]))
        attn_out[:, cols] = mm(ctx_s[...], weight(pl.multiple_of(3 * D + col, 256), 256))
        return carry

    lax.fori_loop(0, 3, weight_grads, 0)
    outs.append(pltpu.make_async_copy(p_att, p_out, out_sem.at[2]))
    outs.append(pltpu.make_async_copy(attn_out, attn_hbm, out_sem.at[3]))
    start(outs[2:])
    for k, ref in enumerate((dq_s, dk_s, dv_s)):
        att_sums[k : k + 1, :] = jnp.sum(ref[...].astype(F32), 0, keepdims=True)
    att_sums[3:8, :] = jnp.zeros((5, D), F32)
    for t in range(3, 9):
        net.done(t)
    net.drain()
    sent(small_z + small_y + segs + halo + own)
    for copy in outs:
        copy.wait()


def front(lay, u_up, u_down, qkv, dense, tok, grad, seg, vectors):
    rows = tok.shape[0]
    span = 3 * rows
    r = qkv.shape[0]
    n = len(CHUNKS)
    outs = (
        jax.ShapeDtypeStruct(grad_shape(lay, 1, r), BF),
        jax.ShapeDtypeStruct(grad_shape(lay, 2, r), BF),
        jax.ShapeDtypeStruct(grad_shape(lay, 0, r), BF),
        jax.ShapeDtypeStruct((2 * rows, D), BF),
        jax.ShapeDtypeStruct((rows, D), F32),
        jax.ShapeDtypeStruct((rows, D), F32),
        jax.ShapeDtypeStruct((8, D), F32),
        jax.ShapeDtypeStruct((1, FF), F32),
        jax.ShapeDtypeStruct((8, D), F32),
    )
    vmem = pl.BlockSpec(memory_space=pltpu.VMEM)
    lx, ly, lz = max(1, lay.nx - 1), max(1, lay.ny - 1), max(1, lay.nz - 1)

    def v(shape, dtype=BF):
        return pltpu.VMEM(shape, dtype)

    return pl.pallas_call(
        functools.partial(front_kernel, lay, rows),
        name="front",
        out_shape=outs,
        in_specs=hbm(2) + [vmem] * (5 + len(vectors)),
        out_specs=tuple(hbm(6)) + (vmem,) * 3,
        scratch_shapes=[
            v((SMALL_ROWS, LANES), F32), v((r, 4 * D)), v(grad_shape(lay, 0, r)), v((2 * rows, D)), v((rows, D), F32), v((rows, D), F32),
            v(grad_shape(lay, 0, r)), v((lay.nz, lay.ny, SMALL_ROWS, LANES), F32), v((2, rows, D)),
            v((2, 1, rows), jnp.int32), v((span, D)), v((D, span)), v((rows, D)), v((span, D)),
            v((span, D)), v((rows, D)), v((rows, D)), v((D, rows)), v((rows, D)), v((span, D)),
            v((span, D)), v((span, LANES), F32), v((span, LANES), F32), v((span, LANES), F32),
            v((span, rows), F32), v((span, LANES), F32), v((span, LANES), F32), v((1, 3 * D), F32),
            v((2, span, 256), F32), v((2, span, 256)), v((2, span, 256)),
            dma(n + 1), dma(n, lz), dma(n, lz), dma(n, ly), dma(n, ly), dma(n, lx), dma(n, lx),
            dma(n), dma(n), dma(lay.nz + ly), dma(lay.nz + ly), dma(6), dma(6), dma(4),
        ],
        compiler_params=pltpu.CompilerParams(
            collective_id=0, has_side_effects=True, vmem_limit_bytes=VMEM_LIMIT
        ),
    )(u_up, u_down, qkv, dense, tok, grad, seg, *vectors)


class Reduce:
    def __init__(self, lay, ps, fs, bufs, sems):
        (ca, ra1, rb1, ra2, rb2, ra3) = bufs
        (c_s, c_r, x_s, x_r, y_s, y_r, z_s, z_r, fx_s, fx_r, fc_s, fc_r) = sems
        x, c, z, y = lay.coords()
        xs, cs, zs, ys = line_peers(lay)
        self.steps = []
        for t, (g, i) in enumerate(CHUNKS):
            p, f = ps[g], fs[g]
            other_x = [wrap(x + 1 + k, lay.nx) for k in range(lay.nx - 1)]
            other_y = [wrap(y + 1 + k, lay.ny) for k in range(lay.ny - 1)]
            other_z = [wrap(z + 1 + k, lay.nz) for k in range(lay.nz - 1)]

            def over_x(pieces, slot):
                return [
                    remote(piece, slot.at[k], x_s.at[t, k], x_r.at[t, k], xs[k])
                    for k, piece in enumerate(pieces)
                ]

            def over_y(pieces, slot):
                return [
                    remote(piece, slot.at[k], y_s.at[t, k], y_r.at[t, k], ys[k])
                    for k, piece in enumerate(pieces)
                ]

            def into(dst, slot, count):
                return functools.partial(add_into, dst, [slot.at[k] for k in range(count)])

            core_slot = ca[g].at[i]
            core = [
                remote(view(lay, p, g, i, 1 - c, ALL, ALL, ALL), core_slot, c_s.at[t], c_r.at[t], cs[0])
            ]
            add_core = functools.partial(add_into, view(lay, p, g, i, c, ALL, ALL, ALL), [core_slot])
            if i < 2:
                slot1, slot2 = ra1[g].at[i], ra2[g].at[i]
                first = over_x([view(lay, p, g, i, c, k, ALL, ALL) for k in other_x], slot1)
                add_1 = into(view(lay, p, g, i, c, x, ALL, ALL), slot1, lay.nx - 1)
                second = over_y([view(lay, p, g, i, c, x, ALL, k) for k in other_y], slot2)
                add_2 = into(view(lay, p, g, i, c, x, ALL, y), slot2, lay.ny - 1)
            else:
                slot1, slot2 = rb1[g].at[0], rb2[g].at[0]
                first = over_y([view(lay, p, g, i, c, ALL, ALL, k) for k in other_y], slot1)
                add_1 = into(view(lay, p, g, i, c, ALL, ALL, y), slot1, lay.ny - 1)
                second = over_x([view(lay, p, g, i, c, k, ALL, y) for k in other_x], slot2)
                add_2 = into(view(lay, p, g, i, c, x, ALL, y), slot2, lay.nx - 1)
            slot3 = ra3[g].at[i]
            third = [
                remote(view(lay, p, g, i, c, x, k, y), slot3.at[n], z_s.at[t, n], z_r.at[t, n], zs[n])
                for n, k in enumerate(other_z)
            ]
            out = shard_view(lay, f, g, i, c, x)
            own = view(lay, p, g, i, c, x, z, y)
            finish = functools.partial(
                set_sum, out, [own] + [slot3.at[k] for k in range(lay.nz - 1)]
            )
            share_x = [
                remote(out, out, fx_s.at[t, k], fx_r.at[t, k], peer) for k, peer in enumerate(xs)
            ]
            both = shard_view(lay, f, g, i, c, ALL)
            share_c = [remote(both, both, fc_s.at[t], fc_r.at[t], cs[0])]
            self.steps.append(
                (
                    (core, first, second, third, share_x, share_c),
                    (None, add_core, add_1, add_2, finish, None),
                )
            )

    def step(self, t, k):
        copies, adds = self.steps[t]
        if k > 0:
            arrive(copies[k - 1])
        if k < len(copies):
            if adds[k] is not None:
                adds[k]()
            start(copies[k])

    def drain(self):
        for copies, _ in self.steps:
            for group in copies:
                sent(group)


def set_sum(out, srcs):
    total = srcs[0][...].astype(F32)
    for src in srcs[1:]:
        total = total + src[...].astype(F32)
    out[...] = total.astype(BF)


def add_into(dst, srcs):
    lead = dst.shape[:-2]

    def body(j, carry):
        index = []
        rest = j
        for size in reversed(lead):
            index.append(lax.rem(rest, size))
            rest = rest // size
        index = tuple(reversed(index))
        total = dst[index].astype(F32)
        for src in srcs:
            total = total + src[index].astype(F32)
        dst[index] = total.astype(BF)
        return carry

    lax.fori_loop(0, math.prod(lead), body, 0)


def norm_back(grad, gain, normed, factor):
    inner = grad * gain
    return factor * (
        inner
        - jnp.mean(inner, -1, keepdims=True)
        - normed * jnp.mean(inner * normed, -1, keepdims=True)
    )


FF_CHUNKS = FF // D


def back_kernel(
    lay, rows, docs,
    g_up, g_down, p_in, prev_in, own_in, attn_in, vectors, up_add, att_sums, tok, grad, seg,
    output, input_grad, f_att, f_up, f_down, vec_out,
    p_att, fg_prev, fg_own, attn_out, p_up, p_down, w_up, w_down, second_in, second_t, act_s, pg_s, sg_acc, hop, home,
    ca, ra1, rb1, ra2, rb2, ra3, v_c, v_x, v_y, v_z, *sems,
):
    (c_s, c_r, x_s, x_r, y_s, y_r, z_s, z_r, fx_s, fx_r, fc_s, fc_r, v_s, v_r, w_sem, h_s, h_r, in_sem) = sems
    r = p_in.shape[2]
    x, c, z, y = lay.coords()
    xs, cs, zs, ys = line_peers(lay)
    total = lay.dp * lay.fsdp
    b = lax.axis_index("dp") * lay.fsdp + lax.axis_index("fsdp")

    def stream(k):
        t = wrap(b + k, total)
        return {"dp": t // lay.fsdp, "fsdp": lax.rem(t, lay.fsdp)}

    around = [stream(2), stream(-2), stream(1), stream(-1)]
    near_z = lay.nz // FF_CHUNKS
    loads = []
    for k in range(FF_CHUNKS):
        slot = k % 2
        loads.append(
            (
                pltpu.make_async_copy(
                    g_up.at[:, :, :, pl.ds(D * k, D)], w_up.at[slot], w_sem.at[0, k]
                ),
                pltpu.make_async_copy(
                    g_down.at[pl.ds(near_z * k, near_z)], w_down.at[slot], w_sem.at[1, k]
                ),
            )
        )
    taken = [
        pltpu.make_async_copy(
            p_in.at[:, :, :, pl.ds(1024 * i, 1024)], p_att.at[:, :, :, pl.ds(1024 * i, 1024)],
            in_sem.at[i],
        )
        for i in range(3)
    ]
    taken.append(pltpu.make_async_copy(prev_in, fg_prev, in_sem.at[3]))
    taken.append(pltpu.make_async_copy(attn_in, attn_out, in_sem.at[4]))
    taken.append(pltpu.make_async_copy(own_in, fg_own, in_sem.at[5]))
    start(taken[:4])
    start(loads[0])
    start(taken[4:])
    start(loads[1])
    barrier_with(xs + cs + zs + ys + around)
    net = Reduce(
        lay, (p_att, p_up, p_down), (f_att, f_up, f_down), (ca, ra1, rb1, ra2, rb2, ra3), sems[:12]
    )
    for t in range(3):
        taken[t].wait()
        net.step(t, 0)
    net.step(0, 1)
    net.step(1, 1)
    net.step(2, 1)
    taken[3].wait()
    even = lax.rem(b, 2) == 0
    quarter = rows // 4
    to_next, to_last, to_owner = [], [], []
    for k in range(4):
        near = fg_prev.at[pl.ds(rows + k * quarter, quarter)]
        far = fg_prev.at[pl.ds(k * quarter, quarter)]
        part = pl.ds(k * quarter, quarter)
        to_next.append(remote(near, hop.at[part], h_s.at[k], h_r.at[k], around[2]))
        to_last.append(remote(near, hop.at[part], h_s.at[k], h_r.at[k], around[3]))
        to_owner.append(remote(far, home.at[part], h_s.at[4 + k], h_r.at[4 + k], around[1]))

    def hop_halo(k):
        @pl.when(even)
        def _():
            to_next[k].start()

        @pl.when(jnp.logical_not(even))
        def _():
            to_last[k].start()

    def forward_halo(k):
        to_last[k].wait_recv()
        at = pl.ds(k * quarter, quarter)

        @pl.when(jnp.logical_not(even))
        def _():
            fg_prev[at, :] = (fg_prev[at, :].astype(F32) + hop[at, :].astype(F32)).astype(BF)

        to_owner[k].start()

    hop_halo(0)

    gain_first, gain_second = vectors[0:1, :], vectors[2:3, :]
    normed, factor = norm_parts(tok[...].astype(F32))
    value = (normed * gain_second + vectors[3:4, :]).astype(BF)
    second_in[...] = value
    second_t[...] = value.T
    cot = grad[...].astype(F32)
    taken[4].wait()
    taken[5].wait()
    output_base = attn_out
    output_base[...] = attn_out[...] + tok[...].astype(F32) + vectors[4:5, :]
    sg_acc[...] = jnp.zeros_like(sg_acc)
    mine = v_c.at[c]
    mine[...] = jnp.zeros((16, D), F32)

    step = net.step
    events = [
        [(hop_halo, 1)],
        [],
        [(step, 2, 2)],
        [(step, 3, 0), (step, 0, 2)],
        [(step, 3, 1), (forward_halo, 0), (hop_halo, 2)],
        [(step, 4, 0), (step, 1, 2)],
        [(step, 4, 1), (forward_halo, 1), (hop_halo, 3), (step, 2, 3)],
        [(step, 5, 0), (step, 6, 0), (step, 7, 0), (step, 8, 0), (step, 0, 3)],
    ]
    root = math.sqrt(0.5)
    level = 1.0 / math.sqrt(2.0 * math.pi)

    def chunk(k, squares):
        slot = lax.rem(k, 2)
        for n in range(FF_CHUNKS):

            @pl.when(k == n)
            def _(n=n):
                loads[n][0].wait()
                loads[n][1].wait()

        down = w_down[slot].reshape(D, D)
        for j in range(3):
            tile = slice(256 * j, 256 * (j + 1))
            col = pl.ds(pl.multiple_of(D * k + 256 * j, 256), 256)
            pre = mm(second_in[...], w_up[slot, :, :, :, tile].reshape(D, 256)) + up_add[:, col]
            hidden = mm(grad[...], down[tile, :], NT)
            half = 0.5 + 0.5 * lax.erf(pre * root)
            act = (pre * half).astype(BF)
            slope = half + pre * jnp.exp(-0.5 * pre * pre) * level
            pg = (hidden * slope).astype(BF)
            act_s[:, tile] = act
            pg_s[:, tile] = pg
            wide = act.astype(F32)
            squares = squares + jnp.sum(wide * wide, -1, keepdims=True)
            v_c[c, pl.ds(8 + k, 1), tile] = jnp.sum(pg.astype(F32), 0, keepdims=True)

        def hook(half):
            for n in range(FF_CHUNKS):

                @pl.when(k == n)
                def _(n=n):
                    if half == 1 and n + 2 < FF_CHUNKS:
                        start(loads[n + 2])
                    for event, *where in events[2 * n + half]:
                        event(*where)

        hook(0)
        p_up[:, :, :, pl.ds(pl.multiple_of(D * k, 256), D)] = (
            mm(second_t[...], pg_s[...]).astype(BF).reshape(lay.nz, lay.ny, r, D)
        )
        p_down[pl.ds(near_z * k, near_z)] = (
            mm(act_s[...].T, grad[...]).astype(BF).reshape(near_z, lay.ny, 4, r, D)
        )
        output_base[...] += mm(act_s[...], down)
        sg_acc[...] += mm(pg_s[...], w_up[slot].reshape(D, D), NT)
        hook(1)
        return squares

    squares = lax.fori_loop(0, FF_CHUNKS, chunk, jnp.zeros((rows, 1), F32))
    run = lambda *pairs: [step(t, k) for t, k in pairs]
    run((5, 1), (6, 1), (3, 2))
    output[...] = output_base[...].astype(BF)
    forward_halo(2)
    run((1, 3), (8, 1), (7, 1), (2, 4))
    cot_sum = jnp.sum(grad[...].astype(F32), 0, keepdims=True)
    run((0, 4))
    forward_halo(3)

    def put(k, value):
        v_c[c, k : k + 1, :] = value

    put(4, cot_sum)
    for k in range(3):
        put(5 + k, att_sums[k : k + 1, :])
    cot = grad[...].astype(F32)
    token_norm = squares * jnp.sum(cot * cot, -1, keepdims=True) * (1.0 / (FF * D))
    docs_of = jnp.broadcast_to(seg[...].astype(F32), (LANES, rows)).T[:, 0:1]
    doc = lax.broadcasted_iota(jnp.int32, (rows, D), 1).astype(F32)
    member = jnp.where((docs_of == doc) & (doc < docs), 1.0, 0.0)
    put(12, jnp.sum(token_norm * member, 0, keepdims=True))
    put(13, jnp.sum(member, 0, keepdims=True))
    run((4, 2))
    keep = jnp.where(even, 1.0, 0.0).astype(F32)

    def norms(k):
        to_owner[k].wait_recv()
        at = slice(k * quarter, (k + 1) * quarter)
        first_grad = fg_own[at, :] + home[at, :].astype(F32) + hop[at, :].astype(F32) * keep
        second_grad = sg_acc[at, :]
        normed, factor = norm_parts(tok[at, :].astype(F32))
        input_grad[at, :] = (
            grad[at, :].astype(F32)
            + norm_back(first_grad, gain_first, normed, factor)
            + norm_back(second_grad, gain_second, normed, factor)
        ).astype(BF)
        sums = [first_grad * normed, first_grad, second_grad * normed, second_grad]
        return [jnp.sum(value, 0, keepdims=True) for value in sums]

    def add_up(left, right):
        return [p + q for p, q in zip(left, right)]

    sums = norms(0)
    run((5, 2), (1, 4))
    sums = add_up(sums, norms(1))
    run((6, 2), (3, 3))
    sums = add_up(sums, norms(2))
    sums = add_up(sums, norms(3))
    for k in range(4):
        put(k, sums[k])
    run((8, 2))

    at = [0, 1, lay.nx, lay.nx + lay.ny - 1]

    def spread(ref, own, peers, base):
        return [
            remote(ref.at[own], ref.at[own], v_s.at[base + k], v_r.at[base + k], p)
            for k, p in enumerate(peers)
        ]

    vec_c = spread(v_c, c, cs, at[0])
    vec_x = spread(v_x, x, xs, at[1])
    vec_y = spread(v_y, y, ys, at[2])
    vec_z = spread(v_z, z, zs, at[3])

    def add_all(ref, size):
        value = ref[0]
        for k in range(1, size):
            value = value + ref[k]
        return value

    start(vec_c)
    run((7, 2), (4, 3))
    arrive(vec_c)
    v_x[x] = add_all(v_c, 2)
    start(vec_x)
    run((2, 5), (0, 5), (3, 4), (6, 3), (5, 3))
    arrive(vec_x)
    v_y[y] = add_all(v_x, lay.nx)
    start(vec_y)
    run((1, 5), (8, 3), (4, 4), (3, 5), (7, 3))
    arrive(vec_y)
    v_z[z] = add_all(v_y, lay.ny)
    start(vec_z)
    run((6, 4), (5, 4), (4, 5), (8, 4), (6, 5), (5, 5), (7, 4), (8, 5))
    arrive(vec_z)
    vec_out[...] = add_all(v_z, lay.nz)
    run((7, 5))
    for t in range(9):
        net.step(t, 6)
    net.drain()
    sent(vec_c + vec_x + vec_y + vec_z)
    sent(to_next + to_owner)


def back(lay, g_up, g_down, p_att, fg_prev, fg_own, attn_out, vectors, up_add, att_sums, tok, grad, seg):
    rows = tok.shape[0]
    r = p_att.shape[2]
    n = len(CHUNKS)
    docs = DOC_DEV * lay.dp * lay.fsdp
    outs = (
        jax.ShapeDtypeStruct((rows, D), BF),
        jax.ShapeDtypeStruct((rows, D), BF),
        jax.ShapeDtypeStruct((r, 4 * D), BF),
        jax.ShapeDtypeStruct((r, 4 * D), BF),
        jax.ShapeDtypeStruct((4, r, D), BF),
        jax.ShapeDtypeStruct((16, D), F32),
    )
    lx, ly, lz = max(1, lay.nx - 1), max(1, lay.ny - 1), max(1, lay.nz - 1)

    def v(shape, dtype=BF):
        return pltpu.VMEM(shape, dtype)

    def bufs(chunks, peers, x_all, z_all, y_all):
        return [v((chunks,) + peers + part_shape(lay, g, x_all, z_all, y_all, r)) for g in range(3)]

    scratch = [
        v(grad_shape(lay, 0, r)), v((2 * rows, D)), v((rows, D), F32), v((rows, D), F32),
        v(grad_shape(lay, 1, r)), v(grad_shape(lay, 2, r)),
        v((2, lay.nz, lay.ny, r, D)), v((2, lay.nz // FF_CHUNKS, lay.ny, 4, r, D)),
        v((rows, D)), v((D, rows)), v((rows, D)), v((rows, D)), v((rows, D), F32),
        v((rows, D)), v((rows, D)),
        bufs(3, (), True, True, True),
        bufs(2, (lx,), False, True, True),
        bufs(1, (ly,), True, True, False),
        bufs(2, (ly,), False, True, False),
        bufs(1, (lx,), False, True, False),
        bufs(3, (lz,), False, False, False),
    ]
    vecs = [v((k, 16, D), F32) for k in (2, lay.nx, lay.ny, lay.nz)]
    nv = 1 + lay.nx + lay.ny + lay.nz
    sems = [
        dma(n), dma(n), dma(n, lx), dma(n, lx), dma(n, ly), dma(n, ly), dma(n, lz), dma(n, lz),
        dma(n, lx), dma(n, lx), dma(n), dma(n), dma(nv), dma(nv), dma(2, FF_CHUNKS), dma(8), dma(8), dma(6),
    ]
    vmem = pl.BlockSpec(memory_space=pltpu.VMEM)
    return pl.pallas_call(
        functools.partial(back_kernel, lay, rows, docs),
        name="back",
        out_shape=outs,
        in_specs=hbm(6) + [vmem] * 6,
        out_specs=(vmem,) * 6,
        scratch_shapes=scratch + vecs + sems,
        compiler_params=pltpu.CompilerParams(
            collective_id=1, has_side_effects=True, vmem_limit_bytes=VMEM_LIMIT
        ),
    )(g_up, g_down, p_att, fg_prev, fg_own, attn_out, vectors, up_add, att_sums, tok, grad, seg)


def finish_kernel(
    lay, docs, r, f_att, f_up, f_down, vec, out_in, grad_in,
    output, input_grad, fg, fb, sg, sb, qkv_w, qkv_b, dense_w, up_w, up_b, down_w, ob, norms,
):
    output[...] = out_in[...]
    input_grad[...] = grad_in[...]
    shard = lax.axis_index("fsdp")

    def by_head(row_count, kind):
        left = lax.broadcasted_iota(jnp.int32, (row_count, LANES), 1) < HD
        for p in range(PAIRS):
            q, k, v = (kind(n, p) for n in range(3))
            turned = pltpu.roll(k, HD, 1)
            yield jnp.where(left, q, turned)
            yield jnp.where(left, v, q)
            yield jnp.where(left, turned, v)

    def block(k, p):
        return f_att[:, k * D + p * LANES : k * D + (p + 1) * LANES].astype(F32)

    for n, value in enumerate(by_head(r, block)):
        qkv_w[:, n * LANES : (n + 1) * LANES] = value
    dense_w[...] = f_att[:, 3 * D :].astype(F32)
    up_w[...] = f_up[...].astype(F32)
    down_w[...] = f_down[...].astype(F32)

    def own(row, width):
        length = row.shape[1]
        wide = jnp.broadcast_to(row, (8, length))
        turned = pltpu.roll(wide, lax.rem(length - shard * width, length), 1)
        return turned[0:1, :width].reshape(width)

    for k, ref in enumerate((fg, fb, sg, sb, ob)):
        ref[...] = own(vec[k : k + 1, :], r)
    bias = list(by_head(1, lambda k, p: vec[5 + k : 6 + k, p * LANES : (p + 1) * LANES]))
    qkv_b[...] = own(jnp.concatenate(bias, 1), 3 * r)
    up_b[...] = own(jnp.concatenate([vec[8 + k : 9 + k, :] for k in range(4)], 1), 4 * r)
    norms[...] = (vec[12:13, :docs] / vec[13:14, :docs]).reshape(docs)


def finish(lay, output, input_grad, f_att, f_up, f_down, vec):
    r = f_att.shape[0]
    docs = DOC_DEV * lay.dp * lay.fsdp
    vmem = pl.BlockSpec(memory_space=pltpu.VMEM)
    shapes = [
        (r,), (r,), (r,), (r,), (r, 3 * D), (3 * r,), (r, D), (r, FF), (4 * r,), (4, r, D), (r,), (docs,),
    ]
    return pl.pallas_call(
        functools.partial(finish_kernel, lay, docs, r),
        name="finish",
        out_shape=tuple(jax.ShapeDtypeStruct(v.shape, v.dtype) for v in (output, input_grad))
        + tuple(jax.ShapeDtypeStruct(shape, F32) for shape in shapes),
        in_specs=[vmem] * 6,
        out_specs=(vmem,) * (2 + len(shapes)),
        compiler_params=pltpu.CompilerParams(vmem_limit_bytes=VMEM_LIMIT),
    )(f_att, f_up, f_down, vec, output, input_grad)


def per_device(
    lay, tokens, seg_ids, out_grad, first_gain, first_bias, second_gain, second_bias,
    qkv_weight, qkv_bias, dense_weight, up_weight, up_bias, down_weight, out_bias,
):
    rows = tokens.shape[0]
    r = qkv_weight.shape[0]
    vectors = (first_gain, first_bias, second_gain, second_bias, out_bias, qkv_bias, up_bias)
    seg_row = seg_ids.reshape(1, rows)
    passed = front(
        lay, up_weight, down_weight.reshape(4, r, D), qkv_weight, dense_weight, tokens,
        out_grad, seg_row, vectors,
    )
    summed = back(lay, *passed, tokens, out_grad, seg_row)
    (output, input_grad, fg, fb, sg, sb, qkv_w, qkv_b, dense_w, up_w, up_b, down_w, ob, norms) = finish(
        lay, *summed
    )
    return (
        output, input_grad, fg, fb, sg, sb, qkv_w, qkv_b, dense_w, up_w, up_b,
        down_w.reshape(4 * r, D), ob, norms,
    )


def solution(mesh):
    lay = Layout(mesh.shape["dp"], mesh.shape["fsdp"])
    both = P(("dp", "fsdp"))
    split = P("fsdp")
    in_specs = (both, both, both) + (split,) * 11
    out_specs = (both, both) + (split,) * 11 + (P(),)
    return jax.shard_map(
        functools.partial(per_device, lay), mesh=mesh, in_specs=in_specs, out_specs=out_specs,
        check_vma=False,
    )
```

```python
import functools
import math

import jax
import jax.numpy as jnp
from jax import lax
from jax.experimental import pallas as pl
from jax.experimental.pallas import tpu as pltpu
from jax.sharding import PartitionSpec as P

D = 768
H = 12
HD = 64
FF = 3072
ROT = 16
ROW = 2048
DOC_DEV = 2
LANES = 128
PAIRS = D // LANES
MESH = pl.DeviceIdType.MESH
VMEM_LIMIT = 60 * 1024 * 1024


class Layout:
    def __init__(self, dp, fsdp):
        self.dp, self.fsdp = dp, fsdp
        self.nc = 2
        self.nx = dp // 2
        ny = 1
        while (2 * ny) * (2 * ny) <= fsdp:
            ny *= 2
        self.ny, self.nz = ny, fsdp // ny
        self.sub = max(1, self.nx // 2)
        self.unit = 4 // self.nx
        self.down_unit = 2 // self.sub

    def coords(self):
        d, f = lax.axis_index("dp"), lax.axis_index("fsdp")
        return d // 2, d % 2, f // self.ny, f % self.ny

    def device(self, x, c, z, y):
        return {"dp": x * 2 + c, "fsdp": z * self.ny + y}


def wrap(value, size):
    return lax.rem(value + size, size)


CHUNKS = tuple((g, i) for g in range(3) for i in range(3))
ALL = slice(None)


def grad_shape(lay, group, r):
    return (lay.nz, lay.ny, r, 4 * D) if group < 2 else (lay.nz, lay.ny, 4, r, D)


def span_of(lay, group, i, c, x):
    if group < 2:
        width = 512 // lay.nx
        if x is ALL:
            return pl.ds(pl.multiple_of(1024 * i + 512 * c, LANES), 512), None
        return pl.ds(pl.multiple_of(1024 * i + 512 * c + width * x, LANES), width), None
    width = 256 // lay.sub
    if x is ALL:
        return pl.ds(256 * i, 256), pl.ds(2 * c, 2)
    start = 256 * i + width * lax.rem(x, lay.sub)
    return pl.ds(pl.multiple_of(start, LANES), width), 2 * c + x // lay.sub


def view(lay, ref, group, i, c, x, z, y):
    cols, quarter = span_of(lay, group, i, c, x)
    if group < 2:
        return ref.at[z, y, :, cols]
    return ref.at[z, y, quarter, :, cols]


def shard_view(lay, ref, group, i, c, x):
    cols, quarter = span_of(lay, group, i, c, x)
    if group < 2:
        return ref.at[:, cols]
    return ref.at[quarter, :, cols]


def part_shape(lay, group, x_all, z_all, y_all, r):
    lead = ((lay.nz,) if z_all else ()) + ((lay.ny,) if y_all else ())
    if group < 2:
        return lead + (r, 512 if x_all else 512 // lay.nx)
    return lead + ((2, r, 256) if x_all else (r, 256 // lay.sub))


def barrier_with(peers):
    sem = pltpu.get_barrier_semaphore()
    for peer in peers:
        pl.semaphore_signal(sem, inc=1, device_id=peer, device_id_type=MESH)
    pl.semaphore_wait(sem, len(peers))


def line_peers(lay):
    x, c, z, y = lay.coords()
    xs = [lay.device(wrap(x + k, lay.nx), c, z, y) for k in range(1, lay.nx)]
    ys = [lay.device(x, c, z, wrap(y + k, lay.ny)) for k in range(1, lay.ny)]
    zs = [lay.device(x, c, wrap(z + k, lay.nz), y) for k in range(1, lay.nz)]
    cs = [lay.device(x, 1 - c, z, y)]
    return xs, cs, zs, ys


def remote(src, dst, ssem, rsem, device):
    return pltpu.make_async_remote_copy(
        src_ref=src, dst_ref=dst, send_sem=ssem, recv_sem=rsem, device_id=device, device_id_type=MESH
    )


def start(copies):
    for copy in copies:
        copy.start()


def arrive(copies):
    for copy in copies:
        copy.wait_recv()


def sent(copies):
    for copy in copies:
        copy.wait_send()


def hbm(count):
    return [pl.BlockSpec(memory_space=pltpu.HBM)] * count


def dma(*shape):
    return pltpu.SemaphoreType.DMA(shape)


NT = (((1,), (1,)), ((), ()))
NN = (((1,), (0,)), ((), ()))
TN = (((0,), (0,)), ((), ()))
F32 = jnp.float32
BF = jnp.bfloat16


def mm(a, b, dims=NN):
    return lax.dot_general(a, b, dims, preferred_element_type=F32)


def norm_parts(values):
    middle = jnp.mean(values, -1, keepdims=True)
    centred = values - middle
    factor = lax.rsqrt(jnp.mean(centred * centred, -1, keepdims=True) + 1e-05)
    return centred * factor, factor


def small_plan(r):
    plan, at = [], 0
    for size, within in [(r, LANES)] * 5 + [(3 * r, HD), (4 * r, LANES)]:
        plan.append((at, size, math.gcd(size, within)))
        at += -(-size // LANES)
    return plan


SMALL_ROWS = 16


class Gather:
    def __init__(self, lay, us, gs, sems):
        (z_s, z_r, y_s, y_r, x_s, x_r, c_s, c_r) = sems
        x, c, z, y = lay.coords()
        xs, cs, zs, ys = line_peers(lay)
        self.stages = []
        for t, (g, i) in enumerate(CHUNKS):
            by_y, by_x = (ys, y_s, y_r), (xs, x_s, x_r)
            first, second = (by_y, by_x) if i < 2 else (by_x, by_y)
            middle = (x, ALL, ALL) if i < 2 else (ALL, ALL, y)
            steps = [
                ((zs, z_s, z_r), (x, z, y)),
                (first, (x, ALL, y)),
                (second, middle),
            ]
            stages = []
            for (peers, ss, rs), (px, pz, py) in steps:
                piece = view(lay, gs[g], g, i, c, px, pz, py)
                source = shard_view(lay, us[g], g, i, c, x) if len(stages) == 0 else piece
                stages.append(
                    [remote(source, piece, ss.at[t, k], rs.at[t, k], p) for k, p in enumerate(peers)]
                )
            piece = view(lay, gs[g], g, i, c, ALL, ALL, ALL)
            stages.append([remote(piece, piece, c_s.at[t], c_r.at[t], cs[0])])
            self.stages.append(stages)

    def issue(self, t, stage):
        start(self.stages[t][stage])

    def pass_on(self, t, stage):
        arrive(self.stages[t][stage - 1])
        start(self.stages[t][stage])

    def done(self, t):
        arrive(self.stages[t][3])

    def drain(self):
        for stages in self.stages:
            for copies in stages:
                sent(copies)


class Reduce:
    def __init__(self, lay, ps, fs, bufs, sems, wanted):
        (ca, ra1, rb1, ra2, rb2, ra3) = bufs
        (c_s, c_r, x_s, x_r, y_s, y_r, z_s, z_r, fx_s, fx_r, fc_s, fc_r) = sems
        x, c, z, y = lay.coords()
        xs, cs, zs, ys = line_peers(lay)
        other_x = [wrap(x + 1 + k, lay.nx) for k in range(lay.nx - 1)]
        other_y = [wrap(y + 1 + k, lay.ny) for k in range(lay.ny - 1)]
        other_z = [wrap(z + 1 + k, lay.nz) for k in range(lay.nz - 1)]
        self.copies, self.adds = {}, {}
        for t, stages in wanted.items():
            g, i = CHUNKS[t]
            p = ps[g]

            def along(pieces, slot, peers, ss, rs, t=t):
                return [
                    remote(piece, slot.at[k], ss.at[t, k], rs.at[t, k], peers[k])
                    for k, piece in enumerate(pieces)
                ]

            def into(dst, slot, count):
                return functools.partial(add_into, dst, [slot.at[k] for k in range(count)])

            def part(px, pz, py, p=p, g=g, i=i, core=c):
                return view(lay, p, g, i, core, px, pz, py)

            if 0 in stages:
                slot = ca[g].at[i]
                self.copies[t, 0] = [remote(part(ALL, ALL, ALL, core=1 - c), slot, c_s.at[t], c_r.at[t], cs[0])]
                self.adds[t, 1] = functools.partial(add_into, part(ALL, ALL, ALL), [slot])
            if 1 in stages and i < 2:
                slot = ra1[g].at[i]
                self.copies[t, 1] = along([part(k, ALL, ALL) for k in other_x], slot, xs, x_s, x_r)
                self.adds[t, 2] = into(part(x, ALL, ALL), slot, lay.nx - 1)
            elif 1 in stages:
                slot = rb1[g].at[0]
                self.copies[t, 1] = along([part(ALL, ALL, k) for k in other_y], slot, ys, y_s, y_r)
                self.adds[t, 2] = into(part(ALL, ALL, y), slot, lay.ny - 1)
            if 2 in stages and i < 2:
                slot = ra2[g].at[i]
                self.copies[t, 2] = along([part(x, ALL, k) for k in other_y], slot, ys, y_s, y_r)
                self.adds[t, 3] = into(part(x, ALL, y), slot, lay.ny - 1)
            elif 2 in stages:
                slot = rb2[g].at[0]
                self.copies[t, 2] = along([part(k, ALL, y) for k in other_x], slot, xs, x_s, x_r)
                self.adds[t, 3] = into(part(x, ALL, y), slot, lay.nx - 1)
            if 3 in stages:
                slot = ra3[g].at[i]
                self.copies[t, 3] = along([part(x, k, y) for k in other_z], slot, zs, z_s, z_r)
                out = shard_view(lay, fs[g], g, i, c, x)
                self.adds[t, 4] = functools.partial(
                    set_sum, out, [part(x, z, y)] + [slot.at[k] for k in range(lay.nz - 1)]
                )
                self.copies[t, 4] = [
                    remote(out, out, fx_s.at[t, k], fx_r.at[t, k], peer) for k, peer in enumerate(xs)
                ]
                both = shard_view(lay, fs[g], g, i, c, ALL)
                self.copies[t, 5] = [remote(both, both, fc_s.at[t], fc_r.at[t], cs[0])]

    def settle(self, t, k):
        if k > 0:
            arrive(self.copies[t, k - 1])
            if (t, k) in self.adds:
                self.adds[t, k]()

    def begin(self, t, k):
        start(self.copies[t, k])

    def step(self, t, k):
        self.settle(t, k)
        if k < 6:
            self.begin(t, k)

    def drain(self):
        for group in self.copies.values():
            sent(group)


def set_sum(out, srcs):
    total = srcs[0][...].astype(F32)
    for src in srcs[1:]:
        total = total + src[...].astype(F32)
    out[...] = total.astype(BF)


def add_into(dst, srcs):
    lead = dst.shape[:-2]

    def body(j, carry):
        index = []
        rest = j
        for size in reversed(lead):
            index.append(lax.rem(rest, size))
            rest = rest // size
        index = tuple(reversed(index))
        total = dst[index].astype(F32)
        for src in srcs:
            total = total + src[index].astype(F32)
        dst[index] = total.astype(BF)
        return carry

    lax.fori_loop(0, math.prod(lead), body, 0)


def rope(u, cos, low, high):
    return u * cos + pltpu.roll(u, LANES - 8, 1) * low + pltpu.roll(u, 8, 1) * high


def front_kernel(
    lay, rows,
    u_up, u_down, qkv, dense, tok, grad, seg, v0, v1, v2, v3, v4, v5, v6,
    g_up, g_down, p_out, prev_out, own_out, attn_hbm, vectors, up_add, att_sums,
    small, u_att, p_att, fg_prev, fg_own, attn_out, g_att, g_small, tok_halo, seg_halo, first_all, q_s, k_s, v_s, do_s, ctx_s, ctx_t,
    dq_s, dk_s, dv_s, cos_s, low_s, high_s, bias, dk_acc, dv_acc, qkv_add, s_s, w_s, d_s,
    local_sem, z_s, z_r, y_s, y_r, x_s, x_r, c_s, c_r, sm_s, sm_r, h_s, h_r, out_sem,
    ca, ra1, rb1, rc_s, rc_r, rx_s, rx_r, ry_s, ry_r,
):
    span = 3 * rows
    r = qkv.shape[0]
    n_chunks = len(CHUNKS)
    x, c, z, y = lay.coords()
    xs, cs, zs, ys = line_peers(lay)
    total = lay.dp * lay.fsdp
    plan = small_plan(r)
    for (row, size, _), ref in zip(plan, (v0, v1, v2, v3, v4, v5, v6)):
        value = ref[...].astype(F32).reshape(1, size)
        for k in range(-(-size // LANES)):
            width = min(LANES, size - k * LANES)
            small[row + k : row + k + 1, :width] = value[:, k * LANES : k * LANES + width]
    left = lax.broadcasted_iota(jnp.int32, (r, LANES), 1) < HD
    for p in range(PAIRS):
        parts = [qkv[:, (3 * p + k) * LANES : (3 * p + k + 1) * LANES].astype(F32) for k in range(3)]
        kinds = (
            jnp.where(left, parts[0], parts[1]),
            pltpu.roll(jnp.where(left, parts[2], parts[0]), HD, 1),
            jnp.where(left, parts[1], parts[2]),
        )
        for k, part in enumerate(kinds):
            u_att[:, k * D + p * LANES : k * D + (p + 1) * LANES] = part.astype(BF)
    u_att[:, 3 * D :] = dense[...]
    b = lax.axis_index("dp") * lay.fsdp + lax.axis_index("fsdp")

    def stream(k):
        t = wrap(b + k, total)
        return {"dp": t // lay.fsdp, "fsdp": lax.rem(t, lay.fsdp)}

    around = [stream(2), stream(-2), stream(1), stream(-1)]
    gs = (g_att, g_up, g_down)
    us = (u_att, u_up, u_down)
    locals_ = []
    for t, (g, i) in enumerate(CHUNKS):
        locals_.append(
            pltpu.make_async_copy(
                shard_view(lay, us[g], g, i, c, x), view(lay, gs[g], g, i, c, x, z, y), local_sem.at[t]
            )
        )
    locals_.append(pltpu.make_async_copy(small, g_small.at[z, y], local_sem.at[n_chunks]))
    start(locals_)
    barrier_with(xs + cs + zs + ys + around)
    even = lax.rem(b, 2) == 0
    half = rows // 2
    halo, own, passed = [], [], []
    for k in range(2):
        part = pl.ds(k * half, half)
        halo.append(remote(tok.at[part], tok_halo.at[0, part], h_s.at[k], h_r.at[k], around[0]))
        own.append(remote(tok.at[part], tok_halo.at[1, part], h_s.at[2 + k], h_r.at[2 + k], around[2]))
        passed.append(
            remote(tok_halo.at[0, part], tok_halo.at[1, part], h_s.at[2 + k], h_r.at[2 + k], around[3])
        )
    segs = [
        remote(seg, seg_halo.at[0], h_s.at[4], h_r.at[4], around[0]),
        remote(seg, seg_halo.at[1], h_s.at[5], h_r.at[5], around[2]),
    ]
    small_z = [
        remote(small, g_small.at[z, y], sm_s.at[k], sm_r.at[k], p) for k, p in enumerate(zs)
    ]
    small_y = [
        remote(g_small.at[:, y], g_small.at[:, y], sm_s.at[lay.nz + k], sm_r.at[lay.nz + k], p)
        for k, p in enumerate(ys)
    ]
    net = Gather(lay, us, gs, (z_s, z_r, y_s, y_r, x_s, x_r, c_s, c_r))
    net.issue(0, 0)
    net.issue(2, 0)
    start(small_z)
    start(segs)
    net.issue(1, 0)

    def tables(k, carry):
        at = pl.ds(pl.multiple_of(k * 256, 256), 256)
        lane = lax.broadcasted_iota(jnp.int32, (256, LANES), 1) % HD
        row = lax.broadcasted_iota(jnp.int32, (256, LANES), 0) + k * 256
        place = lax.rem((b - 2) * rows + row + 4 * ROW, ROW).astype(F32)
        rate = jnp.exp((lane % 8).astype(F32) * (-math.log(10000.0) / 8.0))
        angle = place * rate
        sine = jnp.sin(angle)
        cos_s[at, :] = jnp.where(lane < ROT, jnp.cos(angle), 1.0)
        low_s[at, :] = jnp.where(lane < 8, -sine, 0.0)
        high_s[at, :] = jnp.where((lane >= 8) & (lane < ROT), sine, 0.0)
        return carry

    lax.fori_loop(0, 2, tables, 0)
    for t in (0, 2, 1, n_chunks):
        locals_[t].wait()
    net.pass_on(0, 1)
    lax.fori_loop(2, 3, tables, 0)
    net.pass_on(2, 1)
    lax.fori_loop(3, 5, tables, 0)
    arrive(small_z)
    start(small_y)
    net.pass_on(0, 2)
    net.pass_on(1, 1)
    halo[0].start()
    lax.fori_loop(5, span // 256, tables, 0)
    arrive(small_y)
    net.pass_on(2, 2)

    lane_row = lax.broadcasted_iota(jnp.int32, (1, LANES), 1)

    def line(first_row, size, unit, length, source):
        out = []
        for block in range(length // LANES):
            value = None
            for k in range(LANES // unit):
                owner, local = divmod(source(block * (LANES // unit) + k), size // unit)
                row, lane = divmod(local * unit, LANES)
                row += first_row
                piece = g_small[owner // lay.ny, owner % lay.ny, row : row + 1, :]
                if lane != k * unit:
                    piece = pltpu.roll(piece, (k * unit - lane) % LANES, 1)
                value = piece if value is None else jnp.where(lane_row // unit == k, piece, value)
            out.append(value)
        return jnp.concatenate(out, 1)

    def norm_rows(values):
        return norm_parts(values.astype(F32))[0]

    for j in range(5):
        vectors[j : j + 1, :] = line(*plan[j], D, lambda n: n)
    vectors[5:8, :] = jnp.zeros((3, D), F32)
    unit = plan[5][2]
    a_head = HD // unit

    def natural(n):
        kind, rest = divmod(n, D // unit)
        head, part = divmod(rest, a_head)
        return head * 3 * a_head + kind * a_head + part

    qkv_add[...] = line(*plan[5], 3 * D, natural)
    net.pass_on(1, 2)
    up_add[...] = line(*plan[6], FF, lambda n: n)

    def pass_halo(k):
        arrive([halo[k]])

        @pl.when(even)
        def _():
            own[k].start()

        @pl.when(jnp.logical_not(even))
        def _():
            passed[k].start()

    halo[1].start()
    gain, shift = vectors[0:1, :], vectors[1:2, :]
    own_rows = pl.ds(2 * rows, rows)
    first = (norm_rows(tok[...]) * gain + shift).astype(BF)
    first_all[own_rows, :] = first
    pass_halo(0)
    arrive(segs)
    least = jnp.maximum(0, 2 * rows - b * rows)
    keys_doc = jnp.concatenate([seg_halo[0], seg_halo[1], seg[...]], 1).astype(F32)
    keys_doc = jnp.broadcast_to(keys_doc, (LANES, span)).T
    query_doc = seg[0:1, :].astype(F32)

    for k in range(6):
        at = slice(k * 256, (k + 1) * 256)
        key_at = lax.broadcasted_iota(jnp.int32, (256, rows), 0) + k * 256
        query_at = lax.broadcasted_iota(jnp.int32, (256, rows), 1) + 2 * rows
        allowed = (keys_doc[at, 0:1] == query_doc) & (key_at <= query_at) & (key_at >= least)
        bias[at, :] = jnp.where(allowed, 0.0, -1e30)
    for t in range(3, n_chunks):
        locals_[t].wait()
    net.issue(5, 0)
    net.pass_on(0, 3)
    net.pass_on(2, 3)
    net.issue(3, 0)

    def weight(first_col, width):
        value = g_att[:, :, :, pl.ds(first_col, width)]
        return value.reshape(D, width)

    scale = 1.0 / math.sqrt(HD)

    def project(kind, j, at, out, factor):
        col = pl.multiple_of(kind * D + 256 * j, 256)
        value = mm(first_all[at, :], weight(col, 256)) + qkv_add[:, pl.ds(col, 256)]
        for k in range(2):
            u = value[:, k * LANES : (k + 1) * LANES]
            if kind < 2:
                u = rope(u, cos_s[at, :], low_s[at, :], high_s[at, :])
            if factor is not None:
                u = u * factor
            out[:, pl.ds(pl.multiple_of(256 * j + LANES * k, LANES), LANES)] = u.astype(BF)

    def own_queries(j, carry):
        project(0, j, own_rows, q_s, scale)
        return carry

    def own_keys(j, carry):
        project(1, j, own_rows, k_s.at[own_rows], None)
        return carry

    def own_values(j, carry):
        project(2, j, own_rows, v_s.at[own_rows], None)
        return carry

    net.done(0)
    lax.fori_loop(0, 3, own_queries, 0)
    lax.fori_loop(0, 1, own_keys, 0)
    pass_halo(1)
    net.pass_on(1, 3)
    net.issue(4, 0)
    net.done(2)
    do_s[...] = mm(grad[...], weight(3 * D, D), NT).astype(BF)
    lax.fori_loop(2, 3, own_values, 0)
    net.pass_on(5, 1)
    net.done(1)
    lax.fori_loop(1, 3, own_keys, 0)
    lax.fori_loop(0, 2, own_values, 0)
    own[0].wait_recv()
    net.pass_on(3, 1)

    def earlier_norms(k):
        for n in range(2):
            near = pl.ds(k * half, half)
            before = norm_rows(tok_halo[n, near, :]) * gain + shift
            first_all[pl.ds(n * rows + k * half, half), :] = before.astype(BF)

    earlier_norms(0)
    net.issue(8, 0)
    own[1].wait_recv()
    earlier_norms(1)
    net.pass_on(4, 1)
    net.pass_on(5, 2)

    def earlier_projections(j, carry):
        for k in range(2):
            at = pl.ds(k * rows, rows)
            project(1, j, at, k_s.at[at], None)
            project(2, j, at, v_s.at[at], None)
        return carry

    lax.fori_loop(0, 3, earlier_projections, 0)
    net.pass_on(3, 2)
    net.issue(6, 0)

    go, send, end = net.pass_on, net.issue, net.done
    later = [
        [(go, 8, 1), (send, 7, 0), (go, 4, 2)],
        [(go, 5, 3)],
        [(go, 6, 1)],
        [(go, 3, 3), (go, 7, 1)],
        [(go, 8, 2), (go, 6, 2)],
        [(go, 4, 3), (go, 7, 2)],
        [],
        [(go, 8, 3)],
        [],
        [(go, 6, 3)],
        [(go, 7, 3)],
        [],
    ]
    tile = 256

    def pair(p, carry):
        lanes = pl.ds(pl.multiple_of(p * LANES, LANES), LANES)
        v_t, k_t = v_s[:, lanes].T, k_s[:, lanes].T
        do_t = do_s[:, lanes].astype(F32).T
        lane = lax.broadcasted_iota(jnp.int32, (tile, LANES), 1)
        zero = jnp.zeros((), BF)
        for t in range(rows // tile):
            cols = slice(t * tile, (t + 1) * tile)
            kl = 2 * rows + (t + 1) * tile
            pieces = [slice(k * tile, (k + 1) * tile) for k in range(kl // tile)]
            qms = [jnp.where((lane // HD) == hh, q_s[cols, lanes], zero) for hh in range(2)]
            doms = [jnp.where((lane // HD) == hh, do_s[cols, lanes], zero) for hh in range(2)]
            tops, norms = [], []
            for hh in range(2):
                top = None
                for at in pieces:
                    st = mm(k_s[at, lanes], qms[hh], NT) + bias[at, cols]
                    s_s[hh, at, :] = st
                    most = jnp.max(st, 0, keepdims=True)
                    top = most if top is None else jnp.maximum(top, most)
                tops.append(top)
            for hh in range(2):
                total_e = None
                for at in pieces:
                    e = jnp.exp(s_s[hh, at, :] - tops[hh])
                    s_s[hh, at, :] = e
                    part = jnp.sum(e, 0, keepdims=True)
                    total_e = part if total_e is None else total_e + part
                norms.append(1.0 / total_e)
            outs, dqs = [], []
            for hh in range(2):
                for at in pieces:
                    w_s[hh, at, :] = (s_s[hh, at, :] * norms[hh]).astype(BF)
            for hh in range(2):
                part = slice(hh * HD, (hh + 1) * HD)
                o_t = mm(v_t[part, :kl], w_s[hh, :kl, :])
                delta = jnp.sum(o_t * do_t[part, cols], 0, keepdims=True)
                outs.append(o_t)
                for at in pieces:
                    dp = mm(v_s[at, lanes], doms[hh], NT)
                    d_s[hh, at, :] = ((s_s[hh, at, :] * norms[hh]) * (dp - delta)).astype(BF)
                dqs.append(mm(k_t[part, :kl], d_s[hh, :kl, :]))
            for k, at in enumerate(pieces):
                dk = mm(d_s[0, at, :], qms[0]) + mm(d_s[1, at, :], qms[1])
                dv = mm(w_s[0, at, :], doms[0]) + mm(w_s[1, at, :], doms[1])
                if t == 0 or k == len(pieces) - 1:
                    dk_acc[at, :] = dk
                    dv_acc[at, :] = dv
                else:
                    dk_acc[at, :] += dk
                    dv_acc[at, :] += dv
            o_pair = jnp.concatenate(outs, 0)
            ctx_t[lanes, cols] = o_pair.astype(BF)
            ctx_s[cols, lanes] = o_pair.T.astype(BF)
            dq = jnp.concatenate(dqs, 0).T * scale
            at = slice(2 * rows + t * tile, 2 * rows + (t + 1) * tile)
            dq_s[cols, lanes] = rope(dq, cos_s[at, :], -low_s[at, :], -high_s[at, :]).astype(BF)
            for k in range(PAIRS):

                @pl.when(p == k)
                def _(k=k, t=t):
                    for event, *where in later[2 * k + t]:
                        event(*where)

        dk_s[:, lanes] = rope(dk_acc[...], cos_s[...], -low_s[...], -high_s[...]).astype(BF)
        dv_s[:, lanes] = dv_acc[...].astype(BF)
        return carry

    lax.fori_loop(0, PAIRS, pair, 0)

    sums = Reduce(
        lay, (p_att,), None, ((ca,), (ra1,), (rb1,), None, None, None),
        (rc_s, rc_r, rx_s, rx_r, ry_s, ry_r) + (None,) * 6, {0: (0, 1), 1: (0,), 2: (0, 1)},
    )
    outs = []

    def leave(i):
        cols = pl.ds(1024 * i, 1024)
        copy = pltpu.make_async_copy(p_att.at[:, :, :, cols], p_out.at[:, :, :, cols], out_sem.at[i])
        copy.start()
        outs.append(copy)

    def put(kind, j, value):
        p_att[:, :, :, kind * D + 256 * j : kind * D + 256 * (j + 1)] = value.astype(BF).reshape(
            lay.nz, lay.ny, r, 256
        )

    def tile_of(ref, j):
        return ref[:, slice(256 * j, 256 * (j + 1))]

    def weight_grad(kind, j):
        if kind == 0:
            put(0, j, mm(first_all[own_rows, :], tile_of(dq_s, j), TN))
        elif kind == 3:
            put(3, j, mm(ctx_t[...], tile_of(grad, j)))
        else:
            put(kind, j, mm(first_all[...], tile_of((dk_s, dv_s)[kind - 1], j), TN))

    for kind, j in ((1, 0), (0, 0), (0, 1), (0, 2)):
        weight_grad(kind, j)
    sums.step(0, 0)
    for kind, j in ((2, 2), (3, 0), (3, 1), (3, 2)):
        weight_grad(kind, j)
    sums.step(0, 1)
    sums.step(2, 0)
    for kind, j in ((1, 1), (1, 2)):
        weight_grad(kind, j)
    sums.step(2, 1)
    for kind, j in ((2, 0), (2, 1)):
        weight_grad(kind, j)
    sums.step(1, 0)

    def earlier_grad(k, carry):
        at = pl.ds(pl.multiple_of(k * 256, 256), 256)
        value = mm(dk_s[at, :], weight(D, D), NT) + mm(dv_s[at, :], weight(2 * D, D), NT)
        fg_prev[at, :] = value.astype(BF)
        return carry

    lax.fori_loop(0, 2 * rows // 256, earlier_grad, 0)
    outs.append(pltpu.make_async_copy(fg_prev, prev_out, out_sem.at[3]))
    outs[-1].start()
    sums.settle(1, 1)
    leave(1)
    for k in range(rows // 256):
        at = slice(2 * rows + 256 * k, 2 * rows + 256 * (k + 1))
        near = slice(256 * k, 256 * (k + 1))
        fg_own[near, :] = (
            mm(dk_s[at, :], weight(D, D), NT)
            + mm(dv_s[at, :], weight(2 * D, D), NT)
            + mm(dq_s[near, :], weight(0, D), NT)
        )
    outs.append(pltpu.make_async_copy(fg_own, own_out, out_sem.at[4]))
    outs[-1].start()

    def attention_out(j, carry):
        col = pl.multiple_of(256 * j, 256)
        attn_out[:, pl.ds(col, 256)] = mm(ctx_s[...], weight(pl.multiple_of(3 * D + col, 256), 256))
        return carry

    lax.fori_loop(0, 3, attention_out, 0)
    outs.append(pltpu.make_async_copy(attn_out, attn_hbm, out_sem.at[5]))
    outs[-1].start()
    for k, ref in enumerate((dq_s, dk_s, dv_s)):
        att_sums[k : k + 1, :] = jnp.sum(ref[...].astype(F32), 0, keepdims=True)
    att_sums[3:8, :] = jnp.zeros((5, D), F32)
    sums.settle(0, 2)
    leave(0)
    sums.settle(2, 2)
    leave(2)
    sums.drain()
    for t in range(3, 9):
        net.done(t)
    net.drain()
    sent(small_z + small_y + segs + halo + own)
    for copy in outs:
        copy.wait()


def front(lay, u_up, u_down, qkv, dense, tok, grad, seg, vectors):
    rows = tok.shape[0]
    span = 3 * rows
    r = qkv.shape[0]
    n = len(CHUNKS)
    outs = (
        jax.ShapeDtypeStruct(grad_shape(lay, 1, r), BF),
        jax.ShapeDtypeStruct(grad_shape(lay, 2, r), BF),
        jax.ShapeDtypeStruct(grad_shape(lay, 0, r), BF),
        jax.ShapeDtypeStruct((2 * rows, D), BF),
        jax.ShapeDtypeStruct((rows, D), F32),
        jax.ShapeDtypeStruct((rows, D), F32),
        jax.ShapeDtypeStruct((8, D), F32),
        jax.ShapeDtypeStruct((1, FF), F32),
        jax.ShapeDtypeStruct((8, D), F32),
    )
    vmem = pl.BlockSpec(memory_space=pltpu.VMEM)
    lx, ly, lz = max(1, lay.nx - 1), max(1, lay.ny - 1), max(1, lay.nz - 1)

    def v(shape, dtype=BF):
        return pltpu.VMEM(shape, dtype)

    return pl.pallas_call(
        functools.partial(front_kernel, lay, rows),
        name="front",
        out_shape=outs,
        in_specs=hbm(2) + [vmem] * (5 + len(vectors)),
        out_specs=tuple(hbm(6)) + (vmem,) * 3,
        scratch_shapes=[
            v((SMALL_ROWS, LANES), F32), v((r, 4 * D)), v(grad_shape(lay, 0, r)), v((2 * rows, D)), v((rows, D), F32), v((rows, D), F32),
            v(grad_shape(lay, 0, r)), v((lay.nz, lay.ny, SMALL_ROWS, LANES), F32), v((2, rows, D)),
            v((2, 1, rows), jnp.int32), v((span, D)), v((rows, D)), v((span, D)),
            v((span, D)), v((rows, D)), v((rows, D)), v((D, rows)), v((rows, D)), v((span, D)),
            v((span, D)), v((span, LANES), F32), v((span, LANES), F32), v((span, LANES), F32),
            v((span, rows), F32), v((span, LANES), F32), v((span, LANES), F32), v((1, 3 * D), F32),
            v((2, span, 256), F32), v((2, span, 256)), v((2, span, 256)),
            dma(n + 1), dma(n, lz), dma(n, lz), dma(n, ly), dma(n, ly), dma(n, lx), dma(n, lx),
            dma(n), dma(n), dma(lay.nz + ly), dma(lay.nz + ly), dma(6), dma(6), dma(6),
            v((3,) + part_shape(lay, 0, True, True, True, r)),
            v((1, lx) + part_shape(lay, 0, False, True, True, r)),
            v((1, ly) + part_shape(lay, 0, True, True, False, r)),
            dma(3), dma(3), dma(3, lx), dma(3, lx), dma(3, ly), dma(3, ly),
        ],
        compiler_params=pltpu.CompilerParams(
            collective_id=0, has_side_effects=True, vmem_limit_bytes=VMEM_LIMIT
        ),
    )(u_up, u_down, qkv, dense, tok, grad, seg, *vectors)


def norm_back(grad, gain, normed, factor):
    inner = grad * gain
    return factor * (
        inner
        - jnp.mean(inner, -1, keepdims=True)
        - normed * jnp.mean(inner * normed, -1, keepdims=True)
    )


FF_CHUNKS = FF // D


def back_kernel(
    lay, rows, docs,
    g_up, g_down, p_in, prev_in, own_in, attn_in, vectors, up_add, att_sums, tok, grad, seg,
    output, input_grad, f_att, f_up, f_down, vec_out,
    p_att, fg_prev, fg_own, attn_out, p_up, p_down, w_up, w_down, second_in, second_t, act_s, pg_s, sg_acc, hop, home,
    ca, ra1, rb1, ra2, rb2, ra3, v_c, v_x, v_y, v_z, *sems,
):
    (c_s, c_r, x_s, x_r, y_s, y_r, z_s, z_r, fx_s, fx_r, fc_s, fc_r, v_s, v_r, w_sem, h_s, h_r, in_sem) = sems
    r = p_in.shape[2]
    x, c, z, y = lay.coords()
    xs, cs, zs, ys = line_peers(lay)
    total = lay.dp * lay.fsdp
    b = lax.axis_index("dp") * lay.fsdp + lax.axis_index("fsdp")

    def stream(k):
        t = wrap(b + k, total)
        return {"dp": t // lay.fsdp, "fsdp": lax.rem(t, lay.fsdp)}

    around = [stream(2), stream(-2), stream(1), stream(-1)]
    near_z = lay.nz // FF_CHUNKS
    loads = []
    for k in range(FF_CHUNKS):
        slot = k % 2
        loads.append(
            (
                pltpu.make_async_copy(
                    g_up.at[:, :, :, pl.ds(D * k, D)], w_up.at[slot], w_sem.at[0, k]
                ),
                pltpu.make_async_copy(
                    g_down.at[pl.ds(near_z * k, near_z)], w_down.at[slot], w_sem.at[1, k]
                ),
            )
        )
    taken = [
        pltpu.make_async_copy(
            p_in.at[:, :, :, pl.ds(1024 * i, 1024)], p_att.at[:, :, :, pl.ds(1024 * i, 1024)],
            in_sem.at[i],
        )
        for i in range(3)
    ]
    taken.append(pltpu.make_async_copy(prev_in, fg_prev, in_sem.at[3]))
    taken.append(pltpu.make_async_copy(attn_in, attn_out, in_sem.at[4]))
    taken.append(pltpu.make_async_copy(own_in, fg_own, in_sem.at[5]))
    start(taken[:4])
    start(loads[0])
    start(taken[4:])
    start(loads[1])
    barrier_with(xs + cs + zs + ys + around)
    wanted = {t: (0, 1, 2, 3) for t in range(3, len(CHUNKS))}
    wanted.update({0: (2, 3), 1: (1, 2, 3), 2: (2, 3)})
    net = Reduce(
        lay, (p_att, p_up, p_down), (f_att, f_up, f_down),
        ((None,) + tuple(ca), ra1, (None,) + tuple(rb1), ra2, rb2, ra3), sems[:12], wanted,
    )
    for t, k in ((1, 1), (2, 2), (0, 2)):
        taken[t].wait()
        net.begin(t, k)
    taken[3].wait()
    even = lax.rem(b, 2) == 0
    quarter = rows // 4
    to_next, to_last, to_owner = [], [], []
    for k in range(4):
        near = fg_prev.at[pl.ds(rows + k * quarter, quarter)]
        far = fg_prev.at[pl.ds(k * quarter, quarter)]
        part = pl.ds(k * quarter, quarter)
        to_next.append(remote(near, hop.at[part], h_s.at[k], h_r.at[k], around[2]))
        to_last.append(remote(near, hop.at[part], h_s.at[k], h_r.at[k], around[3]))
        to_owner.append(remote(far, home.at[part], h_s.at[4 + k], h_r.at[4 + k], around[1]))

    def hop_halo(k):
        @pl.when(even)
        def _():
            to_next[k].start()

        @pl.when(jnp.logical_not(even))
        def _():
            to_last[k].start()

    def forward_halo(k):
        to_last[k].wait_recv()
        at = pl.ds(k * quarter, quarter)

        @pl.when(jnp.logical_not(even))
        def _():
            fg_prev[at, :] = (fg_prev[at, :].astype(F32) + hop[at, :].astype(F32)).astype(BF)

        to_owner[k].start()

    hop_halo(0)
    hop_halo(1)

    gain_first, gain_second = vectors[0:1, :], vectors[2:3, :]
    normed, factor = norm_parts(tok[...].astype(F32))
    value = (normed * gain_second + vectors[3:4, :]).astype(BF)
    second_in[...] = value
    second_t[...] = value.T
    cot = grad[...].astype(F32)
    taken[4].wait()
    taken[5].wait()
    output_base = attn_out
    output_base[...] = attn_out[...] + tok[...].astype(F32) + vectors[4:5, :]
    sg_acc[...] = jnp.zeros_like(sg_acc)
    mine = v_c.at[c]
    mine[...] = jnp.zeros((16, D), F32)

    step = net.step
    events = [
        [],
        [(step, 0, 3)],
        [(hop_halo, 2)],
        [(step, 3, 0), (step, 1, 2), (forward_halo, 0)],
        [(step, 3, 1), (step, 2, 3), (hop_halo, 3)],
        [(step, 4, 0), (forward_halo, 1)],
        [(step, 4, 1), (step, 0, 4)],
        [(step, 5, 0), (step, 6, 0), (step, 7, 0), (step, 8, 0), (step, 2, 4)],
    ]
    root = math.sqrt(0.5)
    level = 1.0 / math.sqrt(2.0 * math.pi)

    def chunk(k, squares):
        slot = lax.rem(k, 2)
        for n in range(FF_CHUNKS):

            @pl.when(k == n)
            def _(n=n):
                loads[n][0].wait()
                loads[n][1].wait()

        down = w_down[slot].reshape(D, D)
        for j in range(3):
            tile = slice(256 * j, 256 * (j + 1))
            col = pl.ds(pl.multiple_of(D * k + 256 * j, 256), 256)
            pre = mm(second_in[...], w_up[slot, :, :, :, tile].reshape(D, 256)) + up_add[:, col]
            hidden = mm(grad[...], down[tile, :], NT)
            half = 0.5 + 0.5 * lax.erf(pre * root)
            act = (pre * half).astype(BF)
            slope = half + pre * jnp.exp(-0.5 * pre * pre) * level
            pg = (hidden * slope).astype(BF)
            act_s[:, tile] = act
            pg_s[:, tile] = pg
            wide = act.astype(F32)
            squares = squares + jnp.sum(wide * wide, -1, keepdims=True)
            v_c[c, pl.ds(8 + k, 1), tile] = jnp.sum(pg.astype(F32), 0, keepdims=True)

        def hook(half):
            for n in range(FF_CHUNKS):

                @pl.when(k == n)
                def _(n=n):
                    if half == 1 and n + 2 < FF_CHUNKS:
                        start(loads[n + 2])
                    for event, *where in events[2 * n + half]:
                        event(*where)

        hook(0)
        p_up[:, :, :, pl.ds(pl.multiple_of(D * k, 256), D)] = (
            mm(second_t[...], pg_s[...]).astype(BF).reshape(lay.nz, lay.ny, r, D)
        )
        p_down[pl.ds(near_z * k, near_z)] = (
            mm(act_s[...].T, grad[...]).astype(BF).reshape(near_z, lay.ny, 4, r, D)
        )
        output_base[...] += mm(act_s[...], down)
        sg_acc[...] += mm(pg_s[...], w_up[slot].reshape(D, D), NT)
        hook(1)
        return squares

    squares = lax.fori_loop(0, FF_CHUNKS, chunk, jnp.zeros((rows, 1), F32))
    run = lambda *pairs: [step(t, k) for t, k in pairs]
    run((5, 1), (6, 1), (3, 2), (1, 3))
    output[...] = output_base[...].astype(BF)
    forward_halo(2)
    cot_sum = jnp.sum(grad[...].astype(F32), 0, keepdims=True)
    forward_halo(3)
    run((4, 2), (5, 2), (7, 1), (8, 1), (1, 4))

    def put(k, value):
        v_c[c, k : k + 1, :] = value

    put(4, cot_sum)
    for k in range(3):
        put(5 + k, att_sums[k : k + 1, :])
    cot = grad[...].astype(F32)
    token_norm = squares * jnp.sum(cot * cot, -1, keepdims=True) * (1.0 / (FF * D))
    docs_of = jnp.broadcast_to(seg[...].astype(F32), (LANES, rows)).T[:, 0:1]
    doc = lax.broadcasted_iota(jnp.int32, (rows, D), 1).astype(F32)
    member = jnp.where((docs_of == doc) & (doc < docs), 1.0, 0.0)
    put(12, jnp.sum(token_norm * member, 0, keepdims=True))
    put(13, jnp.sum(member, 0, keepdims=True))
    keep = jnp.where(even, 1.0, 0.0).astype(F32)

    def norms(k):
        to_owner[k].wait_recv()
        at = slice(k * quarter, (k + 1) * quarter)
        first_grad = fg_own[at, :] + home[at, :].astype(F32) + hop[at, :].astype(F32) * keep
        second_grad = sg_acc[at, :]
        normed, factor = norm_parts(tok[at, :].astype(F32))
        input_grad[at, :] = (
            grad[at, :].astype(F32)
            + norm_back(first_grad, gain_first, normed, factor)
            + norm_back(second_grad, gain_second, normed, factor)
        ).astype(BF)
        sums = [first_grad * normed, first_grad, second_grad * normed, second_grad]
        return [jnp.sum(value, 0, keepdims=True) for value in sums]

    def add_up(left, right):
        return [p + q for p, q in zip(left, right)]

    sums = norms(0)
    run((3, 3))
    sums = add_up(sums, norms(1))
    run((6, 2))
    sums = add_up(sums, norms(2))
    sums = add_up(sums, norms(3))
    for k in range(4):
        put(k, sums[k])
    run((4, 3))

    at = [0, 1, lay.nx, lay.nx + lay.ny - 1]

    def spread(ref, own, peers, base):
        return [
            remote(ref.at[own], ref.at[own], v_s.at[base + k], v_r.at[base + k], p)
            for k, p in enumerate(peers)
        ]

    vec_c = spread(v_c, c, cs, at[0])
    vec_x = spread(v_x, x, xs, at[1])
    vec_y = spread(v_y, y, ys, at[2])
    vec_z = spread(v_z, z, zs, at[3])

    def add_all(ref, size):
        value = ref[0]
        for k in range(1, size):
            value = value + ref[k]
        return value

    start(vec_c)
    run((5, 3), (7, 2))
    arrive(vec_c)
    v_x[x] = add_all(v_c, 2)
    start(vec_x)
    run((3, 4), (8, 2), (6, 3))
    arrive(vec_x)
    v_y[y] = add_all(v_x, lay.nx)
    start(vec_y)
    run((4, 4), (7, 3), (8, 3), (5, 4))
    arrive(vec_y)
    v_z[z] = add_all(v_y, lay.ny)
    start(vec_z)
    run((6, 4), (0, 5), (1, 5), (2, 5), (3, 5), (4, 5), (5, 5), (7, 4), (6, 5), (8, 4))
    arrive(vec_z)
    vec_out[...] = add_all(v_z, lay.nz)
    run((7, 5), (8, 5))
    for t in range(9):
        net.step(t, 6)
    net.drain()
    sent(vec_c + vec_x + vec_y + vec_z)
    sent(to_next + to_owner)


def back(lay, g_up, g_down, p_att, fg_prev, fg_own, attn_out, vectors, up_add, att_sums, tok, grad, seg):
    rows = tok.shape[0]
    r = p_att.shape[2]
    n = len(CHUNKS)
    docs = DOC_DEV * lay.dp * lay.fsdp
    outs = (
        jax.ShapeDtypeStruct((rows, D), BF),
        jax.ShapeDtypeStruct((rows, D), BF),
        jax.ShapeDtypeStruct((r, 4 * D), BF),
        jax.ShapeDtypeStruct((r, 4 * D), BF),
        jax.ShapeDtypeStruct((4, r, D), BF),
        jax.ShapeDtypeStruct((16, D), F32),
    )
    lx, ly, lz = max(1, lay.nx - 1), max(1, lay.ny - 1), max(1, lay.nz - 1)

    def v(shape, dtype=BF):
        return pltpu.VMEM(shape, dtype)

    def bufs(chunks, peers, x_all, z_all, y_all, first=0):
        return [
            v((chunks,) + peers + part_shape(lay, g, x_all, z_all, y_all, r)) for g in range(first, 3)
        ]

    scratch = [
        v(grad_shape(lay, 0, r)), v((2 * rows, D)), v((rows, D), F32), v((rows, D), F32),
        v(grad_shape(lay, 1, r)), v(grad_shape(lay, 2, r)),
        v((2, lay.nz, lay.ny, r, D)), v((2, lay.nz // FF_CHUNKS, lay.ny, 4, r, D)),
        v((rows, D)), v((D, rows)), v((rows, D)), v((rows, D)), v((rows, D), F32),
        v((rows, D)), v((rows, D)),
        bufs(3, (), True, True, True, 1),
        bufs(2, (lx,), False, True, True),
        bufs(1, (ly,), True, True, False, 1),
        bufs(2, (ly,), False, True, False),
        bufs(1, (lx,), False, True, False),
        bufs(3, (lz,), False, False, False),
    ]
    vecs = [v((k, 16, D), F32) for k in (2, lay.nx, lay.ny, lay.nz)]
    nv = 1 + lay.nx + lay.ny + lay.nz
    sems = [
        dma(n), dma(n), dma(n, lx), dma(n, lx), dma(n, ly), dma(n, ly), dma(n, lz), dma(n, lz),
        dma(n, lx), dma(n, lx), dma(n), dma(n), dma(nv), dma(nv), dma(2, FF_CHUNKS), dma(8), dma(8), dma(6),
    ]
    vmem = pl.BlockSpec(memory_space=pltpu.VMEM)
    return pl.pallas_call(
        functools.partial(back_kernel, lay, rows, docs),
        name="back",
        out_shape=outs,
        in_specs=hbm(6) + [vmem] * 6,
        out_specs=(vmem,) * 6,
        scratch_shapes=scratch + vecs + sems,
        compiler_params=pltpu.CompilerParams(
            collective_id=1, has_side_effects=True, vmem_limit_bytes=VMEM_LIMIT
        ),
    )(g_up, g_down, p_att, fg_prev, fg_own, attn_out, vectors, up_add, att_sums, tok, grad, seg)


def finish_kernel(
    lay, docs, r, f_att, f_up, f_down, vec, out_in, grad_in,
    output, input_grad, fg, fb, sg, sb, qkv_w, qkv_b, dense_w, up_w, up_b, down_w, ob, norms,
):
    output[...] = out_in[...]
    input_grad[...] = grad_in[...]
    shard = lax.axis_index("fsdp")

    def by_head(row_count, kind):
        left = lax.broadcasted_iota(jnp.int32, (row_count, LANES), 1) < HD
        for p in range(PAIRS):
            q, k, v = (kind(n, p) for n in range(3))
            turned = pltpu.roll(k, HD, 1)
            yield jnp.where(left, q, turned)
            yield jnp.where(left, v, q)
            yield jnp.where(left, turned, v)

    def block(k, p):
        return f_att[:, k * D + p * LANES : k * D + (p + 1) * LANES].astype(F32)

    for n, value in enumerate(by_head(r, block)):
        qkv_w[:, n * LANES : (n + 1) * LANES] = value
    dense_w[...] = f_att[:, 3 * D :].astype(F32)
    up_w[...] = f_up[...].astype(F32)
    down_w[...] = f_down[...].astype(F32)

    def own(row, width):
        length = row.shape[1]
        wide = jnp.broadcast_to(row, (8, length))
        turned = pltpu.roll(wide, lax.rem(length - shard * width, length), 1)
        return turned[0:1, :width].reshape(width)

    for k, ref in enumerate((fg, fb, sg, sb, ob)):
        ref[...] = own(vec[k : k + 1, :], r)
    bias = list(by_head(1, lambda k, p: vec[5 + k : 6 + k, p * LANES : (p + 1) * LANES]))
    qkv_b[...] = own(jnp.concatenate(bias, 1), 3 * r)
    up_b[...] = own(jnp.concatenate([vec[8 + k : 9 + k, :] for k in range(4)], 1), 4 * r)
    norms[...] = (vec[12:13, :docs] / vec[13:14, :docs]).reshape(docs)


def finish(lay, output, input_grad, f_att, f_up, f_down, vec):
    r = f_att.shape[0]
    docs = DOC_DEV * lay.dp * lay.fsdp
    vmem = pl.BlockSpec(memory_space=pltpu.VMEM)
    shapes = [
        (r,), (r,), (r,), (r,), (r, 3 * D), (3 * r,), (r, D), (r, FF), (4 * r,), (4, r, D), (r,), (docs,),
    ]
    return pl.pallas_call(
        functools.partial(finish_kernel, lay, docs, r),
        name="finish",
        out_shape=tuple(jax.ShapeDtypeStruct(v.shape, v.dtype) for v in (output, input_grad))
        + tuple(jax.ShapeDtypeStruct(shape, F32) for shape in shapes),
        in_specs=[vmem] * 6,
        out_specs=(vmem,) * (2 + len(shapes)),
        compiler_params=pltpu.CompilerParams(vmem_limit_bytes=VMEM_LIMIT),
    )(f_att, f_up, f_down, vec, output, input_grad)


def per_device(
    lay, tokens, seg_ids, out_grad, first_gain, first_bias, second_gain, second_bias,
    qkv_weight, qkv_bias, dense_weight, up_weight, up_bias, down_weight, out_bias,
):
    rows = tokens.shape[0]
    r = qkv_weight.shape[0]
    vectors = (first_gain, first_bias, second_gain, second_bias, out_bias, qkv_bias, up_bias)
    seg_row = seg_ids.reshape(1, rows)
    passed = front(
        lay, up_weight, down_weight.reshape(4, r, D), qkv_weight, dense_weight, tokens,
        out_grad, seg_row, vectors,
    )
    summed = back(lay, *passed, tokens, out_grad, seg_row)
    (output, input_grad, fg, fb, sg, sb, qkv_w, qkv_b, dense_w, up_w, up_b, down_w, ob, norms) = finish(
        lay, *summed
    )
    return (
        output, input_grad, fg, fb, sg, sb, qkv_w, qkv_b, dense_w, up_w, up_b,
        down_w.reshape(4 * r, D), ob, norms,
    )


def solution(mesh):
    lay = Layout(mesh.shape["dp"], mesh.shape["fsdp"])
    both = P(("dp", "fsdp"))
    split = P("fsdp")
    in_specs = (both, both, both) + (split,) * 11
    out_specs = (both, both) + (split,) * 11 + (P(),)
    return jax.shard_map(
        functools.partial(per_device, lay), mesh=mesh, in_specs=in_specs, out_specs=out_specs,
        check_vma=False,
    )
```

```python
import functools
import math

import jax
import jax.numpy as jnp
from jax import lax
from jax.experimental import pallas as pl
from jax.experimental.pallas import tpu as pltpu
from jax.sharding import PartitionSpec as P

D = 768
H = 12
HD = 64
FF = 3072
ROT = 16
ROW = 2048
DOC_DEV = 2
LANES = 128
PAIRS = D // LANES
MESH = pl.DeviceIdType.MESH
VMEM_LIMIT = 60 * 1024 * 1024


class Layout:
    def __init__(self, dp, fsdp):
        self.dp, self.fsdp = dp, fsdp
        self.nc = 2
        self.nx = dp // 2
        ny = 1
        while (2 * ny) * (2 * ny) <= fsdp:
            ny *= 2
        self.ny, self.nz = ny, fsdp // ny
        self.sub = max(1, self.nx // 2)
        self.unit = 4 // self.nx
        self.down_unit = 2 // self.sub

    def coords(self):
        d, f = lax.axis_index("dp"), lax.axis_index("fsdp")
        return d // 2, d % 2, f // self.ny, f % self.ny

    def device(self, x, c, z, y):
        return {"dp": x * 2 + c, "fsdp": z * self.ny + y}


def wrap(value, size):
    return lax.rem(value + size, size)


CHUNKS = tuple((g, i) for g in range(3) for i in range(3))
ALL = slice(None)


def grad_shape(lay, group, r):
    return (lay.nz, lay.ny, r, 4 * D) if group < 2 else (lay.nz, lay.ny, 4, r, D)


def span_of(lay, group, i, c, x):
    if group < 2:
        width = 512 // lay.nx
        if x is ALL:
            return pl.ds(pl.multiple_of(1024 * i + 512 * c, LANES), 512), None
        return pl.ds(pl.multiple_of(1024 * i + 512 * c + width * x, LANES), width), None
    width = 256 // lay.sub
    if x is ALL:
        return pl.ds(256 * i, 256), pl.ds(2 * c, 2)
    start = 256 * i + width * lax.rem(x, lay.sub)
    return pl.ds(pl.multiple_of(start, LANES), width), 2 * c + x // lay.sub


def view(lay, ref, group, i, c, x, z, y):
    cols, quarter = span_of(lay, group, i, c, x)
    if group < 2:
        return ref.at[z, y, :, cols]
    return ref.at[z, y, quarter, :, cols]


def shard_view(lay, ref, group, i, c, x):
    cols, quarter = span_of(lay, group, i, c, x)
    if group < 2:
        return ref.at[:, cols]
    return ref.at[quarter, :, cols]


def part_shape(lay, group, x_all, z_all, y_all, r):
    lead = ((lay.nz,) if z_all else ()) + ((lay.ny,) if y_all else ())
    if group < 2:
        return lead + (r, 512 if x_all else 512 // lay.nx)
    return lead + ((2, r, 256) if x_all else (r, 256 // lay.sub))


def barrier_with(peers):
    sem = pltpu.get_barrier_semaphore()
    for peer in peers:
        pl.semaphore_signal(sem, inc=1, device_id=peer, device_id_type=MESH)
    pl.semaphore_wait(sem, len(peers))


def line_peers(lay):
    x, c, z, y = lay.coords()
    xs = [lay.device(wrap(x + k, lay.nx), c, z, y) for k in range(1, lay.nx)]
    ys = [lay.device(x, c, z, wrap(y + k, lay.ny)) for k in range(1, lay.ny)]
    zs = [lay.device(x, c, wrap(z + k, lay.nz), y) for k in range(1, lay.nz)]
    cs = [lay.device(x, 1 - c, z, y)]
    return xs, cs, zs, ys


def remote(src, dst, ssem, rsem, device):
    return pltpu.make_async_remote_copy(
        src_ref=src, dst_ref=dst, send_sem=ssem, recv_sem=rsem, device_id=device, device_id_type=MESH
    )


def start(copies):
    for copy in copies:
        copy.start()


def arrive(copies):
    for copy in copies:
        copy.wait_recv()


def sent(copies):
    for copy in copies:
        copy.wait_send()


def hbm(count):
    return [pl.BlockSpec(memory_space=pltpu.HBM)] * count


def dma(*shape):
    return pltpu.SemaphoreType.DMA(shape)


NT = (((1,), (1,)), ((), ()))
NN = (((1,), (0,)), ((), ()))
TN = (((0,), (0,)), ((), ()))
F32 = jnp.float32
BF = jnp.bfloat16


def mm(a, b, dims=NN):
    return lax.dot_general(a, b, dims, preferred_element_type=F32)


def norm_parts(values):
    middle = jnp.mean(values, -1, keepdims=True)
    centred = values - middle
    factor = lax.rsqrt(jnp.mean(centred * centred, -1, keepdims=True) + 1e-05)
    return centred * factor, factor


def small_plan(r):
    plan, at = [], 0
    for size, within in [(r, LANES)] * 5 + [(3 * r, HD), (4 * r, LANES)]:
        plan.append((at, size, math.gcd(size, within)))
        at += -(-size // LANES)
    return plan


SMALL_ROWS = 16


class Gather:
    def __init__(self, lay, us, gs, sems):
        (z_s, z_r, y_s, y_r, x_s, x_r, c_s, c_r) = sems
        x, c, z, y = lay.coords()
        xs, cs, zs, ys = line_peers(lay)
        self.stages = []
        for t, (g, i) in enumerate(CHUNKS):
            by_y, by_x = (ys, y_s, y_r), (xs, x_s, x_r)
            first, second = (by_y, by_x) if i < 2 else (by_x, by_y)
            middle = (x, ALL, ALL) if i < 2 else (ALL, ALL, y)
            steps = [
                ((zs, z_s, z_r), (x, z, y)),
                (first, (x, ALL, y)),
                (second, middle),
            ]
            stages = []
            for (peers, ss, rs), (px, pz, py) in steps:
                piece = view(lay, gs[g], g, i, c, px, pz, py)
                source = shard_view(lay, us[g], g, i, c, x) if len(stages) == 0 else piece
                stages.append(
                    [remote(source, piece, ss.at[t, k], rs.at[t, k], p) for k, p in enumerate(peers)]
                )
            piece = view(lay, gs[g], g, i, c, ALL, ALL, ALL)
            stages.append([remote(piece, piece, c_s.at[t], c_r.at[t], cs[0])])
            self.stages.append(stages)

    def issue(self, t, stage):
        start(self.stages[t][stage])

    def pass_on(self, t, stage):
        arrive(self.stages[t][stage - 1])
        start(self.stages[t][stage])

    def done(self, t):
        arrive(self.stages[t][3])

    def drain(self):
        for stages in self.stages:
            for copies in stages:
                sent(copies)


class Reduce:
    def __init__(self, lay, ps, fs, bufs, sems, wanted):
        (ca, ra1, rb1, ra2, rb2, ra3) = bufs
        (c_s, c_r, x_s, x_r, y_s, y_r, z_s, z_r, fx_s, fx_r, fc_s, fc_r) = sems
        x, c, z, y = lay.coords()
        xs, cs, zs, ys = line_peers(lay)
        other_x = [wrap(x + 1 + k, lay.nx) for k in range(lay.nx - 1)]
        other_y = [wrap(y + 1 + k, lay.ny) for k in range(lay.ny - 1)]
        other_z = [wrap(z + 1 + k, lay.nz) for k in range(lay.nz - 1)]
        self.copies, self.adds = {}, {}
        for t, stages in wanted.items():
            g, i = CHUNKS[t]
            p = ps[g]

            def along(pieces, slot, peers, ss, rs, t=t):
                return [
                    remote(piece, slot.at[k], ss.at[t, k], rs.at[t, k], peers[k])
                    for k, piece in enumerate(pieces)
                ]

            def into(dst, slot, count):
                return functools.partial(add_into, dst, [slot.at[k] for k in range(count)])

            def part(px, pz, py, p=p, g=g, i=i, core=c):
                return view(lay, p, g, i, core, px, pz, py)

            if 0 in stages:
                slot = ca[g].at[i]
                self.copies[t, 0] = [remote(part(ALL, ALL, ALL, core=1 - c), slot, c_s.at[t], c_r.at[t], cs[0])]
                self.adds[t, 1] = functools.partial(add_into, part(ALL, ALL, ALL), [slot])
            if 1 in stages and i < 2:
                slot = ra1[g].at[i]
                self.copies[t, 1] = along([part(k, ALL, ALL) for k in other_x], slot, xs, x_s, x_r)
                self.adds[t, 2] = into(part(x, ALL, ALL), slot, lay.nx - 1)
            elif 1 in stages:
                slot = rb1[g].at[0]
                self.copies[t, 1] = along([part(ALL, ALL, k) for k in other_y], slot, ys, y_s, y_r)
                self.adds[t, 2] = into(part(ALL, ALL, y), slot, lay.ny - 1)
            if 2 in stages and i < 2:
                slot = ra2[g].at[i]
                self.copies[t, 2] = along([part(x, ALL, k) for k in other_y], slot, ys, y_s, y_r)
                self.adds[t, 3] = into(part(x, ALL, y), slot, lay.ny - 1)
            elif 2 in stages:
                slot = rb2[g].at[0]
                self.copies[t, 2] = along([part(k, ALL, y) for k in other_x], slot, xs, x_s, x_r)
                self.adds[t, 3] = into(part(x, ALL, y), slot, lay.nx - 1)
            if 3 in stages:
                slot = ra3[g].at[i]
                self.copies[t, 3] = along([part(x, k, y) for k in other_z], slot, zs, z_s, z_r)
                out = shard_view(lay, fs[g], g, i, c, x)
                self.adds[t, 4] = functools.partial(
                    set_sum, out, [part(x, z, y)] + [slot.at[k] for k in range(lay.nz - 1)]
                )
                self.copies[t, 4] = [
                    remote(out, out, fx_s.at[t, k], fx_r.at[t, k], peer) for k, peer in enumerate(xs)
                ]
                both = shard_view(lay, fs[g], g, i, c, ALL)
                self.copies[t, 5] = [remote(both, both, fc_s.at[t], fc_r.at[t], cs[0])]

    def settle(self, t, k):
        if k > 0:
            arrive(self.copies[t, k - 1])
            if (t, k) in self.adds:
                self.adds[t, k]()

    def begin(self, t, k):
        start(self.copies[t, k])

    def step(self, t, k):
        self.settle(t, k)
        if k < 6:
            self.begin(t, k)

    def drain(self):
        for group in self.copies.values():
            sent(group)


def set_sum(out, srcs):
    total = srcs[0][...].astype(F32)
    for src in srcs[1:]:
        total = total + src[...].astype(F32)
    out[...] = total.astype(BF)


def add_into(dst, srcs):
    lead = dst.shape[:-2]

    def body(j, carry):
        index = []
        rest = j
        for size in reversed(lead):
            index.append(lax.rem(rest, size))
            rest = rest // size
        index = tuple(reversed(index))
        total = dst[index].astype(F32)
        for src in srcs:
            total = total + src[index].astype(F32)
        dst[index] = total.astype(BF)
        return carry

    lax.fori_loop(0, math.prod(lead), body, 0)


def rope(u, cos, low, high):
    return u * cos + pltpu.roll(u, LANES - 8, 1) * low + pltpu.roll(u, 8, 1) * high


def front_kernel(
    lay, rows,
    u_up, u_down, qkv, dense, tok, grad, seg, v0, v1, v2, v3, v4, v5, v6,
    g_up, g_down, p_out, prev_out, own_out, attn_hbm, vectors, up_add, att_sums,
    small, u_att, p_att, fg_prev, fg_own, attn_out, g_att, g_small, tok_halo, seg_halo, first_all, q_s, k_s, v_s, do_s, ctx_s, ctx_t,
    dq_s, dk_s, dv_s, cos_s, low_s, high_s, bias, dk_acc, dv_acc, qkv_add, s_s, w_s, d_s,
    local_sem, z_s, z_r, y_s, y_r, x_s, x_r, c_s, c_r, sm_s, sm_r, h_s, h_r, out_sem,
    ca, ra1, rb1, rc_s, rc_r, rx_s, rx_r, ry_s, ry_r,
):
    span = 3 * rows
    r = qkv.shape[0]
    n_chunks = len(CHUNKS)
    x, c, z, y = lay.coords()
    xs, cs, zs, ys = line_peers(lay)
    total = lay.dp * lay.fsdp
    plan = small_plan(r)
    for (row, size, _), ref in zip(plan, (v0, v1, v2, v3, v4, v5, v6)):
        value = ref[...].astype(F32).reshape(1, size)
        for k in range(-(-size // LANES)):
            width = min(LANES, size - k * LANES)
            small[row + k : row + k + 1, :width] = value[:, k * LANES : k * LANES + width]
    left = lax.broadcasted_iota(jnp.int32, (r, LANES), 1) < HD
    for p in range(PAIRS):
        parts = [qkv[:, (3 * p + k) * LANES : (3 * p + k + 1) * LANES].astype(F32) for k in range(3)]
        kinds = (
            jnp.where(left, parts[0], parts[1]),
            pltpu.roll(jnp.where(left, parts[2], parts[0]), HD, 1),
            jnp.where(left, parts[1], parts[2]),
        )
        for k, part in enumerate(kinds):
            u_att[:, k * D + p * LANES : k * D + (p + 1) * LANES] = part.astype(BF)
    u_att[:, 3 * D :] = dense[...]
    b = lax.axis_index("dp") * lay.fsdp + lax.axis_index("fsdp")

    def stream(k):
        t = wrap(b + k, total)
        return {"dp": t // lay.fsdp, "fsdp": lax.rem(t, lay.fsdp)}

    around = [stream(2), stream(-2), stream(1), stream(-1)]
    gs = (g_att, g_up, g_down)
    us = (u_att, u_up, u_down)
    locals_ = []
    for t, (g, i) in enumerate(CHUNKS):
        locals_.append(
            pltpu.make_async_copy(
                shard_view(lay, us[g], g, i, c, x), view(lay, gs[g], g, i, c, x, z, y), local_sem.at[t]
            )
        )
    locals_.append(pltpu.make_async_copy(small, g_small.at[z, y], local_sem.at[n_chunks]))
    start(locals_)
    barrier_with(xs + cs + zs + ys + around)
    even = lax.rem(b, 2) == 0
    half = rows // 2
    halo, own, passed = [], [], []
    for k in range(2):
        part = pl.ds(k * half, half)
        halo.append(remote(tok.at[part], tok_halo.at[0, part], h_s.at[k], h_r.at[k], around[0]))
        own.append(remote(tok.at[part], tok_halo.at[1, part], h_s.at[2 + k], h_r.at[2 + k], around[2]))
        passed.append(
            remote(tok_halo.at[0, part], tok_halo.at[1, part], h_s.at[2 + k], h_r.at[2 + k], around[3])
        )
    segs = [
        remote(seg, seg_halo.at[0], h_s.at[4], h_r.at[4], around[0]),
        remote(seg, seg_halo.at[1], h_s.at[5], h_r.at[5], around[2]),
    ]
    small_z = [
        remote(small, g_small.at[z, y], sm_s.at[k], sm_r.at[k], p) for k, p in enumerate(zs)
    ]
    small_y = [
        remote(g_small.at[:, y], g_small.at[:, y], sm_s.at[lay.nz + k], sm_r.at[lay.nz + k], p)
        for k, p in enumerate(ys)
    ]
    net = Gather(lay, us, gs, (z_s, z_r, y_s, y_r, x_s, x_r, c_s, c_r))
    net.issue(0, 0)
    net.issue(2, 0)
    start(small_z)
    start(segs)
    net.issue(1, 0)

    def tables(k, carry):
        at = pl.ds(pl.multiple_of(k * 256, 256), 256)
        lane = lax.broadcasted_iota(jnp.int32, (256, LANES), 1) % HD
        row = lax.broadcasted_iota(jnp.int32, (256, LANES), 0) + k * 256
        place = lax.rem((b - 2) * rows + row + 4 * ROW, ROW).astype(F32)
        rate = jnp.exp((lane % 8).astype(F32) * (-math.log(10000.0) / 8.0))
        angle = place * rate
        sine = jnp.sin(angle)
        cos_s[at, :] = jnp.where(lane < ROT, jnp.cos(angle), 1.0)
        low_s[at, :] = jnp.where(lane < 8, -sine, 0.0)
        high_s[at, :] = jnp.where((lane >= 8) & (lane < ROT), sine, 0.0)
        return carry

    lax.fori_loop(0, 2, tables, 0)
    for t in (0, 2, 1, n_chunks):
        locals_[t].wait()
    net.pass_on(0, 1)
    lax.fori_loop(2, 3, tables, 0)
    net.pass_on(2, 1)
    lax.fori_loop(3, 5, tables, 0)
    arrive(small_z)
    start(small_y)
    net.pass_on(0, 2)
    net.pass_on(1, 1)
    halo[0].start()
    lax.fori_loop(5, span // 256, tables, 0)
    arrive(small_y)
    net.pass_on(2, 2)

    lane_row = lax.broadcasted_iota(jnp.int32, (1, LANES), 1)

    def line(first_row, size, unit, length, source):
        out = []
        for block in range(length // LANES):
            value = None
            for k in range(LANES // unit):
                owner, local = divmod(source(block * (LANES // unit) + k), size // unit)
                row, lane = divmod(local * unit, LANES)
                row += first_row
                piece = g_small[owner // lay.ny, owner % lay.ny, row : row + 1, :]
                if lane != k * unit:
                    piece = pltpu.roll(piece, (k * unit - lane) % LANES, 1)
                value = piece if value is None else jnp.where(lane_row // unit == k, piece, value)
            out.append(value)
        return jnp.concatenate(out, 1)

    def norm_rows(values):
        return norm_parts(values.astype(F32))[0]

    for j in range(5):
        vectors[j : j + 1, :] = line(*plan[j], D, lambda n: n)
    vectors[5:8, :] = jnp.zeros((3, D), F32)
    unit = plan[5][2]
    a_head = HD // unit

    def natural(n):
        kind, rest = divmod(n, D // unit)
        head, part = divmod(rest, a_head)
        return head * 3 * a_head + kind * a_head + part

    qkv_add[...] = line(*plan[5], 3 * D, natural)
    net.pass_on(1, 2)
    up_add[...] = line(*plan[6], FF, lambda n: n)

    def pass_halo(k):
        arrive([halo[k]])

        @pl.when(even)
        def _():
            own[k].start()

        @pl.when(jnp.logical_not(even))
        def _():
            passed[k].start()

    halo[1].start()
    gain, shift = vectors[0:1, :], vectors[1:2, :]
    own_rows = pl.ds(2 * rows, rows)
    first = (norm_rows(tok[...]) * gain + shift).astype(BF)
    first_all[own_rows, :] = first
    pass_halo(0)
    arrive(segs)
    least = jnp.maximum(0, 2 * rows - b * rows)
    keys_doc = jnp.concatenate([seg_halo[0], seg_halo[1], seg[...]], 1).astype(F32)
    keys_doc = jnp.broadcast_to(keys_doc, (LANES, span)).T
    query_doc = seg[0:1, :].astype(F32)

    for k in range(6):
        at = slice(k * 256, (k + 1) * 256)
        key_at = lax.broadcasted_iota(jnp.int32, (256, rows), 0) + k * 256
        query_at = lax.broadcasted_iota(jnp.int32, (256, rows), 1) + 2 * rows
        allowed = (keys_doc[at, 0:1] == query_doc) & (key_at <= query_at) & (key_at >= least)
        bias[at, :] = jnp.where(allowed, 0.0, -1e30)
    for t in range(3, n_chunks):
        locals_[t].wait()
    net.issue(5, 0)
    net.pass_on(0, 3)
    net.pass_on(2, 3)
    net.issue(3, 0)

    def weight(first_col, width):
        value = g_att[:, :, :, pl.ds(first_col, width)]
        return value.reshape(D, width)

    scale = 1.0 / math.sqrt(HD)

    def project(kind, j, at, out, factor):
        col = pl.multiple_of(kind * D + 256 * j, 256)
        value = mm(first_all[at, :], weight(col, 256)) + qkv_add[:, pl.ds(col, 256)]
        for k in range(2):
            u = value[:, k * LANES : (k + 1) * LANES]
            if kind < 2:
                u = rope(u, cos_s[at, :], low_s[at, :], high_s[at, :])
            if factor is not None:
                u = u * factor
            out[:, pl.ds(pl.multiple_of(256 * j + LANES * k, LANES), LANES)] = u.astype(BF)

    def own_queries(j, carry):
        project(0, j, own_rows, q_s, scale)
        return carry

    def own_keys(j, carry):
        project(1, j, own_rows, k_s.at[own_rows], None)
        return carry

    def own_values(j, carry):
        project(2, j, own_rows, v_s.at[own_rows], None)
        return carry

    net.done(0)
    lax.fori_loop(0, 3, own_queries, 0)
    lax.fori_loop(0, 1, own_keys, 0)
    pass_halo(1)
    net.pass_on(1, 3)
    net.issue(4, 0)
    net.done(2)
    do_s[...] = mm(grad[...], weight(3 * D, D), NT).astype(BF)
    lax.fori_loop(2, 3, own_values, 0)
    net.pass_on(5, 1)
    net.done(1)
    lax.fori_loop(1, 3, own_keys, 0)
    lax.fori_loop(0, 2, own_values, 0)
    own[0].wait_recv()
    net.pass_on(3, 1)

    def earlier_norms(k):
        for n in range(2):
            near = pl.ds(k * half, half)
            before = norm_rows(tok_halo[n, near, :]) * gain + shift
            first_all[pl.ds(n * rows + k * half, half), :] = before.astype(BF)

    earlier_norms(0)
    net.issue(8, 0)
    own[1].wait_recv()
    earlier_norms(1)
    net.pass_on(4, 1)
    net.pass_on(5, 2)

    def earlier_projections(j, carry):
        for k in range(2):
            at = pl.ds(k * rows, rows)
            project(1, j, at, k_s.at[at], None)
            project(2, j, at, v_s.at[at], None)
        return carry

    lax.fori_loop(0, 3, earlier_projections, 0)
    net.pass_on(3, 2)
    net.issue(6, 0)

    go, send, end = net.pass_on, net.issue, net.done
    later = [
        [(go, 8, 1), (send, 7, 0), (go, 4, 2)],
        [(go, 5, 3), (go, 6, 1), (go, 3, 3), (go, 7, 1)],
        [(go, 8, 2), (go, 6, 2)],
        [(go, 4, 3), (go, 7, 2)],
        [(go, 8, 3), (go, 6, 3)],
        [(go, 7, 3)],
    ]
    tile = 256

    def pair(p, carry):
        lanes = pl.ds(pl.multiple_of(p * LANES, LANES), LANES)
        v_t, k_t = v_s[:, lanes].T, k_s[:, lanes].T
        do_t = do_s[:, lanes].astype(F32).T
        lane = lax.broadcasted_iota(jnp.int32, (tile, LANES), 1)
        zero = jnp.zeros((), BF)
        units = [(t, hh) for t in range(rows // tile) for hh in range(2)]
        count = len(units)
        tops, totals, norms = [None] * count, [None] * count, [None] * count
        outs, dqs = [None] * count, [None] * count
        written = set()

        def masked(ref, u):
            t, hh = units[u]
            return jnp.where((lane // HD) == hh, ref[t * tile : (t + 1) * tile, lanes], zero)

        def pieces(u):
            kl = 2 * rows + (units[u][0] + 1) * tile
            return [slice(k * LANES, (k + 1) * LANES) for k in range(kl // LANES)]

        def scores(u, at, qm):
            t = units[u][0]
            st = mm(k_s[at, lanes], qm, NT) + bias[at, t * tile : (t + 1) * tile]
            s_s[u % 2, at, :] = st
            most = jnp.max(st, 0, keepdims=True)
            tops[u] = most if tops[u] is None else jnp.maximum(tops[u], most)

        def exponents(u, at):
            e = jnp.exp(s_s[u % 2, at, :] - tops[u])
            s_s[u % 2, at, :] = e
            part = jnp.sum(e, 0, keepdims=True)
            totals[u] = part if totals[u] is None else totals[u] + part

        def key_value_grads(u, at, qm, dom):
            dk, dv = mm(d_s[u % 2, at, :], qm), mm(w_s[u % 2, at, :], dom)
            if at.start in written:
                dk_acc[at, :] += dk
                dv_acc[at, :] += dv
            else:
                dk_acc[at, :] = dk
                dv_acc[at, :] = dv
                written.add(at.start)

        qm = masked(q_s, 0)
        for at in pieces(0):
            scores(0, at, qm)
        for u in range(count):
            t, hh = units[u]
            part = slice(hh * HD, (hh + 1) * HD)
            cols = slice(t * tile, (t + 1) * tile)
            kl = 2 * rows + (t + 1) * tile
            mine = pieces(u)
            after = pieces(u + 1) if u + 1 < count else []
            before = pieces(u - 1) if u > 0 else []
            if after:
                qm = masked(q_s, u + 1)
            for k in range(max(len(mine), len(after))):
                if k < len(after):
                    scores(u + 1, after[k], qm)
                if k < len(mine):
                    exponents(u, mine[k])
            norms[u] = 1.0 / totals[u]
            if before:
                q_last, do_last = masked(q_s, u - 1), masked(do_s, u - 1)
            for k in range(max(len(mine), len(before))):
                if k < len(before):
                    key_value_grads(u - 1, before[k], q_last, do_last)
                if k < len(mine):
                    w_s[u % 2, mine[k], :] = (s_s[u % 2, mine[k], :] * norms[u]).astype(BF)
            o_t = mm(v_t[part, :kl], w_s[u % 2, :kl, :])
            delta = jnp.sum(o_t * do_t[part, cols], 0, keepdims=True)
            outs[u] = o_t
            dom = masked(do_s, u)
            for at in mine:
                dp = mm(v_s[at, lanes], dom, NT)
                d_s[u % 2, at, :] = ((s_s[u % 2, at, :] * norms[u]) * (dp - delta)).astype(BF)
            dqs[u] = mm(k_t[part, :kl], d_s[u % 2, :kl, :])
            if hh == 0:
                continue
            o_pair = jnp.concatenate(outs[u - 1 : u + 1], 0)
            ctx_t[lanes, cols] = o_pair.astype(BF)
            ctx_s[cols, lanes] = o_pair.T.astype(BF)
            dq = jnp.concatenate(dqs[u - 1 : u + 1], 0).T * scale
            at = slice(2 * rows + t * tile, 2 * rows + (t + 1) * tile)
            dq_s[cols, lanes] = rope(dq, cos_s[at, :], -low_s[at, :], -high_s[at, :]).astype(BF)
        q_last, do_last = masked(q_s, count - 1), masked(do_s, count - 1)
        for at in pieces(count - 1):
            key_value_grads(count - 1, at, q_last, do_last)
        dk_s[:, lanes] = rope(dk_acc[...], cos_s[...], -low_s[...], -high_s[...]).astype(BF)
        dv_s[:, lanes] = dv_acc[...].astype(BF)
        for k in range(PAIRS):

            @pl.when(p == k)
            def _(k=k):
                for event, *where in later[k]:
                    event(*where)

        return carry

    lax.fori_loop(0, PAIRS, pair, 0)

    sums = Reduce(
        lay, (p_att,), None, ((ca,), (ra1,), (rb1,), None, None, None),
        (rc_s, rc_r, rx_s, rx_r, ry_s, ry_r) + (None,) * 6, {0: (0, 1), 1: (0,), 2: (0, 1)},
    )
    outs = []

    def leave(i):
        cols = pl.ds(1024 * i, 1024)
        copy = pltpu.make_async_copy(p_att.at[:, :, :, cols], p_out.at[:, :, :, cols], out_sem.at[i])
        copy.start()
        outs.append(copy)

    def put(kind, j, value):
        p_att[:, :, :, kind * D + 256 * j : kind * D + 256 * (j + 1)] = value.astype(BF).reshape(
            lay.nz, lay.ny, r, 256
        )

    def tile_of(ref, j):
        return ref[:, slice(256 * j, 256 * (j + 1))]

    def weight_grad(kind, j):
        if kind == 0:
            put(0, j, mm(first_all[own_rows, :], tile_of(dq_s, j), TN))
        elif kind == 3:
            put(3, j, mm(ctx_t[...], tile_of(grad, j)))
        else:
            put(kind, j, mm(first_all[...], tile_of((dk_s, dv_s)[kind - 1], j), TN))

    for kind, j in ((1, 0), (0, 0), (0, 1), (0, 2)):
        weight_grad(kind, j)
    sums.step(0, 0)
    for kind, j in ((2, 2), (3, 0), (3, 1), (3, 2)):
        weight_grad(kind, j)
    sums.step(0, 1)
    sums.step(2, 0)
    for kind, j in ((1, 1), (1, 2)):
        weight_grad(kind, j)
    sums.step(2, 1)
    for kind, j in ((2, 0), (2, 1)):
        weight_grad(kind, j)
    sums.step(1, 0)

    def earlier_grad(k, carry):
        at = pl.ds(pl.multiple_of(k * 256, 256), 256)
        value = mm(dk_s[at, :], weight(D, D), NT) + mm(dv_s[at, :], weight(2 * D, D), NT)
        fg_prev[at, :] = value.astype(BF)
        return carry

    lax.fori_loop(0, 2 * rows // 256, earlier_grad, 0)
    outs.append(pltpu.make_async_copy(fg_prev, prev_out, out_sem.at[3]))
    outs[-1].start()
    sums.settle(1, 1)
    leave(1)
    for k in range(rows // 256):
        at = slice(2 * rows + 256 * k, 2 * rows + 256 * (k + 1))
        near = slice(256 * k, 256 * (k + 1))
        fg_own[near, :] = (
            mm(dk_s[at, :], weight(D, D), NT)
            + mm(dv_s[at, :], weight(2 * D, D), NT)
            + mm(dq_s[near, :], weight(0, D), NT)
        )
    outs.append(pltpu.make_async_copy(fg_own, own_out, out_sem.at[4]))
    outs[-1].start()

    def attention_out(j, carry):
        col = pl.multiple_of(256 * j, 256)
        attn_out[:, pl.ds(col, 256)] = mm(ctx_s[...], weight(pl.multiple_of(3 * D + col, 256), 256))
        return carry

    lax.fori_loop(0, 3, attention_out, 0)
    outs.append(pltpu.make_async_copy(attn_out, attn_hbm, out_sem.at[5]))
    outs[-1].start()
    for k, ref in enumerate((dq_s, dk_s, dv_s)):
        att_sums[k : k + 1, :] = jnp.sum(ref[...].astype(F32), 0, keepdims=True)
    att_sums[3:8, :] = jnp.zeros((5, D), F32)
    sums.settle(0, 2)
    leave(0)
    sums.settle(2, 2)
    leave(2)
    sums.drain()
    for t in range(3, 9):
        net.done(t)
    net.drain()
    sent(small_z + small_y + segs + halo + own)
    for copy in outs:
        copy.wait()


def front(lay, u_up, u_down, qkv, dense, tok, grad, seg, vectors):
    rows = tok.shape[0]
    span = 3 * rows
    r = qkv.shape[0]
    n = len(CHUNKS)
    outs = (
        jax.ShapeDtypeStruct(grad_shape(lay, 1, r), BF),
        jax.ShapeDtypeStruct(grad_shape(lay, 2, r), BF),
        jax.ShapeDtypeStruct(grad_shape(lay, 0, r), BF),
        jax.ShapeDtypeStruct((2 * rows, D), BF),
        jax.ShapeDtypeStruct((rows, D), F32),
        jax.ShapeDtypeStruct((rows, D), F32),
        jax.ShapeDtypeStruct((8, D), F32),
        jax.ShapeDtypeStruct((1, FF), F32),
        jax.ShapeDtypeStruct((8, D), F32),
    )
    vmem = pl.BlockSpec(memory_space=pltpu.VMEM)
    lx, ly, lz = max(1, lay.nx - 1), max(1, lay.ny - 1), max(1, lay.nz - 1)

    def v(shape, dtype=BF):
        return pltpu.VMEM(shape, dtype)

    return pl.pallas_call(
        functools.partial(front_kernel, lay, rows),
        name="front",
        out_shape=outs,
        in_specs=hbm(2) + [vmem] * (5 + len(vectors)),
        out_specs=tuple(hbm(6)) + (vmem,) * 3,
        scratch_shapes=[
            v((SMALL_ROWS, LANES), F32), v((r, 4 * D)), v(grad_shape(lay, 0, r)), v((2 * rows, D)), v((rows, D), F32), v((rows, D), F32),
            v(grad_shape(lay, 0, r)), v((lay.nz, lay.ny, SMALL_ROWS, LANES), F32), v((2, rows, D)),
            v((2, 1, rows), jnp.int32), v((span, D)), v((rows, D)), v((span, D)),
            v((span, D)), v((rows, D)), v((rows, D)), v((D, rows)), v((rows, D)), v((span, D)),
            v((span, D)), v((span, LANES), F32), v((span, LANES), F32), v((span, LANES), F32),
            v((span, rows), F32), v((span, LANES), F32), v((span, LANES), F32), v((1, 3 * D), F32),
            v((2, span, 256), F32), v((2, span, 256)), v((2, span, 256)),
            dma(n + 1), dma(n, lz), dma(n, lz), dma(n, ly), dma(n, ly), dma(n, lx), dma(n, lx),
            dma(n), dma(n), dma(lay.nz + ly), dma(lay.nz + ly), dma(6), dma(6), dma(6),
            v((3,) + part_shape(lay, 0, True, True, True, r)),
            v((1, lx) + part_shape(lay, 0, False, True, True, r)),
            v((1, ly) + part_shape(lay, 0, True, True, False, r)),
            dma(3), dma(3), dma(3, lx), dma(3, lx), dma(3, ly), dma(3, ly),
        ],
        compiler_params=pltpu.CompilerParams(
            collective_id=0, has_side_effects=True, vmem_limit_bytes=VMEM_LIMIT
        ),
    )(u_up, u_down, qkv, dense, tok, grad, seg, *vectors)


def norm_back(grad, gain, normed, factor):
    inner = grad * gain
    return factor * (
        inner
        - jnp.mean(inner, -1, keepdims=True)
        - normed * jnp.mean(inner * normed, -1, keepdims=True)
    )


FF_CHUNKS = FF // D


def back_kernel(
    lay, rows, docs,
    g_up, g_down, p_in, prev_in, own_in, attn_in, vectors, up_add, att_sums, tok, grad, seg,
    out_hbm, input_hbm, att_hbm, up_hbm, down_hbm, vec_out,
    output, input_grad, f_att, f_up, f_down, p_att, fg_prev, fg_own, attn_out, p_up, p_down, w_up, w_down, second_in, second_t, act_s, pg_s, sg_acc, hop, home,
    ca, ra1, rb1, ra2, rb2, ra3, v_c, v_x, v_y, v_z, *sems,
):
    (c_s, c_r, x_s, x_r, y_s, y_r, z_s, z_r, fx_s, fx_r, fc_s, fc_r, v_s, v_r, w_sem, h_s, h_r, in_sem, out_sem) = sems
    r = p_in.shape[2]
    x, c, z, y = lay.coords()
    xs, cs, zs, ys = line_peers(lay)
    total = lay.dp * lay.fsdp
    b = lax.axis_index("dp") * lay.fsdp + lax.axis_index("fsdp")

    def stream(k):
        t = wrap(b + k, total)
        return {"dp": t // lay.fsdp, "fsdp": lax.rem(t, lay.fsdp)}

    around = [stream(2), stream(-2), stream(1), stream(-1)]
    near_z = lay.nz // FF_CHUNKS
    loads = []
    for k in range(FF_CHUNKS):
        slot = k % 2
        loads.append(
            (
                pltpu.make_async_copy(
                    g_up.at[:, :, :, pl.ds(D * k, D)], w_up.at[slot], w_sem.at[0, k]
                ),
                pltpu.make_async_copy(
                    g_down.at[pl.ds(near_z * k, near_z)], w_down.at[slot], w_sem.at[1, k]
                ),
            )
        )
    taken = [
        pltpu.make_async_copy(
            p_in.at[:, :, :, pl.ds(1024 * i, 1024)], p_att.at[:, :, :, pl.ds(1024 * i, 1024)],
            in_sem.at[i],
        )
        for i in range(3)
    ]
    taken.append(pltpu.make_async_copy(prev_in, fg_prev, in_sem.at[3]))
    taken.append(pltpu.make_async_copy(attn_in, attn_out, in_sem.at[4]))
    taken.append(pltpu.make_async_copy(own_in, fg_own, in_sem.at[5]))
    start(taken[:4])
    start(loads[0])
    start(taken[4:])
    start(loads[1])
    barrier_with(xs + cs + zs + ys + around)
    wanted = {t: (0, 1, 2, 3) for t in range(3, len(CHUNKS))}
    wanted.update({0: (2, 3), 1: (1, 2, 3), 2: (2, 3)})
    net = Reduce(
        lay, (p_att, p_up, p_down), (f_att, f_up, f_down),
        ((None,) + tuple(ca), ra1, (None,) + tuple(rb1), ra2, rb2, ra3), sems[:12], wanted,
    )
    for t, k in ((1, 1), (2, 2), (0, 2)):
        taken[t].wait()
        net.begin(t, k)
    taken[3].wait()
    even = lax.rem(b, 2) == 0
    quarter = rows // 4
    to_next, to_last, to_owner = [], [], []
    for k in range(4):
        near = fg_prev.at[pl.ds(rows + k * quarter, quarter)]
        far = fg_prev.at[pl.ds(k * quarter, quarter)]
        part = pl.ds(k * quarter, quarter)
        to_next.append(remote(near, hop.at[part], h_s.at[k], h_r.at[k], around[2]))
        to_last.append(remote(near, hop.at[part], h_s.at[k], h_r.at[k], around[3]))
        to_owner.append(remote(far, home.at[part], h_s.at[4 + k], h_r.at[4 + k], around[1]))

    def hop_halo(k):
        @pl.when(even)
        def _():
            to_next[k].start()

        @pl.when(jnp.logical_not(even))
        def _():
            to_last[k].start()

    def forward_halo(k):
        to_last[k].wait_recv()
        at = pl.ds(k * quarter, quarter)

        @pl.when(jnp.logical_not(even))
        def _():
            fg_prev[at, :] = (fg_prev[at, :].astype(F32) + hop[at, :].astype(F32)).astype(BF)

        to_owner[k].start()

    hop_halo(0)
    hop_halo(1)

    gain_first, gain_second = vectors[0:1, :], vectors[2:3, :]
    normed, factor = norm_parts(tok[...].astype(F32))
    value = (normed * gain_second + vectors[3:4, :]).astype(BF)
    second_in[...] = value
    second_t[...] = value.T
    cot = grad[...].astype(F32)
    taken[4].wait()
    taken[5].wait()
    output_base = attn_out
    output_base[...] = attn_out[...] + tok[...].astype(F32) + vectors[4:5, :]
    sg_acc[...] = jnp.zeros_like(sg_acc)
    mine = v_c.at[c]
    mine[...] = jnp.zeros((16, D), F32)

    step = net.step
    events = [
        [],
        [(step, 0, 3)],
        [(hop_halo, 2)],
        [(step, 3, 0), (step, 1, 2), (forward_halo, 0)],
        [(step, 3, 1), (step, 2, 3), (hop_halo, 3)],
        [(step, 4, 0), (forward_halo, 1)],
        [(step, 4, 1), (step, 0, 4)],
        [(step, 5, 0), (step, 6, 0), (step, 7, 0), (step, 8, 0), (step, 2, 4)],
    ]
    root = math.sqrt(0.5)
    level = 1.0 / math.sqrt(2.0 * math.pi)

    def chunk(k, squares):
        slot = lax.rem(k, 2)
        for n in range(FF_CHUNKS):

            @pl.when(k == n)
            def _(n=n):
                loads[n][0].wait()
                loads[n][1].wait()

        down = w_down[slot].reshape(D, D)
        for j in range(3):
            tile = slice(256 * j, 256 * (j + 1))
            col = pl.ds(pl.multiple_of(D * k + 256 * j, 256), 256)
            pre = mm(second_in[...], w_up[slot, :, :, :, tile].reshape(D, 256)) + up_add[:, col]
            hidden = mm(grad[...], down[tile, :], NT)
            half = 0.5 + 0.5 * lax.erf(pre * root)
            act = (pre * half).astype(BF)
            slope = half + pre * jnp.exp(-0.5 * pre * pre) * level
            pg = (hidden * slope).astype(BF)
            act_s[:, tile] = act
            pg_s[:, tile] = pg
            wide = act.astype(F32)
            squares = squares + jnp.sum(wide * wide, -1, keepdims=True)
            v_c[c, pl.ds(8 + k, 1), tile] = jnp.sum(pg.astype(F32), 0, keepdims=True)

        def hook(half):
            for n in range(FF_CHUNKS):

                @pl.when(k == n)
                def _(n=n):
                    if half == 1 and n + 2 < FF_CHUNKS:
                        start(loads[n + 2])
                    for event, *where in events[2 * n + half]:
                        event(*where)

        hook(0)
        p_up[:, :, :, pl.ds(pl.multiple_of(D * k, 256), D)] = (
            mm(second_t[...], pg_s[...]).astype(BF).reshape(lay.nz, lay.ny, r, D)
        )
        p_down[pl.ds(near_z * k, near_z)] = (
            mm(act_s[...].T, grad[...]).astype(BF).reshape(near_z, lay.ny, 4, r, D)
        )
        output_base[...] += mm(act_s[...], down)
        sg_acc[...] += mm(pg_s[...], w_up[slot].reshape(D, D), NT)
        hook(1)
        return squares

    squares = lax.fori_loop(0, FF_CHUNKS, chunk, jnp.zeros((rows, 1), F32))
    run = lambda *pairs: [step(t, k) for t, k in pairs]
    run((5, 1), (6, 1), (3, 2), (1, 3))
    output[...] = output_base[...].astype(BF)
    left = []

    def leave(k, ref, target):
        copy = pltpu.make_async_copy(ref, target, out_sem.at[k])
        copy.start()
        left.append(copy)

    leave(0, output, out_hbm)
    forward_halo(2)
    cot_sum = jnp.sum(grad[...].astype(F32), 0, keepdims=True)
    forward_halo(3)
    def put(k, value):
        v_c[c, k : k + 1, :] = value

    put(4, cot_sum)
    for k in range(3):
        put(5 + k, att_sums[k : k + 1, :])
    cot = grad[...].astype(F32)
    token_norm = squares * jnp.sum(cot * cot, -1, keepdims=True) * (1.0 / (FF * D))
    docs_of = jnp.broadcast_to(seg[...].astype(F32), (LANES, rows)).T[:, 0:1]
    doc = lax.broadcasted_iota(jnp.int32, (rows, D), 1).astype(F32)
    member = jnp.where((docs_of == doc) & (doc < docs), 1.0, 0.0)
    put(12, jnp.sum(token_norm * member, 0, keepdims=True))
    put(13, jnp.sum(member, 0, keepdims=True))
    run((4, 2), (5, 2), (7, 1), (8, 1), (1, 4))
    keep = jnp.where(even, 1.0, 0.0).astype(F32)

    def norms(k):
        to_owner[k].wait_recv()
        at = slice(k * quarter, (k + 1) * quarter)
        first_grad = fg_own[at, :] + home[at, :].astype(F32) + hop[at, :].astype(F32) * keep
        second_grad = sg_acc[at, :]
        normed, factor = norm_parts(tok[at, :].astype(F32))
        input_grad[at, :] = (
            grad[at, :].astype(F32)
            + norm_back(first_grad, gain_first, normed, factor)
            + norm_back(second_grad, gain_second, normed, factor)
        ).astype(BF)
        sums = [first_grad * normed, first_grad, second_grad * normed, second_grad]
        return [jnp.sum(value, 0, keepdims=True) for value in sums]

    def add_up(left, right):
        return [p + q for p, q in zip(left, right)]

    sums = norms(0)
    run((3, 3))
    sums = add_up(sums, norms(1))
    run((6, 2))
    sums = add_up(sums, norms(2))
    sums = add_up(sums, norms(3))
    leave(1, input_grad, input_hbm)
    for k in range(4):
        put(k, sums[k])
    run((4, 3))

    at = [0, 1, lay.nx, lay.nx + lay.ny - 1]

    def spread(ref, own, peers, base):
        return [
            remote(ref.at[own], ref.at[own], v_s.at[base + k], v_r.at[base + k], p)
            for k, p in enumerate(peers)
        ]

    vec_c = spread(v_c, c, cs, at[0])
    vec_x = spread(v_x, x, xs, at[1])
    vec_y = spread(v_y, y, ys, at[2])
    vec_z = spread(v_z, z, zs, at[3])

    def add_all(ref, size):
        value = ref[0]
        for k in range(1, size):
            value = value + ref[k]
        return value

    start(vec_c)
    run((5, 3), (8, 2))
    arrive(vec_c)
    v_x[x] = add_all(v_c, 2)
    start(vec_x)
    run((7, 2), (3, 4), (6, 3), (8, 3), (7, 3))
    arrive(vec_x)
    v_y[y] = add_all(v_x, lay.nx)
    start(vec_y)
    run((4, 4), (5, 4))
    arrive(vec_y)
    v_z[z] = add_all(v_y, lay.ny)
    start(vec_z)
    run((6, 4), (0, 5), (1, 5), (2, 5), (3, 5), (4, 5), (5, 5), (8, 4))
    run((0, 6), (1, 6), (2, 6))
    leave(2, f_att, att_hbm)
    run((6, 5), (3, 6), (4, 6), (5, 6), (7, 4))
    leave(3, f_up, up_hbm)
    arrive(vec_z)
    vec_out[...] = add_all(v_z, lay.nz)
    run((8, 5), (7, 5), (6, 6), (8, 6), (7, 6))
    leave(4, f_down, down_hbm)
    net.drain()
    sent(vec_c + vec_x + vec_y + vec_z)
    sent(to_next + to_owner)
    for copy in left:
        copy.wait()


def back(lay, g_up, g_down, p_att, fg_prev, fg_own, attn_out, vectors, up_add, att_sums, tok, grad, seg):
    rows = tok.shape[0]
    r = p_att.shape[2]
    n = len(CHUNKS)
    docs = DOC_DEV * lay.dp * lay.fsdp
    outs = (
        jax.ShapeDtypeStruct((rows, D), BF),
        jax.ShapeDtypeStruct((rows, D), BF),
        jax.ShapeDtypeStruct((r, 4 * D), BF),
        jax.ShapeDtypeStruct((r, 4 * D), BF),
        jax.ShapeDtypeStruct((4, r, D), BF),
        jax.ShapeDtypeStruct((16, D), F32),
    )
    lx, ly, lz = max(1, lay.nx - 1), max(1, lay.ny - 1), max(1, lay.nz - 1)

    def v(shape, dtype=BF):
        return pltpu.VMEM(shape, dtype)

    def bufs(chunks, peers, x_all, z_all, y_all, first=0):
        return [
            v((chunks,) + peers + part_shape(lay, g, x_all, z_all, y_all, r)) for g in range(first, 3)
        ]

    scratch = [
        v((rows, D)), v((rows, D)), v((r, 4 * D)), v((r, 4 * D)), v((4, r, D)),
        v(grad_shape(lay, 0, r)), v((2 * rows, D)), v((rows, D), F32), v((rows, D), F32),
        v(grad_shape(lay, 1, r)), v(grad_shape(lay, 2, r)),
        v((2, lay.nz, lay.ny, r, D)), v((2, lay.nz // FF_CHUNKS, lay.ny, 4, r, D)),
        v((rows, D)), v((D, rows)), v((rows, D)), v((rows, D)), v((rows, D), F32),
        v((rows, D)), v((rows, D)),
        bufs(3, (), True, True, True, 1),
        bufs(2, (lx,), False, True, True),
        bufs(1, (ly,), True, True, False, 1),
        bufs(2, (ly,), False, True, False),
        bufs(1, (lx,), False, True, False),
        bufs(3, (lz,), False, False, False),
    ]
    vecs = [v((k, 16, D), F32) for k in (2, lay.nx, lay.ny, lay.nz)]
    nv = 1 + lay.nx + lay.ny + lay.nz
    sems = [
        dma(n), dma(n), dma(n, lx), dma(n, lx), dma(n, ly), dma(n, ly), dma(n, lz), dma(n, lz),
        dma(n, lx), dma(n, lx), dma(n), dma(n), dma(nv), dma(nv), dma(2, FF_CHUNKS), dma(8), dma(8), dma(6), dma(5),
    ]
    vmem = pl.BlockSpec(memory_space=pltpu.VMEM)
    return pl.pallas_call(
        functools.partial(back_kernel, lay, rows, docs),
        name="back",
        out_shape=outs,
        in_specs=hbm(6) + [vmem] * 6,
        out_specs=tuple(hbm(5)) + (vmem,),
        scratch_shapes=scratch + vecs + sems,
        compiler_params=pltpu.CompilerParams(
            collective_id=1, has_side_effects=True, vmem_limit_bytes=VMEM_LIMIT
        ),
    )(g_up, g_down, p_att, fg_prev, fg_own, attn_out, vectors, up_add, att_sums, tok, grad, seg)


def finish_kernel(
    lay, docs, r, f_att, f_up, f_down, vec, out_in, grad_in,
    output, input_grad, fg, fb, sg, sb, qkv_w, qkv_b, dense_w, up_w, up_b, down_w, ob, norms,
):
    output[...] = out_in[...]
    input_grad[...] = grad_in[...]
    shard = lax.axis_index("fsdp")

    def by_head(row_count, kind):
        left = lax.broadcasted_iota(jnp.int32, (row_count, LANES), 1) < HD
        for p in range(PAIRS):
            q, k, v = (kind(n, p) for n in range(3))
            turned = pltpu.roll(k, HD, 1)
            yield jnp.where(left, q, turned)
            yield jnp.where(left, v, q)
            yield jnp.where(left, turned, v)

    def block(k, p):
        return f_att[:, k * D + p * LANES : k * D + (p + 1) * LANES].astype(F32)

    for n, value in enumerate(by_head(r, block)):
        qkv_w[:, n * LANES : (n + 1) * LANES] = value
    dense_w[...] = f_att[:, 3 * D :].astype(F32)
    up_w[...] = f_up[...].astype(F32)
    down_w[...] = f_down[...].astype(F32)

    def own(row, width):
        length = row.shape[1]
        wide = jnp.broadcast_to(row, (8, length))
        turned = pltpu.roll(wide, lax.rem(length - shard * width, length), 1)
        return turned[0:1, :width].reshape(width)

    for k, ref in enumerate((fg, fb, sg, sb, ob)):
        ref[...] = own(vec[k : k + 1, :], r)
    bias = list(by_head(1, lambda k, p: vec[5 + k : 6 + k, p * LANES : (p + 1) * LANES]))
    qkv_b[...] = own(jnp.concatenate(bias, 1), 3 * r)
    up_b[...] = own(jnp.concatenate([vec[8 + k : 9 + k, :] for k in range(4)], 1), 4 * r)
    norms[...] = (vec[12:13, :docs] / vec[13:14, :docs]).reshape(docs)


def finish(lay, output, input_grad, f_att, f_up, f_down, vec):
    r = f_att.shape[0]
    docs = DOC_DEV * lay.dp * lay.fsdp
    vmem = pl.BlockSpec(memory_space=pltpu.VMEM)
    shapes = [
        (r,), (r,), (r,), (r,), (r, 3 * D), (3 * r,), (r, D), (r, FF), (4 * r,), (4, r, D), (r,), (docs,),
    ]
    return pl.pallas_call(
        functools.partial(finish_kernel, lay, docs, r),
        name="finish",
        out_shape=tuple(jax.ShapeDtypeStruct(v.shape, v.dtype) for v in (output, input_grad))
        + tuple(jax.ShapeDtypeStruct(shape, F32) for shape in shapes),
        in_specs=[vmem] * 6,
        out_specs=(vmem,) * (2 + len(shapes)),
        compiler_params=pltpu.CompilerParams(vmem_limit_bytes=VMEM_LIMIT),
    )(f_att, f_up, f_down, vec, output, input_grad)


def per_device(
    lay, tokens, seg_ids, out_grad, first_gain, first_bias, second_gain, second_bias,
    qkv_weight, qkv_bias, dense_weight, up_weight, up_bias, down_weight, out_bias,
):
    rows = tokens.shape[0]
    r = qkv_weight.shape[0]
    vectors = (first_gain, first_bias, second_gain, second_bias, out_bias, qkv_bias, up_bias)
    seg_row = seg_ids.reshape(1, rows)
    passed = front(
        lay, up_weight, down_weight.reshape(4, r, D), qkv_weight, dense_weight, tokens,
        out_grad, seg_row, vectors,
    )
    summed = back(lay, *passed, tokens, out_grad, seg_row)
    (output, input_grad, fg, fb, sg, sb, qkv_w, qkv_b, dense_w, up_w, up_b, down_w, ob, norms) = finish(
        lay, *summed
    )
    return (
        output, input_grad, fg, fb, sg, sb, qkv_w, qkv_b, dense_w, up_w, up_b,
        down_w.reshape(4 * r, D), ob, norms,
    )


def solution(mesh):
    lay = Layout(mesh.shape["dp"], mesh.shape["fsdp"])
    both = P(("dp", "fsdp"))
    split = P("fsdp")
    in_specs = (both, both, both) + (split,) * 11
    out_specs = (both, both) + (split,) * 11 + (P(),)
    return jax.shard_map(
        functools.partial(per_device, lay), mesh=mesh, in_specs=in_specs, out_specs=out_specs,
        check_vma=False,
    )
```

```python
import functools
import math

import jax
import jax.numpy as jnp
from jax import lax
from jax.experimental import pallas as pl
from jax.experimental.pallas import tpu as pltpu
from jax.sharding import PartitionSpec as P

D = 768
H = 12
HD = 64
FF = 3072
ROT = 16
ROW = 2048
DOC_DEV = 2
LANES = 128
PAIRS = D // LANES
MESH = pl.DeviceIdType.MESH
VMEM_LIMIT = 60 * 1024 * 1024


class Layout:
    def __init__(self, dp, fsdp):
        self.dp, self.fsdp = dp, fsdp
        self.nc = 2
        self.nx = dp // 2
        ny = 1
        while (2 * ny) * (2 * ny) <= fsdp:
            ny *= 2
        self.ny, self.nz = ny, fsdp // ny
        self.sub = max(1, self.nx // 2)
        self.unit = 4 // self.nx
        self.down_unit = 2 // self.sub

    def coords(self):
        d, f = lax.axis_index("dp"), lax.axis_index("fsdp")
        return d // 2, d % 2, f // self.ny, f % self.ny

    def device(self, x, c, z, y):
        return {"dp": x * 2 + c, "fsdp": z * self.ny + y}


def wrap(value, size):
    return lax.rem(value + size, size)


CHUNKS = tuple((g, i) for g in range(3) for i in range(3))
LAST = len(CHUNKS) - 1
ALL = slice(None)


def grad_shape(lay, group, r):
    return (lay.nz, lay.ny, r, 4 * D) if group < 2 else (lay.nz, lay.ny, 4, r, D)


def span_of(lay, group, i, c, x):
    if group < 2:
        width = 512 // lay.nx
        if x is ALL:
            return pl.ds(pl.multiple_of(1024 * i + 512 * c, LANES), 512), None
        return pl.ds(pl.multiple_of(1024 * i + 512 * c + width * x, LANES), width), None
    width = 256 // lay.sub
    if x is ALL:
        return pl.ds(256 * i, 256), pl.ds(2 * c, 2)
    start = 256 * i + width * lax.rem(x, lay.sub)
    return pl.ds(pl.multiple_of(start, LANES), width), 2 * c + x // lay.sub


def view(lay, ref, group, i, c, x, z, y):
    cols, quarter = span_of(lay, group, i, c, x)
    if group < 2:
        return ref.at[z, y, :, cols]
    return ref.at[z, y, quarter, :, cols]


def shard_view(lay, ref, group, i, c, x):
    cols, quarter = span_of(lay, group, i, c, x)
    if group < 2:
        return ref.at[:, cols]
    return ref.at[quarter, :, cols]


def part_shape(lay, group, x_all, z_all, y_all, r):
    lead = ((lay.nz,) if z_all else ()) + ((lay.ny,) if y_all else ())
    if group < 2:
        return lead + (r, 512 if x_all else 512 // lay.nx)
    return lead + ((2, r, 256) if x_all else (r, 256 // lay.sub))


def greet(peers):
    sem = pltpu.get_barrier_semaphore()
    for peer in peers:
        pl.semaphore_signal(sem, inc=1, device_id=peer, device_id_type=MESH)


def wait_greetings(peers):
    pl.semaphore_wait(pltpu.get_barrier_semaphore(), len(peers))


def line_peers(lay):
    x, c, z, y = lay.coords()
    xs = [lay.device(wrap(x + k, lay.nx), c, z, y) for k in range(1, lay.nx)]
    ys = [lay.device(x, c, z, wrap(y + k, lay.ny)) for k in range(1, lay.ny)]
    zs = [lay.device(x, c, wrap(z + k, lay.nz), y) for k in range(1, lay.nz)]
    cs = [lay.device(x, 1 - c, z, y)]
    return xs, cs, zs, ys


def remote(src, dst, ssem, rsem, device):
    return pltpu.make_async_remote_copy(
        src_ref=src, dst_ref=dst, send_sem=ssem, recv_sem=rsem, device_id=device, device_id_type=MESH
    )


def start(copies):
    for copy in copies:
        copy.start()


def arrive(copies):
    for copy in copies:
        copy.wait_recv()


def sent(copies):
    for copy in copies:
        copy.wait_send()


def hbm(count):
    return [pl.BlockSpec(memory_space=pltpu.HBM)] * count


def dma(*shape):
    return pltpu.SemaphoreType.DMA(shape)


NT = (((1,), (1,)), ((), ()))
NN = (((1,), (0,)), ((), ()))
TN = (((0,), (0,)), ((), ()))
F32 = jnp.float32
BF = jnp.bfloat16


def mm(a, b, dims=NN):
    return lax.dot_general(a, b, dims, preferred_element_type=F32)


def norm_parts(values):
    middle = jnp.mean(values, -1, keepdims=True)
    centred = values - middle
    factor = lax.rsqrt(jnp.mean(centred * centred, -1, keepdims=True) + 1e-05)
    return centred * factor, factor


def small_plan(r):
    plan, at = [], 0
    for size, within in [(r, LANES)] * 5 + [(3 * r, HD), (4 * r, LANES)]:
        plan.append((at, size, math.gcd(size, within)))
        at += -(-size // LANES)
    return plan


SMALL_ROWS = 16


class Gather:
    def __init__(self, lay, us, gs, sems):
        (z_s, z_r, y_s, y_r, x_s, x_r, c_s, c_r) = sems
        x, c, z, y = lay.coords()
        xs, cs, zs, ys = line_peers(lay)
        self.stages = []
        for t, (g, i) in enumerate(CHUNKS):
            by_y, by_x = (ys, y_s, y_r), (xs, x_s, x_r)
            first, second = (by_y, by_x) if i < 2 else (by_x, by_y)
            middle = (x, ALL, ALL) if i < 2 else (ALL, ALL, y)
            steps = [
                ((zs, z_s, z_r), (x, z, y)),
                (first, (x, ALL, y)),
                (second, middle),
            ]
            stages = []
            for (peers, ss, rs), (px, pz, py) in steps:
                piece = view(lay, gs[g], g, i, c, px, pz, py)
                source = shard_view(lay, us[g], g, i, c, x) if len(stages) == 0 else piece
                stages.append(
                    [remote(source, piece, ss.at[t, k], rs.at[t, k], p) for k, p in enumerate(peers)]
                )
            piece = view(lay, gs[g], g, i, c, ALL, ALL, ALL)
            stages.append([remote(piece, piece, c_s.at[t], c_r.at[t], cs[0])])
            self.stages.append(stages)

    def issue(self, t, stage):
        start(self.stages[t][stage])

    def pass_on(self, t, stage):
        arrive(self.stages[t][stage - 1])
        start(self.stages[t][stage])

    def done(self, t):
        arrive(self.stages[t][3])

    def drain(self):
        for stages in self.stages:
            for copies in stages:
                sent(copies)


class Reduce:
    def __init__(self, lay, ps, fs, bufs, sems, wanted):
        (ca, ra1, rb1, ra2, rb2, ra3, rz, rx) = bufs
        (c_s, c_r, x_s, x_r, y_s, y_r, z_s, z_r, fx_s, fx_r, fc_s, fc_r) = sems
        x, c, z, y = lay.coords()
        xs, cs, zs, ys = line_peers(lay)
        other_x = [wrap(x + 1 + k, lay.nx) for k in range(lay.nx - 1)]
        other_y = [wrap(y + 1 + k, lay.ny) for k in range(lay.ny - 1)]
        other_z = [wrap(z + 1 + k, lay.nz) for k in range(lay.nz - 1)]
        self.copies, self.adds = {}, {}
        for t, stages in wanted.items():
            g, i = CHUNKS[t]
            p = ps[g]

            def along(pieces, slot, peers, ss, rs, t=t):
                return [
                    remote(piece, slot.at[k], ss.at[t, k], rs.at[t, k], peers[k])
                    for k, piece in enumerate(pieces)
                ]

            def into(dst, slot, count):
                return functools.partial(add_into, dst, [slot.at[k] for k in range(count)])

            def part(px, pz, py, p=p, g=g, i=i, core=c):
                return view(lay, p, g, i, core, px, pz, py)

            if 0 in stages:
                slot = ca[g].at[i]
                self.copies[t, 0] = [remote(part(ALL, ALL, ALL, core=1 - c), slot, c_s.at[t], c_r.at[t], cs[0])]
                self.adds[t, 1] = functools.partial(add_into, part(ALL, ALL, ALL), [slot])
            if 1 in stages and i < 2:
                slot = ra1[g].at[i]
                self.copies[t, 1] = along([part(k, ALL, ALL) for k in other_x], slot, xs, x_s, x_r)
                self.adds[t, 2] = into(part(x, ALL, ALL), slot, lay.nx - 1)
            elif 1 in stages:
                slot = rb1[g].at[0]
                self.copies[t, 1] = along([part(ALL, ALL, k) for k in other_y], slot, ys, y_s, y_r)
                self.adds[t, 2] = into(part(ALL, ALL, y), slot, lay.ny - 1)
            if t == LAST:
                self.copies[t, 2] = along([part(ALL, k, y) for k in other_z], rz, zs, z_s, z_r)
                own = part(ALL, z, y)
                self.adds[t, 3] = into(own, rz, lay.nz - 1)
                self.copies[t, 3] = [
                    remote(own, rx.at[x], x_s.at[t, k], x_r.at[t, k], peer) for k, peer in enumerate(xs)
                ]
                both = shard_view(lay, fs[g], g, i, c, ALL)
                self.adds[t, 4] = functools.partial(all_sum, both, own, rx, x)
                self.copies[t, 4] = [remote(both, both, fc_s.at[t], fc_r.at[t], cs[0])]
                continue
            if 2 in stages and i < 2:
                slot = ra2[g].at[i]
                self.copies[t, 2] = along([part(x, ALL, k) for k in other_y], slot, ys, y_s, y_r)
                self.adds[t, 3] = into(part(x, ALL, y), slot, lay.ny - 1)
            elif 2 in stages:
                slot = rb2[g].at[0]
                self.copies[t, 2] = along([part(k, ALL, y) for k in other_x], slot, xs, x_s, x_r)
                self.adds[t, 3] = into(part(x, ALL, y), slot, lay.nx - 1)
            if 3 in stages:
                slot = ra3[g].at[i]
                self.copies[t, 3] = along([part(x, k, y) for k in other_z], slot, zs, z_s, z_r)
                out = shard_view(lay, fs[g], g, i, c, x)
                self.adds[t, 4] = functools.partial(
                    set_sum, out, [part(x, z, y)] + [slot.at[k] for k in range(lay.nz - 1)]
                )
                self.copies[t, 4] = [
                    remote(out, out, fx_s.at[t, k], fx_r.at[t, k], peer) for k, peer in enumerate(xs)
                ]
                both = shard_view(lay, fs[g], g, i, c, ALL)
                self.copies[t, 5] = [remote(both, both, fc_s.at[t], fc_r.at[t], cs[0])]

    def settle(self, t, k):
        if (t, k - 1) in self.copies:
            arrive(self.copies[t, k - 1])
            if (t, k) in self.adds:
                self.adds[t, k]()

    def begin(self, t, k):
        start(self.copies.get((t, k), ()))

    def step(self, t, k):
        self.settle(t, k)
        if k < 6:
            self.begin(t, k)

    def drain(self):
        for group in self.copies.values():
            sent(group)


def all_sum(out, own, slots, at):
    slots[at] = own[...]
    set_sum(out, [slots.at[k] for k in range(slots.shape[0])])


def set_sum(out, srcs):
    total = srcs[0][...].astype(F32)
    for src in srcs[1:]:
        total = total + src[...].astype(F32)
    out[...] = total.astype(BF)


def add_into(dst, srcs):
    lead = dst.shape[:-2]

    def body(j, carry):
        index = []
        rest = j
        for size in reversed(lead):
            index.append(lax.rem(rest, size))
            rest = rest // size
        index = tuple(reversed(index))
        total = dst[index].astype(F32)
        for src in srcs:
            total = total + src[index].astype(F32)
        dst[index] = total.astype(BF)
        return carry

    lax.fori_loop(0, math.prod(lead), body, 0)


def rope(u, cos, low, high):
    return u * cos + pltpu.roll(u, LANES - 8, 1) * low + pltpu.roll(u, 8, 1) * high


def front_kernel(
    lay, rows,
    u_up, u_down, qkv_in, dense_in, tok_in, grad_in, seg, v0, v1, v2, v3, v4, v5, v6,
    g_up, g_down, p_out, prev_out, own_out, attn_hbm, vectors, up_add, att_sums,
    qkv, tok, grad, small, u_att, p_att, fg_prev, fg_own, attn_out, g_att, g_small, tok_halo, seg_halo, first_all, q_s, k_s, v_s, do_s, ctx_s, ctx_t,
    dq_s, dk_s, dv_s, cos_s, low_s, high_s, bias, dk_acc, dv_acc, qkv_add, s_s, w_s, d_s,
    local_sem, z_s, z_r, y_s, y_r, x_s, x_r, c_s, c_r, sm_s, sm_r, h_s, h_r, out_sem,
    ca, ra1, rb1, rc_s, rc_r, rx_s, rx_r, ry_s, ry_r, load_sem,
):
    span = 3 * rows
    r = qkv_in.shape[0]
    n_chunks = len(CHUNKS)
    x, c, z, y = lay.coords()
    xs, cs, zs, ys = line_peers(lay)
    total = lay.dp * lay.fsdp
    b = lax.axis_index("dp") * lay.fsdp + lax.axis_index("fsdp")

    def stream(k):
        t = wrap(b + k, total)
        return {"dp": t // lay.fsdp, "fsdp": lax.rem(t, lay.fsdp)}

    around = [stream(2), stream(-2), stream(1), stream(-1)]
    peers = xs + cs + zs + ys + around
    greet(peers)
    loads = [
        pltpu.make_async_copy(src, dst, load_sem.at[n])
        for n, (src, dst) in enumerate(
            ((qkv_in, qkv), (dense_in, u_att.at[:, pl.ds(3 * D, D)]), (tok_in, tok), (grad_in, grad))
        )
    ]
    start(loads)
    plan = small_plan(r)
    for (row, size, _), ref in zip(plan, (v0, v1, v2, v3, v4, v5, v6)):
        value = ref[...].astype(F32).reshape(1, size)
        for k in range(-(-size // LANES)):
            width = min(LANES, size - k * LANES)
            small[row + k : row + k + 1, :width] = value[:, k * LANES : k * LANES + width]
    loads[0].wait()
    left = lax.broadcasted_iota(jnp.int32, (r, LANES), 1) < HD
    for p in range(PAIRS):
        parts = [qkv[:, (3 * p + k) * LANES : (3 * p + k + 1) * LANES].astype(F32) for k in range(3)]
        kinds = (
            jnp.where(left, parts[0], parts[1]),
            pltpu.roll(jnp.where(left, parts[2], parts[0]), HD, 1),
            jnp.where(left, parts[1], parts[2]),
        )
        for k, part in enumerate(kinds):
            u_att[:, k * D + p * LANES : k * D + (p + 1) * LANES] = part.astype(BF)
    for copy in loads[1:]:
        copy.wait()
    gs = (g_att, g_up, g_down)
    us = (u_att, u_up, u_down)
    locals_ = []
    for t, (g, i) in enumerate(CHUNKS):
        locals_.append(
            pltpu.make_async_copy(
                shard_view(lay, us[g], g, i, c, x), view(lay, gs[g], g, i, c, x, z, y), local_sem.at[t]
            )
        )
    locals_.append(pltpu.make_async_copy(small, g_small.at[z, y], local_sem.at[n_chunks]))
    start(locals_)
    wait_greetings(peers)
    even = lax.rem(b, 2) == 0
    half = rows // 2
    halo, own, passed = [], [], []
    for k in range(2):
        part = pl.ds(k * half, half)
        halo.append(remote(tok.at[part], tok_halo.at[0, part], h_s.at[k], h_r.at[k], around[0]))
        own.append(remote(tok.at[part], tok_halo.at[1, part], h_s.at[2 + k], h_r.at[2 + k], around[2]))
        passed.append(
            remote(tok_halo.at[0, part], tok_halo.at[1, part], h_s.at[2 + k], h_r.at[2 + k], around[3])
        )
    segs = [
        remote(seg, seg_halo.at[0], h_s.at[4], h_r.at[4], around[0]),
        remote(seg, seg_halo.at[1], h_s.at[5], h_r.at[5], around[2]),
    ]
    small_z = [
        remote(small, g_small.at[z, y], sm_s.at[k], sm_r.at[k], p) for k, p in enumerate(zs)
    ]
    small_y = [
        remote(g_small.at[:, y], g_small.at[:, y], sm_s.at[lay.nz + k], sm_r.at[lay.nz + k], p)
        for k, p in enumerate(ys)
    ]
    net = Gather(lay, us, gs, (z_s, z_r, y_s, y_r, x_s, x_r, c_s, c_r))
    net.issue(0, 0)
    net.issue(2, 0)
    start(small_z)
    start(segs)
    net.issue(1, 0)

    def tables(k, carry):
        at = pl.ds(pl.multiple_of(k * 256, 256), 256)
        lane = lax.broadcasted_iota(jnp.int32, (256, LANES), 1) % HD
        row = lax.broadcasted_iota(jnp.int32, (256, LANES), 0) + k * 256
        place = lax.rem((b - 2) * rows + row + 4 * ROW, ROW).astype(F32)
        rate = jnp.exp((lane % 8).astype(F32) * (-math.log(10000.0) / 8.0))
        angle = place * rate
        sine = jnp.sin(angle)
        cos_s[at, :] = jnp.where(lane < ROT, jnp.cos(angle), 1.0)
        low_s[at, :] = jnp.where(lane < 8, -sine, 0.0)
        high_s[at, :] = jnp.where((lane >= 8) & (lane < ROT), sine, 0.0)
        return carry

    lax.fori_loop(0, 2, tables, 0)
    for t in (0, 2, 1, n_chunks):
        locals_[t].wait()
    net.pass_on(0, 1)
    lax.fori_loop(2, 3, tables, 0)
    net.pass_on(2, 1)
    lax.fori_loop(3, 5, tables, 0)
    arrive(small_z)
    start(small_y)
    net.pass_on(0, 2)
    net.pass_on(1, 1)
    halo[0].start()
    lax.fori_loop(5, span // 256, tables, 0)
    arrive(small_y)
    net.pass_on(2, 2)

    lane_row = lax.broadcasted_iota(jnp.int32, (1, LANES), 1)

    def line(first_row, size, unit, length, source):
        out = []
        for block in range(length // LANES):
            value = None
            for k in range(LANES // unit):
                owner, local = divmod(source(block * (LANES // unit) + k), size // unit)
                row, lane = divmod(local * unit, LANES)
                row += first_row
                piece = g_small[owner // lay.ny, owner % lay.ny, row : row + 1, :]
                if lane != k * unit:
                    piece = pltpu.roll(piece, (k * unit - lane) % LANES, 1)
                value = piece if value is None else jnp.where(lane_row // unit == k, piece, value)
            out.append(value)
        return jnp.concatenate(out, 1)

    def norm_rows(values):
        return norm_parts(values.astype(F32))[0]

    for j in range(5):
        vectors[j : j + 1, :] = line(*plan[j], D, lambda n: n)
    vectors[5:8, :] = jnp.zeros((3, D), F32)
    unit = plan[5][2]
    a_head = HD // unit

    def natural(n):
        kind, rest = divmod(n, D // unit)
        head, part = divmod(rest, a_head)
        return head * 3 * a_head + kind * a_head + part

    qkv_add[...] = line(*plan[5], 3 * D, natural)
    net.pass_on(1, 2)
    up_add[...] = line(*plan[6], FF, lambda n: n)

    def pass_halo(k):
        arrive([halo[k]])

        @pl.when(even)
        def _():
            own[k].start()

        @pl.when(jnp.logical_not(even))
        def _():
            passed[k].start()

    halo[1].start()
    gain, shift = vectors[0:1, :], vectors[1:2, :]
    own_rows = pl.ds(2 * rows, rows)
    first = (norm_rows(tok[...]) * gain + shift).astype(BF)
    first_all[own_rows, :] = first
    pass_halo(0)
    arrive(segs)
    least = jnp.maximum(0, 2 * rows - b * rows)
    keys_doc = jnp.concatenate([seg_halo[0], seg_halo[1], seg[...]], 1).astype(F32)
    keys_doc = jnp.broadcast_to(keys_doc, (LANES, span)).T
    query_doc = seg[0:1, :].astype(F32)

    for k in range(6):
        at = slice(k * 256, (k + 1) * 256)
        key_at = lax.broadcasted_iota(jnp.int32, (256, rows), 0) + k * 256
        query_at = lax.broadcasted_iota(jnp.int32, (256, rows), 1) + 2 * rows
        allowed = (keys_doc[at, 0:1] == query_doc) & (key_at <= query_at) & (key_at >= least)
        bias[at, :] = jnp.where(allowed, 0.0, -1e30)
    for t in range(3, n_chunks):
        locals_[t].wait()
    net.issue(5, 0)
    net.pass_on(0, 3)
    net.pass_on(2, 3)
    net.issue(3, 0)

    def weight(first_col, width):
        value = g_att[:, :, :, pl.ds(first_col, width)]
        return value.reshape(D, width)

    scale = 1.0 / math.sqrt(HD)

    def project(kind, j, at, out, factor):
        col = pl.multiple_of(kind * D + 256 * j, 256)
        value = mm(first_all[at, :], weight(col, 256)) + qkv_add[:, pl.ds(col, 256)]
        for k in range(2):
            u = value[:, k * LANES : (k + 1) * LANES]
            if kind < 2:
                u = rope(u, cos_s[at, :], low_s[at, :], high_s[at, :])
            if factor is not None:
                u = u * factor
            out[:, pl.ds(pl.multiple_of(256 * j + LANES * k, LANES), LANES)] = u.astype(BF)

    def own_queries(j, carry):
        project(0, j, own_rows, q_s, scale)
        return carry

    def own_keys(j, carry):
        project(1, j, own_rows, k_s.at[own_rows], None)
        return carry

    def own_values(j, carry):
        project(2, j, own_rows, v_s.at[own_rows], None)
        return carry

    net.done(0)
    lax.fori_loop(0, 3, own_queries, 0)
    lax.fori_loop(0, 1, own_keys, 0)
    pass_halo(1)
    net.pass_on(1, 3)
    net.issue(4, 0)
    net.done(2)
    do_s[...] = mm(grad[...], weight(3 * D, D), NT).astype(BF)
    lax.fori_loop(2, 3, own_values, 0)
    net.pass_on(5, 1)
    net.done(1)
    lax.fori_loop(1, 3, own_keys, 0)
    lax.fori_loop(0, 2, own_values, 0)
    own[0].wait_recv()
    net.pass_on(3, 1)

    def earlier_norms(k):
        for n in range(2):
            near = pl.ds(k * half, half)
            before = norm_rows(tok_halo[n, near, :]) * gain + shift
            first_all[pl.ds(n * rows + k * half, half), :] = before.astype(BF)

    earlier_norms(0)
    net.issue(8, 0)
    own[1].wait_recv()
    earlier_norms(1)
    net.pass_on(4, 1)
    net.pass_on(5, 2)

    def earlier_projections(j, carry):
        for k in range(2):
            at = pl.ds(k * rows, rows)
            project(1, j, at, k_s.at[at], None)
            project(2, j, at, v_s.at[at], None)
        return carry

    lax.fori_loop(0, 3, earlier_projections, 0)
    net.pass_on(3, 2)
    net.issue(6, 0)

    go, send, end = net.pass_on, net.issue, net.done
    later = [
        [(go, 8, 1), (send, 7, 0), (go, 4, 2)],
        [(go, 5, 3), (go, 6, 1), (go, 3, 3), (go, 7, 1)],
        [(go, 8, 2), (go, 6, 2)],
        [(go, 4, 3), (go, 7, 2)],
        [(go, 8, 3), (go, 6, 3)],
        [(go, 7, 3)],
    ]
    tile = 256

    def pair(p, carry):
        lanes = pl.ds(pl.multiple_of(p * LANES, LANES), LANES)
        v_t, k_t = v_s[:, lanes].T, k_s[:, lanes].T
        do_t = do_s[:, lanes].astype(F32).T
        lane = lax.broadcasted_iota(jnp.int32, (tile, LANES), 1)
        zero = jnp.zeros((), BF)
        units = [(t, hh) for t in range(rows // tile) for hh in range(2)]
        count = len(units)
        tops, totals, norms = [None] * count, [None] * count, [None] * count
        outs, dqs = [None] * count, [None] * count
        written = set()

        def masked(ref, u):
            t, hh = units[u]
            return jnp.where((lane // HD) == hh, ref[t * tile : (t + 1) * tile, lanes], zero)

        def pieces(u):
            kl = 2 * rows + (units[u][0] + 1) * tile
            return [slice(k * LANES, (k + 1) * LANES) for k in range(kl // LANES)]

        def scores(u, at, qm):
            t = units[u][0]
            st = mm(k_s[at, lanes], qm, NT) + bias[at, t * tile : (t + 1) * tile]
            s_s[u % 2, at, :] = st
            most = jnp.max(st, 0, keepdims=True)
            tops[u] = most if tops[u] is None else jnp.maximum(tops[u], most)

        def exponents(u, at):
            e = jnp.exp(s_s[u % 2, at, :] - tops[u])
            s_s[u % 2, at, :] = e
            part = jnp.sum(e, 0, keepdims=True)
            totals[u] = part if totals[u] is None else totals[u] + part

        def key_value_grads(u, at, qm, dom):
            dk, dv = mm(d_s[u % 2, at, :], qm), mm(w_s[u % 2, at, :], dom)
            if at.start in written:
                dk_acc[at, :] += dk
                dv_acc[at, :] += dv
            else:
                dk_acc[at, :] = dk
                dv_acc[at, :] = dv
                written.add(at.start)

        qm = masked(q_s, 0)
        for at in pieces(0):
            scores(0, at, qm)
        for u in range(count):
            t, hh = units[u]
            part = slice(hh * HD, (hh + 1) * HD)
            cols = slice(t * tile, (t + 1) * tile)
            kl = 2 * rows + (t + 1) * tile
            mine = pieces(u)
            after = pieces(u + 1) if u + 1 < count else []
            before = pieces(u - 1) if u > 0 else []
            if after:
                qm = masked(q_s, u + 1)
            for k in range(max(len(mine), len(after))):
                if k < len(after):
                    scores(u + 1, after[k], qm)
                if k < len(mine):
                    exponents(u, mine[k])
            norms[u] = 1.0 / totals[u]
            if before:
                q_last, do_last = masked(q_s, u - 1), masked(do_s, u - 1)
            for k in range(max(len(mine), len(before))):
                if k < len(before):
                    key_value_grads(u - 1, before[k], q_last, do_last)
                if k < len(mine):
                    w_s[u % 2, mine[k], :] = (s_s[u % 2, mine[k], :] * norms[u]).astype(BF)
            o_t = mm(v_t[part, :kl], w_s[u % 2, :kl, :])
            delta = jnp.sum(o_t * do_t[part, cols], 0, keepdims=True)
            outs[u] = o_t
            dom = masked(do_s, u)
            for at in mine:
                dp = mm(v_s[at, lanes], dom, NT)
                d_s[u % 2, at, :] = ((s_s[u % 2, at, :] * norms[u]) * (dp - delta)).astype(BF)
            dqs[u] = mm(k_t[part, :kl], d_s[u % 2, :kl, :])
            if hh == 0:
                continue
            o_pair = jnp.concatenate(outs[u - 1 : u + 1], 0)
            ctx_t[lanes, cols] = o_pair.astype(BF)
            ctx_s[cols, lanes] = o_pair.T.astype(BF)
            dq = jnp.concatenate(dqs[u - 1 : u + 1], 0).T * scale
            at = slice(2 * rows + t * tile, 2 * rows + (t + 1) * tile)
            dq_s[cols, lanes] = rope(dq, cos_s[at, :], -low_s[at, :], -high_s[at, :]).astype(BF)
        q_last, do_last = masked(q_s, count - 1), masked(do_s, count - 1)
        for at in pieces(count - 1):
            key_value_grads(count - 1, at, q_last, do_last)
        dk_s[:, lanes] = rope(dk_acc[...], cos_s[...], -low_s[...], -high_s[...]).astype(BF)
        dv_s[:, lanes] = dv_acc[...].astype(BF)
        for k in range(PAIRS):

            @pl.when(p == k)
            def _(k=k):
                for event, *where in later[k]:
                    event(*where)

        return carry

    lax.fori_loop(0, PAIRS, pair, 0)

    sums = Reduce(
        lay, (p_att,), None, ((ca,), (ra1,), (rb1,), None, None, None, None, None),
        (rc_s, rc_r, rx_s, rx_r, ry_s, ry_r) + (None,) * 6, {0: (0, 1), 1: (0,), 2: (0, 1)},
    )
    outs = []

    def leave(i):
        cols = pl.ds(1024 * i, 1024)
        copy = pltpu.make_async_copy(p_att.at[:, :, :, cols], p_out.at[:, :, :, cols], out_sem.at[i])
        copy.start()
        outs.append(copy)

    def put(kind, j, value):
        p_att[:, :, :, kind * D + 256 * j : kind * D + 256 * (j + 1)] = value.astype(BF).reshape(
            lay.nz, lay.ny, r, 256
        )

    def tile_of(ref, j):
        return ref[:, slice(256 * j, 256 * (j + 1))]

    def weight_grad(kind, j):
        if kind == 0:
            put(0, j, mm(first_all[own_rows, :], tile_of(dq_s, j), TN))
        elif kind == 3:
            put(3, j, mm(ctx_t[...], tile_of(grad, j)))
        else:
            put(kind, j, mm(first_all[...], tile_of((dk_s, dv_s)[kind - 1], j), TN))

    for kind, j in ((1, 0), (0, 0), (0, 1), (0, 2)):
        weight_grad(kind, j)
    sums.step(0, 0)
    for kind, j in ((2, 2), (3, 0), (3, 1), (3, 2)):
        weight_grad(kind, j)
    sums.step(0, 1)
    sums.step(2, 0)
    for kind, j in ((1, 1), (1, 2)):
        weight_grad(kind, j)
    sums.step(2, 1)
    for kind, j in ((2, 0), (2, 1)):
        weight_grad(kind, j)
    sums.step(1, 0)

    def earlier_grad(k, carry):
        at = pl.ds(pl.multiple_of(k * 256, 256), 256)
        value = mm(dk_s[at, :], weight(D, D), NT) + mm(dv_s[at, :], weight(2 * D, D), NT)
        fg_prev[at, :] = value.astype(BF)
        return carry

    lax.fori_loop(0, 2 * rows // 256, earlier_grad, 0)
    outs.append(pltpu.make_async_copy(fg_prev, prev_out, out_sem.at[3]))
    outs[-1].start()
    sums.settle(1, 1)
    leave(1)
    for k in range(rows // 256):
        at = slice(2 * rows + 256 * k, 2 * rows + 256 * (k + 1))
        near = slice(256 * k, 256 * (k + 1))
        fg_own[near, :] = (
            mm(dk_s[at, :], weight(D, D), NT)
            + mm(dv_s[at, :], weight(2 * D, D), NT)
            + mm(dq_s[near, :], weight(0, D), NT)
        )
    outs.append(pltpu.make_async_copy(fg_own, own_out, out_sem.at[4]))
    outs[-1].start()

    def attention_out(j, carry):
        col = pl.multiple_of(256 * j, 256)
        attn_out[:, pl.ds(col, 256)] = mm(ctx_s[...], weight(pl.multiple_of(3 * D + col, 256), 256))
        return carry

    lax.fori_loop(0, 3, attention_out, 0)
    outs.append(pltpu.make_async_copy(attn_out, attn_hbm, out_sem.at[5]))
    outs[-1].start()
    for k, ref in enumerate((dq_s, dk_s, dv_s)):
        att_sums[k : k + 1, :] = jnp.sum(ref[...].astype(F32), 0, keepdims=True)
    att_sums[3:8, :] = jnp.zeros((5, D), F32)
    sums.settle(0, 2)
    leave(0)
    sums.settle(2, 2)
    leave(2)
    sums.drain()
    for t in range(3, 9):
        net.done(t)
    net.drain()
    sent(small_z + small_y + segs + halo + own)
    for copy in outs:
        copy.wait()


def front(lay, u_up, u_down, qkv, dense, tok, grad, seg, vectors):
    rows = tok.shape[0]
    span = 3 * rows
    r = qkv.shape[0]
    n = len(CHUNKS)
    outs = (
        jax.ShapeDtypeStruct(grad_shape(lay, 1, r), BF),
        jax.ShapeDtypeStruct(grad_shape(lay, 2, r), BF),
        jax.ShapeDtypeStruct(grad_shape(lay, 0, r), BF),
        jax.ShapeDtypeStruct((2 * rows, D), BF),
        jax.ShapeDtypeStruct((rows, D), F32),
        jax.ShapeDtypeStruct((rows, D), F32),
        jax.ShapeDtypeStruct((8, D), F32),
        jax.ShapeDtypeStruct((1, FF), F32),
        jax.ShapeDtypeStruct((8, D), F32),
    )
    vmem = pl.BlockSpec(memory_space=pltpu.VMEM)
    lx, ly, lz = max(1, lay.nx - 1), max(1, lay.ny - 1), max(1, lay.nz - 1)

    def v(shape, dtype=BF):
        return pltpu.VMEM(shape, dtype)

    return pl.pallas_call(
        functools.partial(front_kernel, lay, rows),
        name="front",
        out_shape=outs,
        in_specs=hbm(6) + [vmem] * (1 + len(vectors)),
        out_specs=tuple(hbm(6)) + (vmem,) * 3,
        scratch_shapes=[
            v((r, 3 * D)), v((rows, D)), v((rows, D)), v((SMALL_ROWS, LANES), F32), v((r, 4 * D)), v(grad_shape(lay, 0, r)), v((2 * rows, D)), v((rows, D), F32), v((rows, D), F32),
            v(grad_shape(lay, 0, r)), v((lay.nz, lay.ny, SMALL_ROWS, LANES), F32), v((2, rows, D)),
            v((2, 1, rows), jnp.int32), v((span, D)), v((rows, D)), v((span, D)),
            v((span, D)), v((rows, D)), v((rows, D)), v((D, rows)), v((rows, D)), v((span, D)),
            v((span, D)), v((span, LANES), F32), v((span, LANES), F32), v((span, LANES), F32),
            v((span, rows), F32), v((span, LANES), F32), v((span, LANES), F32), v((1, 3 * D), F32),
            v((2, span, 256), F32), v((2, span, 256)), v((2, span, 256)),
            dma(n + 1), dma(n, lz), dma(n, lz), dma(n, ly), dma(n, ly), dma(n, lx), dma(n, lx),
            dma(n), dma(n), dma(lay.nz + ly), dma(lay.nz + ly), dma(6), dma(6), dma(6),
            v((3,) + part_shape(lay, 0, True, True, True, r)),
            v((1, lx) + part_shape(lay, 0, False, True, True, r)),
            v((1, ly) + part_shape(lay, 0, True, True, False, r)),
            dma(3), dma(3), dma(3, lx), dma(3, lx), dma(3, ly), dma(3, ly), dma(4),
        ],
        compiler_params=pltpu.CompilerParams(
            collective_id=0, has_side_effects=True, vmem_limit_bytes=VMEM_LIMIT
        ),
    )(u_up, u_down, qkv, dense, tok, grad, seg, *vectors)


def norm_back(grad, gain, normed, factor):
    inner = grad * gain
    return factor * (
        inner
        - jnp.mean(inner, -1, keepdims=True)
        - normed * jnp.mean(inner * normed, -1, keepdims=True)
    )


FF_CHUNKS = FF // D


def back_kernel(
    lay, rows, docs,
    g_up, g_down, p_in, prev_in, own_in, attn_in, tok_in, grad_in, vectors, up_add, att_sums, seg,
    out_hbm, input_hbm, att_hbm, up_hbm, down_hbm, vec_out,
    tok, grad, output, input_grad, f_att, f_up, f_down, p_att, fg_prev, fg_own, attn_out, p_up, p_down, w_up, w_down, second_in, second_t, act_s, pg_s, sg_acc, hop, home,
    ca, ra1, rb1, ra2, rb2, ra3, rz, rx, v_c, v_x, v_y, v_z, *sems,
):
    (c_s, c_r, x_s, x_r, y_s, y_r, z_s, z_r, fx_s, fx_r, fc_s, fc_r, v_s, v_r, w_sem, h_s, h_r, in_sem, out_sem) = sems
    r = p_in.shape[2]
    x, c, z, y = lay.coords()
    xs, cs, zs, ys = line_peers(lay)
    total = lay.dp * lay.fsdp
    b = lax.axis_index("dp") * lay.fsdp + lax.axis_index("fsdp")

    def stream(k):
        t = wrap(b + k, total)
        return {"dp": t // lay.fsdp, "fsdp": lax.rem(t, lay.fsdp)}

    around = [stream(2), stream(-2), stream(1), stream(-1)]
    near_z = lay.nz // FF_CHUNKS
    loads = []
    for k in range(FF_CHUNKS):
        slot = k % 2
        loads.append(
            (
                pltpu.make_async_copy(
                    g_up.at[:, :, :, pl.ds(D * k, D)], w_up.at[slot], w_sem.at[0, k]
                ),
                pltpu.make_async_copy(
                    g_down.at[pl.ds(near_z * k, near_z)], w_down.at[slot], w_sem.at[1, k]
                ),
            )
        )
    peers = xs + cs + zs + ys + around
    greet(peers)
    taken = [
        pltpu.make_async_copy(
            p_in.at[:, :, :, pl.ds(1024 * i, 1024)], p_att.at[:, :, :, pl.ds(1024 * i, 1024)],
            in_sem.at[i],
        )
        for i in range(3)
    ]
    taken.append(pltpu.make_async_copy(prev_in, fg_prev, in_sem.at[3]))
    taken.append(pltpu.make_async_copy(attn_in, attn_out, in_sem.at[4]))
    taken.append(pltpu.make_async_copy(own_in, fg_own, in_sem.at[5]))
    taken.append(pltpu.make_async_copy(tok_in, tok, in_sem.at[6]))
    taken.append(pltpu.make_async_copy(grad_in, grad, in_sem.at[7]))
    start(taken[:4])
    start(taken[6:])
    start(loads[0])
    start(taken[4:6])
    start(loads[1])
    wait_greetings(peers)
    wanted = {t: (0, 1, 2, 3) for t in range(3, len(CHUNKS))}
    wanted.update({0: (2, 3), 1: (1, 2, 3), 2: (2, 3)})
    net = Reduce(
        lay, (p_att, p_up, p_down), (f_att, f_up, f_down),
        ((None,) + tuple(ca), ra1, (None,) + tuple(rb1), ra2, rb2, ra3, rz, rx), sems[:12], wanted,
    )
    for t, k in ((1, 1), (2, 2), (0, 2)):
        taken[t].wait()
        net.begin(t, k)
    taken[3].wait()
    even = lax.rem(b, 2) == 0
    quarter = rows // 4
    to_next, to_last, to_owner = [], [], []
    for k in range(4):
        near = fg_prev.at[pl.ds(rows + k * quarter, quarter)]
        far = fg_prev.at[pl.ds(k * quarter, quarter)]
        part = pl.ds(k * quarter, quarter)
        to_next.append(remote(near, hop.at[part], h_s.at[k], h_r.at[k], around[2]))
        to_last.append(remote(near, hop.at[part], h_s.at[k], h_r.at[k], around[3]))
        to_owner.append(remote(far, home.at[part], h_s.at[4 + k], h_r.at[4 + k], around[1]))

    def hop_halo(k):
        @pl.when(even)
        def _():
            to_next[k].start()

        @pl.when(jnp.logical_not(even))
        def _():
            to_last[k].start()

    def forward_halo(k):
        to_last[k].wait_recv()
        at = pl.ds(k * quarter, quarter)

        @pl.when(jnp.logical_not(even))
        def _():
            fg_prev[at, :] = (fg_prev[at, :].astype(F32) + hop[at, :].astype(F32)).astype(BF)

        to_owner[k].start()

    hop_halo(0)
    hop_halo(1)

    gain_first, gain_second = vectors[0:1, :], vectors[2:3, :]
    taken[6].wait()
    taken[7].wait()
    normed, factor = norm_parts(tok[...].astype(F32))
    value = (normed * gain_second + vectors[3:4, :]).astype(BF)
    second_in[...] = value
    second_t[...] = value.T
    cot = grad[...].astype(F32)
    taken[4].wait()
    taken[5].wait()
    output_base = attn_out
    output_base[...] = attn_out[...] + tok[...].astype(F32) + vectors[4:5, :]
    sg_acc[...] = jnp.zeros_like(sg_acc)
    mine = v_c.at[c]
    mine[...] = jnp.zeros((16, D), F32)

    step = net.step
    events = [
        [],
        [(step, 0, 3)],
        [(hop_halo, 2)],
        [(step, 3, 0), (step, 1, 2), (forward_halo, 0)],
        [(step, 3, 1), (step, 2, 3), (hop_halo, 3)],
        [(step, 4, 0), (forward_halo, 1)],
        [(step, 4, 1), (step, 0, 4)],
        [(step, 8, 0), (step, 6, 0), (step, 5, 0), (step, 7, 0), (step, 2, 4)],
    ]
    root = math.sqrt(0.5)
    level = 1.0 / math.sqrt(2.0 * math.pi)

    def chunk(k, squares):
        slot = lax.rem(k, 2)
        for n in range(FF_CHUNKS):

            @pl.when(k == n)
            def _(n=n):
                loads[n][0].wait()
                loads[n][1].wait()

        down = w_down[slot].reshape(D, D)
        for j in range(3):
            tile = slice(256 * j, 256 * (j + 1))
            col = pl.ds(pl.multiple_of(D * k + 256 * j, 256), 256)
            pre = mm(second_in[...], w_up[slot, :, :, :, tile].reshape(D, 256)) + up_add[:, col]
            hidden = mm(grad[...], down[tile, :], NT)
            half = 0.5 + 0.5 * lax.erf(pre * root)
            act = (pre * half).astype(BF)
            slope = half + pre * jnp.exp(-0.5 * pre * pre) * level
            pg = (hidden * slope).astype(BF)
            act_s[:, tile] = act
            pg_s[:, tile] = pg
            wide = act.astype(F32)
            squares = squares + jnp.sum(wide * wide, -1, keepdims=True)
            v_c[c, pl.ds(8 + k, 1), tile] = jnp.sum(pg.astype(F32), 0, keepdims=True)

        def hook(half):
            for n in range(FF_CHUNKS):

                @pl.when(k == n)
                def _(n=n):
                    if half == 1 and n + 2 < FF_CHUNKS:
                        start(loads[n + 2])
                    for event, *where in events[2 * n + half]:
                        event(*where)

        hook(0)
        p_up[:, :, :, pl.ds(pl.multiple_of(D * k, 256), D)] = (
            mm(second_t[...], pg_s[...]).astype(BF).reshape(lay.nz, lay.ny, r, D)
        )
        p_down[pl.ds(near_z * k, near_z)] = (
            mm(act_s[...].T, grad[...]).astype(BF).reshape(near_z, lay.ny, 4, r, D)
        )
        output_base[...] += mm(act_s[...], down)
        sg_acc[...] += mm(pg_s[...], w_up[slot].reshape(D, D), NT)
        hook(1)
        return squares

    squares = lax.fori_loop(0, FF_CHUNKS, chunk, jnp.zeros((rows, 1), F32))
    run = lambda *pairs: [step(t, k) for t, k in pairs]
    run((8, 1), (6, 1), (3, 2), (1, 3))
    output[...] = output_base[...].astype(BF)
    left = []

    def leave(k, ref, target):
        copy = pltpu.make_async_copy(ref, target, out_sem.at[k])
        copy.start()
        left.append(copy)

    leave(0, output, out_hbm)
    forward_halo(2)
    cot_sum = jnp.sum(grad[...].astype(F32), 0, keepdims=True)
    forward_halo(3)
    def put(k, value):
        v_c[c, k : k + 1, :] = value

    put(4, cot_sum)
    for k in range(3):
        put(5 + k, att_sums[k : k + 1, :])
    cot = grad[...].astype(F32)
    token_norm = squares * jnp.sum(cot * cot, -1, keepdims=True) * (1.0 / (FF * D))
    docs_of = jnp.broadcast_to(seg[...].astype(F32), (LANES, rows)).T[:, 0:1]
    doc = lax.broadcasted_iota(jnp.int32, (rows, D), 1).astype(F32)
    member = jnp.where((docs_of == doc) & (doc < docs), 1.0, 0.0)
    put(12, jnp.sum(token_norm * member, 0, keepdims=True))
    put(13, jnp.sum(member, 0, keepdims=True))
    run((4, 2), (5, 1), (7, 1), (8, 2), (1, 4))
    keep = jnp.where(even, 1.0, 0.0).astype(F32)

    def norms(k):
        to_owner[k].wait_recv()
        at = slice(k * quarter, (k + 1) * quarter)
        first_grad = fg_own[at, :] + home[at, :].astype(F32) + hop[at, :].astype(F32) * keep
        second_grad = sg_acc[at, :]
        normed, factor = norm_parts(tok[at, :].astype(F32))
        input_grad[at, :] = (
            grad[at, :].astype(F32)
            + norm_back(first_grad, gain_first, normed, factor)
            + norm_back(second_grad, gain_second, normed, factor)
        ).astype(BF)
        sums = [first_grad * normed, first_grad, second_grad * normed, second_grad]
        return [jnp.sum(value, 0, keepdims=True) for value in sums]

    def add_up(left, right):
        return [p + q for p, q in zip(left, right)]

    sums = norms(0)
    run((3, 3))
    sums = add_up(sums, norms(1))
    run((6, 2))
    sums = add_up(sums, norms(2))
    run((4, 3))
    sums = add_up(sums, norms(3))
    leave(1, input_grad, input_hbm)
    for k in range(4):
        put(k, sums[k])
    run((8, 3))

    at = [0, 1, lay.nx, lay.nx + lay.ny - 1]

    def spread(ref, own, peers, base):
        return [
            remote(ref.at[own], ref.at[own], v_s.at[base + k], v_r.at[base + k], p)
            for k, p in enumerate(peers)
        ]

    vec_c = spread(v_c, c, cs, at[0])
    vec_x = spread(v_x, x, xs, at[1])
    vec_y = spread(v_y, y, ys, at[2])
    vec_z = spread(v_z, z, zs, at[3])

    def add_all(ref, size):
        value = ref[0]
        for k in range(1, size):
            value = value + ref[k]
        return value

    start(vec_c)
    run((7, 2))
    arrive(vec_c)
    v_x[x] = add_all(v_c, 2)
    start(vec_x)
    run((5, 2), (6, 3), (3, 4), (5, 3), (7, 3))
    arrive(vec_x)
    v_y[y] = add_all(v_x, lay.nx)
    start(vec_y)
    run((4, 4), (8, 4))
    arrive(vec_y)
    v_z[z] = add_all(v_y, lay.ny)
    start(vec_z)
    run((0, 5), (1, 5), (2, 5), (3, 5), (4, 5), (6, 4), (5, 4), (6, 5), (5, 5))
    run((0, 6), (1, 6), (2, 6))
    leave(2, f_att, att_hbm)
    run((7, 4), (3, 6), (4, 6), (5, 6))
    leave(3, f_up, up_hbm)
    arrive(vec_z)
    vec_out[...] = add_all(v_z, lay.nz)
    run((8, 5), (7, 5), (6, 6), (8, 6), (7, 6))
    leave(4, f_down, down_hbm)
    net.drain()
    sent(vec_c + vec_x + vec_y + vec_z)
    sent(to_next + to_owner)
    for copy in left:
        copy.wait()


def back(lay, g_up, g_down, p_att, fg_prev, fg_own, attn_out, vectors, up_add, att_sums, tok, grad, seg):
    rows = tok.shape[0]
    r = p_att.shape[2]
    n = len(CHUNKS)
    docs = DOC_DEV * lay.dp * lay.fsdp
    outs = (
        jax.ShapeDtypeStruct((rows, D), BF),
        jax.ShapeDtypeStruct((rows, D), BF),
        jax.ShapeDtypeStruct((r, 4 * D), BF),
        jax.ShapeDtypeStruct((r, 4 * D), BF),
        jax.ShapeDtypeStruct((4, r, D), BF),
        jax.ShapeDtypeStruct((16, D), F32),
    )
    lx, ly, lz = max(1, lay.nx - 1), max(1, lay.ny - 1), max(1, lay.nz - 1)

    def v(shape, dtype=BF):
        return pltpu.VMEM(shape, dtype)

    def bufs(chunks, peers, x_all, z_all, y_all, first=0):
        return [
            v((chunks,) + peers + part_shape(lay, g, x_all, z_all, y_all, r)) for g in range(first, 3)
        ]

    scratch = [
        v((rows, D)), v((rows, D)), v((rows, D)), v((rows, D)), v((r, 4 * D)), v((r, 4 * D)), v((4, r, D)),
        v(grad_shape(lay, 0, r)), v((2 * rows, D)), v((rows, D), F32), v((rows, D), F32),
        v(grad_shape(lay, 1, r)), v(grad_shape(lay, 2, r)),
        v((2, lay.nz, lay.ny, r, D)), v((2, lay.nz // FF_CHUNKS, lay.ny, 4, r, D)),
        v((rows, D)), v((D, rows)), v((rows, D)), v((rows, D)), v((rows, D), F32),
        v((rows, D)), v((rows, D)),
        bufs(3, (), True, True, True, 1),
        bufs(2, (lx,), False, True, True),
        bufs(1, (ly,), True, True, False, 1),
        bufs(2, (ly,), False, True, False),
        bufs(1, (lx,), False, True, False),
        bufs(3, (lz,), False, False, False),
        v((lz,) + part_shape(lay, 2, True, False, False, r)),
        v((lay.nx,) + part_shape(lay, 2, True, False, False, r)),
    ]
    vecs = [v((k, 16, D), F32) for k in (2, lay.nx, lay.ny, lay.nz)]
    nv = 1 + lay.nx + lay.ny + lay.nz
    sems = [
        dma(n), dma(n), dma(n, lx), dma(n, lx), dma(n, ly), dma(n, ly), dma(n, lz), dma(n, lz),
        dma(n, lx), dma(n, lx), dma(n), dma(n), dma(nv), dma(nv), dma(2, FF_CHUNKS), dma(8), dma(8), dma(8), dma(5),
    ]
    vmem = pl.BlockSpec(memory_space=pltpu.VMEM)
    return pl.pallas_call(
        functools.partial(back_kernel, lay, rows, docs),
        name="back",
        out_shape=outs,
        in_specs=hbm(8) + [vmem] * 4,
        out_specs=tuple(hbm(5)) + (vmem,),
        scratch_shapes=scratch + vecs + sems,
        compiler_params=pltpu.CompilerParams(
            collective_id=1, has_side_effects=True, vmem_limit_bytes=VMEM_LIMIT
        ),
    )(g_up, g_down, p_att, fg_prev, fg_own, attn_out, tok, grad, vectors, up_add, att_sums, seg)


def finish_kernel(
    lay, docs, r, f_att, f_up, f_down, vec, out_in, grad_in,
    output, input_grad, fg, fb, sg, sb, qkv_w, qkv_b, dense_w, up_w, up_b, down_w, ob, norms,
):
    output[...] = out_in[...]
    input_grad[...] = grad_in[...]
    shard = lax.axis_index("fsdp")

    def by_head(row_count, kind):
        left = lax.broadcasted_iota(jnp.int32, (row_count, LANES), 1) < HD
        for p in range(PAIRS):
            q, k, v = (kind(n, p) for n in range(3))
            turned = pltpu.roll(k, HD, 1)
            yield jnp.where(left, q, turned)
            yield jnp.where(left, v, q)
            yield jnp.where(left, turned, v)

    def block(k, p):
        return f_att[:, k * D + p * LANES : k * D + (p + 1) * LANES].astype(F32)

    for n, value in enumerate(by_head(r, block)):
        qkv_w[:, n * LANES : (n + 1) * LANES] = value
    dense_w[...] = f_att[:, 3 * D :].astype(F32)
    up_w[...] = f_up[...].astype(F32)
    down_w[...] = f_down[...].astype(F32)

    def own(row, width):
        length = row.shape[1]
        wide = jnp.broadcast_to(row, (8, length))
        turned = pltpu.roll(wide, lax.rem(length - shard * width, length), 1)
        return turned[0:1, :width].reshape(width)

    for k, ref in enumerate((fg, fb, sg, sb, ob)):
        ref[...] = own(vec[k : k + 1, :], r)
    bias = list(by_head(1, lambda k, p: vec[5 + k : 6 + k, p * LANES : (p + 1) * LANES]))
    qkv_b[...] = own(jnp.concatenate(bias, 1), 3 * r)
    up_b[...] = own(jnp.concatenate([vec[8 + k : 9 + k, :] for k in range(4)], 1), 4 * r)
    norms[...] = (vec[12:13, :docs] / vec[13:14, :docs]).reshape(docs)


def finish(lay, output, input_grad, f_att, f_up, f_down, vec):
    r = f_att.shape[0]
    docs = DOC_DEV * lay.dp * lay.fsdp
    vmem = pl.BlockSpec(memory_space=pltpu.VMEM)
    shapes = [
        (r,), (r,), (r,), (r,), (r, 3 * D), (3 * r,), (r, D), (r, FF), (4 * r,), (4, r, D), (r,), (docs,),
    ]
    return pl.pallas_call(
        functools.partial(finish_kernel, lay, docs, r),
        name="finish",
        out_shape=tuple(jax.ShapeDtypeStruct(v.shape, v.dtype) for v in (output, input_grad))
        + tuple(jax.ShapeDtypeStruct(shape, F32) for shape in shapes),
        in_specs=[vmem] * 6,
        out_specs=(vmem,) * (2 + len(shapes)),
        compiler_params=pltpu.CompilerParams(vmem_limit_bytes=VMEM_LIMIT),
    )(f_att, f_up, f_down, vec, output, input_grad)


def per_device(
    lay, tokens, seg_ids, out_grad, first_gain, first_bias, second_gain, second_bias,
    qkv_weight, qkv_bias, dense_weight, up_weight, up_bias, down_weight, out_bias,
):
    rows = tokens.shape[0]
    r = qkv_weight.shape[0]
    vectors = (first_gain, first_bias, second_gain, second_bias, out_bias, qkv_bias, up_bias)
    seg_row = seg_ids.reshape(1, rows)
    passed = front(
        lay, up_weight, down_weight.reshape(4, r, D), qkv_weight, dense_weight, tokens,
        out_grad, seg_row, vectors,
    )
    summed = back(lay, *passed, tokens, out_grad, seg_row)
    (output, input_grad, fg, fb, sg, sb, qkv_w, qkv_b, dense_w, up_w, up_b, down_w, ob, norms) = finish(
        lay, *summed
    )
    return (
        output, input_grad, fg, fb, sg, sb, qkv_w, qkv_b, dense_w, up_w, up_b,
        down_w.reshape(4 * r, D), ob, norms,
    )


def solution(mesh):
    lay = Layout(mesh.shape["dp"], mesh.shape["fsdp"])
    both = P(("dp", "fsdp"))
    split = P("fsdp")
    in_specs = (both, both, both) + (split,) * 11
    out_specs = (both, both) + (split,) * 11 + (P(),)
    return jax.shard_map(
        functools.partial(per_device, lay), mesh=mesh, in_specs=in_specs, out_specs=out_specs,
        check_vma=False,
    )
```

```python
import functools
import math

import jax
import jax.numpy as jnp
from jax import lax
from jax.experimental import pallas as pl
from jax.experimental.pallas import tpu as pltpu
from jax.sharding import PartitionSpec as P

D = 768
H = 12
HD = 64
FF = 3072
ROT = 16
ROW = 2048
DOC_DEV = 2
LANES = 128
PAIRS = D // LANES
MESH = pl.DeviceIdType.MESH
VMEM_LIMIT = 60 * 1024 * 1024


class Layout:
    def __init__(self, dp, fsdp):
        self.dp, self.fsdp = dp, fsdp
        self.nc = 2
        self.nx = dp // 2
        ny = 1
        while (2 * ny) * (2 * ny) <= fsdp:
            ny *= 2
        self.ny, self.nz = ny, fsdp // ny
        self.sub = max(1, self.nx // 2)
        self.unit = 4 // self.nx
        self.down_unit = 2 // self.sub

    def coords(self):
        d, f = lax.axis_index("dp"), lax.axis_index("fsdp")
        return d // 2, d % 2, f // self.ny, f % self.ny

    def device(self, x, c, z, y):
        return {"dp": x * 2 + c, "fsdp": z * self.ny + y}


def wrap(value, size):
    return lax.rem(value + size, size)


CHUNKS = tuple((g, i) for g in range(3) for i in range(3))
LAST = len(CHUNKS) - 1
ALL = slice(None)


def grad_shape(lay, group, r):
    return (lay.nz, lay.ny, r, 4 * D) if group < 2 else (lay.nz, lay.ny, 4, r, D)


def span_of(lay, group, i, c, x):
    if group < 2:
        width = 512 // lay.nx
        if x is ALL:
            return pl.ds(pl.multiple_of(1024 * i + 512 * c, LANES), 512), None
        return pl.ds(pl.multiple_of(1024 * i + 512 * c + width * x, LANES), width), None
    width = 256 // lay.sub
    if x is ALL:
        return pl.ds(256 * i, 256), pl.ds(2 * c, 2)
    start = 256 * i + width * lax.rem(x, lay.sub)
    return pl.ds(pl.multiple_of(start, LANES), width), 2 * c + x // lay.sub


def view(lay, ref, group, i, c, x, z, y):
    cols, quarter = span_of(lay, group, i, c, x)
    if group < 2:
        return ref.at[z, y, :, cols]
    return ref.at[z, y, quarter, :, cols]


def shard_view(lay, ref, group, i, c, x):
    cols, quarter = span_of(lay, group, i, c, x)
    if group < 2:
        return ref.at[:, cols]
    return ref.at[quarter, :, cols]


def part_shape(lay, group, x_all, z_all, y_all, r):
    lead = ((lay.nz,) if z_all else ()) + ((lay.ny,) if y_all else ())
    if group < 2:
        return lead + (r, 512 if x_all else 512 // lay.nx)
    return lead + ((2, r, 256) if x_all else (r, 256 // lay.sub))


def greet(peers):
    sem = pltpu.get_barrier_semaphore()
    for peer in peers:
        pl.semaphore_signal(sem, inc=1, device_id=peer, device_id_type=MESH)


def wait_greetings(peers):
    pl.semaphore_wait(pltpu.get_barrier_semaphore(), len(peers))


def line_peers(lay):
    x, c, z, y = lay.coords()
    xs = [lay.device(wrap(x + k, lay.nx), c, z, y) for k in range(1, lay.nx)]
    ys = [lay.device(x, c, z, wrap(y + k, lay.ny)) for k in range(1, lay.ny)]
    zs = [lay.device(x, c, wrap(z + k, lay.nz), y) for k in range(1, lay.nz)]
    cs = [lay.device(x, 1 - c, z, y)]
    return xs, cs, zs, ys


def remote(src, dst, ssem, rsem, device):
    return pltpu.make_async_remote_copy(
        src_ref=src, dst_ref=dst, send_sem=ssem, recv_sem=rsem, device_id=device, device_id_type=MESH
    )


def start(copies):
    for copy in copies:
        copy.start()


def arrive(copies):
    for copy in copies:
        copy.wait_recv()


def sent(copies):
    for copy in copies:
        copy.wait_send()


def hbm(count):
    return [pl.BlockSpec(memory_space=pltpu.HBM)] * count


def dma(*shape):
    return pltpu.SemaphoreType.DMA(shape)


NT = (((1,), (1,)), ((), ()))
NN = (((1,), (0,)), ((), ()))
TN = (((0,), (0,)), ((), ()))
F32 = jnp.float32
BF = jnp.bfloat16


def mm(a, b, dims=NN):
    return lax.dot_general(a, b, dims, preferred_element_type=F32)


def norm_parts(values):
    middle = jnp.mean(values, -1, keepdims=True)
    centred = values - middle
    factor = lax.rsqrt(jnp.mean(centred * centred, -1, keepdims=True) + 1e-05)
    return centred * factor, factor


def small_plan(r):
    plan, at = [], 0
    for size, within in [(r, LANES)] * 5 + [(3 * r, HD), (4 * r, LANES)]:
        plan.append((at, size, math.gcd(size, within)))
        at += -(-size // LANES)
    return plan


SMALL_ROWS = 16


class Gather:
    def __init__(self, lay, us, gs, sems):
        (z_s, z_r, y_s, y_r, x_s, x_r, c_s, c_r) = sems
        x, c, z, y = lay.coords()
        xs, cs, zs, ys = line_peers(lay)
        self.stages = []
        for t, (g, i) in enumerate(CHUNKS):
            by_y, by_x = (ys, y_s, y_r), (xs, x_s, x_r)
            first, second = (by_y, by_x) if i < 2 else (by_x, by_y)
            middle = (x, ALL, ALL) if i < 2 else (ALL, ALL, y)
            steps = [
                ((zs, z_s, z_r), (x, z, y)),
                (first, (x, ALL, y)),
                (second, middle),
            ]
            stages = []
            for (peers, ss, rs), (px, pz, py) in steps:
                piece = view(lay, gs[g], g, i, c, px, pz, py)
                source = shard_view(lay, us[g], g, i, c, x) if len(stages) == 0 else piece
                stages.append(
                    [remote(source, piece, ss.at[t, k], rs.at[t, k], p) for k, p in enumerate(peers)]
                )
            piece = view(lay, gs[g], g, i, c, ALL, ALL, ALL)
            stages.append([remote(piece, piece, c_s.at[t], c_r.at[t], cs[0])])
            self.stages.append(stages)

    def issue(self, t, stage):
        start(self.stages[t][stage])

    def pass_on(self, t, stage):
        arrive(self.stages[t][stage - 1])
        start(self.stages[t][stage])

    def done(self, t):
        arrive(self.stages[t][3])

    def drain(self):
        for stages in self.stages:
            for copies in stages:
                sent(copies)


class Reduce:
    def __init__(self, lay, ps, fs, bufs, sems, wanted):
        (ca, ra1, rb1, ra2, rb2, ra3, rz, rx) = bufs
        (c_s, c_r, x_s, x_r, y_s, y_r, z_s, z_r, fx_s, fx_r, fc_s, fc_r) = sems
        x, c, z, y = lay.coords()
        xs, cs, zs, ys = line_peers(lay)
        other_x = [wrap(x + 1 + k, lay.nx) for k in range(lay.nx - 1)]
        other_y = [wrap(y + 1 + k, lay.ny) for k in range(lay.ny - 1)]
        other_z = [wrap(z + 1 + k, lay.nz) for k in range(lay.nz - 1)]
        self.copies, self.adds = {}, {}
        for t, stages in wanted.items():
            g, i = CHUNKS[t]
            p = ps[g]

            def along(pieces, slot, peers, ss, rs, t=t):
                return [
                    remote(piece, slot.at[k], ss.at[t, k], rs.at[t, k], peers[k])
                    for k, piece in enumerate(pieces)
                ]

            def into(dst, slot, count):
                return functools.partial(add_into, dst, [slot.at[k] for k in range(count)])

            def part(px, pz, py, p=p, g=g, i=i, core=c):
                return view(lay, p, g, i, core, px, pz, py)

            if 0 in stages:
                slot = ca[g].at[i]
                self.copies[t, 0] = [remote(part(ALL, ALL, ALL, core=1 - c), slot, c_s.at[t], c_r.at[t], cs[0])]
                self.adds[t, 1] = functools.partial(add_into, part(ALL, ALL, ALL), [slot])
            if 1 in stages and i < 2:
                slot = ra1[g].at[i]
                self.copies[t, 1] = along([part(k, ALL, ALL) for k in other_x], slot, xs, x_s, x_r)
                self.adds[t, 2] = into(part(x, ALL, ALL), slot, lay.nx - 1)
            elif 1 in stages:
                slot = rb1[g].at[0]
                self.copies[t, 1] = along([part(ALL, ALL, k) for k in other_y], slot, ys, y_s, y_r)
                self.adds[t, 2] = into(part(ALL, ALL, y), slot, lay.ny - 1)
            if t == LAST:
                self.copies[t, 2] = along([part(ALL, k, y) for k in other_z], rz, zs, z_s, z_r)
                own = part(ALL, z, y)
                self.adds[t, 3] = into(own, rz, lay.nz - 1)
                self.copies[t, 3] = [
                    remote(own, rx.at[x], x_s.at[t, k], x_r.at[t, k], peer) for k, peer in enumerate(xs)
                ]
                both = shard_view(lay, fs[g], g, i, c, ALL)
                self.adds[t, 4] = functools.partial(all_sum, both, own, rx, x)
                self.copies[t, 4] = [remote(both, both, fc_s.at[t], fc_r.at[t], cs[0])]
                continue
            if 2 in stages and i < 2:
                slot = ra2[g].at[i]
                self.copies[t, 2] = along([part(x, ALL, k) for k in other_y], slot, ys, y_s, y_r)
                self.adds[t, 3] = into(part(x, ALL, y), slot, lay.ny - 1)
            elif 2 in stages:
                slot = rb2[g].at[0]
                self.copies[t, 2] = along([part(k, ALL, y) for k in other_x], slot, xs, x_s, x_r)
                self.adds[t, 3] = into(part(x, ALL, y), slot, lay.nx - 1)
            if 3 in stages:
                slot = ra3[g].at[i]
                self.copies[t, 3] = along([part(x, k, y) for k in other_z], slot, zs, z_s, z_r)
                out = shard_view(lay, fs[g], g, i, c, x)
                self.adds[t, 4] = functools.partial(
                    set_sum, out, [part(x, z, y)] + [slot.at[k] for k in range(lay.nz - 1)]
                )
                self.copies[t, 4] = [
                    remote(out, out, fx_s.at[t, k], fx_r.at[t, k], peer) for k, peer in enumerate(xs)
                ]
                both = shard_view(lay, fs[g], g, i, c, ALL)
                self.copies[t, 5] = [remote(both, both, fc_s.at[t], fc_r.at[t], cs[0])]

    def settle(self, t, k):
        if (t, k - 1) in self.copies:
            arrive(self.copies[t, k - 1])
            if (t, k) in self.adds:
                self.adds[t, k]()

    def begin(self, t, k):
        start(self.copies.get((t, k), ()))

    def step(self, t, k):
        self.settle(t, k)
        if k < 6:
            self.begin(t, k)

    def drain(self):
        for group in self.copies.values():
            sent(group)


def all_sum(out, own, slots, at):
    slots[at] = own[...]
    set_sum(out, [slots.at[k] for k in range(slots.shape[0])])


def set_sum(out, srcs):
    total = srcs[0][...].astype(F32)
    for src in srcs[1:]:
        total = total + src[...].astype(F32)
    out[...] = total.astype(BF)


def add_into(dst, srcs):
    lead = dst.shape[:-2]

    def body(j, carry):
        index = []
        rest = j
        for size in reversed(lead):
            index.append(lax.rem(rest, size))
            rest = rest // size
        index = tuple(reversed(index))
        total = dst[index].astype(F32)
        for src in srcs:
            total = total + src[index].astype(F32)
        dst[index] = total.astype(BF)
        return carry

    lax.fori_loop(0, math.prod(lead), body, 0)


def rope(u, cos, low, high):
    return u * cos + pltpu.roll(u, LANES - 8, 1) * low + pltpu.roll(u, 8, 1) * high


def front_kernel(
    lay, rows,
    u_up, u_down, qkv_in, dense_in, tok_in, grad_in, seg, v0, v1, v2, v3, v4, v5, v6,
    g_up, g_down, p_out, prev_out, own_out, attn_hbm, vectors, up_add, att_sums,
    qkv, tok, grad, small, u_att, p_att, fg_prev, fg_own, attn_out, g_att, g_small, tok_halo, seg_halo, first_all, q_s, k_s, v_s, do_s, ctx_s, ctx_t,
    dq_s, dk_s, dv_s, cos_s, low_s, high_s, bias, dk_acc, dv_acc, qkv_add, s_s, w_s, d_s,
    local_sem, z_s, z_r, y_s, y_r, x_s, x_r, c_s, c_r, sm_s, sm_r, h_s, h_r, out_sem,
    ca, ra1, rb1, rc_s, rc_r, rx_s, rx_r, ry_s, ry_r, load_sem,
):
    span = 3 * rows
    r = qkv_in.shape[0]
    n_chunks = len(CHUNKS)
    x, c, z, y = lay.coords()
    xs, cs, zs, ys = line_peers(lay)
    total = lay.dp * lay.fsdp
    b = lax.axis_index("dp") * lay.fsdp + lax.axis_index("fsdp")

    def stream(k):
        t = wrap(b + k, total)
        return {"dp": t // lay.fsdp, "fsdp": lax.rem(t, lay.fsdp)}

    around = [stream(2), stream(-2), stream(1), stream(-1)]
    peers = xs + cs + zs + ys + around
    greet(peers)
    loads = [
        pltpu.make_async_copy(src, dst, load_sem.at[n])
        for n, (src, dst) in enumerate(
            ((qkv_in, qkv), (dense_in, u_att.at[:, pl.ds(3 * D, D)]), (tok_in, tok), (grad_in, grad))
        )
    ]
    start(loads)
    plan = small_plan(r)
    for (row, size, _), ref in zip(plan, (v0, v1, v2, v3, v4, v5, v6)):
        value = ref[...].astype(F32).reshape(1, size)
        for k in range(-(-size // LANES)):
            width = min(LANES, size - k * LANES)
            small[row + k : row + k + 1, :width] = value[:, k * LANES : k * LANES + width]
    loads[0].wait()
    left = lax.broadcasted_iota(jnp.int32, (r, LANES), 1) < HD
    for p in range(PAIRS):
        parts = [qkv[:, (3 * p + k) * LANES : (3 * p + k + 1) * LANES].astype(F32) for k in range(3)]
        kinds = (
            jnp.where(left, parts[0], parts[1]),
            pltpu.roll(jnp.where(left, parts[2], parts[0]), HD, 1),
            jnp.where(left, parts[1], parts[2]),
        )
        for k, part in enumerate(kinds):
            u_att[:, k * D + p * LANES : k * D + (p + 1) * LANES] = part.astype(BF)
    for copy in loads[1:]:
        copy.wait()
    gs = (g_att, g_up, g_down)
    us = (u_att, u_up, u_down)
    locals_ = []
    for t, (g, i) in enumerate(CHUNKS):
        locals_.append(
            pltpu.make_async_copy(
                shard_view(lay, us[g], g, i, c, x), view(lay, gs[g], g, i, c, x, z, y), local_sem.at[t]
            )
        )
    locals_.append(pltpu.make_async_copy(small, g_small.at[z, y], local_sem.at[n_chunks]))
    start(locals_)
    wait_greetings(peers)
    even = lax.rem(b, 2) == 0
    half = rows // 2
    halo, own, passed = [], [], []
    for k in range(2):
        part = pl.ds(k * half, half)
        halo.append(remote(tok.at[part], tok_halo.at[0, part], h_s.at[k], h_r.at[k], around[0]))
        own.append(remote(tok.at[part], tok_halo.at[1, part], h_s.at[2 + k], h_r.at[2 + k], around[2]))
        passed.append(
            remote(tok_halo.at[0, part], tok_halo.at[1, part], h_s.at[2 + k], h_r.at[2 + k], around[3])
        )
    segs = [
        remote(seg, seg_halo.at[0], h_s.at[4], h_r.at[4], around[0]),
        remote(seg, seg_halo.at[1], h_s.at[5], h_r.at[5], around[2]),
    ]
    small_z = [
        remote(small, g_small.at[z, y], sm_s.at[k], sm_r.at[k], p) for k, p in enumerate(zs)
    ]
    small_y = [
        remote(g_small.at[:, y], g_small.at[:, y], sm_s.at[lay.nz + k], sm_r.at[lay.nz + k], p)
        for k, p in enumerate(ys)
    ]
    net = Gather(lay, us, gs, (z_s, z_r, y_s, y_r, x_s, x_r, c_s, c_r))
    net.issue(0, 0)
    net.issue(2, 0)
    start(small_z)
    start(segs)
    net.issue(1, 0)

    def tables(k, carry):
        at = pl.ds(pl.multiple_of(k * 256, 256), 256)
        lane = lax.broadcasted_iota(jnp.int32, (256, LANES), 1) % HD
        row = lax.broadcasted_iota(jnp.int32, (256, LANES), 0) + k * 256
        place = lax.rem((b - 2) * rows + row + 4 * ROW, ROW).astype(F32)
        rate = jnp.exp((lane % 8).astype(F32) * (-math.log(10000.0) / 8.0))
        angle = place * rate
        sine = jnp.sin(angle)
        cos_s[at, :] = jnp.where(lane < ROT, jnp.cos(angle), 1.0)
        low_s[at, :] = jnp.where(lane < 8, -sine, 0.0)
        high_s[at, :] = jnp.where((lane >= 8) & (lane < ROT), sine, 0.0)
        return carry

    lax.fori_loop(0, 2, tables, 0)
    for t in (0, 2, 1, n_chunks):
        locals_[t].wait()
    net.pass_on(0, 1)
    lax.fori_loop(2, 3, tables, 0)
    net.pass_on(2, 1)
    lax.fori_loop(3, 5, tables, 0)
    arrive(small_z)
    start(small_y)
    net.pass_on(0, 2)
    net.pass_on(1, 1)
    halo[0].start()
    lax.fori_loop(5, span // 256, tables, 0)
    arrive(small_y)
    net.pass_on(2, 2)

    lane_row = lax.broadcasted_iota(jnp.int32, (1, LANES), 1)

    def line(first_row, size, unit, length, source):
        out = []
        for block in range(length // LANES):
            value = None
            for k in range(LANES // unit):
                owner, local = divmod(source(block * (LANES // unit) + k), size // unit)
                row, lane = divmod(local * unit, LANES)
                row += first_row
                piece = g_small[owner // lay.ny, owner % lay.ny, row : row + 1, :]
                if lane != k * unit:
                    piece = pltpu.roll(piece, (k * unit - lane) % LANES, 1)
                value = piece if value is None else jnp.where(lane_row // unit == k, piece, value)
            out.append(value)
        return jnp.concatenate(out, 1)

    def norm_rows(values):
        return norm_parts(values.astype(F32))[0]

    for j in range(5):
        vectors[j : j + 1, :] = line(*plan[j], D, lambda n: n)
    vectors[5:8, :] = jnp.zeros((3, D), F32)
    unit = plan[5][2]
    a_head = HD // unit

    def natural(n):
        kind, rest = divmod(n, D // unit)
        head, part = divmod(rest, a_head)
        return head * 3 * a_head + kind * a_head + part

    qkv_add[...] = line(*plan[5], 3 * D, natural)
    net.pass_on(1, 2)
    up_add[...] = line(*plan[6], FF, lambda n: n)

    def pass_halo(k):
        arrive([halo[k]])

        @pl.when(even)
        def _():
            own[k].start()

        @pl.when(jnp.logical_not(even))
        def _():
            passed[k].start()

    halo[1].start()
    gain, shift = vectors[0:1, :], vectors[1:2, :]
    own_rows = pl.ds(2 * rows, rows)
    first = (norm_rows(tok[...]) * gain + shift).astype(BF)
    first_all[own_rows, :] = first
    pass_halo(0)
    arrive(segs)
    least = jnp.maximum(0, 2 * rows - b * rows)
    keys_doc = jnp.concatenate([seg_halo[0], seg_halo[1], seg[...]], 1).astype(F32)
    keys_doc = jnp.broadcast_to(keys_doc, (LANES, span)).T
    query_doc = seg[0:1, :].astype(F32)

    for k in range(6):
        at = slice(k * 256, (k + 1) * 256)
        key_at = lax.broadcasted_iota(jnp.int32, (256, rows), 0) + k * 256
        query_at = lax.broadcasted_iota(jnp.int32, (256, rows), 1) + 2 * rows
        allowed = (keys_doc[at, 0:1] == query_doc) & (key_at <= query_at) & (key_at >= least)
        bias[at, :] = jnp.where(allowed, 0.0, -1e30)
    for t in range(3, n_chunks):
        locals_[t].wait()
    net.issue(5, 0)
    net.pass_on(0, 3)
    net.pass_on(2, 3)
    net.issue(3, 0)

    def weight(first_col, width):
        value = g_att[:, :, :, pl.ds(first_col, width)]
        return value.reshape(D, width)

    scale = 1.0 / math.sqrt(HD)

    def project(kind, j, at, out, factor):
        col = pl.multiple_of(kind * D + 256 * j, 256)
        value = mm(first_all[at, :], weight(col, 256)) + qkv_add[:, pl.ds(col, 256)]
        for k in range(2):
            u = value[:, k * LANES : (k + 1) * LANES]
            if kind < 2:
                u = rope(u, cos_s[at, :], low_s[at, :], high_s[at, :])
            if factor is not None:
                u = u * factor
            out[:, pl.ds(pl.multiple_of(256 * j + LANES * k, LANES), LANES)] = u.astype(BF)

    def own_queries(j, carry):
        project(0, j, own_rows, q_s, scale)
        return carry

    def own_keys(j, carry):
        project(1, j, own_rows, k_s.at[own_rows], None)
        return carry

    def own_values(j, carry):
        project(2, j, own_rows, v_s.at[own_rows], None)
        return carry

    net.done(0)
    lax.fori_loop(0, 3, own_queries, 0)
    lax.fori_loop(0, 1, own_keys, 0)
    pass_halo(1)
    net.pass_on(1, 3)
    net.issue(4, 0)
    net.done(2)
    do_s[...] = mm(grad[...], weight(3 * D, D), NT).astype(BF)
    lax.fori_loop(2, 3, own_values, 0)
    net.pass_on(5, 1)
    net.done(1)
    lax.fori_loop(1, 3, own_keys, 0)
    lax.fori_loop(0, 2, own_values, 0)
    own[0].wait_recv()
    net.pass_on(3, 1)

    def earlier_norms(k):
        for n in range(2):
            near = pl.ds(k * half, half)
            before = norm_rows(tok_halo[n, near, :]) * gain + shift
            first_all[pl.ds(n * rows + k * half, half), :] = before.astype(BF)

    earlier_norms(0)
    net.issue(8, 0)
    own[1].wait_recv()
    earlier_norms(1)
    net.pass_on(4, 1)
    net.pass_on(5, 2)

    def earlier_projections(j, carry):
        for k in range(2):
            at = pl.ds(k * rows, rows)
            project(1, j, at, k_s.at[at], None)
            project(2, j, at, v_s.at[at], None)
        return carry

    lax.fori_loop(0, 3, earlier_projections, 0)
    net.pass_on(3, 2)
    net.issue(6, 0)

    go, send, end = net.pass_on, net.issue, net.done
    later = [
        [(go, 8, 1), (send, 7, 0), (go, 4, 2)],
        [(go, 5, 3), (go, 6, 1), (go, 3, 3), (go, 7, 1)],
        [(go, 8, 2), (go, 6, 2)],
        [(go, 4, 3), (go, 7, 2)],
        [(go, 8, 3), (go, 6, 3)],
        [(go, 7, 3)],
    ]
    tile = 256

    def pair(p, carry):
        lanes = pl.ds(pl.multiple_of(p * LANES, LANES), LANES)
        v_t, k_t = v_s[:, lanes].T, k_s[:, lanes].T
        do_t = do_s[:, lanes].astype(F32).T
        lane = lax.broadcasted_iota(jnp.int32, (tile, LANES), 1)
        zero = jnp.zeros((), BF)
        units = [(t, hh) for t in range(rows // tile) for hh in range(2)]
        count = len(units)
        tops, totals, norms = [None] * count, [None] * count, [None] * count
        outs, dqs = [None] * count, [None] * count
        written = set()

        def masked(ref, u):
            t, hh = units[u]
            return jnp.where((lane // HD) == hh, ref[t * tile : (t + 1) * tile, lanes], zero)

        def pieces(u):
            kl = 2 * rows + (units[u][0] + 1) * tile
            return [slice(k * LANES, (k + 1) * LANES) for k in range(kl // LANES)]

        def scores(u, at, qm):
            t = units[u][0]
            st = mm(k_s[at, lanes], qm, NT) + bias[at, t * tile : (t + 1) * tile]
            s_s[u % 2, at, :] = st
            most = jnp.max(st, 0, keepdims=True)
            tops[u] = most if tops[u] is None else jnp.maximum(tops[u], most)

        def exponents(u, at):
            e = jnp.exp(s_s[u % 2, at, :] - tops[u])
            s_s[u % 2, at, :] = e
            part = jnp.sum(e, 0, keepdims=True)
            totals[u] = part if totals[u] is None else totals[u] + part

        def key_value_grads(u, at, qm, dom):
            dk, dv = mm(d_s[u % 2, at, :], qm), mm(w_s[u % 2, at, :], dom)
            if at.start in written:
                dk_acc[at, :] += dk
                dv_acc[at, :] += dv
            else:
                dk_acc[at, :] = dk
                dv_acc[at, :] = dv
                written.add(at.start)

        qm = masked(q_s, 0)
        for at in pieces(0):
            scores(0, at, qm)
        for u in range(count):
            t, hh = units[u]
            part = slice(hh * HD, (hh + 1) * HD)
            cols = slice(t * tile, (t + 1) * tile)
            kl = 2 * rows + (t + 1) * tile
            mine = pieces(u)
            after = pieces(u + 1) if u + 1 < count else []
            before = pieces(u - 1) if u > 0 else []
            if after:
                qm = masked(q_s, u + 1)
            for k in range(max(len(mine), len(after))):
                if k < len(after):
                    scores(u + 1, after[k], qm)
                if k < len(mine):
                    exponents(u, mine[k])
            norms[u] = 1.0 / totals[u]
            if before:
                q_last, do_last = masked(q_s, u - 1), masked(do_s, u - 1)
            for k in range(max(len(mine), len(before))):
                if k < len(before):
                    key_value_grads(u - 1, before[k], q_last, do_last)
                if k < len(mine):
                    w_s[u % 2, mine[k], :] = (s_s[u % 2, mine[k], :] * norms[u]).astype(BF)
            o_t = mm(v_t[part, :kl], w_s[u % 2, :kl, :])
            delta = jnp.sum(o_t * do_t[part, cols], 0, keepdims=True)
            outs[u] = o_t
            dom = masked(do_s, u)
            for at in mine:
                dp = mm(v_s[at, lanes], dom, NT)
                d_s[u % 2, at, :] = ((s_s[u % 2, at, :] * norms[u]) * (dp - delta)).astype(BF)
            dqs[u] = mm(k_t[part, :kl], d_s[u % 2, :kl, :])
            if hh == 0:
                continue
            o_pair = jnp.concatenate(outs[u - 1 : u + 1], 0)
            ctx_t[lanes, cols] = o_pair.astype(BF)
            ctx_s[cols, lanes] = o_pair.T.astype(BF)
            dq = jnp.concatenate(dqs[u - 1 : u + 1], 0).T * scale
            at = slice(2 * rows + t * tile, 2 * rows + (t + 1) * tile)
            dq_s[cols, lanes] = rope(dq, cos_s[at, :], -low_s[at, :], -high_s[at, :]).astype(BF)
        q_last, do_last = masked(q_s, count - 1), masked(do_s, count - 1)
        for at in pieces(count - 1):
            key_value_grads(count - 1, at, q_last, do_last)
        dk_s[:, lanes] = rope(dk_acc[...], cos_s[...], -low_s[...], -high_s[...]).astype(BF)
        dv_s[:, lanes] = dv_acc[...].astype(BF)
        for k in range(PAIRS):

            @pl.when(p == k)
            def _(k=k):
                for event, *where in later[k]:
                    event(*where)

        return carry

    lax.fori_loop(0, PAIRS, pair, 0)

    sums = Reduce(
        lay, (p_att,), None, ((ca,), (ra1,), (rb1,), None, None, None, None, None),
        (rc_s, rc_r, rx_s, rx_r, ry_s, ry_r) + (None,) * 6, {0: (0, 1), 1: (0,), 2: (0, 1)},
    )
    outs = []

    def leave(i):
        cols = pl.ds(1024 * i, 1024)
        copy = pltpu.make_async_copy(p_att.at[:, :, :, cols], p_out.at[:, :, :, cols], out_sem.at[i])
        copy.start()
        outs.append(copy)

    def put(kind, j, value):
        p_att[:, :, :, kind * D + 256 * j : kind * D + 256 * (j + 1)] = value.astype(BF).reshape(
            lay.nz, lay.ny, r, 256
        )

    def tile_of(ref, j):
        return ref[:, slice(256 * j, 256 * (j + 1))]

    def weight_grad(kind, j):
        if kind == 0:
            put(0, j, mm(first_all[own_rows, :], tile_of(dq_s, j), TN))
        elif kind == 3:
            put(3, j, mm(ctx_t[...], tile_of(grad, j)))
        else:
            put(kind, j, mm(first_all[...], tile_of((dk_s, dv_s)[kind - 1], j), TN))

    for kind, j in ((1, 0), (0, 0), (0, 1), (0, 2)):
        weight_grad(kind, j)
    sums.step(0, 0)
    for kind, j in ((2, 2), (3, 0), (3, 1), (3, 2)):
        weight_grad(kind, j)
    sums.step(0, 1)
    sums.step(2, 0)
    for kind, j in ((1, 1), (1, 2)):
        weight_grad(kind, j)
    sums.step(2, 1)
    for kind, j in ((2, 0), (2, 1)):
        weight_grad(kind, j)
    sums.step(1, 0)

    def earlier_grad(k, carry):
        at = pl.ds(pl.multiple_of(k * 256, 256), 256)
        value = mm(dk_s[at, :], weight(D, D), NT) + mm(dv_s[at, :], weight(2 * D, D), NT)
        fg_prev[at, :] = value.astype(BF)
        return carry

    lax.fori_loop(0, 2 * rows // 256, earlier_grad, 0)
    outs.append(pltpu.make_async_copy(fg_prev, prev_out, out_sem.at[3]))
    outs[-1].start()
    sums.settle(1, 1)
    leave(1)
    for k in range(rows // 256):
        at = slice(2 * rows + 256 * k, 2 * rows + 256 * (k + 1))
        near = slice(256 * k, 256 * (k + 1))
        fg_own[near, :] = (
            mm(dk_s[at, :], weight(D, D), NT)
            + mm(dv_s[at, :], weight(2 * D, D), NT)
            + mm(dq_s[near, :], weight(0, D), NT)
        )
    outs.append(pltpu.make_async_copy(fg_own, own_out, out_sem.at[4]))
    outs[-1].start()

    def attention_out(j, carry):
        col = pl.multiple_of(256 * j, 256)
        attn_out[:, pl.ds(col, 256)] = mm(ctx_s[...], weight(pl.multiple_of(3 * D + col, 256), 256))
        return carry

    lax.fori_loop(0, 3, attention_out, 0)
    outs.append(pltpu.make_async_copy(attn_out, attn_hbm, out_sem.at[5]))
    outs[-1].start()
    for k, ref in enumerate((dq_s, dk_s, dv_s)):
        att_sums[k : k + 1, :] = jnp.sum(ref[...].astype(F32), 0, keepdims=True)
    att_sums[3:8, :] = jnp.zeros((5, D), F32)
    sums.settle(0, 2)
    leave(0)
    sums.settle(2, 2)
    leave(2)
    sums.drain()
    for t in range(3, 9):
        net.done(t)
    net.drain()
    sent(small_z + small_y + segs + halo + own)
    for copy in outs:
        copy.wait()


def front(lay, u_up, u_down, qkv, dense, tok, grad, seg, vectors):
    rows = tok.shape[0]
    span = 3 * rows
    r = qkv.shape[0]
    n = len(CHUNKS)
    outs = (
        jax.ShapeDtypeStruct(grad_shape(lay, 1, r), BF),
        jax.ShapeDtypeStruct(grad_shape(lay, 2, r), BF),
        jax.ShapeDtypeStruct(grad_shape(lay, 0, r), BF),
        jax.ShapeDtypeStruct((2 * rows, D), BF),
        jax.ShapeDtypeStruct((rows, D), F32),
        jax.ShapeDtypeStruct((rows, D), F32),
        jax.ShapeDtypeStruct((8, D), F32),
        jax.ShapeDtypeStruct((1, FF), F32),
        jax.ShapeDtypeStruct((8, D), F32),
    )
    vmem = pl.BlockSpec(memory_space=pltpu.VMEM)
    lx, ly, lz = max(1, lay.nx - 1), max(1, lay.ny - 1), max(1, lay.nz - 1)

    def v(shape, dtype=BF):
        return pltpu.VMEM(shape, dtype)

    return pl.pallas_call(
        functools.partial(front_kernel, lay, rows),
        name="front",
        out_shape=outs,
        in_specs=hbm(6) + [vmem] * (1 + len(vectors)),
        out_specs=tuple(hbm(6)) + (vmem,) * 3,
        scratch_shapes=[
            v((r, 3 * D)), v((rows, D)), v((rows, D)), v((SMALL_ROWS, LANES), F32), v((r, 4 * D)), v(grad_shape(lay, 0, r)), v((2 * rows, D)), v((rows, D), F32), v((rows, D), F32),
            v(grad_shape(lay, 0, r)), v((lay.nz, lay.ny, SMALL_ROWS, LANES), F32), v((2, rows, D)),
            v((2, 1, rows), jnp.int32), v((span, D)), v((rows, D)), v((span, D)),
            v((span, D)), v((rows, D)), v((rows, D)), v((D, rows)), v((rows, D)), v((span, D)),
            v((span, D)), v((span, LANES), F32), v((span, LANES), F32), v((span, LANES), F32),
            v((span, rows), F32), v((span, LANES), F32), v((span, LANES), F32), v((1, 3 * D), F32),
            v((2, span, 256), F32), v((2, span, 256)), v((2, span, 256)),
            dma(n + 1), dma(n, lz), dma(n, lz), dma(n, ly), dma(n, ly), dma(n, lx), dma(n, lx),
            dma(n), dma(n), dma(lay.nz + ly), dma(lay.nz + ly), dma(6), dma(6), dma(6),
            v((3,) + part_shape(lay, 0, True, True, True, r)),
            v((1, lx) + part_shape(lay, 0, False, True, True, r)),
            v((1, ly) + part_shape(lay, 0, True, True, False, r)),
            dma(3), dma(3), dma(3, lx), dma(3, lx), dma(3, ly), dma(3, ly), dma(4),
        ],
        compiler_params=pltpu.CompilerParams(
            collective_id=0, has_side_effects=True, vmem_limit_bytes=VMEM_LIMIT
        ),
    )(u_up, u_down, qkv, dense, tok, grad, seg, *vectors)


def norm_back(grad, gain, normed, factor):
    inner = grad * gain
    return factor * (
        inner
        - jnp.mean(inner, -1, keepdims=True)
        - normed * jnp.mean(inner * normed, -1, keepdims=True)
    )


FF_CHUNKS = FF // D


def back_kernel(
    lay, rows, docs,
    g_up, g_down, p_in, prev_in, own_in, attn_in, tok_in, grad_in, vectors, up_add, att_sums, seg,
    out_hbm, input_hbm, att_hbm, up_hbm, down_hbm, vec_out,
    tok, grad, output, input_grad, f_att, f_up, f_down, p_att, fg_prev, fg_own, attn_out, p_up, p_down, w_up, w_down, second_in, second_t, act_s, pg_s, sg_acc, hop, home,
    ca, ra1, rb1, ra2, rb2, ra3, rz, rx, v_c, v_x, v_y, v_z, *sems,
):
    (c_s, c_r, x_s, x_r, y_s, y_r, z_s, z_r, fx_s, fx_r, fc_s, fc_r, v_s, v_r, w_sem, h_s, h_r, in_sem, out_sem) = sems
    r = p_in.shape[2]
    x, c, z, y = lay.coords()
    xs, cs, zs, ys = line_peers(lay)
    total = lay.dp * lay.fsdp
    b = lax.axis_index("dp") * lay.fsdp + lax.axis_index("fsdp")

    def stream(k):
        t = wrap(b + k, total)
        return {"dp": t // lay.fsdp, "fsdp": lax.rem(t, lay.fsdp)}

    around = [stream(2), stream(-2), stream(1), stream(-1)]
    near_z = lay.nz // FF_CHUNKS
    loads = []
    for k in range(FF_CHUNKS):
        slot = k % 2
        loads.append(
            (
                pltpu.make_async_copy(
                    g_up.at[:, :, :, pl.ds(D * k, D)], w_up.at[slot], w_sem.at[0, k]
                ),
                pltpu.make_async_copy(
                    g_down.at[pl.ds(near_z * k, near_z)], w_down.at[slot], w_sem.at[1, k]
                ),
            )
        )
    peers = xs + cs + zs + ys + around
    greet(peers)
    taken = [
        pltpu.make_async_copy(
            p_in.at[:, :, :, pl.ds(1024 * i, 1024)], p_att.at[:, :, :, pl.ds(1024 * i, 1024)],
            in_sem.at[i],
        )
        for i in range(3)
    ]
    taken.append(pltpu.make_async_copy(prev_in, fg_prev, in_sem.at[3]))
    taken.append(pltpu.make_async_copy(attn_in, attn_out, in_sem.at[4]))
    taken.append(pltpu.make_async_copy(own_in, fg_own, in_sem.at[5]))
    taken.append(pltpu.make_async_copy(tok_in, tok, in_sem.at[6]))
    taken.append(pltpu.make_async_copy(grad_in, grad, in_sem.at[7]))
    start(taken[:4])
    start(taken[6:])
    start(loads[0])
    start(taken[4:6])
    start(loads[1])
    wait_greetings(peers)
    wanted = {t: (0, 1, 2, 3) for t in range(3, len(CHUNKS))}
    wanted.update({0: (2, 3), 1: (1, 2, 3), 2: (2, 3)})
    net = Reduce(
        lay, (p_att, p_up, p_down), (f_att, f_up, f_down),
        ((None,) + tuple(ca), ra1, (None,) + tuple(rb1), ra2, rb2, ra3, rz, rx), sems[:12], wanted,
    )
    for t, k in ((1, 1), (2, 2), (0, 2)):
        taken[t].wait()
        net.begin(t, k)
    taken[3].wait()
    even = lax.rem(b, 2) == 0
    quarter = rows // 4
    to_next, to_last, to_owner = [], [], []
    for k in range(4):
        near = fg_prev.at[pl.ds(rows + k * quarter, quarter)]
        far = fg_prev.at[pl.ds(k * quarter, quarter)]
        part = pl.ds(k * quarter, quarter)
        to_next.append(remote(near, hop.at[part], h_s.at[k], h_r.at[k], around[2]))
        to_last.append(remote(near, hop.at[part], h_s.at[k], h_r.at[k], around[3]))
        to_owner.append(remote(far, home.at[part], h_s.at[4 + k], h_r.at[4 + k], around[1]))

    def hop_halo(k):
        @pl.when(even)
        def _():
            to_next[k].start()

        @pl.when(jnp.logical_not(even))
        def _():
            to_last[k].start()

    def forward_halo(k):
        to_last[k].wait_recv()
        at = pl.ds(k * quarter, quarter)

        @pl.when(jnp.logical_not(even))
        def _():
            fg_prev[at, :] = (fg_prev[at, :].astype(F32) + hop[at, :].astype(F32)).astype(BF)

        to_owner[k].start()

    hop_halo(0)
    hop_halo(1)

    gain_first, gain_second = vectors[0:1, :], vectors[2:3, :]
    taken[6].wait()
    taken[7].wait()
    normed, factor = norm_parts(tok[...].astype(F32))
    value = (normed * gain_second + vectors[3:4, :]).astype(BF)
    second_in[...] = value
    second_t[...] = value.T
    cot = grad[...].astype(F32)
    taken[4].wait()
    taken[5].wait()
    output_base = attn_out
    output_base[...] = attn_out[...] + tok[...].astype(F32) + vectors[4:5, :]
    sg_acc[...] = jnp.zeros_like(sg_acc)
    mine = v_c.at[c]
    mine[...] = jnp.zeros((16, D), F32)

    step = net.step
    events = [
        [],
        [(step, 0, 3)],
        [(hop_halo, 2)],
        [(step, 3, 0), (step, 1, 2), (forward_halo, 0)],
        [(step, 3, 1), (step, 2, 3), (hop_halo, 3)],
        [(step, 4, 0), (forward_halo, 1)],
        [(step, 4, 1), (step, 0, 4)],
        [(step, 8, 0), (step, 6, 0), (step, 5, 0), (step, 7, 0), (step, 2, 4)],
    ]
    root = math.sqrt(0.5)
    level = 1.0 / math.sqrt(2.0 * math.pi)

    def chunk(k, squares):
        slot = lax.rem(k, 2)
        for n in range(FF_CHUNKS):

            @pl.when(k == n)
            def _(n=n):
                loads[n][0].wait()
                loads[n][1].wait()

        down = w_down[slot].reshape(D, D)
        for j in range(3):
            tile = slice(256 * j, 256 * (j + 1))
            col = pl.ds(pl.multiple_of(D * k + 256 * j, 256), 256)
            pre = mm(second_in[...], w_up[slot, :, :, :, tile].reshape(D, 256)) + up_add[:, col]
            hidden = mm(grad[...], down[tile, :], NT)
            half = 0.5 + 0.5 * lax.erf(pre * root)
            act = (pre * half).astype(BF)
            slope = half + pre * jnp.exp(-0.5 * pre * pre) * level
            pg = (hidden * slope).astype(BF)
            act_s[:, tile] = act
            pg_s[:, tile] = pg
            wide = act.astype(F32)
            squares = squares + jnp.sum(wide * wide, -1, keepdims=True)
            v_c[c, pl.ds(8 + k, 1), tile] = jnp.sum(pg.astype(F32), 0, keepdims=True)

        def hook(half):
            for n in range(FF_CHUNKS):

                @pl.when(k == n)
                def _(n=n):
                    if half == 1 and n + 2 < FF_CHUNKS:
                        start(loads[n + 2])
                    for event, *where in events[2 * n + half]:
                        event(*where)

        hook(0)
        p_up[:, :, :, pl.ds(pl.multiple_of(D * k, 256), D)] = (
            mm(second_t[...], pg_s[...]).astype(BF).reshape(lay.nz, lay.ny, r, D)
        )
        p_down[pl.ds(near_z * k, near_z)] = (
            mm(act_s[...].T, grad[...]).astype(BF).reshape(near_z, lay.ny, 4, r, D)
        )
        output_base[...] += mm(act_s[...], down)
        sg_acc[...] += mm(pg_s[...], w_up[slot].reshape(D, D), NT)
        hook(1)
        return squares

    squares = lax.fori_loop(0, FF_CHUNKS, chunk, jnp.zeros((rows, 1), F32))
    run = lambda *pairs: [step(t, k) for t, k in pairs]
    run((8, 1), (6, 1), (3, 2), (1, 3))
    output[...] = output_base[...].astype(BF)
    left = []

    def leave(k, ref, target):
        copy = pltpu.make_async_copy(ref, target, out_sem.at[k])
        copy.start()
        left.append(copy)

    leave(0, output, out_hbm)
    forward_halo(2)
    cot_sum = jnp.sum(grad[...].astype(F32), 0, keepdims=True)
    forward_halo(3)
    def put(k, value):
        v_c[c, k : k + 1, :] = value

    put(4, cot_sum)
    for k in range(3):
        put(5 + k, att_sums[k : k + 1, :])
    cot = grad[...].astype(F32)
    token_norm = squares * jnp.sum(cot * cot, -1, keepdims=True) * (1.0 / (FF * D))
    docs_of = jnp.broadcast_to(seg[...].astype(F32), (LANES, rows)).T[:, 0:1]
    doc = lax.broadcasted_iota(jnp.int32, (rows, D), 1).astype(F32)
    member = jnp.where((docs_of == doc) & (doc < docs), 1.0, 0.0)
    put(12, jnp.sum(token_norm * member, 0, keepdims=True))
    put(13, jnp.sum(member, 0, keepdims=True))
    run((4, 2), (5, 1), (7, 1), (8, 2), (1, 4))
    keep = jnp.where(even, 1.0, 0.0).astype(F32)

    def norms(k):
        to_owner[k].wait_recv()
        at = slice(k * quarter, (k + 1) * quarter)
        first_grad = fg_own[at, :] + home[at, :].astype(F32) + hop[at, :].astype(F32) * keep
        second_grad = sg_acc[at, :]
        normed, factor = norm_parts(tok[at, :].astype(F32))
        input_grad[at, :] = (
            grad[at, :].astype(F32)
            + norm_back(first_grad, gain_first, normed, factor)
            + norm_back(second_grad, gain_second, normed, factor)
        ).astype(BF)
        sums = [first_grad * normed, first_grad, second_grad * normed, second_grad]
        return [jnp.sum(value, 0, keepdims=True) for value in sums]

    def add_up(left, right):
        return [p + q for p, q in zip(left, right)]

    sums = norms(0)
    run((3, 3))
    sums = add_up(sums, norms(1))
    run((6, 2))
    sums = add_up(sums, norms(2))
    run((4, 3))
    sums = add_up(sums, norms(3))
    leave(1, input_grad, input_hbm)
    for k in range(4):
        put(k, sums[k])
    run((8, 3))

    at = [0, 1, lay.nx, lay.nx + lay.ny - 1]

    def spread(ref, own, peers, base):
        return [
            remote(ref.at[own], ref.at[own], v_s.at[base + k], v_r.at[base + k], p)
            for k, p in enumerate(peers)
        ]

    vec_c = spread(v_c, c, cs, at[0])
    vec_x = spread(v_x, x, xs, at[1])
    vec_y = spread(v_y, y, ys, at[2])
    vec_z = spread(v_z, z, zs, at[3])

    def add_all(ref, size):
        value = ref[0]
        for k in range(1, size):
            value = value + ref[k]
        return value

    start(vec_c)
    run((5, 2))
    arrive(vec_c)
    v_x[x] = add_all(v_c, 2)
    start(vec_x)
    run((7, 2), (6, 3), (5, 3), (3, 4), (7, 3))
    arrive(vec_x)
    v_y[y] = add_all(v_x, lay.nx)
    start(vec_y)
    run((4, 4), (8, 4))
    arrive(vec_y)
    v_z[z] = add_all(v_y, lay.ny)
    start(vec_z)
    run((0, 5), (1, 5), (2, 5), (3, 5), (4, 5), (6, 4), (5, 4), (6, 5), (5, 5))
    run((0, 6), (1, 6), (2, 6))
    leave(2, f_att, att_hbm)
    run((7, 4), (3, 6), (4, 6), (5, 6))
    leave(3, f_up, up_hbm)
    arrive(vec_z)
    vec_out[...] = add_all(v_z, lay.nz)
    run((8, 5), (7, 5), (6, 6), (8, 6), (7, 6))
    leave(4, f_down, down_hbm)
    net.drain()
    sent(vec_c + vec_x + vec_y + vec_z)
    sent(to_next + to_owner)
    for copy in left:
        copy.wait()


def back(lay, g_up, g_down, p_att, fg_prev, fg_own, attn_out, vectors, up_add, att_sums, tok, grad, seg):
    rows = tok.shape[0]
    r = p_att.shape[2]
    n = len(CHUNKS)
    docs = DOC_DEV * lay.dp * lay.fsdp
    outs = (
        jax.ShapeDtypeStruct((rows, D), BF),
        jax.ShapeDtypeStruct((rows, D), BF),
        jax.ShapeDtypeStruct((r, 4 * D), BF),
        jax.ShapeDtypeStruct((r, 4 * D), BF),
        jax.ShapeDtypeStruct((4, r, D), BF),
        jax.ShapeDtypeStruct((16, D), F32),
    )
    lx, ly, lz = max(1, lay.nx - 1), max(1, lay.ny - 1), max(1, lay.nz - 1)

    def v(shape, dtype=BF):
        return pltpu.VMEM(shape, dtype)

    def bufs(chunks, peers, x_all, z_all, y_all, first=0):
        return [
            v((chunks,) + peers + part_shape(lay, g, x_all, z_all, y_all, r)) for g in range(first, 3)
        ]

    scratch = [
        v((rows, D)), v((rows, D)), v((rows, D)), v((rows, D)), v((r, 4 * D)), v((r, 4 * D)), v((4, r, D)),
        v(grad_shape(lay, 0, r)), v((2 * rows, D)), v((rows, D), F32), v((rows, D), F32),
        v(grad_shape(lay, 1, r)), v(grad_shape(lay, 2, r)),
        v((2, lay.nz, lay.ny, r, D)), v((2, lay.nz // FF_CHUNKS, lay.ny, 4, r, D)),
        v((rows, D)), v((D, rows)), v((rows, D)), v((rows, D)), v((rows, D), F32),
        v((rows, D)), v((rows, D)),
        bufs(3, (), True, True, True, 1),
        bufs(2, (lx,), False, True, True),
        bufs(1, (ly,), True, True, False, 1),
        bufs(2, (ly,), False, True, False),
        bufs(1, (lx,), False, True, False),
        bufs(3, (lz,), False, False, False),
        v((lz,) + part_shape(lay, 2, True, False, False, r)),
        v((lay.nx,) + part_shape(lay, 2, True, False, False, r)),
    ]
    vecs = [v((k, 16, D), F32) for k in (2, lay.nx, lay.ny, lay.nz)]
    nv = 1 + lay.nx + lay.ny + lay.nz
    sems = [
        dma(n), dma(n), dma(n, lx), dma(n, lx), dma(n, ly), dma(n, ly), dma(n, lz), dma(n, lz),
        dma(n, lx), dma(n, lx), dma(n), dma(n), dma(nv), dma(nv), dma(2, FF_CHUNKS), dma(8), dma(8), dma(8), dma(5),
    ]
    vmem = pl.BlockSpec(memory_space=pltpu.VMEM)
    return pl.pallas_call(
        functools.partial(back_kernel, lay, rows, docs),
        name="back",
        out_shape=outs,
        in_specs=hbm(8) + [vmem] * 4,
        out_specs=tuple(hbm(5)) + (vmem,),
        scratch_shapes=scratch + vecs + sems,
        compiler_params=pltpu.CompilerParams(
            collective_id=1, has_side_effects=True, vmem_limit_bytes=VMEM_LIMIT
        ),
    )(g_up, g_down, p_att, fg_prev, fg_own, attn_out, tok, grad, vectors, up_add, att_sums, seg)


def finish_kernel(
    lay, docs, r, f_att, f_up, f_down, vec, out_in, grad_in,
    output, input_grad, fg, fb, sg, sb, qkv_w, qkv_b, dense_w, up_w, up_b, down_w, ob, norms,
):
    output[...] = out_in[...]
    input_grad[...] = grad_in[...]
    shard = lax.axis_index("fsdp")

    def by_head(row_count, kind):
        left = lax.broadcasted_iota(jnp.int32, (row_count, LANES), 1) < HD
        for p in range(PAIRS):
            q, k, v = (kind(n, p) for n in range(3))
            turned = pltpu.roll(k, HD, 1)
            yield jnp.where(left, q, turned)
            yield jnp.where(left, v, q)
            yield jnp.where(left, turned, v)

    def block(k, p):
        return f_att[:, k * D + p * LANES : k * D + (p + 1) * LANES].astype(F32)

    for n, value in enumerate(by_head(r, block)):
        qkv_w[:, n * LANES : (n + 1) * LANES] = value
    dense_w[...] = f_att[:, 3 * D :].astype(F32)
    up_w[...] = f_up[...].astype(F32)
    down_w[...] = f_down[...].astype(F32)

    def own(row, width):
        length = row.shape[1]
        wide = jnp.broadcast_to(row, (8, length))
        turned = pltpu.roll(wide, lax.rem(length - shard * width, length), 1)
        return turned[0:1, :width].reshape(width)

    for k, ref in enumerate((fg, fb, sg, sb, ob)):
        ref[...] = own(vec[k : k + 1, :], r)
    bias = list(by_head(1, lambda k, p: vec[5 + k : 6 + k, p * LANES : (p + 1) * LANES]))
    qkv_b[...] = own(jnp.concatenate(bias, 1), 3 * r)
    up_b[...] = own(jnp.concatenate([vec[8 + k : 9 + k, :] for k in range(4)], 1), 4 * r)
    norms[...] = (vec[12:13, :docs] / vec[13:14, :docs]).reshape(docs)


def finish(lay, output, input_grad, f_att, f_up, f_down, vec):
    r = f_att.shape[0]
    docs = DOC_DEV * lay.dp * lay.fsdp
    vmem = pl.BlockSpec(memory_space=pltpu.VMEM)
    shapes = [
        (r,), (r,), (r,), (r,), (r, 3 * D), (3 * r,), (r, D), (r, FF), (4 * r,), (4, r, D), (r,), (docs,),
    ]
    return pl.pallas_call(
        functools.partial(finish_kernel, lay, docs, r),
        name="finish",
        out_shape=tuple(jax.ShapeDtypeStruct(v.shape, v.dtype) for v in (output, input_grad))
        + tuple(jax.ShapeDtypeStruct(shape, F32) for shape in shapes),
        in_specs=[vmem] * 6,
        out_specs=(vmem,) * (2 + len(shapes)),
        compiler_params=pltpu.CompilerParams(vmem_limit_bytes=VMEM_LIMIT),
    )(f_att, f_up, f_down, vec, output, input_grad)


def per_device(
    lay, tokens, seg_ids, out_grad, first_gain, first_bias, second_gain, second_bias,
    qkv_weight, qkv_bias, dense_weight, up_weight, up_bias, down_weight, out_bias,
):
    rows = tokens.shape[0]
    r = qkv_weight.shape[0]
    vectors = (first_gain, first_bias, second_gain, second_bias, out_bias, qkv_bias, up_bias)
    seg_row = seg_ids.reshape(1, rows)
    passed = front(
        lay, up_weight, down_weight.reshape(4, r, D), qkv_weight, dense_weight, tokens,
        out_grad, seg_row, vectors,
    )
    summed = back(lay, *passed, tokens, out_grad, seg_row)
    (output, input_grad, fg, fb, sg, sb, qkv_w, qkv_b, dense_w, up_w, up_b, down_w, ob, norms) = finish(
        lay, *summed
    )
    return (
        output, input_grad, fg, fb, sg, sb, qkv_w, qkv_b, dense_w, up_w, up_b,
        down_w.reshape(4 * r, D), ob, norms,
    )


def solution(mesh):
    lay = Layout(mesh.shape["dp"], mesh.shape["fsdp"])
    both = P(("dp", "fsdp"))
    split = P("fsdp")
    in_specs = (both, both, both) + (split,) * 11
    out_specs = (both, both) + (split,) * 11 + (P(),)
    return jax.shard_map(
        functools.partial(per_device, lay), mesh=mesh, in_specs=in_specs, out_specs=out_specs,
        check_vma=False,
    )
```

```python
import functools
import math

import jax
import jax.numpy as jnp
from jax import lax
from jax.experimental import pallas as pl
from jax.experimental.pallas import tpu as pltpu
from jax.sharding import PartitionSpec as P

D = 768
H = 12
HD = 64
FF = 3072
ROT = 16
ROW = 2048
DOC_DEV = 2
LANES = 128
PAIRS = D // LANES
MESH = pl.DeviceIdType.MESH
VMEM_LIMIT = 60 * 1024 * 1024


class Layout:
    def __init__(self, dp, fsdp):
        self.dp, self.fsdp = dp, fsdp
        self.nc = 2
        self.nx = dp // 2
        ny = 1
        while (2 * ny) * (2 * ny) <= fsdp:
            ny *= 2
        self.ny, self.nz = ny, fsdp // ny
        self.sub = max(1, self.nx // 2)
        self.unit = 4 // self.nx
        self.down_unit = 2 // self.sub

    def coords(self):
        d, f = lax.axis_index("dp"), lax.axis_index("fsdp")
        return d // 2, d % 2, f // self.ny, f % self.ny

    def device(self, x, c, z, y):
        return {"dp": x * 2 + c, "fsdp": z * self.ny + y}


def wrap(value, size):
    return lax.rem(value + size, size)


CHUNKS = tuple((g, i) for g in range(3) for i in range(3))
LAST = len(CHUNKS) - 1
ALL = slice(None)


def grad_shape(lay, group, r):
    return (lay.nz, lay.ny, r, 4 * D) if group < 2 else (lay.nz, lay.ny, 4, r, D)


def span_of(lay, group, i, c, x):
    if group < 2:
        width = 512 // lay.nx
        if x is ALL:
            return pl.ds(pl.multiple_of(1024 * i + 512 * c, LANES), 512), None
        return pl.ds(pl.multiple_of(1024 * i + 512 * c + width * x, LANES), width), None
    width = 256 // lay.sub
    if x is ALL:
        return pl.ds(256 * i, 256), pl.ds(2 * c, 2)
    start = 256 * i + width * lax.rem(x, lay.sub)
    return pl.ds(pl.multiple_of(start, LANES), width), 2 * c + x // lay.sub


def view(lay, ref, group, i, c, x, z, y):
    cols, quarter = span_of(lay, group, i, c, x)
    if group < 2:
        return ref.at[z, y, :, cols]
    return ref.at[z, y, quarter, :, cols]


def shard_view(lay, ref, group, i, c, x):
    cols, quarter = span_of(lay, group, i, c, x)
    if group < 2:
        return ref.at[:, cols]
    return ref.at[quarter, :, cols]


def part_shape(lay, group, x_all, z_all, y_all, r):
    lead = ((lay.nz,) if z_all else ()) + ((lay.ny,) if y_all else ())
    if group < 2:
        return lead + (r, 512 if x_all else 512 // lay.nx)
    return lead + ((2, r, 256) if x_all else (r, 256 // lay.sub))


def greet(peers):
    sem = pltpu.get_barrier_semaphore()
    for peer in peers:
        pl.semaphore_signal(sem, inc=1, device_id=peer, device_id_type=MESH)


def wait_greetings(peers):
    pl.semaphore_wait(pltpu.get_barrier_semaphore(), len(peers))


def line_peers(lay):
    x, c, z, y = lay.coords()
    xs = [lay.device(wrap(x + k, lay.nx), c, z, y) for k in range(1, lay.nx)]
    ys = [lay.device(x, c, z, wrap(y + k, lay.ny)) for k in range(1, lay.ny)]
    zs = [lay.device(x, c, wrap(z + k, lay.nz), y) for k in range(1, lay.nz)]
    cs = [lay.device(x, 1 - c, z, y)]
    return xs, cs, zs, ys


def remote(src, dst, ssem, rsem, device):
    return pltpu.make_async_remote_copy(
        src_ref=src, dst_ref=dst, send_sem=ssem, recv_sem=rsem, device_id=device, device_id_type=MESH
    )


def start(copies):
    for copy in copies:
        copy.start()


def arrive(copies):
    for copy in copies:
        copy.wait_recv()


def sent(copies):
    for copy in copies:
        copy.wait_send()


def hbm(count):
    return [pl.BlockSpec(memory_space=pltpu.HBM)] * count


def dma(*shape):
    return pltpu.SemaphoreType.DMA(shape)


NT = (((1,), (1,)), ((), ()))
NN = (((1,), (0,)), ((), ()))
TN = (((0,), (0,)), ((), ()))
F32 = jnp.float32
BF = jnp.bfloat16


def mm(a, b, dims=NN):
    return lax.dot_general(a, b, dims, preferred_element_type=F32)


def norm_parts(values):
    middle = jnp.mean(values, -1, keepdims=True)
    centred = values - middle
    factor = lax.rsqrt(jnp.mean(centred * centred, -1, keepdims=True) + 1e-05)
    return centred * factor, factor


def small_plan(r):
    plan, at = [], 0
    for size, within in [(r, LANES)] * 5 + [(3 * r, HD), (4 * r, LANES)]:
        plan.append((at, size, math.gcd(size, within)))
        at += -(-size // LANES)
    return plan


SMALL_ROWS = 16


class Gather:
    def __init__(self, lay, us, gs, sems):
        (z_s, z_r, y_s, y_r, x_s, x_r, c_s, c_r) = sems
        x, c, z, y = lay.coords()
        xs, cs, zs, ys = line_peers(lay)
        self.stages = []
        for t, (g, i) in enumerate(CHUNKS):
            by_y, by_x = (ys, y_s, y_r), (xs, x_s, x_r)
            first, second = (by_y, by_x) if i < 2 else (by_x, by_y)
            middle = (x, ALL, ALL) if i < 2 else (ALL, ALL, y)
            steps = [
                ((zs, z_s, z_r), (x, z, y)),
                (first, (x, ALL, y)),
                (second, middle),
            ]
            stages = []
            for (peers, ss, rs), (px, pz, py) in steps:
                piece = view(lay, gs[g], g, i, c, px, pz, py)
                source = shard_view(lay, us[g], g, i, c, x) if len(stages) == 0 else piece
                stages.append(
                    [remote(source, piece, ss.at[t, k], rs.at[t, k], p) for k, p in enumerate(peers)]
                )
            piece = view(lay, gs[g], g, i, c, ALL, ALL, ALL)
            stages.append([remote(piece, piece, c_s.at[t], c_r.at[t], cs[0])])
            self.stages.append(stages)

    def issue(self, t, stage):
        start(self.stages[t][stage])

    def pass_on(self, t, stage):
        arrive(self.stages[t][stage - 1])
        start(self.stages[t][stage])

    def done(self, t):
        arrive(self.stages[t][3])

    def drain(self):
        for stages in self.stages:
            for copies in stages:
                sent(copies)


class Reduce:
    def __init__(self, lay, ps, fs, bufs, sems, wanted):
        (ca, ra1, rb1, ra2, rb2, ra3, rz, rx) = bufs
        (c_s, c_r, x_s, x_r, y_s, y_r, z_s, z_r, fx_s, fx_r, fc_s, fc_r) = sems
        x, c, z, y = lay.coords()
        xs, cs, zs, ys = line_peers(lay)
        other_x = [wrap(x + 1 + k, lay.nx) for k in range(lay.nx - 1)]
        other_y = [wrap(y + 1 + k, lay.ny) for k in range(lay.ny - 1)]
        other_z = [wrap(z + 1 + k, lay.nz) for k in range(lay.nz - 1)]
        self.copies, self.adds = {}, {}
        for t, stages in wanted.items():
            g, i = CHUNKS[t]
            p = ps[g]

            def along(pieces, slot, peers, ss, rs, t=t):
                return [
                    remote(piece, slot.at[k], ss.at[t, k], rs.at[t, k], peers[k])
                    for k, piece in enumerate(pieces)
                ]

            def into(dst, slot, count):
                return functools.partial(add_into, dst, [slot.at[k] for k in range(count)])

            def part(px, pz, py, p=p, g=g, i=i, core=c):
                return view(lay, p, g, i, core, px, pz, py)

            if 0 in stages:
                slot = ca[g].at[i]
                self.copies[t, 0] = [remote(part(ALL, ALL, ALL, core=1 - c), slot, c_s.at[t], c_r.at[t], cs[0])]
                self.adds[t, 1] = functools.partial(add_into, part(ALL, ALL, ALL), [slot])
            if 1 in stages and i < 2:
                slot = ra1[g].at[i]
                self.copies[t, 1] = along([part(k, ALL, ALL) for k in other_x], slot, xs, x_s, x_r)
                self.adds[t, 2] = into(part(x, ALL, ALL), slot, lay.nx - 1)
            elif 1 in stages:
                slot = rb1[g].at[0]
                self.copies[t, 1] = along([part(ALL, ALL, k) for k in other_y], slot, ys, y_s, y_r)
                self.adds[t, 2] = into(part(ALL, ALL, y), slot, lay.ny - 1)
            if t == LAST:
                self.copies[t, 2] = along([part(ALL, k, y) for k in other_z], rz, zs, z_s, z_r)
                own = part(ALL, z, y)
                self.adds[t, 3] = into(own, rz, lay.nz - 1)
                self.copies[t, 3] = [
                    remote(own, rx.at[x], x_s.at[t, k], x_r.at[t, k], peer) for k, peer in enumerate(xs)
                ]
                both = shard_view(lay, fs[g], g, i, c, ALL)
                self.adds[t, 4] = functools.partial(all_sum, both, own, rx, x)
                self.copies[t, 4] = [remote(both, both, fc_s.at[t], fc_r.at[t], cs[0])]
                continue
            if 2 in stages and i < 2:
                slot = ra2[g].at[i]
                self.copies[t, 2] = along([part(x, ALL, k) for k in other_y], slot, ys, y_s, y_r)
                self.adds[t, 3] = into(part(x, ALL, y), slot, lay.ny - 1)
            elif 2 in stages:
                slot = rb2[g].at[0]
                self.copies[t, 2] = along([part(k, ALL, y) for k in other_x], slot, xs, x_s, x_r)
                self.adds[t, 3] = into(part(x, ALL, y), slot, lay.nx - 1)
            if 3 in stages:
                slot = ra3[g].at[i]
                self.copies[t, 3] = along([part(x, k, y) for k in other_z], slot, zs, z_s, z_r)
                out = shard_view(lay, fs[g], g, i, c, x)
                self.adds[t, 4] = functools.partial(
                    set_sum, out, [part(x, z, y)] + [slot.at[k] for k in range(lay.nz - 1)]
                )
                self.copies[t, 4] = [
                    remote(out, out, fx_s.at[t, k], fx_r.at[t, k], peer) for k, peer in enumerate(xs)
                ]
                both = shard_view(lay, fs[g], g, i, c, ALL)
                self.copies[t, 5] = [remote(both, both, fc_s.at[t], fc_r.at[t], cs[0])]

    def settle(self, t, k):
        if (t, k - 1) in self.copies:
            arrive(self.copies[t, k - 1])
            if (t, k) in self.adds:
                self.adds[t, k]()

    def begin(self, t, k):
        start(self.copies.get((t, k), ()))

    def step(self, t, k):
        self.settle(t, k)
        if k < 6:
            self.begin(t, k)

    def drain(self):
        for group in self.copies.values():
            sent(group)


def all_sum(out, own, slots, at):
    slots[at] = own[...]
    set_sum(out, [slots.at[k] for k in range(slots.shape[0])])


def set_sum(out, srcs):
    total = srcs[0][...].astype(F32)
    for src in srcs[1:]:
        total = total + src[...].astype(F32)
    out[...] = total.astype(BF)


def add_into(dst, srcs):
    lead = dst.shape[:-2]

    def body(j, carry):
        index = []
        rest = j
        for size in reversed(lead):
            index.append(lax.rem(rest, size))
            rest = rest // size
        index = tuple(reversed(index))
        total = dst[index].astype(F32)
        for src in srcs:
            total = total + src[index].astype(F32)
        dst[index] = total.astype(BF)
        return carry

    lax.fori_loop(0, math.prod(lead), body, 0)


def rope(u, cos, low, high):
    return u * cos + pltpu.roll(u, LANES - 8, 1) * low + pltpu.roll(u, 8, 1) * high


def front_kernel(
    lay, rows,
    u_up, u_down, qkv_in, dense_in, tok_in, grad_in, seg, v0, v1, v2, v3, v4, v5, v6,
    g_up, g_down, p_out, prev_out, own_out, attn_hbm, vectors, up_add, att_sums,
    qkv, tok, grad, small, u_att, p_att, fg_prev, fg_own, attn_out, g_att, g_small, tok_halo, seg_halo, first_all, q_s, k_s, v_s, do_s, ctx_s, ctx_t,
    dq_s, dk_s, dv_s, cos_s, low_s, high_s, bias, dk_acc, dv_acc, qkv_add, s_s, w_s, d_s,
    local_sem, z_s, z_r, y_s, y_r, x_s, x_r, c_s, c_r, sm_s, sm_r, h_s, h_r, out_sem,
    ca, ra1, rb1, rc_s, rc_r, rx_s, rx_r, ry_s, ry_r, load_sem,
):
    span = 3 * rows
    r = qkv_in.shape[0]
    n_chunks = len(CHUNKS)
    x, c, z, y = lay.coords()
    xs, cs, zs, ys = line_peers(lay)
    total = lay.dp * lay.fsdp
    b = lax.axis_index("dp") * lay.fsdp + lax.axis_index("fsdp")

    def stream(k):
        t = wrap(b + k, total)
        return {"dp": t // lay.fsdp, "fsdp": lax.rem(t, lay.fsdp)}

    around = [stream(2), stream(-2), stream(1), stream(-1)]
    peers = xs + cs + zs + ys + around
    greet(peers)
    loads = [
        pltpu.make_async_copy(src, dst, load_sem.at[n])
        for n, (src, dst) in enumerate(
            ((qkv_in, qkv), (dense_in, u_att.at[:, pl.ds(3 * D, D)]), (tok_in, tok), (grad_in, grad))
        )
    ]
    start(loads)
    plan = small_plan(r)
    for (row, size, _), ref in zip(plan, (v0, v1, v2, v3, v4, v5, v6)):
        value = ref[...].astype(F32).reshape(1, size)
        for k in range(-(-size // LANES)):
            width = min(LANES, size - k * LANES)
            small[row + k : row + k + 1, :width] = value[:, k * LANES : k * LANES + width]
    loads[0].wait()
    left = lax.broadcasted_iota(jnp.int32, (r, LANES), 1) < HD
    for p in range(PAIRS):
        parts = [qkv[:, (3 * p + k) * LANES : (3 * p + k + 1) * LANES].astype(F32) for k in range(3)]
        kinds = (
            jnp.where(left, parts[0], parts[1]),
            pltpu.roll(jnp.where(left, parts[2], parts[0]), HD, 1),
            jnp.where(left, parts[1], parts[2]),
        )
        for k, part in enumerate(kinds):
            u_att[:, k * D + p * LANES : k * D + (p + 1) * LANES] = part.astype(BF)
    for copy in loads[1:]:
        copy.wait()
    gs = (g_att, g_up, g_down)
    us = (u_att, u_up, u_down)
    locals_ = []
    for t, (g, i) in enumerate(CHUNKS):
        locals_.append(
            pltpu.make_async_copy(
                shard_view(lay, us[g], g, i, c, x), view(lay, gs[g], g, i, c, x, z, y), local_sem.at[t]
            )
        )
    locals_.append(pltpu.make_async_copy(small, g_small.at[z, y], local_sem.at[n_chunks]))
    start(locals_)
    wait_greetings(peers)
    even = lax.rem(b, 2) == 0
    half = rows // 2
    halo, own, passed = [], [], []
    for k in range(2):
        part = pl.ds(k * half, half)
        halo.append(remote(tok.at[part], tok_halo.at[0, part], h_s.at[k], h_r.at[k], around[0]))
        own.append(remote(tok.at[part], tok_halo.at[1, part], h_s.at[2 + k], h_r.at[2 + k], around[2]))
        passed.append(
            remote(tok_halo.at[0, part], tok_halo.at[1, part], h_s.at[2 + k], h_r.at[2 + k], around[3])
        )
    segs = [
        remote(seg, seg_halo.at[0], h_s.at[4], h_r.at[4], around[0]),
        remote(seg, seg_halo.at[1], h_s.at[5], h_r.at[5], around[2]),
    ]
    small_z = [
        remote(small, g_small.at[z, y], sm_s.at[k], sm_r.at[k], p) for k, p in enumerate(zs)
    ]
    small_y = [
        remote(g_small.at[:, y], g_small.at[:, y], sm_s.at[lay.nz + k], sm_r.at[lay.nz + k], p)
        for k, p in enumerate(ys)
    ]
    net = Gather(lay, us, gs, (z_s, z_r, y_s, y_r, x_s, x_r, c_s, c_r))
    net.issue(0, 0)
    net.issue(2, 0)
    start(small_z)
    start(segs)
    net.issue(1, 0)

    def tables(k, carry):
        at = pl.ds(pl.multiple_of(k * 256, 256), 256)
        lane = lax.broadcasted_iota(jnp.int32, (256, LANES), 1) % HD
        row = lax.broadcasted_iota(jnp.int32, (256, LANES), 0) + k * 256
        place = lax.rem((b - 2) * rows + row + 4 * ROW, ROW).astype(F32)
        rate = jnp.exp((lane % 8).astype(F32) * (-math.log(10000.0) / 8.0))
        angle = place * rate
        sine = jnp.sin(angle)
        cos_s[at, :] = jnp.where(lane < ROT, jnp.cos(angle), 1.0)
        low_s[at, :] = jnp.where(lane < 8, -sine, 0.0)
        high_s[at, :] = jnp.where((lane >= 8) & (lane < ROT), sine, 0.0)
        return carry

    lax.fori_loop(0, 2, tables, 0)
    for t in (0, 2, 1, n_chunks):
        locals_[t].wait()
    net.pass_on(0, 1)
    lax.fori_loop(2, 3, tables, 0)
    net.pass_on(2, 1)
    lax.fori_loop(3, 5, tables, 0)
    arrive(small_z)
    start(small_y)
    net.pass_on(0, 2)
    net.pass_on(1, 1)
    halo[0].start()
    lax.fori_loop(5, span // 256, tables, 0)
    arrive(small_y)
    net.pass_on(2, 2)

    lane_row = lax.broadcasted_iota(jnp.int32, (1, LANES), 1)

    def line(first_row, size, unit, length, source):
        out = []
        for block in range(length // LANES):
            value = None
            for k in range(LANES // unit):
                owner, local = divmod(source(block * (LANES // unit) + k), size // unit)
                row, lane = divmod(local * unit, LANES)
                row += first_row
                piece = g_small[owner // lay.ny, owner % lay.ny, row : row + 1, :]
                if lane != k * unit:
                    piece = pltpu.roll(piece, (k * unit - lane) % LANES, 1)
                value = piece if value is None else jnp.where(lane_row // unit == k, piece, value)
            out.append(value)
        return jnp.concatenate(out, 1)

    def norm_rows(values):
        return norm_parts(values.astype(F32))[0]

    for j in range(5):
        vectors[j : j + 1, :] = line(*plan[j], D, lambda n: n)
    vectors[5:8, :] = jnp.zeros((3, D), F32)
    unit = plan[5][2]
    a_head = HD // unit

    def natural(n):
        kind, rest = divmod(n, D // unit)
        head, part = divmod(rest, a_head)
        return head * 3 * a_head + kind * a_head + part

    qkv_add[...] = line(*plan[5], 3 * D, natural)
    net.pass_on(1, 2)
    up_add[...] = line(*plan[6], FF, lambda n: n)

    def pass_halo(k):
        arrive([halo[k]])

        @pl.when(even)
        def _():
            own[k].start()

        @pl.when(jnp.logical_not(even))
        def _():
            passed[k].start()

    halo[1].start()
    gain, shift = vectors[0:1, :], vectors[1:2, :]
    own_rows = pl.ds(2 * rows, rows)
    first = (norm_rows(tok[...]) * gain + shift).astype(BF)
    first_all[own_rows, :] = first
    pass_halo(0)
    arrive(segs)
    least = jnp.maximum(0, 2 * rows - b * rows)
    keys_doc = jnp.concatenate([seg_halo[0], seg_halo[1], seg[...]], 1).astype(F32)
    keys_doc = jnp.broadcast_to(keys_doc, (LANES, span)).T
    query_doc = seg[0:1, :].astype(F32)

    for k in range(6):
        at = slice(k * 256, (k + 1) * 256)
        key_at = lax.broadcasted_iota(jnp.int32, (256, rows), 0) + k * 256
        query_at = lax.broadcasted_iota(jnp.int32, (256, rows), 1) + 2 * rows
        allowed = (keys_doc[at, 0:1] == query_doc) & (key_at <= query_at) & (key_at >= least)
        bias[at, :] = jnp.where(allowed, 0.0, -1e30)
    for t in range(3, n_chunks):
        locals_[t].wait()
    net.issue(5, 0)
    net.pass_on(0, 3)
    net.pass_on(2, 3)
    net.issue(3, 0)

    def weight(first_col, width):
        value = g_att[:, :, :, pl.ds(first_col, width)]
        return value.reshape(D, width)

    scale = 1.0 / math.sqrt(HD)

    def project(kind, j, at, out, factor):
        col = pl.multiple_of(kind * D + 256 * j, 256)
        value = mm(first_all[at, :], weight(col, 256)) + qkv_add[:, pl.ds(col, 256)]
        for k in range(2):
            u = value[:, k * LANES : (k + 1) * LANES]
            if kind < 2:
                u = rope(u, cos_s[at, :], low_s[at, :], high_s[at, :])
            if factor is not None:
                u = u * factor
            out[:, pl.ds(pl.multiple_of(256 * j + LANES * k, LANES), LANES)] = u.astype(BF)

    def own_queries(j, carry):
        project(0, j, own_rows, q_s, scale)
        return carry

    def own_keys(j, carry):
        project(1, j, own_rows, k_s.at[own_rows], None)
        return carry

    def own_values(j, carry):
        project(2, j, own_rows, v_s.at[own_rows], None)
        return carry

    net.done(0)
    lax.fori_loop(0, 3, own_queries, 0)
    lax.fori_loop(0, 1, own_keys, 0)
    pass_halo(1)
    net.pass_on(1, 3)
    net.issue(4, 0)
    net.done(2)
    do_s[...] = mm(grad[...], weight(3 * D, D), NT).astype(BF)
    lax.fori_loop(2, 3, own_values, 0)
    net.pass_on(5, 1)
    net.done(1)
    lax.fori_loop(1, 3, own_keys, 0)
    lax.fori_loop(0, 2, own_values, 0)
    own[0].wait_recv()
    net.pass_on(3, 1)

    def earlier_norms(k):
        for n in range(2):
            near = pl.ds(k * half, half)
            before = norm_rows(tok_halo[n, near, :]) * gain + shift
            first_all[pl.ds(n * rows + k * half, half), :] = before.astype(BF)

    earlier_norms(0)
    net.issue(8, 0)
    own[1].wait_recv()
    earlier_norms(1)
    net.pass_on(4, 1)
    net.pass_on(5, 2)

    def earlier_projections(j, carry):
        for k in range(2):
            at = pl.ds(k * rows, rows)
            project(1, j, at, k_s.at[at], None)
            project(2, j, at, v_s.at[at], None)
        return carry

    lax.fori_loop(0, 3, earlier_projections, 0)
    net.pass_on(3, 2)
    net.issue(6, 0)

    go, send, end = net.pass_on, net.issue, net.done
    later = [
        [(go, 8, 1), (send, 7, 0), (go, 4, 2)],
        [(go, 5, 3), (go, 6, 1), (go, 3, 3), (go, 7, 1)],
        [(go, 8, 2), (go, 6, 2)],
        [(go, 4, 3), (go, 7, 2)],
        [(go, 8, 3)],
        [(go, 6, 3)],
    ]
    tile = 256

    def pair(p, carry):
        lanes = pl.ds(pl.multiple_of(p * LANES, LANES), LANES)
        v_t, k_t = v_s[:, lanes].T, k_s[:, lanes].T
        do_t = do_s[:, lanes].astype(F32).T
        lane = lax.broadcasted_iota(jnp.int32, (tile, LANES), 1)
        zero = jnp.zeros((), BF)
        units = [(t, hh) for t in range(rows // tile) for hh in range(2)]
        count = len(units)
        tops, totals, norms = [None] * count, [None] * count, [None] * count
        outs, dqs = [None] * count, [None] * count
        written = set()

        def masked(ref, u):
            t, hh = units[u]
            return jnp.where((lane // HD) == hh, ref[t * tile : (t + 1) * tile, lanes], zero)

        def pieces(u):
            kl = 2 * rows + (units[u][0] + 1) * tile
            return [slice(k * LANES, (k + 1) * LANES) for k in range(kl // LANES)]

        def scores(u, at, qm):
            t = units[u][0]
            st = mm(k_s[at, lanes], qm, NT) + bias[at, t * tile : (t + 1) * tile]
            s_s[u % 2, at, :] = st
            most = jnp.max(st, 0, keepdims=True)
            tops[u] = most if tops[u] is None else jnp.maximum(tops[u], most)

        def exponents(u, at):
            e = jnp.exp(s_s[u % 2, at, :] - tops[u])
            s_s[u % 2, at, :] = e
            part = jnp.sum(e, 0, keepdims=True)
            totals[u] = part if totals[u] is None else totals[u] + part

        def key_value_grads(u, at, qm, dom):
            dk, dv = mm(d_s[u % 2, at, :], qm), mm(w_s[u % 2, at, :], dom)
            if at.start in written:
                dk_acc[at, :] += dk
                dv_acc[at, :] += dv
            else:
                dk_acc[at, :] = dk
                dv_acc[at, :] = dv
                written.add(at.start)

        qm = masked(q_s, 0)
        for at in pieces(0):
            scores(0, at, qm)
        for u in range(count):
            t, hh = units[u]
            part = slice(hh * HD, (hh + 1) * HD)
            cols = slice(t * tile, (t + 1) * tile)
            kl = 2 * rows + (t + 1) * tile
            mine = pieces(u)
            after = pieces(u + 1) if u + 1 < count else []
            before = pieces(u - 1) if u > 0 else []
            if after:
                qm = masked(q_s, u + 1)
            for k in range(max(len(mine), len(after))):
                if k < len(after):
                    scores(u + 1, after[k], qm)
                if k < len(mine):
                    exponents(u, mine[k])
            norms[u] = 1.0 / totals[u]
            if before:
                q_last, do_last = masked(q_s, u - 1), masked(do_s, u - 1)
            for k in range(max(len(mine), len(before))):
                if k < len(before):
                    key_value_grads(u - 1, before[k], q_last, do_last)
                if k < len(mine):
                    w_s[u % 2, mine[k], :] = (s_s[u % 2, mine[k], :] * norms[u]).astype(BF)
            o_t = mm(v_t[part, :kl], w_s[u % 2, :kl, :])
            delta = jnp.sum(o_t * do_t[part, cols], 0, keepdims=True)
            outs[u] = o_t
            dom = masked(do_s, u)
            for at in mine:
                dp = mm(v_s[at, lanes], dom, NT)
                d_s[u % 2, at, :] = ((s_s[u % 2, at, :] * norms[u]) * (dp - delta)).astype(BF)
            dqs[u] = mm(k_t[part, :kl], d_s[u % 2, :kl, :])
            if hh == 0:
                continue
            o_pair = jnp.concatenate(outs[u - 1 : u + 1], 0)
            ctx_t[lanes, cols] = o_pair.astype(BF)
            ctx_s[cols, lanes] = o_pair.T.astype(BF)
            dq = jnp.concatenate(dqs[u - 1 : u + 1], 0).T * scale
            at = slice(2 * rows + t * tile, 2 * rows + (t + 1) * tile)
            dq_s[cols, lanes] = rope(dq, cos_s[at, :], -low_s[at, :], -high_s[at, :]).astype(BF)
        q_last, do_last = masked(q_s, count - 1), masked(do_s, count - 1)
        for at in pieces(count - 1):
            key_value_grads(count - 1, at, q_last, do_last)
        dk_s[:, lanes] = rope(dk_acc[...], cos_s[...], -low_s[...], -high_s[...]).astype(BF)
        dv_s[:, lanes] = dv_acc[...].astype(BF)
        for k in range(PAIRS):

            @pl.when(p == k)
            def _(k=k):
                for event, *where in later[k]:
                    event(*where)

        return carry

    lax.fori_loop(0, PAIRS, pair, 0)

    sums = Reduce(
        lay, (p_att,), None, ((ca,), (ra1,), (rb1,), None, None, None, None, None),
        (rc_s, rc_r, rx_s, rx_r, ry_s, ry_r) + (None,) * 6, {0: (0, 1), 1: (0,), 2: (0, 1)},
    )
    outs = []

    def leave(i):
        cols = pl.ds(1024 * i, 1024)
        copy = pltpu.make_async_copy(p_att.at[:, :, :, cols], p_out.at[:, :, :, cols], out_sem.at[i])
        copy.start()
        outs.append(copy)

    def put(kind, j, value):
        p_att[:, :, :, kind * D + 256 * j : kind * D + 256 * (j + 1)] = value.astype(BF).reshape(
            lay.nz, lay.ny, r, 256
        )

    def tile_of(ref, j):
        return ref[:, slice(256 * j, 256 * (j + 1))]

    def weight_grad(kind, j):
        if kind == 0:
            put(0, j, mm(first_all[own_rows, :], tile_of(dq_s, j), TN))
        elif kind == 3:
            put(3, j, mm(ctx_t[...], tile_of(grad, j)))
        else:
            put(kind, j, mm(first_all[...], tile_of((dk_s, dv_s)[kind - 1], j), TN))

    for kind, j in ((1, 0), (0, 0), (0, 1), (0, 2)):
        weight_grad(kind, j)
    sums.step(0, 0)
    for kind, j in ((2, 2), (3, 0), (3, 1), (3, 2)):
        weight_grad(kind, j)
    sums.step(0, 1)
    sums.step(2, 0)
    net.pass_on(7, 3)
    for kind, j in ((1, 1), (1, 2)):
        weight_grad(kind, j)
    sums.step(2, 1)
    for kind, j in ((2, 0), (2, 1)):
        weight_grad(kind, j)
    sums.step(1, 0)

    def earlier_grad(k, carry):
        at = pl.ds(pl.multiple_of(k * 256, 256), 256)
        value = mm(dk_s[at, :], weight(D, D), NT) + mm(dv_s[at, :], weight(2 * D, D), NT)
        fg_prev[at, :] = value.astype(BF)
        return carry

    lax.fori_loop(0, 2 * rows // 256, earlier_grad, 0)
    outs.append(pltpu.make_async_copy(fg_prev, prev_out, out_sem.at[3]))
    outs[-1].start()
    sums.settle(1, 1)
    leave(1)
    for k in range(rows // 256):
        at = slice(2 * rows + 256 * k, 2 * rows + 256 * (k + 1))
        near = slice(256 * k, 256 * (k + 1))
        fg_own[near, :] = (
            mm(dk_s[at, :], weight(D, D), NT)
            + mm(dv_s[at, :], weight(2 * D, D), NT)
            + mm(dq_s[near, :], weight(0, D), NT)
        )
    outs.append(pltpu.make_async_copy(fg_own, own_out, out_sem.at[4]))
    outs[-1].start()

    def attention_out(j, carry):
        col = pl.multiple_of(256 * j, 256)
        attn_out[:, pl.ds(col, 256)] = mm(ctx_s[...], weight(pl.multiple_of(3 * D + col, 256), 256))
        return carry

    lax.fori_loop(0, 3, attention_out, 0)
    outs.append(pltpu.make_async_copy(attn_out, attn_hbm, out_sem.at[5]))
    outs[-1].start()
    for k, ref in enumerate((dq_s, dk_s, dv_s)):
        att_sums[k : k + 1, :] = jnp.sum(ref[...].astype(F32), 0, keepdims=True)
    att_sums[3:8, :] = jnp.zeros((5, D), F32)
    sums.settle(0, 2)
    leave(0)
    sums.settle(2, 2)
    leave(2)
    sums.drain()
    for t in range(3, 9):
        net.done(t)
    net.drain()
    sent(small_z + small_y + segs + halo + own)
    for copy in outs:
        copy.wait()


def front(lay, u_up, u_down, qkv, dense, tok, grad, seg, vectors):
    rows = tok.shape[0]
    span = 3 * rows
    r = qkv.shape[0]
    n = len(CHUNKS)
    outs = (
        jax.ShapeDtypeStruct(grad_shape(lay, 1, r), BF),
        jax.ShapeDtypeStruct(grad_shape(lay, 2, r), BF),
        jax.ShapeDtypeStruct(grad_shape(lay, 0, r), BF),
        jax.ShapeDtypeStruct((2 * rows, D), BF),
        jax.ShapeDtypeStruct((rows, D), F32),
        jax.ShapeDtypeStruct((rows, D), F32),
        jax.ShapeDtypeStruct((8, D), F32),
        jax.ShapeDtypeStruct((1, FF), F32),
        jax.ShapeDtypeStruct((8, D), F32),
    )
    vmem = pl.BlockSpec(memory_space=pltpu.VMEM)
    lx, ly, lz = max(1, lay.nx - 1), max(1, lay.ny - 1), max(1, lay.nz - 1)

    def v(shape, dtype=BF):
        return pltpu.VMEM(shape, dtype)

    return pl.pallas_call(
        functools.partial(front_kernel, lay, rows),
        name="front",
        out_shape=outs,
        in_specs=hbm(6) + [vmem] * (1 + len(vectors)),
        out_specs=tuple(hbm(6)) + (vmem,) * 3,
        scratch_shapes=[
            v((r, 3 * D)), v((rows, D)), v((rows, D)), v((SMALL_ROWS, LANES), F32), v((r, 4 * D)), v(grad_shape(lay, 0, r)), v((2 * rows, D)), v((rows, D), F32), v((rows, D), F32),
            v(grad_shape(lay, 0, r)), v((lay.nz, lay.ny, SMALL_ROWS, LANES), F32), v((2, rows, D)),
            v((2, 1, rows), jnp.int32), v((span, D)), v((rows, D)), v((span, D)),
            v((span, D)), v((rows, D)), v((rows, D)), v((D, rows)), v((rows, D)), v((span, D)),
            v((span, D)), v((span, LANES), F32), v((span, LANES), F32), v((span, LANES), F32),
            v((span, rows), F32), v((span, LANES), F32), v((span, LANES), F32), v((1, 3 * D), F32),
            v((2, span, 256), F32), v((2, span, 256)), v((2, span, 256)),
            dma(n + 1), dma(n, lz), dma(n, lz), dma(n, ly), dma(n, ly), dma(n, lx), dma(n, lx),
            dma(n), dma(n), dma(lay.nz + ly), dma(lay.nz + ly), dma(6), dma(6), dma(6),
            v((3,) + part_shape(lay, 0, True, True, True, r)),
            v((1, lx) + part_shape(lay, 0, False, True, True, r)),
            v((1, ly) + part_shape(lay, 0, True, True, False, r)),
            dma(3), dma(3), dma(3, lx), dma(3, lx), dma(3, ly), dma(3, ly), dma(4),
        ],
        compiler_params=pltpu.CompilerParams(
            collective_id=0, has_side_effects=True, vmem_limit_bytes=VMEM_LIMIT
        ),
    )(u_up, u_down, qkv, dense, tok, grad, seg, *vectors)


def norm_back(grad, gain, normed, factor):
    inner = grad * gain
    return factor * (
        inner
        - jnp.mean(inner, -1, keepdims=True)
        - normed * jnp.mean(inner * normed, -1, keepdims=True)
    )


FF_CHUNKS = FF // D


def back_kernel(
    lay, rows, docs,
    g_up, g_down, p_in, prev_in, own_in, attn_in, tok_in, grad_in, vectors, up_add, att_sums, seg,
    out_hbm, input_hbm, att_hbm, up_hbm, down_hbm, vec_out,
    tok, grad, output, input_grad, f_att, f_up, f_down, p_att, fg_prev, fg_own, attn_out, p_up, p_down, w_up, w_down, second_in, second_t, act_s, pg_s, sg_acc, hop, home,
    ca, ra1, rb1, ra2, rb2, ra3, rz, rx, v_c, v_x, v_y, v_z, *sems,
):
    (c_s, c_r, x_s, x_r, y_s, y_r, z_s, z_r, fx_s, fx_r, fc_s, fc_r, v_s, v_r, w_sem, h_s, h_r, in_sem, out_sem) = sems
    r = p_in.shape[2]
    x, c, z, y = lay.coords()
    xs, cs, zs, ys = line_peers(lay)
    total = lay.dp * lay.fsdp
    b = lax.axis_index("dp") * lay.fsdp + lax.axis_index("fsdp")

    def stream(k):
        t = wrap(b + k, total)
        return {"dp": t // lay.fsdp, "fsdp": lax.rem(t, lay.fsdp)}

    around = [stream(2), stream(-2), stream(1), stream(-1)]
    near_z = lay.nz // FF_CHUNKS
    loads = []
    for k in range(FF_CHUNKS):
        slot = k % 2
        loads.append(
            (
                pltpu.make_async_copy(
                    g_up.at[:, :, :, pl.ds(D * k, D)], w_up.at[slot], w_sem.at[0, k]
                ),
                pltpu.make_async_copy(
                    g_down.at[pl.ds(near_z * k, near_z)], w_down.at[slot], w_sem.at[1, k]
                ),
            )
        )
    peers = xs + cs + zs + ys + around
    greet(peers)
    taken = [
        pltpu.make_async_copy(
            p_in.at[:, :, :, pl.ds(1024 * i, 1024)], p_att.at[:, :, :, pl.ds(1024 * i, 1024)],
            in_sem.at[i],
        )
        for i in range(3)
    ]
    taken.append(pltpu.make_async_copy(prev_in, fg_prev, in_sem.at[3]))
    taken.append(pltpu.make_async_copy(attn_in, attn_out, in_sem.at[4]))
    taken.append(pltpu.make_async_copy(own_in, fg_own, in_sem.at[5]))
    taken.append(pltpu.make_async_copy(tok_in, tok, in_sem.at[6]))
    taken.append(pltpu.make_async_copy(grad_in, grad, in_sem.at[7]))
    start(taken[:4])
    start(taken[6:])
    start(loads[0])
    start(taken[4:6])
    start(loads[1])
    wait_greetings(peers)
    wanted = {t: (0, 1, 2, 3) for t in range(3, len(CHUNKS))}
    wanted.update({0: (2, 3), 1: (1, 2, 3), 2: (2, 3)})
    net = Reduce(
        lay, (p_att, p_up, p_down), (f_att, f_up, f_down),
        ((None,) + tuple(ca), ra1, (None,) + tuple(rb1), ra2, rb2, ra3, rz, rx), sems[:12], wanted,
    )
    for t, k in ((1, 1), (2, 2), (0, 2)):
        taken[t].wait()
        net.begin(t, k)
    taken[3].wait()
    even = lax.rem(b, 2) == 0
    quarter = rows // 4
    to_next, to_last, to_owner = [], [], []
    for k in range(4):
        near = fg_prev.at[pl.ds(rows + k * quarter, quarter)]
        far = fg_prev.at[pl.ds(k * quarter, quarter)]
        part = pl.ds(k * quarter, quarter)
        to_next.append(remote(near, hop.at[part], h_s.at[k], h_r.at[k], around[2]))
        to_last.append(remote(near, hop.at[part], h_s.at[k], h_r.at[k], around[3]))
        to_owner.append(remote(far, home.at[part], h_s.at[4 + k], h_r.at[4 + k], around[1]))

    def hop_halo(k):
        @pl.when(even)
        def _():
            to_next[k].start()

        @pl.when(jnp.logical_not(even))
        def _():
            to_last[k].start()

    def forward_halo(k):
        to_last[k].wait_recv()
        at = pl.ds(k * quarter, quarter)

        @pl.when(jnp.logical_not(even))
        def _():
            fg_prev[at, :] = (fg_prev[at, :].astype(F32) + hop[at, :].astype(F32)).astype(BF)

        to_owner[k].start()

    hop_halo(0)
    hop_halo(1)

    gain_first, gain_second = vectors[0:1, :], vectors[2:3, :]
    taken[6].wait()
    taken[7].wait()
    normed, factor = norm_parts(tok[...].astype(F32))
    value = (normed * gain_second + vectors[3:4, :]).astype(BF)
    second_in[...] = value
    second_t[...] = value.T
    cot = grad[...].astype(F32)
    taken[4].wait()
    taken[5].wait()
    output_base = attn_out
    output_base[...] = attn_out[...] + tok[...].astype(F32) + vectors[4:5, :]
    sg_acc[...] = jnp.zeros_like(sg_acc)
    mine = v_c.at[c]
    mine[...] = jnp.zeros((16, D), F32)

    step = net.step
    events = [
        [],
        [(step, 0, 3)],
        [(hop_halo, 2)],
        [(step, 3, 0), (step, 1, 2), (forward_halo, 0)],
        [(step, 3, 1), (step, 2, 3), (hop_halo, 3)],
        [(step, 4, 0), (forward_halo, 1)],
        [(step, 4, 1), (step, 0, 4)],
        [(step, 8, 0), (step, 6, 0), (step, 5, 0), (step, 7, 0), (step, 2, 4)],
    ]
    root = math.sqrt(0.5)
    level = 1.0 / math.sqrt(2.0 * math.pi)

    def chunk(k, squares):
        slot = lax.rem(k, 2)
        for n in range(FF_CHUNKS):

            @pl.when(k == n)
            def _(n=n):
                loads[n][0].wait()
                loads[n][1].wait()

        down = w_down[slot].reshape(D, D)
        for j in range(3):
            tile = slice(256 * j, 256 * (j + 1))
            col = pl.ds(pl.multiple_of(D * k + 256 * j, 256), 256)
            pre = mm(second_in[...], w_up[slot, :, :, :, tile].reshape(D, 256)) + up_add[:, col]
            hidden = mm(grad[...], down[tile, :], NT)
            half = 0.5 + 0.5 * lax.erf(pre * root)
            act = (pre * half).astype(BF)
            slope = half + pre * jnp.exp(-0.5 * pre * pre) * level
            pg = (hidden * slope).astype(BF)
            act_s[:, tile] = act
            pg_s[:, tile] = pg
            wide = act.astype(F32)
            squares = squares + jnp.sum(wide * wide, -1, keepdims=True)
            v_c[c, pl.ds(8 + k, 1), tile] = jnp.sum(pg.astype(F32), 0, keepdims=True)

        def hook(half):
            for n in range(FF_CHUNKS):

                @pl.when(k == n)
                def _(n=n):
                    if half == 1 and n + 2 < FF_CHUNKS:
                        start(loads[n + 2])
                    for event, *where in events[2 * n + half]:
                        event(*where)

        hook(0)
        p_up[:, :, :, pl.ds(pl.multiple_of(D * k, 256), D)] = (
            mm(second_t[...], pg_s[...]).astype(BF).reshape(lay.nz, lay.ny, r, D)
        )
        p_down[pl.ds(near_z * k, near_z)] = (
            mm(act_s[...].T, grad[...]).astype(BF).reshape(near_z, lay.ny, 4, r, D)
        )
        output_base[...] += mm(act_s[...], down)
        sg_acc[...] += mm(pg_s[...], w_up[slot].reshape(D, D), NT)
        hook(1)
        return squares

    squares = lax.fori_loop(0, FF_CHUNKS, chunk, jnp.zeros((rows, 1), F32))
    run = lambda *pairs: [step(t, k) for t, k in pairs]
    run((8, 1), (6, 1), (3, 2), (1, 3))
    output[...] = output_base[...].astype(BF)
    left = []

    def leave(k, ref, target):
        copy = pltpu.make_async_copy(ref, target, out_sem.at[k])
        copy.start()
        left.append(copy)

    leave(0, output, out_hbm)
    forward_halo(2)
    cot_sum = jnp.sum(grad[...].astype(F32), 0, keepdims=True)
    forward_halo(3)
    def put(k, value):
        v_c[c, k : k + 1, :] = value

    put(4, cot_sum)
    for k in range(3):
        put(5 + k, att_sums[k : k + 1, :])
    cot = grad[...].astype(F32)
    token_norm = squares * jnp.sum(cot * cot, -1, keepdims=True) * (1.0 / (FF * D))
    docs_of = jnp.broadcast_to(seg[...].astype(F32), (LANES, rows)).T[:, 0:1]
    doc = lax.broadcasted_iota(jnp.int32, (rows, D), 1).astype(F32)
    member = jnp.where((docs_of == doc) & (doc < docs), 1.0, 0.0)
    put(12, jnp.sum(token_norm * member, 0, keepdims=True))
    put(13, jnp.sum(member, 0, keepdims=True))
    run((4, 2), (5, 1), (7, 1), (8, 2), (1, 4))
    keep = jnp.where(even, 1.0, 0.0).astype(F32)

    def norms(k):
        to_owner[k].wait_recv()
        at = slice(k * quarter, (k + 1) * quarter)
        first_grad = fg_own[at, :] + home[at, :].astype(F32) + hop[at, :].astype(F32) * keep
        second_grad = sg_acc[at, :]
        normed, factor = norm_parts(tok[at, :].astype(F32))
        input_grad[at, :] = (
            grad[at, :].astype(F32)
            + norm_back(first_grad, gain_first, normed, factor)
            + norm_back(second_grad, gain_second, normed, factor)
        ).astype(BF)
        sums = [first_grad * normed, first_grad, second_grad * normed, second_grad]
        return [jnp.sum(value, 0, keepdims=True) for value in sums]

    def add_up(left, right):
        return [p + q for p, q in zip(left, right)]

    sums = norms(0)
    run((3, 3))
    sums = add_up(sums, norms(1))
    run((6, 2))
    sums = add_up(sums, norms(2))
    run((4, 3))
    sums = add_up(sums, norms(3))
    leave(1, input_grad, input_hbm)
    for k in range(4):
        put(k, sums[k])
    run((8, 3))

    at = [0, 1, lay.nx, lay.nx + lay.ny - 1]

    def spread(ref, own, peers, base):
        return [
            remote(ref.at[own], ref.at[own], v_s.at[base + k], v_r.at[base + k], p)
            for k, p in enumerate(peers)
        ]

    vec_c = spread(v_c, c, cs, at[0])
    vec_x = spread(v_x, x, xs, at[1])
    vec_y = spread(v_y, y, ys, at[2])
    vec_z = spread(v_z, z, zs, at[3])

    def add_all(ref, size):
        value = ref[0]
        for k in range(1, size):
            value = value + ref[k]
        return value

    start(vec_c)
    run((5, 2))
    arrive(vec_c)
    v_x[x] = add_all(v_c, 2)
    start(vec_x)
    run((7, 2), (6, 3), (5, 3), (3, 4), (7, 3))
    arrive(vec_x)
    v_y[y] = add_all(v_x, lay.nx)
    start(vec_y)
    run((4, 4), (8, 4))
    arrive(vec_y)
    v_z[z] = add_all(v_y, lay.ny)
    start(vec_z)
    run((0, 5), (1, 5), (2, 5), (3, 5), (4, 5), (6, 4), (5, 4), (6, 5), (5, 5))
    run((0, 6), (1, 6), (2, 6))
    leave(2, f_att, att_hbm)
    run((7, 4), (3, 6), (4, 6), (5, 6))
    leave(3, f_up, up_hbm)
    arrive(vec_z)
    vec_out[...] = add_all(v_z, lay.nz)
    run((8, 5), (7, 5), (6, 6), (8, 6), (7, 6))
    leave(4, f_down, down_hbm)
    net.drain()
    sent(vec_c + vec_x + vec_y + vec_z)
    sent(to_next + to_owner)
    for copy in left:
        copy.wait()


def back(lay, g_up, g_down, p_att, fg_prev, fg_own, attn_out, vectors, up_add, att_sums, tok, grad, seg):
    rows = tok.shape[0]
    r = p_att.shape[2]
    n = len(CHUNKS)
    docs = DOC_DEV * lay.dp * lay.fsdp
    outs = (
        jax.ShapeDtypeStruct((rows, D), BF),
        jax.ShapeDtypeStruct((rows, D), BF),
        jax.ShapeDtypeStruct((r, 4 * D), BF),
        jax.ShapeDtypeStruct((r, 4 * D), BF),
        jax.ShapeDtypeStruct((4, r, D), BF),
        jax.ShapeDtypeStruct((16, D), F32),
    )
    lx, ly, lz = max(1, lay.nx - 1), max(1, lay.ny - 1), max(1, lay.nz - 1)

    def v(shape, dtype=BF):
        return pltpu.VMEM(shape, dtype)

    def bufs(chunks, peers, x_all, z_all, y_all, first=0):
        return [
            v((chunks,) + peers + part_shape(lay, g, x_all, z_all, y_all, r)) for g in range(first, 3)
        ]

    scratch = [
        v((rows, D)), v((rows, D)), v((rows, D)), v((rows, D)), v((r, 4 * D)), v((r, 4 * D)), v((4, r, D)),
        v(grad_shape(lay, 0, r)), v((2 * rows, D)), v((rows, D), F32), v((rows, D), F32),
        v(grad_shape(lay, 1, r)), v(grad_shape(lay, 2, r)),
        v((2, lay.nz, lay.ny, r, D)), v((2, lay.nz // FF_CHUNKS, lay.ny, 4, r, D)),
        v((rows, D)), v((D, rows)), v((rows, D)), v((rows, D)), v((rows, D), F32),
        v((rows, D)), v((rows, D)),
        bufs(3, (), True, True, True, 1),
        bufs(2, (lx,), False, True, True),
        bufs(1, (ly,), True, True, False, 1),
        bufs(2, (ly,), False, True, False),
        bufs(1, (lx,), False, True, False),
        bufs(3, (lz,), False, False, False),
        v((lz,) + part_shape(lay, 2, True, False, False, r)),
        v((lay.nx,) + part_shape(lay, 2, True, False, False, r)),
    ]
    vecs = [v((k, 16, D), F32) for k in (2, lay.nx, lay.ny, lay.nz)]
    nv = 1 + lay.nx + lay.ny + lay.nz
    sems = [
        dma(n), dma(n), dma(n, lx), dma(n, lx), dma(n, ly), dma(n, ly), dma(n, lz), dma(n, lz),
        dma(n, lx), dma(n, lx), dma(n), dma(n), dma(nv), dma(nv), dma(2, FF_CHUNKS), dma(8), dma(8), dma(8), dma(5),
    ]
    vmem = pl.BlockSpec(memory_space=pltpu.VMEM)
    return pl.pallas_call(
        functools.partial(back_kernel, lay, rows, docs),
        name="back",
        out_shape=outs,
        in_specs=hbm(8) + [vmem] * 4,
        out_specs=tuple(hbm(5)) + (vmem,),
        scratch_shapes=scratch + vecs + sems,
        compiler_params=pltpu.CompilerParams(
            collective_id=1, has_side_effects=True, vmem_limit_bytes=VMEM_LIMIT
        ),
    )(g_up, g_down, p_att, fg_prev, fg_own, attn_out, tok, grad, vectors, up_add, att_sums, seg)


def finish_kernel(
    lay, docs, r, f_att, f_up, f_down, vec, out_in, grad_in,
    output, input_grad, fg, fb, sg, sb, qkv_w, qkv_b, dense_w, up_w, up_b, down_w, ob, norms,
):
    output[...] = out_in[...]
    input_grad[...] = grad_in[...]
    shard = lax.axis_index("fsdp")

    def by_head(row_count, kind):
        left = lax.broadcasted_iota(jnp.int32, (row_count, LANES), 1) < HD
        for p in range(PAIRS):
            q, k, v = (kind(n, p) for n in range(3))
            turned = pltpu.roll(k, HD, 1)
            yield jnp.where(left, q, turned)
            yield jnp.where(left, v, q)
            yield jnp.where(left, turned, v)

    def block(k, p):
        return f_att[:, k * D + p * LANES : k * D + (p + 1) * LANES].astype(F32)

    for n, value in enumerate(by_head(r, block)):
        qkv_w[:, n * LANES : (n + 1) * LANES] = value
    dense_w[...] = f_att[:, 3 * D :].astype(F32)
    up_w[...] = f_up[...].astype(F32)
    down_w[...] = f_down[...].astype(F32)

    def own(row, width):
        length = row.shape[1]
        wide = jnp.broadcast_to(row, (8, length))
        turned = pltpu.roll(wide, lax.rem(length - shard * width, length), 1)
        return turned[0:1, :width].reshape(width)

    for k, ref in enumerate((fg, fb, sg, sb, ob)):
        ref[...] = own(vec[k : k + 1, :], r)
    bias = list(by_head(1, lambda k, p: vec[5 + k : 6 + k, p * LANES : (p + 1) * LANES]))
    qkv_b[...] = own(jnp.concatenate(bias, 1), 3 * r)
    up_b[...] = own(jnp.concatenate([vec[8 + k : 9 + k, :] for k in range(4)], 1), 4 * r)
    norms[...] = (vec[12:13, :docs] / vec[13:14, :docs]).reshape(docs)


def finish(lay, output, input_grad, f_att, f_up, f_down, vec):
    r = f_att.shape[0]
    docs = DOC_DEV * lay.dp * lay.fsdp
    vmem = pl.BlockSpec(memory_space=pltpu.VMEM)
    shapes = [
        (r,), (r,), (r,), (r,), (r, 3 * D), (3 * r,), (r, D), (r, FF), (4 * r,), (4, r, D), (r,), (docs,),
    ]
    return pl.pallas_call(
        functools.partial(finish_kernel, lay, docs, r),
        name="finish",
        out_shape=tuple(jax.ShapeDtypeStruct(v.shape, v.dtype) for v in (output, input_grad))
        + tuple(jax.ShapeDtypeStruct(shape, F32) for shape in shapes),
        in_specs=[vmem] * 6,
        out_specs=(vmem,) * (2 + len(shapes)),
        compiler_params=pltpu.CompilerParams(vmem_limit_bytes=VMEM_LIMIT),
    )(f_att, f_up, f_down, vec, output, input_grad)


def per_device(
    lay, tokens, seg_ids, out_grad, first_gain, first_bias, second_gain, second_bias,
    qkv_weight, qkv_bias, dense_weight, up_weight, up_bias, down_weight, out_bias,
):
    rows = tokens.shape[0]
    r = qkv_weight.shape[0]
    vectors = (first_gain, first_bias, second_gain, second_bias, out_bias, qkv_bias, up_bias)
    seg_row = seg_ids.reshape(1, rows)
    passed = front(
        lay, up_weight, down_weight.reshape(4, r, D), qkv_weight, dense_weight, tokens,
        out_grad, seg_row, vectors,
    )
    summed = back(lay, *passed, tokens, out_grad, seg_row)
    (output, input_grad, fg, fb, sg, sb, qkv_w, qkv_b, dense_w, up_w, up_b, down_w, ob, norms) = finish(
        lay, *summed
    )
    return (
        output, input_grad, fg, fb, sg, sb, qkv_w, qkv_b, dense_w, up_w, up_b,
        down_w.reshape(4 * r, D), ob, norms,
    )


def solution(mesh):
    lay = Layout(mesh.shape["dp"], mesh.shape["fsdp"])
    both = P(("dp", "fsdp"))
    split = P("fsdp")
    in_specs = (both, both, both) + (split,) * 11
    out_specs = (both, both) + (split,) * 11 + (P(),)
    return jax.shard_map(
        functools.partial(per_device, lay), mesh=mesh, in_specs=in_specs, out_specs=out_specs,
        check_vma=False,
    )
```
